32 devices in a mesh: dp: 16 (over z, y, core), mp: 2 (over x).
Axes of the slice: x: 2, y: 2, z: 4, core: 2. Of those that a mesh axis runs over, the one named last changes fastest.
Arguments:
- tokens: bfloat16 [32, 1024, 1024], P('dp', 'mp'), may hold values from -6 to 6
- cotangent: bfloat16 [32, 1024, 1024], P('dp', 'mp'), may hold values from -6 to 6
- buckets: int32 [32], P('dp'), may hold values from 0 to 7
- counts: int32 [8], replicated, may hold values from 1000 to 3999
- lead_table: bfloat16 [8, 1024], replicated, may hold values from -3 to 3
- norm1_gain: bfloat16 [1024], replicated, may hold values from 0.25 to 1.75
- norm1_shift: bfloat16 [1024], replicated, may hold values from -1 to 1
- w_qkv: bfloat16 [1024, 3, 1024], P(None, None, 'mp'), may hold values from -0.1875 to 0.1875
- qv_bias: bfloat16 [2, 1024], P(None, 'mp'), may hold values from -0.59765625 to 0.59765625
- w_out: bfloat16 [1024, 1024], P('mp'), may hold values from -1.5 to 1.5
- out_bias: bfloat16 [1024], replicated, may hold values from -1 to 1
- norm2_gain: bfloat16 [1024], replicated, may hold values from 0.25 to 1.75
- norm2_shift: bfloat16 [1024], replicated, may hold values from -1 to 1
- w_fc1: bfloat16 [1024, 4096], P(None, 'mp'), may hold values from -0.1875 to 0.1875
- fc1_bias: bfloat16 [4096], P('mp'), may hold values from -1.5 to 1.5
- w_fc2: bfloat16 [4096, 1024], P('mp'), may hold values from -0.09375 to 0.09375
- fc2_bias: bfloat16 [1024], replicated, may hold values from -1 to 1
Outputs:
- block_output: bfloat16 [32, 1024, 1024], P('dp', 'mp')
- input_grad: float32 [32, 1024, 1024], P('dp', 'mp')
- lead_grad: float32 [8, 1024], replicated
- norm1_gain_grad: float32 [1024], replicated
- norm1_shift_grad: float32 [1024], replicated
- qkv_grad: float32 [1024, 3, 1024], P(None, None, 'mp')
- qv_bias_grad: float32 [2, 1024], P(None, 'mp')
- out_grad: float32 [1024, 1024], P('mp')
- out_bias_grad: float32 [1024], replicated
- norm2_gain_grad: float32 [1024], replicated
- norm2_shift_grad: float32 [1024], replicated
- fc1_grad: float32 [1024, 4096], P(None, 'mp')
- fc1_bias_grad: float32 [4096], P('mp')
- fc2_grad: float32 [4096, 1024], P('mp')
- fc2_bias_grad: float32 [1024], replicated
The draws below stay inside these ranges and needn't reach their ends.
All inputs are finite; a program needn't handle non-finite values.
Results may differ from the reference program's by a relative error of at most 0.02.
Values may be sent and summed in bfloat16 or wider, within the bound.
No kernel may reach another device: no remote copies, remote signals or barrier semaphores. Data moves between devices by JAX's collectives and lax.ppermute only.
A program may use at most 320 MiB of HBM per device.

```python
import jax
import jax.numpy as jnp
from jax import lax

D = 1024
H = 16
HD = 64
FF = 4096
SEQ = 1024
BUCKETS = 8
SAMPLES = 32


def place_ends(result, own_key, least, largest):
    spot = [jax.random.randint(jax.random.fold_in(own_key, axis), (), 0, length) for axis, length in enumerate(result.shape)]
    widest = result.shape.index(max(result.shape))
    next_to = spot[:widest] + [(spot[widest] + 1) % result.shape[widest]] + spot[widest + 1:]
    return result.at[tuple(spot)].set(least).at[tuple(next_to)].set(largest)


def steps_of(key, dims, shards, low, top_value):
    def one(dim, parts):
        draws = jax.random.uniform(jax.random.fold_in(jax.random.fold_in(key, 6), dim), (parts,), jnp.float32, low / len(shards), top_value / len(shards))
        return jnp.repeat(jnp.exp(draws), dims[dim] // parts).reshape((-1,) + (1,) * (len(dims) - dim - 1))

    factor_of = one(*shards[0])
    for cut in shards[1:]:
        factor_of = factor_of * one(*cut)
    return factor_of


def centred(stream_key, dims, deviation, reach, cuts=(), kind=jnp.bfloat16):
    result = jax.random.normal(stream_key, dims, jnp.float32) * deviation
    if len(cuts) > 0:
        result = steps_of(stream_key, dims, cuts, -0.22, 0.18) * result
    return jnp.clip(result, min=-reach, max=reach).astype(kind)


def setup_inputs(seed: int = 0) -> dict:
    streams_of = jax.random.split(jax.random.key(seed), 18)
    tokens = centred(streams_of[0], (SAMPLES, SEQ, D), 1.0, 6.0, ((0, 16), (1, 2)))
    cotangent = centred(streams_of[1], (SAMPLES, SEQ, D), 1.0, 6.0, ((0, 16), (1, 2)))
    buckets = place_ends(jax.random.randint(streams_of[2], (SAMPLES,), 0, BUCKETS), jax.random.fold_in(streams_of[2], 1), 0, BUCKETS - 1).astype(jnp.int32)
    counts = place_ends(jax.random.randint(streams_of[3], (BUCKETS,), 1000, 4000), jax.random.fold_in(streams_of[3], 1), 1000, 3999).astype(jnp.int32)
    lead_table = centred(streams_of[4], (BUCKETS, D), 0.5, 3.0)
    norm1_gain = jnp.clip(1.0 + 0.15 * jax.random.normal(streams_of[5], (D,), jnp.float32), 0.25, 1.75).astype(jnp.bfloat16)
    norm1_shift = centred(streams_of[6], (D,), 0.2, 1.0)
    w_qkv = centred(streams_of[7], (D, 3, D), D ** -0.5, 0.1875, ((2, 2),))
    qv_bias = centred(streams_of[8], (2, D), 0.1, 0.59765625, ((1, 2),))
    w_out = centred(streams_of[9], (D, D), (max(D // 64, 1)) ** -0.5, 1.5, ((0, 2),))
    out_bias = centred(streams_of[10], (D,), 0.2, 1.0)
    norm2_gain = jnp.clip(1.0 + 0.15 * jax.random.normal(streams_of[11], (D,), jnp.float32), 0.25, 1.75).astype(jnp.bfloat16)
    norm2_shift = centred(streams_of[12], (D,), 0.2, 1.0)
    w_fc1 = centred(streams_of[13], (D, FF), D ** -0.5, 0.1875, ((1, 2),))
    fc1_bias = centred(streams_of[14], (FF,), 0.3, 1.5, ((0, 2),))
    w_fc2 = centred(streams_of[15], (FF, D), FF ** -0.5, 0.09375, ((0, 2),))
    fc2_bias = centred(streams_of[16], (D,), 0.2, 1.0)
    return {"tokens": tokens, "cotangent": cotangent, "buckets": buckets, "counts": counts, "lead_table": lead_table, "norm1_gain": norm1_gain, "norm1_shift": norm1_shift, "w_qkv": w_qkv, "qv_bias": qv_bias, "w_out": w_out, "out_bias": out_bias, "norm2_gain": norm2_gain, "norm2_shift": norm2_shift, "w_fc1": w_fc1, "fc1_bias": fc1_bias, "w_fc2": w_fc2, "fc2_bias": fc2_bias}


@jax.custom_vjp
def low(v):
    return lax.optimization_barrier(v.astype(jnp.bfloat16)).astype(jnp.float32)

@jax.custom_vjp
def low_back(v):
    return v

def low_keep(v):
    return (low(v), None)

def low_pass(kept, grad):
    return (grad,)

def back_keep(v):
    return (v, None)

def back_low(kept, grad):
    return (low(grad),)
low.defvjp(low_keep, low_pass)
low_back.defvjp(back_keep, back_low)
EPS = 1e-05
HIGH = lax.Precision.HIGHEST

def layer_norm(values, norm_gain, norm_shift):
    center = values - lax.optimization_barrier(jnp.mean(values, axis=-1, keepdims=True))
    spread = lax.optimization_barrier(jnp.mean(center * center, axis=-1, keepdims=True))
    return center * lax.rsqrt(spread + EPS) * norm_gain + norm_shift

def attend_block(query_block, key_heads, value_heads):
    scores = low_back(jnp.einsum('hqd,hkd->hqk', query_block, key_heads, precision=HIGH) * 0.125)
    row_max = lax.optimization_barrier(jnp.max(scores, axis=-1, keepdims=True))
    powers = jnp.exp(scores - row_max)
    attn_weights = powers / lax.optimization_barrier(jnp.sum(powers, axis=-1, keepdims=True))
    return jnp.einsum('hqk,hkd->hqd', low(attn_weights), value_heads, precision=HIGH)

def split_heads(flat_rows):
    return flat_rows.reshape(SEQ, H, HD).transpose(1, 0, 2)

def sample_forward(sample_tokens, table, onehot, params):
    norm1_gain, norm1_shift, w_qkv, qv_bias, w_out, out_bias, norm2_gain, norm2_shift, w_fc1, fc1_bias, w_fc2, fc2_bias = params
    lead_row = jnp.dot(onehot, table, precision=HIGH, preferred_element_type=jnp.float32)
    shifted = sample_tokens + lead_row[None, :]
    normed_one = low(layer_norm(shifted, norm1_gain, norm1_shift))
    project = jnp.einsum('td,dcf->tcf', normed_one, w_qkv, precision=HIGH)
    query_rows = low_back(low(project[:, 0] + qv_bias[0]))
    key_rows = low_back(low(project[:, 1]))
    value_rows = low_back(low(project[:, 2] + qv_bias[1]))
    block_rows = min(512, SEQ)
    query_blocks = split_heads(query_rows).reshape(H, SEQ // block_rows, block_rows, HD).transpose(1, 0, 2, 3)
    key_heads = split_heads(key_rows)
    value_heads = split_heads(value_rows)

    def block_step(query_block):
        return attend_block(query_block, key_heads, value_heads)
    attended = lax.map(jax.checkpoint(block_step), query_blocks)
    attended = attended.transpose(0, 2, 1, 3).reshape(SEQ, D)
    attended = low_back(low(attended))
    branch = low_back(jnp.dot(attended, w_out, precision=HIGH, preferred_element_type=jnp.float32))
    middle = shifted + branch + out_bias
    normed_two = low(layer_norm(middle, norm2_gain, norm2_shift))
    pre_act = low_back(jnp.dot(normed_two, w_fc1, precision=HIGH, preferred_element_type=jnp.float32) + fc1_bias)
    hidden = low(jax.nn.gelu(pre_act, approximate=False))
    mlp_branch = low_back(jnp.dot(hidden, w_fc2, precision=HIGH, preferred_element_type=jnp.float32))
    return middle + mlp_branch + fc2_bias

def reference(tokens, cotangent, buckets, counts, lead_table, norm1_gain, norm1_shift, w_qkv, qv_bias, w_out, out_bias, norm2_gain, norm2_shift, w_fc1, fc1_bias, w_fc2, fc2_bias):
    params = tuple((p.astype(jnp.float32) for p in (norm1_gain, norm1_shift, w_qkv, qv_bias, w_out, out_bias, norm2_gain, norm2_shift, w_fc1, fc1_bias, w_fc2, fc2_bias)))
    lead_rows = lead_table.astype(jnp.float32)
    count_f = counts.astype(jnp.float32)
    loss_weight = jnp.mean(count_f) / count_f[buckets]

    def per_sample(running, per_item):
        table_grad, param_grads = running
        sample_tokens, sample_cot, bucket, weight = per_item
        onehot = (jnp.arange(BUCKETS, dtype=jnp.int32) == bucket).astype(jnp.float32)

        def forward(inputs, table, weights):
            return sample_forward(inputs, table, onehot, weights)
        output, pullback = jax.vjp(forward, sample_tokens.astype(jnp.float32), lead_rows, params)
        input_grad, new_table_grad, new_grads = pullback(weight * sample_cot.astype(jnp.float32))
        table_grad = table_grad + new_table_grad
        param_grads = jax.tree.map(jnp.add, param_grads, new_grads)
        return ((table_grad, param_grads), (output.astype(jnp.bfloat16), input_grad))
    zero_grads = jax.tree.map(jnp.zeros_like, params)
    (table_grad, sums), (outputs, input_grads) = lax.scan(per_sample, (jnp.zeros_like(lead_rows), zero_grads), (tokens, cotangent, buckets, loss_weight))
    return (outputs, input_grads, table_grad, sums[0], sums[1], sums[2], sums[3], sums[4], sums[5], sums[6], sums[7], sums[8], sums[9], sums[10], sums[11])
```

```python
import functools

import jax
import jax.numpy as jnp
from jax import lax
from jax.experimental import pallas as pl
from jax.experimental.pallas import tpu as pltpu
from jax.sharding import PartitionSpec as P

HD = 64


EPS = 1e-05


def norm_forward(values, norm_gain, norm_shift):
    center = values - jnp.mean(values, axis=-1, keepdims=True)
    inverse = lax.rsqrt(jnp.mean(center * center, axis=-1, keepdims=True) + EPS)
    scaled = center * inverse
    return (scaled * norm_gain + norm_shift, scaled, inverse)


def norm_backward(grad_out, scaled, inverse, norm_gain):
    grad_scaled = grad_out * norm_gain
    grad_mean = jnp.mean(grad_scaled, axis=-1, keepdims=True)
    cross_mean = jnp.mean(grad_scaled * scaled, axis=-1, keepdims=True)
    grad_in = inverse * (grad_scaled - grad_mean - scaled * cross_mean)
    gain_grad = jnp.sum(grad_out * scaled, axis=(0, 1))
    shift_grad = jnp.sum(grad_out, axis=(0, 1))
    return (grad_in, gain_grad, shift_grad)


def gelu_slope(pre_act):
    normal_cdf = 0.5 * (1.0 + lax.erf(pre_act * 0.7071067811865476))
    return normal_cdf + pre_act * jnp.exp(-0.5 * pre_act * pre_act) * 0.3989422804014327


def attention_forward(query_all, key_all, value_all, block_rows):
    block_count = query_all.shape[0] // block_rows
    query_blocks = query_all.reshape((block_count, block_rows) + query_all.shape[1:])

    def one_block(query_block):
        scores = (
            jnp.einsum("qshd,kshd->shqk", query_block, key_all, preferred_element_type=jnp.float32)
            * 0.125
        )
        row_max = jnp.max(scores, axis=-1, keepdims=True)
        powers = jnp.exp(scores - row_max)
        exp_total = jnp.sum(powers, axis=-1, keepdims=True)
        attn_weights = (powers / exp_total).astype(jnp.bfloat16)
        attended = jnp.einsum(
            "shqk,kshd->qshd", attn_weights, value_all, preferred_element_type=jnp.float32
        )
        return (attended.astype(jnp.bfloat16), (row_max + jnp.log(exp_total))[..., 0])

    attended, log_total = lax.map(one_block, query_blocks)
    return (attended.reshape(query_all.shape), log_total)


def attention_backward(query_all, key_all, value_all, grad_attended, log_total, block_rows):
    block_count = query_all.shape[0] // block_rows
    query_blocks = query_all.reshape((block_count, block_rows) + query_all.shape[1:])
    grad_blocks = grad_attended.reshape((block_count, block_rows) + query_all.shape[1:])

    def one_block(running, sliced):
        key_grad, value_grad = running
        query_block, grad_block, log_block = sliced
        scores = (
            jnp.einsum("qshd,kshd->shqk", query_block, key_all, preferred_element_type=jnp.float32)
            * 0.125
        )
        attn_weights = jnp.exp(scores - log_block[..., None])
        weight_low = attn_weights.astype(jnp.bfloat16)
        grad_weights = jnp.einsum(
            "qshd,kshd->shqk", grad_block, value_all, preferred_element_type=jnp.float32
        )
        inner = jnp.sum(attn_weights * grad_weights, axis=-1, keepdims=True)
        grad_scores = (attn_weights * (grad_weights - inner)).astype(jnp.bfloat16)
        query_grad = (
            jnp.einsum("shqk,kshd->qshd", grad_scores, key_all, preferred_element_type=jnp.float32)
            * 0.125
        )
        key_grad = (
            key_grad
            + jnp.einsum(
                "shqk,qshd->kshd", grad_scores, query_block, preferred_element_type=jnp.float32
            )
            * 0.125
        )
        value_grad = value_grad + jnp.einsum(
            "shqk,qshd->kshd", weight_low, grad_block, preferred_element_type=jnp.float32
        )
        return ((key_grad, value_grad), query_grad.astype(jnp.bfloat16))

    zero_grad = jnp.zeros(key_all.shape, jnp.float32)
    (key_grad, value_grad), query_grad = lax.scan(
        one_block, (zero_grad, zero_grad), (query_blocks, grad_blocks, log_total)
    )
    return (
        query_grad.reshape(query_all.shape),
        key_grad.astype(jnp.bfloat16),
        value_grad.astype(jnp.bfloat16),
    )


def body(
    tokens,
    cotangent,
    buckets,
    counts,
    lead_table,
    norm1_gain,
    norm1_shift,
    w_qkv,
    qv_bias,
    w_out,
    out_bias,
    norm2_gain,
    norm2_shift,
    w_fc1,
    fc1_bias,
    w_fc2,
    fc2_bias,
):
    samples_here = tokens.shape[0]
    local_rows = tokens.shape[1]
    local_width = w_qkv.shape[2]
    local_heads = local_width // HD
    seq_len = local_rows * lax.axis_size("mp")
    block_rows = min(512, seq_len)
    head_shape = (seq_len, samples_here, local_heads, HD)
    count_f = counts.astype(jnp.float32)
    onehot = (buckets[:, None] == jnp.arange(counts.shape[0], dtype=jnp.int32)[None, :]).astype(
        jnp.float32
    )
    loss_weight = jnp.mean(count_f) / jnp.sum(onehot * count_f[None, :], axis=1)
    lead_rows = jnp.dot(
        onehot,
        lead_table.astype(jnp.float32),
        precision=lax.Precision.HIGHEST,
        preferred_element_type=jnp.float32,
    )
    shifted = jnp.swapaxes(tokens, 0, 1).astype(jnp.float32) + lead_rows[None]
    normed_one, scaled_one, inverse_one = norm_forward(
        shifted, norm1_gain.astype(jnp.float32), norm1_shift.astype(jnp.float32)
    )
    normed_one = normed_one.astype(jnp.bfloat16)
    normed_full = lax.all_gather(normed_one, "mp", axis=0, tiled=True)
    project = jnp.einsum("tsd,dcf->tscf", normed_full, w_qkv, preferred_element_type=jnp.float32)
    bias_f = qv_bias.astype(jnp.float32)
    query_all = (project[:, :, 0] + bias_f[0]).astype(jnp.bfloat16).reshape(head_shape)
    key_all = project[:, :, 1].astype(jnp.bfloat16).reshape(head_shape)
    value_all = (project[:, :, 2] + bias_f[1]).astype(jnp.bfloat16).reshape(head_shape)
    attended, log_total = attention_forward(query_all, key_all, value_all, block_rows)
    attended_flat = attended.reshape(seq_len, samples_here, local_width)
    picked = attended_flat
    branch = lax.psum_scatter(
        jnp.einsum("tsf,fd->tsd", picked, w_out, preferred_element_type=jnp.float32),
        "mp",
        scatter_dimension=0,
        tiled=True,
    )
    middle = shifted + branch + out_bias.astype(jnp.float32)
    gain_two = norm2_gain.astype(jnp.float32)
    normed_two, scaled_two, inverse_two = norm_forward(
        middle, gain_two, norm2_shift.astype(jnp.float32)
    )
    normed_two = normed_two.astype(jnp.bfloat16)
    grad_top = jnp.swapaxes(cotangent, 0, 1).astype(jnp.float32) * loss_weight[None, :, None]
    grad_low = grad_top.astype(jnp.bfloat16)
    fc1_full, fc1_bias_full, fc2_full = (
        lax.all_gather(w_fc1, "mp", axis=1, tiled=True),
        lax.all_gather(fc1_bias, "mp", axis=0, tiled=True),
        lax.all_gather(w_fc2, "mp", axis=0, tiled=True),
    )
    pre_act = jnp.einsum(
        "tsd,df->tsf", normed_two, fc1_full, preferred_element_type=jnp.float32
    ) + fc1_bias_full.astype(jnp.float32)
    hidden = jax.nn.gelu(pre_act, approximate=False).astype(jnp.bfloat16)
    mlp_branch = jnp.einsum("tsf,fd->tsd", hidden, fc2_full, preferred_element_type=jnp.float32)
    output = middle + mlp_branch + fc2_bias.astype(jnp.float32)
    grad_hidden = jnp.einsum("tsd,fd->tsf", grad_low, fc2_full, preferred_element_type=jnp.float32)
    grad_pre = (grad_hidden * gelu_slope(pre_act)).astype(jnp.bfloat16)
    grad_normed_two = jnp.einsum(
        "tsf,df->tsd", grad_pre, fc1_full, preferred_element_type=jnp.float32
    )
    fc1_part = jnp.einsum("tsd,tsf->df", normed_two, grad_pre, preferred_element_type=jnp.float32)
    fc1_bias_part = jnp.sum(grad_pre.astype(jnp.float32), axis=(0, 1))
    fc2_part = jnp.einsum("tsf,tsd->fd", hidden, grad_low, preferred_element_type=jnp.float32)
    fc1_grad, fc1_bias_grad, fc2_grad = (
        lax.psum_scatter(
            fc1_part.astype(jnp.bfloat16), "mp", scatter_dimension=1, tiled=True
        ).astype(jnp.float32),
        lax.psum_scatter(
            fc1_bias_part.astype(jnp.bfloat16), "mp", scatter_dimension=0, tiled=True
        ).astype(jnp.float32),
        lax.psum_scatter(
            fc2_part.astype(jnp.bfloat16), "mp", scatter_dimension=0, tiled=True
        ).astype(jnp.float32),
    )
    fc2_bias_grad = jnp.sum(grad_top, axis=(0, 1))
    grad_from_norm, gain_two_grad, shift_two_grad = norm_backward(
        grad_normed_two, scaled_two, inverse_two, gain_two
    )
    grad_middle = grad_top + grad_from_norm
    out_bias_grad = jnp.sum(grad_middle, axis=(0, 1))
    grad_branch = grad_middle.astype(jnp.bfloat16)
    grad_branch_full = lax.all_gather(grad_branch, "mp", axis=0, tiled=True)
    out_grad = jnp.einsum(
        "tsf,tsd->fd", attended_flat, grad_branch_full, preferred_element_type=jnp.float32
    )
    grad_attended = jnp.einsum(
        "tsd,fd->tsf", grad_branch_full, w_out, preferred_element_type=jnp.float32
    ).astype(jnp.bfloat16)
    query_grad, key_grad, value_grad = attention_backward(
        query_all, key_all, value_all, grad_attended.reshape(head_shape), log_total, block_rows
    )
    grad_project = jnp.stack([query_grad, key_grad, value_grad], axis=2).reshape(
        seq_len, samples_here, 3, local_width
    )
    qkv_grad = jnp.einsum(
        "tsd,tscf->dcf", normed_full, grad_project, preferred_element_type=jnp.float32
    )
    query_bias_grad = jnp.sum(query_grad.astype(jnp.float32), axis=(0, 1)).reshape(local_width)
    value_bias_grad = jnp.sum(value_grad.astype(jnp.float32), axis=(0, 1)).reshape(local_width)
    qv_bias_grad = jnp.stack([query_bias_grad, value_bias_grad])
    picked = grad_project
    grad_normed_one = lax.psum_scatter(
        jnp.einsum("tscf,dcf->tsd", picked, w_qkv, preferred_element_type=jnp.float32).astype(
            jnp.bfloat16
        ),
        "mp",
        scatter_dimension=0,
        tiled=True,
    ).astype(jnp.float32)
    grad_in_one, gain_one_grad, shift_one_grad = norm_backward(
        grad_normed_one, scaled_one, inverse_one, norm1_gain.astype(jnp.float32)
    )
    grad_shifted = grad_middle + grad_in_one
    lead_grad = jnp.dot(
        onehot.T,
        jnp.sum(grad_shifted, axis=0),
        precision=lax.Precision.HIGHEST,
        preferred_element_type=jnp.float32,
    )
    small_grads = jnp.stack(
        [gain_one_grad, shift_one_grad, out_bias_grad, gain_two_grad, shift_two_grad, fc2_bias_grad]
    )
    lead_grad, small_grads = lax.psum((lead_grad, small_grads), ("dp", "mp"))
    qkv_grad, qv_bias_grad, out_grad, fc1_grad, fc1_bias_grad, fc2_grad = (
        lax.psum(qkv_grad.astype(jnp.bfloat16), "dp").astype(jnp.float32),
        lax.psum(qv_bias_grad.astype(jnp.bfloat16), "dp").astype(jnp.float32),
        lax.psum(out_grad.astype(jnp.bfloat16), "dp").astype(jnp.float32),
        lax.psum(fc1_grad.astype(jnp.bfloat16), "dp").astype(jnp.float32),
        lax.psum(fc1_bias_grad.astype(jnp.bfloat16), "dp").astype(jnp.float32),
        lax.psum(fc2_grad.astype(jnp.bfloat16), "dp").astype(jnp.float32),
    )
    block_output = jnp.swapaxes(output, 0, 1).astype(jnp.bfloat16)
    input_grad = jnp.swapaxes(grad_shifted, 0, 1)
    return (
        block_output,
        input_grad,
        lead_grad,
        small_grads[0],
        small_grads[1],
        qkv_grad,
        qv_bias_grad,
        out_grad,
        small_grads[2],
        small_grads[3],
        small_grads[4],
        fc1_grad,
        fc1_bias_grad,
        fc2_grad,
        small_grads[5],
    )


F32 = jnp.float32
BF16 = jnp.bfloat16
NN = (((1,), (0,)), ((), ()))
NT = (((1,), (1,)), ((), ()))
TN = (((0,), (0,)), ((), ()))


def dot(left, right, dims):
    return lax.dot_general(left, right, dims, preferred_element_type=F32)


def attention_forward_kernel(qkv_ref, out_ref, power_ref, inverse_ref):
    outs = []
    for head in range(2):
        lanes = slice(HD * head, HD * head + HD)
        query = qkv_ref[0, :, lanes] * BF16(0.125)
        scores = dot(qkv_ref[1, :, lanes], query, NT)
        powers = jnp.exp(scores - jnp.max(scores, axis=0, keepdims=True))
        inverse = 1.0 / jnp.sum(powers, axis=0, keepdims=True)
        power_low = powers.astype(BF16)
        power_ref[head] = power_low
        inverse_ref[0, head : head + 1, :] = inverse
        outs.append(dot(qkv_ref[2, :, lanes], power_low, TN) * inverse)
    out_ref[...] = jnp.concatenate(outs, axis=0).T.astype(BF16)


def attention_backward_kernel(block, qkv_ref, power_ref, inverse_ref, out_ref, grad_ref, dqkv_ref, sums_ref):
    rows_all = qkv_ref.shape[1]
    out_t = out_ref[...].astype(F32).T
    grad_t = grad_ref[...].astype(F32).T
    for head in range(2):
        lanes = slice(HD * head, HD * head + HD)
        inverse = inverse_ref[0, head : head + 1, :]
        grad_head = grad_t[lanes]
        inner = jnp.sum(grad_head * out_t[lanes], axis=0, keepdims=True) * inverse
        grad_scaled = grad_head * inverse
        grad_low_t = grad_scaled.astype(BF16)
        grad_low = grad_scaled.T.astype(BF16)
        query = qkv_ref[0, :, lanes] * BF16(0.125)
        key = qkv_ref[1, :, lanes]
        value = qkv_ref[2, :, lanes]
        key_t = key.T
        key_grad = value_grad = None
        query_grads = []
        for start in range(0, rows_all, block):
            rows = slice(start, start + block)
            power = power_ref[head, :, rows]
            grad_power = dot(value, grad_low_t[:, rows], NN) - inner[:, rows]
            grad_scores = (power.astype(F32) * grad_power).astype(BF16)
            key_part = dot(grad_scores, query[rows], NN)
            value_part = dot(power, grad_low[rows], NN)
            key_grad = key_part if key_grad is None else key_grad + key_part
            value_grad = value_part if value_grad is None else value_grad + value_part
            query_grads.append(dot(key_t, grad_scores, NN))
        sums_ref[0, :, lanes] = jnp.concatenate(query_grads, axis=1).T * 0.125
        sums_ref[1, :, lanes] = key_grad
        sums_ref[2, :, lanes] = value_grad
    dqkv_ref[...] = sums_ref[...].astype(BF16)


def attend(qkv):
    _, rows, width = qkv.shape
    pairs = width // (2 * HD)
    work = 2 * pairs * rows * rows
    return pl.pallas_call(
        attention_forward_kernel,
        out_shape=(
            jax.ShapeDtypeStruct((rows, width), BF16),
            jax.ShapeDtypeStruct((2 * pairs, rows, rows), BF16),
            jax.ShapeDtypeStruct((pairs, 2, rows), F32),
        ),
        grid=(pairs,),
        in_specs=[pl.BlockSpec((3, rows, 2 * HD), lambda j: (0, 0, j))],
        out_specs=(
            pl.BlockSpec((rows, 2 * HD), lambda j: (0, j)),
            pl.BlockSpec((2, rows, rows), lambda j: (j, 0, 0)),
            pl.BlockSpec((1, 2, rows), lambda j: (j, 0, 0)),
        ),
        compiler_params=pltpu.CompilerParams(vmem_limit_bytes=48 << 20),
        cost_estimate=pl.CostEstimate(
            flops=work * HD * 4 * 4, transcendentals=work, bytes_accessed=work * 2 + 8 * rows * width
        ),
        name="attention_forward",
    )(qkv)


def attend_back(qkv, powers, inverse, attended, grad_attended):
    _, rows, width = qkv.shape
    pairs = width // (2 * HD)
    work = 2 * pairs * rows * rows
    return pl.pallas_call(
        functools.partial(attention_backward_kernel, min(512, rows)),
        out_shape=jax.ShapeDtypeStruct((3, rows, width), BF16),
        grid=(pairs,),
        in_specs=[
            pl.BlockSpec((3, rows, 2 * HD), lambda j: (0, 0, j)),
            pl.BlockSpec((2, rows, rows), lambda j: (j, 0, 0)),
            pl.BlockSpec((1, 2, rows), lambda j: (j, 0, 0)),
            pl.BlockSpec((rows, 2 * HD), lambda j: (0, j)),
            pl.BlockSpec((rows, 2 * HD), lambda j: (0, j)),
        ],
        out_specs=pl.BlockSpec((3, rows, 2 * HD), lambda j: (0, 0, j)),
        scratch_shapes=[pltpu.VMEM((3, rows, 2 * HD), F32)],
        compiler_params=pltpu.CompilerParams(vmem_limit_bytes=48 << 20),
        cost_estimate=pl.CostEstimate(
            flops=work * HD * 8 * 4, transcendentals=0, bytes_accessed=work * 2 + 16 * rows * width
        ),
        name="attention_backward",
    )(qkv, powers, inverse, attended, grad_attended)


def hidden_kernel(normed_ref, weight_ref, bias_ref, hidden_ref, slope_ref):
    rows_all = normed_ref.shape[0]
    block = min(256, rows_all)
    for start in range(0, rows_all, block):
        rows = slice(start, start + block)
        pre_act = dot(normed_ref[rows], weight_ref[...], NN) + bias_ref[...]
        cdf = 0.5 * (1.0 + lax.erf(pre_act * 0.7071067811865476))
        hidden_ref[rows] = (pre_act * cdf).astype(BF16)
        density = jnp.exp(-0.5 * pre_act * pre_act) * 0.3989422804014327
        slope_ref[rows] = (cdf + pre_act * density).astype(BF16)


def hidden_layer(normed, weight, bias):
    rows, width = normed.shape
    units = weight.shape[1]
    tile = min(512, units)
    return pl.pallas_call(
        hidden_kernel,
        out_shape=(jax.ShapeDtypeStruct((rows, units), BF16),) * 2,
        grid=(units // tile,),
        in_specs=[
            pl.BlockSpec((rows, width), lambda j: (0, 0)),
            pl.BlockSpec((width, tile), lambda j: (0, j)),
            pl.BlockSpec((1, tile), lambda j: (0, j)),
        ],
        out_specs=(pl.BlockSpec((rows, tile), lambda j: (0, j)),) * 2,
        compiler_params=pltpu.CompilerParams(vmem_limit_bytes=32 << 20),
        cost_estimate=pl.CostEstimate(
            flops=2 * rows * width * units,
            transcendentals=2 * rows * units,
            bytes_accessed=2 * (rows * width + width * units + 2 * rows * units),
        ),
        name="hidden_layer",
    )(normed, weight, bias)


def after(value, *firsts):
    return lax.optimization_barrier((value, *firsts))[0]


def fast_body(
    tokens,
    cotangent,
    buckets,
    counts,
    lead_table,
    norm1_gain,
    norm1_shift,
    w_qkv,
    qv_bias,
    w_out,
    out_bias,
    norm2_gain,
    norm2_shift,
    w_fc1,
    fc1_bias,
    w_fc2,
    fc2_bias,
):
    replicas = lax.axis_size("dp")
    levels = replicas.bit_length() - 1
    dp_at, mp_at = lax.axis_index("dp"), lax.axis_index("mp")
    bits = [(dp_at >> level) & 1 for level in range(levels)]

    def over_x(value):
        return lax.ppermute(value, "mp", [(0, 1), (1, 0)])

    def over(level, value):
        return lax.ppermute(value, "dp", [(i, i ^ (1 << level)) for i in range(replicas)])

    def joined(bit, mine, theirs, axis=0):
        return jnp.where(
            bit == 0,
            jnp.concatenate([mine, theirs], axis),
            jnp.concatenate([theirs, mine], axis),
        )

    def part(value, index, count, axis=0):
        size = value.shape[axis] // count
        return lax.dynamic_slice_in_dim(value, index * size, size, axis)

    half_rows, width = tokens.shape[1:]
    heads_width = w_qkv.shape[2]
    units = w_fc1.shape[1]

    small = jnp.concatenate([qv_bias.reshape(-1), fc1_bias])
    small_rows = -(-small.shape[0] // width)
    small_rows_padded = -(-small_rows // 16) * 16
    small = jnp.pad(small, (0, small_rows_padded * width - small.shape[0])).reshape(-1, width)
    token_send = jnp.concatenate([part(tokens, 1 - mp_at, 2)[0], small])
    token_recv = over_x(token_send)
    far_small = token_recv[half_rows:].reshape(-1)
    far_qv_bias = far_small[: 2 * heads_width].reshape(2, heads_width)
    far_fc1_bias = far_small[2 * heads_width : 2 * heads_width + units]
    token_rows = jnp.concatenate([part(tokens, mp_at, 2)[0], token_recv[:half_rows]])

    def fetch(weight, *firsts):
        piece = over_x(after(part(weight, bits[0], 2), *firsts))
        return joined(bits[0], piece, over(0, piece)), piece

    def fetch_shared(weight, *firsts):
        piece = over_x(after(part(weight, bits[0] * 2 + bits[1], 4), *firsts))
        piece_y = over(1, piece)
        half = joined(bits[1], piece, piece_y)
        return joined(bits[0], half, over(0, half)), piece

    own_qkv = jnp.transpose(w_qkv, (1, 0, 2))
    far_qkv, qkv_piece = fetch(own_qkv.reshape(-1, heads_width), token_recv)
    far_qkv = far_qkv.reshape(own_qkv.shape)
    far_fc1, fc1_piece = fetch_shared(w_fc1, qkv_piece)
    far_out, out_piece = fetch(w_out, qkv_piece)
    cot_recv = over_x(after(part(cotangent, 1 - mp_at, 2)[0], fc1_piece))
    far_fc2, fc2_piece = fetch_shared(w_fc2, cot_recv)
    cot_rows = jnp.concatenate([part(cotangent, mp_at, 2)[0], cot_recv])

    bucket = lax.dynamic_index_in_dim(buckets, mp_at, 0, keepdims=False)
    count_f = counts.astype(F32)
    loss_weight = jnp.mean(count_f) / lax.dynamic_index_in_dim(count_f, bucket, 0, keepdims=False)
    lead_row = lax.dynamic_index_in_dim(lead_table, bucket, 0).astype(F32)

    def normalise(values):
        center = values - jnp.mean(values, axis=-1, keepdims=True)
        inverse = lax.rsqrt(jnp.mean(center * center, axis=-1, keepdims=True) + EPS)
        return center * inverse, inverse

    def normalise_back(grad_out, scaled, inverse, gain):
        grad_scaled = grad_out * gain
        grad_mean = jnp.mean(grad_scaled, axis=-1, keepdims=True)
        cross_mean = jnp.mean(grad_scaled * scaled, axis=-1, keepdims=True)
        grad_in = inverse * (grad_scaled - grad_mean - scaled * cross_mean)
        return grad_in, jnp.sum(grad_out * scaled, axis=0), jnp.sum(grad_out, axis=0)

    shifted = token_rows.astype(F32) + lead_row
    gain_one = norm1_gain.astype(F32)
    scaled_one, inverse_one = normalise(shifted)
    normed_one = (scaled_one * gain_one + norm1_shift.astype(F32)).astype(BF16)

    def project(weight, bias):
        bias_f = bias.astype(F32)
        bias_three = jnp.stack([bias_f[0], jnp.zeros_like(bias_f[0]), bias_f[1]])
        heads = jnp.einsum("td,cdf->ctf", normed_one, weight, preferred_element_type=F32)
        return (heads + bias_three[:, None, :]).astype(BF16)

    own_heads = project(own_qkv, qv_bias)
    own_attended, own_powers, own_inverse = attend(own_heads)
    far_heads = project(far_qkv, far_qv_bias)
    far_attended, far_powers, far_inverse = attend(far_heads)
    branch = dot(own_attended, w_out, NN) + dot(far_attended, far_out, NN)
    middle = shifted + branch + out_bias.astype(F32)
    gain_two = norm2_gain.astype(F32)
    scaled_two, inverse_two = normalise(middle)
    normed_two = (scaled_two * gain_two + norm2_shift.astype(F32)).astype(BF16)

    own_hidden, own_slope = hidden_layer(normed_two, w_fc1, fc1_bias.astype(F32)[None])
    far_hidden, far_slope = hidden_layer(normed_two, far_fc1, far_fc1_bias.astype(F32)[None])
    grad_top = cot_rows.astype(F32) * loss_weight
    grad_low = grad_top.astype(BF16)

    def reduce_core(keep, send):
        return [(k, over(0, s)) for k, s in zip(keep, send)]

    def total(pair):
        return sum(p.astype(F32) for p in pair)

    def scatter(parts):
        for level in range(1, levels):
            bit = bits[level]
            send = total([part(p, 1 - bit, 2, p.ndim - 2) for p in parts]).astype(BF16)
            parts = [part(p, bit, 2, p.ndim - 2) for p in parts] + [over(level, send)]
            parts = [total(parts).astype(BF16)]
        return parts[0]

    def gather(mine):
        for level in range(levels - 1, 0, -1):
            mine = joined(bits[level], mine, over(level, mine), mine.ndim - 2)
        return mine

    def reduce_x_first(own_pair, far_pair):
        recv = over_x(total(far_pair).astype(BF16))
        return scatter([*own_pair, recv])

    def reduce_y_first(own_pair, far_pair):
        both = [jnp.stack([o, f]) for o, f in zip(own_pair, far_pair)]
        bit = bits[1]
        send = total([part(b, 1 - bit, 2, b.ndim - 2) for b in both]).astype(BF16)
        recv = over(1, send)
        kept = [part(b, bit, 2, b.ndim - 2) for b in both] + [recv]
        recv_x = over_x(total([k[1] for k in kept]).astype(BF16))
        mine = total([k[0] for k in kept] + [recv_x]).astype(BF16)
        for level in range(2, levels):
            bit = bits[level]
            send = part(mine, 1 - bit, 2, mine.ndim - 2)
            mine = total([part(mine, bit, 2, mine.ndim - 2), over(level, send)]).astype(BF16)
        return mine

    low_keep, low_send = part(grad_low, bits[0], 2, 1), part(grad_low, 1 - bits[0], 2, 1)

    def fc2_parts(hidden):
        return dot(hidden, low_keep, TN).astype(BF16), over(0, dot(hidden, low_send, TN).astype(BF16))

    fc2_own_pair, fc2_far_pair = fc2_parts(own_hidden), fc2_parts(far_hidden)
    fc2_mine = reduce_x_first(fc2_own_pair, fc2_far_pair)

    def pre_grad(fc2, slope):
        return (dot(grad_low, fc2, NT) * slope.astype(F32)).astype(BF16)

    own_pre = pre_grad(w_fc2, own_slope)
    far_pre = pre_grad(far_fc2, far_slope)
    grad_normed_two = dot(own_pre, w_fc1, NT) + dot(far_pre, far_fc1, NT)
    two_keep, two_send = part(normed_two, bits[0], 2, 1), part(normed_two, 1 - bits[0], 2, 1)

    def fc1_parts(pre):
        return dot(two_keep, pre, TN).astype(BF16), over(0, dot(two_send, pre, TN).astype(BF16))

    fc1_own_pair, fc1_far_pair = fc1_parts(own_pre), fc1_parts(far_pre)
    fc1_mine = reduce_y_first(fc1_own_pair, fc1_far_pair)

    mlp_branch = dot(own_hidden, w_fc2, NN) + dot(far_hidden, far_fc2, NN)
    output = (middle + mlp_branch + fc2_bias.astype(F32)).astype(BF16)
    output_recv = over_x(output[half_rows:])
    block_output = joined(mp_at, output[None, :half_rows], output_recv[None])

    grad_from_norm, gain_two_grad, shift_two_grad = normalise_back(
        grad_normed_two, scaled_two, inverse_two, gain_two
    )
    grad_middle = grad_top + grad_from_norm
    out_bias_grad = jnp.sum(grad_middle, axis=0)
    fc2_bias_grad = jnp.sum(grad_top, axis=0)
    grad_branch = grad_middle.astype(BF16)

    own_grad_att = dot(grad_branch, w_out, NT).astype(BF16)
    far_grad_att = dot(grad_branch, far_out, NT).astype(BF16)
    branch_keep, branch_send = part(grad_branch, bits[0], 2, 1), part(grad_branch, 1 - bits[0], 2, 1)

    def out_parts(att):
        return dot(att, branch_keep, TN).astype(BF16), over(0, dot(att, branch_send, TN).astype(BF16))

    out_mine = reduce_x_first(out_parts(own_attended), out_parts(far_attended))
    far_dqkv = attend_back(far_heads, far_powers, far_inverse, far_attended, far_grad_att)
    own_dqkv = attend_back(own_heads, own_powers, own_inverse, own_attended, own_grad_att)
    one_keep, one_send = part(normed_one, bits[0], 2, 1), part(normed_one, 1 - bits[0], 2, 1)

    def qkv_parts(dqkv):
        def one(rows):
            return jnp.einsum("td,ctf->cdf", rows, dqkv, preferred_element_type=F32).astype(BF16)

        return one(one_keep), over(0, one(one_send))

    far_qkv_pair = qkv_parts(far_dqkv)
    own_qkv_pair = qkv_parts(own_dqkv)
    qkv_mine = reduce_x_first(own_qkv_pair, far_qkv_pair)

    def back_project(dqkv, weight):
        return jnp.einsum("ctf,cdf->td", dqkv, weight, preferred_element_type=F32)

    grad_normed_one = back_project(far_dqkv, far_qkv) + back_project(own_dqkv, own_qkv)
    grad_in_one, gain_one_grad, shift_one_grad = normalise_back(
        grad_normed_one, scaled_one, inverse_one, gain_one
    )
    grad_shifted = grad_middle + grad_in_one
    grad_recv = over_x(grad_shifted[half_rows:].astype(BF16)).astype(F32)
    input_grad = joined(mp_at, grad_shifted[None, :half_rows], grad_recv[None])

    bucket_rows = jnp.arange(counts.shape[0], dtype=jnp.int32)[:, None] == bucket
    lead_part = jnp.where(bucket_rows, jnp.sum(grad_shifted, axis=0)[None], 0.0)

    def column_sums(value):
        return jnp.sum(value.astype(F32), axis=-2)

    own_bias, far_bias = column_sums(own_dqkv), column_sums(far_dqkv)
    qv_bias_part = joined(mp_at, own_bias, far_bias, 1)
    fc1_bias_part = joined(mp_at, column_sums(own_pre), column_sums(far_pre), 0)
    vectors = jnp.concatenate(
        [
            lead_part,
            jnp.stack(
                [gain_one_grad, shift_one_grad, out_bias_grad, gain_two_grad, shift_two_grad, fc2_bias_grad]
            ),
            qv_bias_part[0::2],
            fc1_bias_part.reshape(-1, width),
        ]
    )
    vectors = vectors + over_x(vectors)
    for level in range(levels):
        vectors = vectors + over(level, vectors)
    table = counts.shape[0]
    lead_grad, singles, rest = vectors[:table], vectors[table : table + 6], vectors[table + 6 :]
    qv_bias_grad = part(rest[:2], mp_at, 2, 1)
    fc1_bias_grad = part(rest[2:].reshape(-1), mp_at, 2)

    fc2_half, fc1_half, out_half, qkv_half = gather(fc2_mine), gather(fc1_mine), gather(out_mine), gather(qkv_mine)

    def finish(half, axis):
        return joined(bits[0], half, over(0, half), axis).astype(F32)

    fc2_grad = finish(fc2_half, 1)
    fc1_grad = finish(fc1_half, 0)
    out_grad = finish(out_half, 1)
    qkv_grad = jnp.transpose(finish(qkv_half, 1), (1, 0, 2))
    return (
        block_output,
        input_grad,
        lead_grad,
        singles[0],
        singles[1],
        qkv_grad,
        qv_bias_grad,
        out_grad,
        singles[2],
        singles[3],
        singles[4],
        fc1_grad,
        fc1_bias_grad,
        fc2_grad,
        singles[5],
    )


def solution(mesh):
    in_specs = (
        P("dp", "mp", None),
        P("dp", "mp", None),
        P("dp"),
        P(),
        P(),
        P(),
        P(),
        P(None, None, "mp"),
        P(None, "mp"),
        P("mp", None),
        P(),
        P(),
        P(),
        P(None, "mp"),
        P("mp"),
        P("mp", None),
        P(),
    )
    out_specs = (
        P("dp", "mp", None),
        P("dp", "mp", None),
        P(),
        P(),
        P(),
        P(None, None, "mp"),
        P(None, "mp"),
        P("mp", None),
        P(),
        P(),
        P(),
        P(None, "mp"),
        P("mp"),
        P("mp", None),
        P(),
    )
    def local(*args):
        replicas = lax.axis_size("dp")
        one_each = args[0].shape[0] == 2 and lax.axis_size("mp") == 2
        chosen = fast_body if one_each and replicas >= 4 and replicas & (replicas - 1) == 0 else body
        return chosen(*args)

    return jax.shard_map(local, mesh=mesh, in_specs=in_specs, out_specs=out_specs, check_vma=False)
```

```python
import functools

import jax
import jax.numpy as jnp
from jax import lax
from jax.experimental import pallas as pl
from jax.experimental.pallas import tpu as pltpu
from jax.sharding import PartitionSpec as P

HD = 64


EPS = 1e-05


def norm_forward(values, norm_gain, norm_shift):
    center = values - jnp.mean(values, axis=-1, keepdims=True)
    inverse = lax.rsqrt(jnp.mean(center * center, axis=-1, keepdims=True) + EPS)
    scaled = center * inverse
    return (scaled * norm_gain + norm_shift, scaled, inverse)


def norm_backward(grad_out, scaled, inverse, norm_gain):
    grad_scaled = grad_out * norm_gain
    grad_mean = jnp.mean(grad_scaled, axis=-1, keepdims=True)
    cross_mean = jnp.mean(grad_scaled * scaled, axis=-1, keepdims=True)
    grad_in = inverse * (grad_scaled - grad_mean - scaled * cross_mean)
    gain_grad = jnp.sum(grad_out * scaled, axis=(0, 1))
    shift_grad = jnp.sum(grad_out, axis=(0, 1))
    return (grad_in, gain_grad, shift_grad)


def gelu_slope(pre_act):
    normal_cdf = 0.5 * (1.0 + lax.erf(pre_act * 0.7071067811865476))
    return normal_cdf + pre_act * jnp.exp(-0.5 * pre_act * pre_act) * 0.3989422804014327


def attention_forward(query_all, key_all, value_all, block_rows):
    block_count = query_all.shape[0] // block_rows
    query_blocks = query_all.reshape((block_count, block_rows) + query_all.shape[1:])

    def one_block(query_block):
        scores = (
            jnp.einsum("qshd,kshd->shqk", query_block, key_all, preferred_element_type=jnp.float32)
            * 0.125
        )
        row_max = jnp.max(scores, axis=-1, keepdims=True)
        powers = jnp.exp(scores - row_max)
        exp_total = jnp.sum(powers, axis=-1, keepdims=True)
        attn_weights = (powers / exp_total).astype(jnp.bfloat16)
        attended = jnp.einsum(
            "shqk,kshd->qshd", attn_weights, value_all, preferred_element_type=jnp.float32
        )
        return (attended.astype(jnp.bfloat16), (row_max + jnp.log(exp_total))[..., 0])

    attended, log_total = lax.map(one_block, query_blocks)
    return (attended.reshape(query_all.shape), log_total)


def attention_backward(query_all, key_all, value_all, grad_attended, log_total, block_rows):
    block_count = query_all.shape[0] // block_rows
    query_blocks = query_all.reshape((block_count, block_rows) + query_all.shape[1:])
    grad_blocks = grad_attended.reshape((block_count, block_rows) + query_all.shape[1:])

    def one_block(running, sliced):
        key_grad, value_grad = running
        query_block, grad_block, log_block = sliced
        scores = (
            jnp.einsum("qshd,kshd->shqk", query_block, key_all, preferred_element_type=jnp.float32)
            * 0.125
        )
        attn_weights = jnp.exp(scores - log_block[..., None])
        weight_low = attn_weights.astype(jnp.bfloat16)
        grad_weights = jnp.einsum(
            "qshd,kshd->shqk", grad_block, value_all, preferred_element_type=jnp.float32
        )
        inner = jnp.sum(attn_weights * grad_weights, axis=-1, keepdims=True)
        grad_scores = (attn_weights * (grad_weights - inner)).astype(jnp.bfloat16)
        query_grad = (
            jnp.einsum("shqk,kshd->qshd", grad_scores, key_all, preferred_element_type=jnp.float32)
            * 0.125
        )
        key_grad = (
            key_grad
            + jnp.einsum(
                "shqk,qshd->kshd", grad_scores, query_block, preferred_element_type=jnp.float32
            )
            * 0.125
        )
        value_grad = value_grad + jnp.einsum(
            "shqk,qshd->kshd", weight_low, grad_block, preferred_element_type=jnp.float32
        )
        return ((key_grad, value_grad), query_grad.astype(jnp.bfloat16))

    zero_grad = jnp.zeros(key_all.shape, jnp.float32)
    (key_grad, value_grad), query_grad = lax.scan(
        one_block, (zero_grad, zero_grad), (query_blocks, grad_blocks, log_total)
    )
    return (
        query_grad.reshape(query_all.shape),
        key_grad.astype(jnp.bfloat16),
        value_grad.astype(jnp.bfloat16),
    )


def body(
    tokens,
    cotangent,
    buckets,
    counts,
    lead_table,
    norm1_gain,
    norm1_shift,
    w_qkv,
    qv_bias,
    w_out,
    out_bias,
    norm2_gain,
    norm2_shift,
    w_fc1,
    fc1_bias,
    w_fc2,
    fc2_bias,
):
    samples_here = tokens.shape[0]
    local_rows = tokens.shape[1]
    local_width = w_qkv.shape[2]
    local_heads = local_width // HD
    seq_len = local_rows * lax.axis_size("mp")
    block_rows = min(512, seq_len)
    head_shape = (seq_len, samples_here, local_heads, HD)
    count_f = counts.astype(jnp.float32)
    onehot = (buckets[:, None] == jnp.arange(counts.shape[0], dtype=jnp.int32)[None, :]).astype(
        jnp.float32
    )
    loss_weight = jnp.mean(count_f) / jnp.sum(onehot * count_f[None, :], axis=1)
    lead_rows = jnp.dot(
        onehot,
        lead_table.astype(jnp.float32),
        precision=lax.Precision.HIGHEST,
        preferred_element_type=jnp.float32,
    )
    shifted = jnp.swapaxes(tokens, 0, 1).astype(jnp.float32) + lead_rows[None]
    normed_one, scaled_one, inverse_one = norm_forward(
        shifted, norm1_gain.astype(jnp.float32), norm1_shift.astype(jnp.float32)
    )
    normed_one = normed_one.astype(jnp.bfloat16)
    normed_full = lax.all_gather(normed_one, "mp", axis=0, tiled=True)
    project = jnp.einsum("tsd,dcf->tscf", normed_full, w_qkv, preferred_element_type=jnp.float32)
    bias_f = qv_bias.astype(jnp.float32)
    query_all = (project[:, :, 0] + bias_f[0]).astype(jnp.bfloat16).reshape(head_shape)
    key_all = project[:, :, 1].astype(jnp.bfloat16).reshape(head_shape)
    value_all = (project[:, :, 2] + bias_f[1]).astype(jnp.bfloat16).reshape(head_shape)
    attended, log_total = attention_forward(query_all, key_all, value_all, block_rows)
    attended_flat = attended.reshape(seq_len, samples_here, local_width)
    picked = attended_flat
    branch = lax.psum_scatter(
        jnp.einsum("tsf,fd->tsd", picked, w_out, preferred_element_type=jnp.float32),
        "mp",
        scatter_dimension=0,
        tiled=True,
    )
    middle = shifted + branch + out_bias.astype(jnp.float32)
    gain_two = norm2_gain.astype(jnp.float32)
    normed_two, scaled_two, inverse_two = norm_forward(
        middle, gain_two, norm2_shift.astype(jnp.float32)
    )
    normed_two = normed_two.astype(jnp.bfloat16)
    grad_top = jnp.swapaxes(cotangent, 0, 1).astype(jnp.float32) * loss_weight[None, :, None]
    grad_low = grad_top.astype(jnp.bfloat16)
    fc1_full, fc1_bias_full, fc2_full = (
        lax.all_gather(w_fc1, "mp", axis=1, tiled=True),
        lax.all_gather(fc1_bias, "mp", axis=0, tiled=True),
        lax.all_gather(w_fc2, "mp", axis=0, tiled=True),
    )
    pre_act = jnp.einsum(
        "tsd,df->tsf", normed_two, fc1_full, preferred_element_type=jnp.float32
    ) + fc1_bias_full.astype(jnp.float32)
    hidden = jax.nn.gelu(pre_act, approximate=False).astype(jnp.bfloat16)
    mlp_branch = jnp.einsum("tsf,fd->tsd", hidden, fc2_full, preferred_element_type=jnp.float32)
    output = middle + mlp_branch + fc2_bias.astype(jnp.float32)
    grad_hidden = jnp.einsum("tsd,fd->tsf", grad_low, fc2_full, preferred_element_type=jnp.float32)
    grad_pre = (grad_hidden * gelu_slope(pre_act)).astype(jnp.bfloat16)
    grad_normed_two = jnp.einsum(
        "tsf,df->tsd", grad_pre, fc1_full, preferred_element_type=jnp.float32
    )
    fc1_part = jnp.einsum("tsd,tsf->df", normed_two, grad_pre, preferred_element_type=jnp.float32)
    fc1_bias_part = jnp.sum(grad_pre.astype(jnp.float32), axis=(0, 1))
    fc2_part = jnp.einsum("tsf,tsd->fd", hidden, grad_low, preferred_element_type=jnp.float32)
    fc1_grad, fc1_bias_grad, fc2_grad = (
        lax.psum_scatter(
            fc1_part.astype(jnp.bfloat16), "mp", scatter_dimension=1, tiled=True
        ).astype(jnp.float32),
        lax.psum_scatter(
            fc1_bias_part.astype(jnp.bfloat16), "mp", scatter_dimension=0, tiled=True
        ).astype(jnp.float32),
        lax.psum_scatter(
            fc2_part.astype(jnp.bfloat16), "mp", scatter_dimension=0, tiled=True
        ).astype(jnp.float32),
    )
    fc2_bias_grad = jnp.sum(grad_top, axis=(0, 1))
    grad_from_norm, gain_two_grad, shift_two_grad = norm_backward(
        grad_normed_two, scaled_two, inverse_two, gain_two
    )
    grad_middle = grad_top + grad_from_norm
    out_bias_grad = jnp.sum(grad_middle, axis=(0, 1))
    grad_branch = grad_middle.astype(jnp.bfloat16)
    grad_branch_full = lax.all_gather(grad_branch, "mp", axis=0, tiled=True)
    out_grad = jnp.einsum(
        "tsf,tsd->fd", attended_flat, grad_branch_full, preferred_element_type=jnp.float32
    )
    grad_attended = jnp.einsum(
        "tsd,fd->tsf", grad_branch_full, w_out, preferred_element_type=jnp.float32
    ).astype(jnp.bfloat16)
    query_grad, key_grad, value_grad = attention_backward(
        query_all, key_all, value_all, grad_attended.reshape(head_shape), log_total, block_rows
    )
    grad_project = jnp.stack([query_grad, key_grad, value_grad], axis=2).reshape(
        seq_len, samples_here, 3, local_width
    )
    qkv_grad = jnp.einsum(
        "tsd,tscf->dcf", normed_full, grad_project, preferred_element_type=jnp.float32
    )
    query_bias_grad = jnp.sum(query_grad.astype(jnp.float32), axis=(0, 1)).reshape(local_width)
    value_bias_grad = jnp.sum(value_grad.astype(jnp.float32), axis=(0, 1)).reshape(local_width)
    qv_bias_grad = jnp.stack([query_bias_grad, value_bias_grad])
    picked = grad_project
    grad_normed_one = lax.psum_scatter(
        jnp.einsum("tscf,dcf->tsd", picked, w_qkv, preferred_element_type=jnp.float32).astype(
            jnp.bfloat16
        ),
        "mp",
        scatter_dimension=0,
        tiled=True,
    ).astype(jnp.float32)
    grad_in_one, gain_one_grad, shift_one_grad = norm_backward(
        grad_normed_one, scaled_one, inverse_one, norm1_gain.astype(jnp.float32)
    )
    grad_shifted = grad_middle + grad_in_one
    lead_grad = jnp.dot(
        onehot.T,
        jnp.sum(grad_shifted, axis=0),
        precision=lax.Precision.HIGHEST,
        preferred_element_type=jnp.float32,
    )
    small_grads = jnp.stack(
        [gain_one_grad, shift_one_grad, out_bias_grad, gain_two_grad, shift_two_grad, fc2_bias_grad]
    )
    lead_grad, small_grads = lax.psum((lead_grad, small_grads), ("dp", "mp"))
    qkv_grad, qv_bias_grad, out_grad, fc1_grad, fc1_bias_grad, fc2_grad = (
        lax.psum(qkv_grad.astype(jnp.bfloat16), "dp").astype(jnp.float32),
        lax.psum(qv_bias_grad.astype(jnp.bfloat16), "dp").astype(jnp.float32),
        lax.psum(out_grad.astype(jnp.bfloat16), "dp").astype(jnp.float32),
        lax.psum(fc1_grad.astype(jnp.bfloat16), "dp").astype(jnp.float32),
        lax.psum(fc1_bias_grad.astype(jnp.bfloat16), "dp").astype(jnp.float32),
        lax.psum(fc2_grad.astype(jnp.bfloat16), "dp").astype(jnp.float32),
    )
    block_output = jnp.swapaxes(output, 0, 1).astype(jnp.bfloat16)
    input_grad = jnp.swapaxes(grad_shifted, 0, 1)
    return (
        block_output,
        input_grad,
        lead_grad,
        small_grads[0],
        small_grads[1],
        qkv_grad,
        qv_bias_grad,
        out_grad,
        small_grads[2],
        small_grads[3],
        small_grads[4],
        fc1_grad,
        fc1_bias_grad,
        fc2_grad,
        small_grads[5],
    )


F32 = jnp.float32
BF16 = jnp.bfloat16
NN = (((1,), (0,)), ((), ()))
NT = (((1,), (1,)), ((), ()))
TN = (((0,), (0,)), ((), ()))
MIB = 1 << 20


def dot(left, right, dims):
    return lax.dot_general(left, right, dims, preferred_element_type=F32)


def whole(array):
    return pl.BlockSpec(array.shape, lambda *_: (0,) * array.ndim)


def kernel_call(body, name, grid, scalars, ins, outs, scratch=(), vmem=40):
    spec = pltpu.PrefetchScalarGridSpec(
        num_scalar_prefetch=len(scalars),
        grid=grid,
        in_specs=[spec for _, spec in ins],
        out_specs=[spec for _, spec in outs],
        scratch_shapes=list(scratch),
    )
    return pl.pallas_call(
        body,
        out_shape=[shape for shape, _ in outs],
        grid_spec=spec,
        compiler_params=pltpu.CompilerParams(vmem_limit_bytes=vmem * MIB),
        cost_estimate=pl.CostEstimate(flops=MIB, transcendentals=0, bytes_accessed=MIB),
        name=name,
    )(*scalars, *[array for array, _ in ins])


def struct(shape, dtype=BF16):
    return jax.ShapeDtypeStruct(shape, dtype)


def centred(values):
    center = values - jnp.mean(values, axis=-1, keepdims=True)
    inverse = lax.rsqrt(jnp.mean(center * center, axis=-1, keepdims=True) + EPS)
    return center * inverse, inverse


def norm_input_grad(grad_out, scaled, inverse, gain):
    grad_scaled = grad_out * gain
    grad_mean = jnp.mean(grad_scaled, axis=-1, keepdims=True)
    cross_mean = jnp.mean(grad_scaled * scaled, axis=-1, keepdims=True)
    return inverse * (grad_scaled - grad_mean - scaled * cross_mean)


def column_sum(values):
    return jnp.sum(values, axis=0, keepdims=True)


def chunk_of(nat_ref, index, size):
    return pl.ds(pl.multiple_of(nat_ref[index] * size, size), size)


def attention_forward_kernel(qkv_ref, out_ref, power_ref, inverse_ref):
    outs = []
    for head in range(2):
        lanes = slice(HD * head, HD * head + HD)
        query = qkv_ref[0, :, lanes] * BF16(0.125)
        scores = dot(qkv_ref[1, :, lanes], query, NT)
        powers = jnp.exp(scores - jnp.max(scores, axis=0, keepdims=True))
        inverse = 1.0 / jnp.sum(powers, axis=0, keepdims=True)
        power_low = powers.astype(BF16)
        power_ref[head] = power_low
        inverse_ref[0, head : head + 1, :] = inverse
        outs.append(dot(qkv_ref[2, :, lanes], power_low, TN) * inverse)
    out_ref[...] = jnp.concatenate(outs, axis=0).T.astype(BF16)


def attend(qkv):
    _, rows, width = qkv.shape
    pairs = width // (2 * HD)
    return kernel_call(
        attention_forward_kernel,
        "attention_forward",
        (pairs,),
        [],
        [(qkv, pl.BlockSpec((3, rows, 2 * HD), lambda j: (0, 0, j)))],
        [
            (struct((rows, width)), pl.BlockSpec((rows, 2 * HD), lambda j: (0, j))),
            (struct((2 * pairs, rows, rows)), pl.BlockSpec((2, rows, rows), lambda j: (j, 0, 0))),
            (struct((pairs, 2, rows), F32), pl.BlockSpec((1, 2, rows), lambda j: (j, 0, 0))),
        ],
    )


def attention_backward_kernel(block, qkv_ref, power_ref, inverse_ref, out_ref, grad_ref, dqkv_ref, sums_ref):
    rows_all = qkv_ref.shape[1]
    out_t = out_ref[...].astype(F32).T
    grad_t = grad_ref[...].astype(F32).T
    for head in range(2):
        lanes = slice(HD * head, HD * head + HD)
        inverse = inverse_ref[0, head : head + 1, :]
        grad_head = grad_t[lanes]
        inner = jnp.sum(grad_head * out_t[lanes], axis=0, keepdims=True) * inverse
        grad_scaled = grad_head * inverse
        grad_low_t = grad_scaled.astype(BF16)
        grad_low = grad_scaled.T.astype(BF16)
        query = qkv_ref[0, :, lanes] * BF16(0.125)
        key = qkv_ref[1, :, lanes]
        value = qkv_ref[2, :, lanes]
        key_t = key.T
        key_grad = value_grad = None
        query_grads = []
        for start in range(0, rows_all, block):
            rows = slice(start, start + block)
            power = power_ref[head, :, rows]
            grad_power = dot(value, grad_low_t[:, rows], NN) - inner[:, rows]
            grad_scores = (power.astype(F32) * grad_power).astype(BF16)
            key_part = dot(grad_scores, query[rows], NN)
            value_part = dot(power, grad_low[rows], NN)
            key_grad = key_part if key_grad is None else key_grad + key_part
            value_grad = value_part if value_grad is None else value_grad + value_part
            query_grads.append(dot(key_t, grad_scores, NN))
        sums_ref[0, :, lanes] = jnp.concatenate(query_grads, axis=1).T * 0.125
        sums_ref[1, :, lanes] = key_grad
        sums_ref[2, :, lanes] = value_grad
    dqkv_ref[...] = sums_ref[...].astype(BF16)


def attend_back(first, count, qkv, powers, inverse, attended, grad_attended):
    _, rows, width = qkv.shape
    block = (3, rows, 2 * HD)
    flat = pl.BlockSpec((rows, 2 * HD), lambda j: (0, j + first))
    return kernel_call(
        functools.partial(attention_backward_kernel, min(512, rows)),
        "attention_backward",
        (count,),
        [],
        [
            (qkv, pl.BlockSpec(block, lambda j: (0, 0, j + first))),
            (powers, pl.BlockSpec((2, rows, rows), lambda j: (j + first, 0, 0))),
            (inverse, pl.BlockSpec((1, 2, rows), lambda j: (j + first, 0, 0))),
            (attended, flat),
            (grad_attended, flat),
        ],
        [(struct((3, rows, 2 * HD * count)), pl.BlockSpec(block, lambda j: (0, 0, j)))],
        [pltpu.VMEM(block, F32)],
    )[0]


def project_own_kernel(at_ref, tokens_ref, recv_ref, lead_ref, gain_ref, shift_ref, weight_ref, bias_ref, rows_ref, normed_ref, heads_ref):
    own = pl.program_id(0) < pl.num_programs(0) // 2
    tokens = jnp.where(own, tokens_ref[0].astype(F32), recv_ref[...].astype(F32))
    rows_ref[...] = tokens.astype(BF16)
    scaled, _ = centred(tokens + lead_ref[...])
    normed = (scaled * gain_ref[...] + shift_ref[...]).astype(BF16)
    normed_ref[...] = normed
    for c in range(3):
        heads_ref[c] = (dot(normed, weight_ref[c], NN) + bias_ref[c : c + 1]).astype(BF16)


def project_own(at, tokens, recv, lead, gain, shift, weight, bias, chunk):
    half, width = tokens.shape[1:]
    heads = weight.shape[2]
    steps = half // chunk
    row = pl.BlockSpec((chunk, width), lambda j, at: (j, 0))
    return kernel_call(
        project_own_kernel,
        "project_own",
        (2 * steps,),
        [at],
        [
            (tokens, pl.BlockSpec((1, chunk, width), lambda j, at: (at[0], jnp.minimum(j, steps - 1), 0))),
            (recv, pl.BlockSpec((chunk, width), lambda j, at: (jnp.maximum(j - steps, 0), 0))),
            *[(v, whole(v)) for v in (lead, gain, shift, weight, bias)],
        ],
        [
            (struct((2 * half, width)), row),
            (struct((2 * half, width)), row),
            (struct((3, 2 * half, heads)), pl.BlockSpec((3, chunk, heads), lambda j, at: (0, j, 0))),
        ],
    )


def project_far_kernel(nat_ref, normed_ref, bias_ref, *refs):
    *pieces, heads_ref = refs
    size = pieces[0].shape[1]
    total = bias_ref[0]
    for k, piece in enumerate(pieces):
        total = total + dot(normed_ref[:, chunk_of(nat_ref, k, size)], piece[0], NN)
    heads_ref[0] = total.astype(BF16)


def project_far(nat, normed, bias, pieces):
    rows = normed.shape[0]
    heads = pieces[0].shape[2]
    first = lambda j, nat: (j, 0, 0)
    return kernel_call(
        project_far_kernel,
        "project_far",
        (3,),
        [nat],
        [
            (normed, whole(normed)),
            (bias[:, None], pl.BlockSpec((1, 1, heads), first)),
            *[(p, pl.BlockSpec((1, *p.shape[1:]), first)) for p in pieces],
        ],
        [(struct((3, rows, heads)), pl.BlockSpec((1, rows, heads), first))],
    )[0]


def middle_kernel(nat_ref, own_ref, far_ref, weight_ref, rows_ref, lead_ref, bias_ref, gain_ref, shift_ref, *refs):
    *pieces, middle_ref, normed_ref = refs
    total = dot(own_ref[...], weight_ref[...], NN)
    for k, piece in enumerate(pieces):
        total = total + dot(far_ref[:, chunk_of(nat_ref, k, piece.shape[0])], piece[...], NN)
    middle = rows_ref[...].astype(F32) + lead_ref[...] + total + bias_ref[...]
    middle_ref[...] = middle
    scaled, _ = centred(middle)
    normed_ref[...] = (scaled * gain_ref[...] + shift_ref[...]).astype(BF16)


def middle_layer(nat, own, far, weight, pieces, rows, lead, bias, gain, shift, chunk):
    count, width = rows.shape
    row = pl.BlockSpec((chunk, width), lambda j, nat: (j, 0))
    heads = pl.BlockSpec((chunk, own.shape[1]), lambda j, nat: (j, 0))
    return kernel_call(
        middle_kernel,
        "middle_layer",
        (count // chunk,),
        [nat],
        [(own, heads), (far, heads), (weight, whole(weight)), (rows, row)]
        + [(v, whole(v)) for v in (lead, bias, gain, shift, *pieces)],
        [(struct((count, width), F32), row), (struct((count, width)), row)],
    )


def gelu_store(pre_act, rows, hidden_ref, slope_ref):
    cdf = 0.5 * (1.0 + lax.erf(pre_act * 0.7071067811865476))
    hidden_ref[rows] = (pre_act * cdf).astype(BF16)
    density = jnp.exp(-0.5 * pre_act * pre_act) * 0.3989422804014327
    slope_ref[rows] = (cdf + pre_act * density).astype(BF16)


def hidden_kernel(block, nat_ref, normed_ref, bias_ref, *refs):
    *pieces, hidden_ref, slope_ref = refs
    size = pieces[0].shape[0]
    for start in range(0, normed_ref.shape[0], block):
        rows = slice(start, start + block)
        pre_act = bias_ref[...]
        for k, piece in enumerate(pieces):
            lanes = slice(None) if len(pieces) == 1 else chunk_of(nat_ref, k, size)
            pre_act = pre_act + dot(normed_ref[rows, lanes], piece[...], NN)
        gelu_store(pre_act, rows, hidden_ref, slope_ref)


def hidden_layer(nat, normed, bias, pieces, chunk):
    rows = normed.shape[0]
    units = pieces[0].shape[1]
    tile = min(512, units)
    column = lambda j, nat: (0, j)
    return kernel_call(
        functools.partial(hidden_kernel, chunk),
        "hidden_layer",
        (units // tile,),
        [nat],
        [(normed, whole(normed)), (bias, pl.BlockSpec((1, tile), column))]
        + [(p, pl.BlockSpec((p.shape[0], tile), column)) for p in pieces],
        [(struct((rows, units)), pl.BlockSpec((rows, tile), column))] * 2,
    )


def product_kernel(_, left_ref, right_ref, out_ref):
    if len(right_ref.shape) == 3:
        out_ref[0] = dot(left_ref[...], right_ref[0], TN).astype(BF16)
    else:
        out_ref[...] = dot(left_ref[...], right_ref[...], TN).astype(BF16)


def grad_right_half(half, left, right):
    rows, columns = left.shape
    kept = right.shape[1] // 2
    tile = min(1024, columns)
    return kernel_call(
        product_kernel,
        "grad_right_half",
        (columns // tile,),
        [half],
        [
            (left, pl.BlockSpec((rows, tile), lambda j, half: (0, j))),
            (right, pl.BlockSpec((rows, kept), lambda j, half: (0, half[0]))),
        ],
        [(struct((columns, kept)), pl.BlockSpec((tile, kept), lambda j, half: (j, 0)))],
    )[0]


def grad_left_half(half, left, right):
    rows = left.shape[0]
    kept = left.shape[1] // 2
    columns = right.shape[-1]
    tile = min(1024, columns)
    left_spec = pl.BlockSpec((rows, kept), lambda j, half: (0, half[0]))
    if right.ndim == 3:
        grid, out_shape = (right.shape[0],), (right.shape[0], kept, columns)
        right_spec = pl.BlockSpec((1, rows, columns), lambda j, half: (j, 0, 0))
        out_spec = pl.BlockSpec((1, kept, columns), lambda j, half: (j, 0, 0))
    else:
        grid, out_shape = (columns // tile,), (kept, columns)
        right_spec = pl.BlockSpec((rows, tile), lambda j, half: (0, j))
        out_spec = pl.BlockSpec((kept, tile), lambda j, half: (0, j))
    return kernel_call(
        product_kernel,
        "grad_left_half",
        grid,
        [half],
        [(left, left_spec), (right, right_spec)],
        [(struct(out_shape), out_spec)],
    )[0]


def pre_grad_store(grad, slope_ref, pre_ref, sum_ref):
    pre = (grad * slope_ref[...].astype(F32)).astype(BF16)
    pre_ref[...] = pre
    sum_ref[...] = column_sum(pre.astype(F32))


def pre_grad_own_kernel(low_ref, weight_ref, slope_ref, pre_ref, sum_ref):
    pre_grad_store(dot(low_ref[...], weight_ref[...], NT), slope_ref, pre_ref, sum_ref)


def pre_grad_own(low, weight, slope):
    rows, width = low.shape
    units = weight.shape[0]
    tile = min(512, units)
    column = lambda j: (0, j)
    return kernel_call(
        pre_grad_own_kernel,
        "pre_grad_own",
        (units // tile,),
        [],
        [
            (low, whole(low)),
            (weight, pl.BlockSpec((tile, width), lambda j: (j, 0))),
            (slope, pl.BlockSpec((rows, tile), column)),
        ],
        [
            (struct((rows, units)), pl.BlockSpec((rows, tile), column)),
            (struct((1, units), F32), pl.BlockSpec((1, tile), column)),
        ],
    )


def pre_grad_far_kernel(nat_ref, low_ref, slope_ref, *refs):
    *pieces, pre_ref, sum_ref = refs
    for k, piece in enumerate(pieces):

        @pl.when(pl.program_id(0) == k)
        def _(piece=piece):
            pre_grad_store(dot(low_ref[...], piece[...], NT), slope_ref, pre_ref, sum_ref)


def pre_grad_far(nat, low, pieces, slope):
    rows = low.shape[0]
    tile = pieces[0].shape[0]
    units = tile * len(pieces)
    column = lambda j, nat: (0, nat[j])
    return kernel_call(
        pre_grad_far_kernel,
        "pre_grad_far",
        (len(pieces),),
        [nat],
        [(low, whole(low)), (slope, pl.BlockSpec((rows, tile), column))] + [(p, whole(p)) for p in pieces],
        [
            (struct((rows, units)), pl.BlockSpec((rows, tile), column)),
            (struct((1, units), F32), pl.BlockSpec((1, tile), column)),
        ],
    )


def add_sums(sums_ref, rows):
    @pl.when(pl.program_id(0) == 0)
    def _():
        sums_ref[...] = jnp.zeros_like(sums_ref)

    for k, row in enumerate(rows):
        sums_ref[k : k + 1, :] += row


def middle_grad_kernel(nat_ref, own_ref, far_ref, weight_ref, middle_ref, cot_ref, loss_ref, gain_ref, *refs):
    *pieces, grad_ref, low_ref, sums_ref, total_ref = refs
    total_ref[...] = dot(own_ref[...], weight_ref[...], NT)
    for k, piece in enumerate(pieces):
        total_ref[:, chunk_of(nat_ref, k, piece.shape[0])] += dot(far_ref[...], piece[...], NT)
    grad = total_ref[...]
    scaled, inverse = centred(middle_ref[...])
    top = cot_ref[...].astype(F32) * loss_ref[...]
    grad_middle = top + norm_input_grad(grad, scaled, inverse, gain_ref[...])
    grad_ref[...] = grad_middle
    low_ref[...] = grad_middle.astype(BF16)
    add_sums(
        sums_ref,
        [column_sum(grad * scaled), column_sum(grad), column_sum(grad_middle), column_sum(top)],
    )


def middle_grad(nat, own, far, weight, pieces, middle, cot, loss, gain, chunk):
    count, width = middle.shape
    row = pl.BlockSpec((chunk, width), lambda j, nat: (j, 0))
    units = pl.BlockSpec((chunk, own.shape[1]), lambda j, nat: (j, 0))
    return kernel_call(
        middle_grad_kernel,
        "middle_grad",
        (count // chunk,),
        [nat],
        [(own, units), (far, units), (weight, whole(weight)), (middle, row), (cot, row)]
        + [(v, whole(v)) for v in (loss, gain, *pieces)],
        [
            (struct((count, width), F32), row),
            (struct((count, width)), row),
            (struct((8, width), F32), pl.BlockSpec((8, width), lambda j, nat: (0, 0))),
        ],
        [pltpu.VMEM((chunk, width), F32)],
    )


def attended_grad_kernel(nat_ref, low_ref, weight_ref, *refs):
    *pieces, own_ref, far_ref = refs
    own_ref[...] = dot(low_ref[...], weight_ref[...], NT).astype(BF16)
    for k, piece in enumerate(pieces):
        far_ref[:, chunk_of(nat_ref, k, piece.shape[0])] = dot(low_ref[...], piece[...], NT).astype(BF16)


def attended_grad(nat, low, weight, pieces, chunk):
    count, width = low.shape
    heads = weight.shape[0]
    out = (struct((count, heads)), pl.BlockSpec((chunk, heads), lambda j, nat: (j, 0)))
    return kernel_call(
        attended_grad_kernel,
        "attended_grad",
        (count // chunk,),
        [nat],
        [(low, pl.BlockSpec((chunk, width), lambda j, nat: (j, 0)))] + [(v, whole(v)) for v in (weight, *pieces)],
        [out, out],
    )


def output_kernel(nat_ref, own_ref, far_ref, weight_ref, middle_ref, bias_ref, *refs):
    *pieces, out_ref = refs
    total = dot(own_ref[...], weight_ref[...], NN)
    for k, piece in enumerate(pieces):
        total = total + dot(far_ref[:, chunk_of(nat_ref, k, piece.shape[0])], piece[...], NN)
    out_ref[...] = (middle_ref[...] + total + bias_ref[...]).astype(BF16)


def output_layer(nat, own, far, weight, pieces, middle, bias, chunk):
    count, width = middle.shape
    row = pl.BlockSpec((chunk, width), lambda j, nat: (j, 0))
    units = pl.BlockSpec((chunk, own.shape[1]), lambda j, nat: (j, 0))
    return kernel_call(
        output_kernel,
        "output_layer",
        (count // chunk,),
        [nat],
        [(own, units), (far, units), (weight, whole(weight)), (middle, row)]
        + [(v, whole(v)) for v in (bias, *pieces)],
        [(struct((count, width)), row)],
    )[0]


def input_grad_kernel(own_count, nat_ref, far_ref, weight_ref, rows_ref, lead_ref, grad_ref, gain_ref, *refs):
    owns, refs = refs[:own_count], refs[own_count:]
    *pieces, out_ref, low_ref, sums_ref, total_ref = refs
    total = None
    at = 0
    for own in owns:
        size = own.shape[2]
        for c in range(3):
            part = dot(own[c], weight_ref[c, :, at : at + size], NT)
            total = part if total is None else total + part
        at += size
    total_ref[...] = total
    for k, piece in enumerate(pieces):
        part = dot(far_ref[0], piece[0], NT) + dot(far_ref[1], piece[1], NT) + dot(far_ref[2], piece[2], NT)
        total_ref[:, chunk_of(nat_ref, k, piece.shape[1])] += part
    grad = total_ref[...]
    scaled, inverse = centred(rows_ref[...].astype(F32) + lead_ref[...])
    grad_shifted = grad_ref[...] + norm_input_grad(grad, scaled, inverse, gain_ref[...])
    out_ref[...] = grad_shifted
    low_ref[...] = grad_shifted.astype(BF16)
    bias_rows = [
        jnp.concatenate([column_sum(d[c].astype(F32)) for d in (*owns, far_ref)], axis=1) for c in (0, 2)
    ]
    add_sums(
        sums_ref, [column_sum(grad * scaled), column_sum(grad), column_sum(grad_shifted), *bias_rows]
    )


def input_grads(nat, owns, far, weight, pieces, rows, lead, grad_middle, gain, chunk):
    count, width = rows.shape
    row = pl.BlockSpec((chunk, width), lambda j, nat: (j, 0))
    heads = lambda d: pl.BlockSpec((3, chunk, d.shape[2]), lambda j, nat: (0, j, 0))
    steps = count // chunk
    half = pl.BlockSpec((chunk, width), lambda j, nat: (jnp.maximum(j - steps // 2, 0), 0))
    return kernel_call(
        functools.partial(input_grad_kernel, len(owns)),
        "input_grads",
        (steps,),
        [nat],
        [
            (far, heads(far)),
            (weight, whole(weight)),
            (rows, row),
            (lead, whole(lead)),
            (grad_middle, row),
            (gain, whole(gain)),
        ]
        + [(d, heads(d)) for d in owns]
        + [(p, whole(p)) for p in pieces],
        [
            (struct((count, width), F32), row),
            (struct((count // 2, width)), half),
            (struct((8, width), F32), pl.BlockSpec((8, width), lambda j, nat: (0, 0))),
        ],
        [pltpu.VMEM((chunk, width), F32)],
    )


def hold(*values):
    return lax.optimization_barrier(values)


def fast_body(
    tokens,
    cotangent,
    buckets,
    counts,
    lead_table,
    norm1_gain,
    norm1_shift,
    w_qkv,
    qv_bias,
    w_out,
    out_bias,
    norm2_gain,
    norm2_shift,
    w_fc1,
    fc1_bias,
    w_fc2,
    fc2_bias,
):
    replicas = lax.axis_size("dp")
    levels = replicas.bit_length() - 1
    dp_at, mp_at = lax.axis_index("dp"), lax.axis_index("mp")
    bits = [(dp_at >> level) & 1 for level in range(levels)]

    def over_x(value):
        return lax.ppermute(value, "mp", [(0, 1), (1, 0)])

    def over(level, value):
        return lax.ppermute(value, "dp", [(i, i ^ (1 << level)) for i in range(replicas)])

    def joined(bit, mine, theirs, axis=0):
        return jnp.where(
            bit == 0,
            jnp.concatenate([mine, theirs], axis),
            jnp.concatenate([theirs, mine], axis),
        )

    def part(value, index, count, axis=0):
        size = value.shape[axis] // count
        return lax.dynamic_slice_in_dim(value, index * size, size, axis)

    half_rows, width = tokens.shape[1:]
    heads_width = w_qkv.shape[2]
    units = w_fc1.shape[1]
    chunk = 256
    core, side = bits[0], bits[1]
    at = jnp.stack([mp_at, core, 1 - core]).astype(jnp.int32)
    keep_half, send_half = at[1:2], at[2:3]
    mine = core * 2 + side
    shared_nat = jnp.stack([mine, mine ^ 1, mine ^ 2, mine ^ 3]).astype(jnp.int32)
    direct_nat = jnp.stack([core * 2, core * 2 + 1, 2 - core * 2, 3 - core * 2]).astype(jnp.int32)
    pair_nat = at[1:3]

    def row_of(vector):
        return vector.astype(F32)[None]

    small = jnp.concatenate([qv_bias.reshape(-1), fc1_bias])
    small_rows = -(-small.shape[0] // width)
    small_rows_padded = -(-small_rows // 16) * 16
    small = jnp.pad(small, (0, small_rows_padded * width - small.shape[0])).reshape(-1, width)
    token_recv = over_x(jnp.concatenate([part(tokens, 1 - mp_at, 2)[0], small]))

    bucket = lax.dynamic_index_in_dim(buckets, mp_at, 0, keepdims=False)
    count_f = counts.astype(F32)
    loss_weight = jnp.mean(count_f) / lax.dynamic_index_in_dim(count_f, bucket, 0, keepdims=False)
    loss_row = jnp.broadcast_to(loss_weight, (1, width))
    lead = lax.dynamic_index_in_dim(lead_table, bucket, 0).astype(F32)
    own_qkv = jnp.transpose(w_qkv, (1, 0, 2))

    token_recv, qkv_send = hold(token_recv, part(own_qkv, mine, 4, 1))
    far_small = token_recv[half_rows:].reshape(-1)

    def bias_three(bias):
        bias_f = bias.astype(F32)
        return jnp.stack([bias_f[0], jnp.zeros_like(bias_f[0]), bias_f[1]])

    far_bias = bias_three(far_small[: 2 * heads_width].reshape(2, heads_width))
    far_fc1_bias = row_of(far_small[2 * heads_width : 2 * heads_width + units])

    qkv_x = over_x(qkv_send)
    gain_one, gain_two = row_of(norm1_gain), row_of(norm2_gain)
    rows, normed_one, own_heads = project_own(
        at[:1], tokens, token_recv, lead, gain_one, row_of(norm1_shift), own_qkv, bias_three(qv_bias), chunk
    )
    own_heads, qkv_x, out_send, fc1_send = hold(own_heads, qkv_x, part(w_out, core, 2), part(w_fc1, mine, 4))

    qkv_y = over(1, qkv_x)
    out_x = over_x(out_send)
    fc1_x = over_x(fc1_send)
    own_attended, own_powers, own_inverse = attend(own_heads)
    own_attended, qkv_x, qkv_y, out_x = hold(own_attended, qkv_x, qkv_y, out_x)

    far_qkv = [qkv_x, qkv_y, over(0, qkv_x), over(0, qkv_y)]
    far_out = [out_x, over(0, out_x)]
    far_heads = project_far(shared_nat, normed_one, far_bias, far_qkv)
    far_heads, fc1_x, cot_send = hold(far_heads, fc1_x, part(cotangent, 1 - mp_at, 2)[0])

    fc1_y = over(1, fc1_x)
    cot_recv = over_x(cot_send)
    far_attended, far_powers, far_inverse = attend(far_heads)
    middle, normed_two = middle_layer(
        pair_nat, own_attended, far_attended, w_out, far_out, rows, lead,
        row_of(out_bias), gain_two, row_of(norm2_shift), chunk,
    )
    normed_two, fc1_x, fc1_y, cot_recv, fc2_send = hold(
        normed_two, fc1_x, fc1_y, cot_recv, part(w_fc2, core * 2, 4)
    )

    fc2_first = over_x(fc2_send)
    far_fc1 = [fc1_x, fc1_y, over(0, fc1_x), over(0, fc1_y)]
    cot_rows = jnp.concatenate([part(cotangent, mp_at, 2)[0], cot_recv])
    grad_low = (cot_rows.astype(F32) * loss_weight).astype(BF16)
    own_hidden, own_slope = hidden_layer(shared_nat, normed_two, row_of(fc1_bias), [w_fc1], chunk)
    far_hidden, far_slope = hidden_layer(shared_nat, normed_two, far_fc1_bias, far_fc1, chunk)
    far_hidden, own_hidden, fc2_first, grad_low, fc2_send = hold(
        far_hidden, own_hidden, fc2_first, grad_low, part(w_fc2, core * 2 + 1, 4)
    )

    def total(values):
        return sum(v.astype(F32) for v in values)

    def low(values):
        return total(values).astype(BF16)

    def halves(values, level):
        axis = values[0].ndim - 2
        bit = bits[level]
        return [part(v, bit, 2, axis) for v in values], [part(v, 1 - bit, 2, axis) for v in values]

    def spread(values, level):
        kept, sent = halves(values, level)
        return kept, over(level, low(sent))

    def collect(value, level):
        return joined(bits[level], value, over(level, value), value.ndim - 2)

    fc2_second = over_x(fc2_send)
    far_recv = over(0, grad_right_half(send_half, far_hidden, grad_low))
    own_recv = over(0, grad_right_half(send_half, own_hidden, grad_low))
    far_keep = grad_right_half(keep_half, far_hidden, grad_low)
    own_keep = grad_right_half(keep_half, own_hidden, grad_low)
    own_keep, far_keep, far_recv, own_recv, fc2_second, grad_low = hold(
        own_keep, far_keep, far_recv, own_recv, fc2_second, grad_low
    )

    fc2_recv = over_x(low([far_keep, far_recv]))
    far_fc2 = [fc2_first, fc2_second, over(0, fc2_first), over(0, fc2_second)]
    own_pre, own_fc1_bias = pre_grad_own(grad_low, w_fc2, own_slope)
    far_pre, far_fc1_bias_sum = pre_grad_far(direct_nat, grad_low, far_fc2, far_slope)
    fc1_far_recv = over(0, grad_left_half(send_half, normed_two, far_pre))
    fc1_far_keep = grad_left_half(keep_half, normed_two, far_pre)
    fc1_own_recv = over(0, grad_left_half(send_half, normed_two, own_pre))
    fc1_own_keep = grad_left_half(keep_half, normed_two, own_pre)
    own_pre, far_pre, fc1_far_keep, fc1_far_recv, fc1_own_keep, fc1_own_recv = hold(
        own_pre, far_pre, fc1_far_keep, fc1_far_recv, fc1_own_keep, fc1_own_recv
    )

    fc1_recv = over_x(low([fc1_far_keep, fc1_far_recv]))
    grad_middle, grad_branch, sums_two = middle_grad(
        shared_nat, own_pre, far_pre, w_fc1, far_fc1, middle, cot_rows, loss_row, gain_two, chunk
    )
    own_grad_att, far_grad_att = attended_grad(pair_nat, grad_branch, w_out, far_out, chunk)
    far_grad_att, own_grad_att, fc2_recv = hold(far_grad_att, own_grad_att, fc2_recv)

    fc2_terms = [own_keep, own_recv, fc2_recv]
    fc2_kept, fc2_recv = spread(fc2_terms, 1)
    out_far_recv = over(0, grad_left_half(send_half, grad_branch, far_attended))
    out_far_keep = grad_left_half(keep_half, grad_branch, far_attended)
    out_own_recv = over(0, grad_left_half(send_half, grad_branch, own_attended))
    out_own_keep = grad_left_half(keep_half, grad_branch, own_attended)
    pairs = heads_width // (2 * HD)
    far_dqkv = attend_back(0, pairs, far_heads, far_powers, far_inverse, far_attended, far_grad_att)
    far_dqkv, fc2_recv, out_far_keep, out_far_recv, own_grad_att = hold(
        far_dqkv, fc2_recv, out_far_keep, out_far_recv, own_grad_att
    )

    fc2_kept, fc2_recv = spread([*fc2_kept, fc2_recv], 2)
    out_recv = over_x(low([out_far_keep, out_far_recv]))
    qkv_far_recv = over(0, grad_left_half(send_half, normed_one, far_dqkv))
    qkv_far_keep = grad_left_half(keep_half, normed_one, far_dqkv)
    own_a = attend_back(0, pairs // 2, own_heads, own_powers, own_inverse, own_attended, own_grad_att)
    own_a, fc2_recv, out_recv, fc1_recv, qkv_far_keep, qkv_far_recv, own_grad_att = hold(
        own_a, fc2_recv, out_recv, fc1_recv, qkv_far_keep, qkv_far_recv, own_grad_att
    )

    fc1_terms = [
        jnp.concatenate(pair, 1)
        for pair in ((fc1_own_keep, out_own_keep), (fc1_own_recv, out_own_recv), (fc1_recv, out_recv))
    ]
    fc1_kept, fc1_recv = spread(fc1_terms, 1)
    qkv_recv = over_x(low([qkv_far_keep, qkv_far_recv]))
    for level in range(3, levels):
        fc2_kept, fc2_recv = spread([*fc2_kept, fc2_recv], level)
    own_b = attend_back(pairs // 2, pairs - pairs // 2, own_heads, own_powers, own_inverse, own_attended, own_grad_att)
    own_b, fc2_recv = hold(own_b, fc2_recv)

    fc2_mine = collect(low([*fc2_kept, fc2_recv]), levels - 1)

    def own_grads(half):
        return jnp.concatenate([grad_left_half(half, normed_one, own_a), grad_left_half(half, normed_one, own_b)], 2)

    qkv_own_recv = over(0, own_grads(send_half))
    qkv_own_keep = own_grads(keep_half)
    grad_shifted, grad_send, sums_one = input_grads(
        shared_nat, [own_a, own_b], far_dqkv, own_qkv, far_qkv, rows, lead, grad_middle, gain_one, chunk
    )
    grad_shifted, fc2_mine, fc1_recv, qkv_own_keep, qkv_own_recv, qkv_recv = hold(
        grad_shifted, fc2_mine, fc1_recv, qkv_own_keep, qkv_own_recv, qkv_recv
    )

    output = output_layer(direct_nat, own_hidden, far_hidden, w_fc2, far_fc2, middle, row_of(fc2_bias), chunk)
    qkv_kept, qkv_recv = spread([qkv_own_keep, qkv_own_recv, qkv_recv], 1)
    fc1_kept, fc1_recv = spread([*fc1_kept, fc1_recv], 2)
    for level in range(levels - 2, 1, -1):
        fc2_mine = collect(fc2_mine, level)
    bucket_rows = jnp.arange(counts.shape[0], dtype=jnp.int32)[:, None] == bucket
    bias_sums = jnp.concatenate([own_fc1_bias, far_fc1_bias_sum], 0)
    vectors = jnp.concatenate(
        [
            jnp.where(bucket_rows, sums_one[2:3], 0.0),
            sums_one[:2],
            sums_two[:4],
            jnp.where(mp_at == 0, sums_one[3:5], jnp.roll(sums_one[3:5], heads_width, 1)),
            jnp.where(mp_at == 0, bias_sums, bias_sums[::-1]).reshape(-1, width),
        ]
    )
    vectors = vectors + over_x(vectors)
    vectors = vectors + over(0, vectors)
    qkv_recv, fc1_recv, fc2_mine, output, vectors = hold(qkv_recv, fc1_recv, fc2_mine, output, vectors)

    output_recv = over_x(output[half_rows:])
    grad_recv = over_x(grad_send)
    fc2_mine = collect(fc2_mine, 1)
    for level in range(1, levels):
        vectors = vectors + over(level, vectors)
    for level in range(2, levels):
        qkv_kept, qkv_recv = spread([*qkv_kept, qkv_recv], level)
    for level in range(3, levels):
        fc1_kept, fc1_recv = spread([*fc1_kept, fc1_recv], level)
    qkv_mine, fc1_mine = low([*qkv_kept, qkv_recv]), low([*fc1_kept, fc1_recv])
    for level in range(levels - 1, 0, -1):
        fc1_mine = collect(fc1_mine, level)
        qkv_mine = collect(qkv_mine, level)
    block_output = joined(mp_at, output[None, :half_rows], output_recv[None])
    input_grad = joined(mp_at, grad_shifted[None, :half_rows], grad_recv[None].astype(F32))

    table = counts.shape[0]
    lead_grad, singles, rest = vectors[:table], vectors[table : table + 6], vectors[table + 6 :]
    qv_bias_grad = part(rest[:2], mp_at, 2, 1)
    fc1_bias_grad = part(rest[2:].reshape(-1), mp_at, 2)

    def finish(half, axis):
        return joined(core, half, over(0, half), axis).astype(F32)

    fc2_grad = finish(fc2_mine, 1)
    fc1_grad = finish(fc1_mine[:, :units], 0)
    out_grad = finish(fc1_mine[:, units:], 0).T
    qkv_grad = jnp.transpose(finish(qkv_mine, 1), (1, 0, 2))
    return (
        block_output,
        input_grad,
        lead_grad,
        singles[0],
        singles[1],
        qkv_grad,
        qv_bias_grad,
        out_grad,
        singles[4],
        singles[2],
        singles[3],
        fc1_grad,
        fc1_bias_grad,
        fc2_grad,
        singles[5],
    )


def solution(mesh):
    in_specs = (
        P("dp", "mp", None),
        P("dp", "mp", None),
        P("dp"),
        P(),
        P(),
        P(),
        P(),
        P(None, None, "mp"),
        P(None, "mp"),
        P("mp", None),
        P(),
        P(),
        P(),
        P(None, "mp"),
        P("mp"),
        P("mp", None),
        P(),
    )
    out_specs = (
        P("dp", "mp", None),
        P("dp", "mp", None),
        P(),
        P(),
        P(),
        P(None, None, "mp"),
        P(None, "mp"),
        P("mp", None),
        P(),
        P(),
        P(),
        P(None, "mp"),
        P("mp"),
        P("mp", None),
        P(),
    )
    def local(*args):
        replicas = lax.axis_size("dp")
        samples, half_rows, width = args[0].shape
        heads_width, units = args[7].shape[2], args[13].shape[1]
        fits = samples == 2 and lax.axis_size("mp") == 2 and replicas >= 16 and replicas & (replicas - 1) == 0
        even = half_rows % 256 == 0 and width == 2 * heads_width == 1024 and units == 2 * width
        return (fast_body if fits and even else body)(*args)

    return jax.shard_map(local, mesh=mesh, in_specs=in_specs, out_specs=out_specs, check_vma=False)
```

```python
import functools
import math

import jax
import jax.numpy as jnp
from jax import lax
from jax.experimental import pallas as pl
from jax.experimental.pallas import tpu as pltpu
from jax.sharding import PartitionSpec as P

HD = 64


EPS = 1e-05


def norm_forward(values, norm_gain, norm_shift):
    center = values - jnp.mean(values, axis=-1, keepdims=True)
    inverse = lax.rsqrt(jnp.mean(center * center, axis=-1, keepdims=True) + EPS)
    scaled = center * inverse
    return (scaled * norm_gain + norm_shift, scaled, inverse)


def norm_backward(grad_out, scaled, inverse, norm_gain):
    grad_scaled = grad_out * norm_gain
    grad_mean = jnp.mean(grad_scaled, axis=-1, keepdims=True)
    cross_mean = jnp.mean(grad_scaled * scaled, axis=-1, keepdims=True)
    grad_in = inverse * (grad_scaled - grad_mean - scaled * cross_mean)
    gain_grad = jnp.sum(grad_out * scaled, axis=(0, 1))
    shift_grad = jnp.sum(grad_out, axis=(0, 1))
    return (grad_in, gain_grad, shift_grad)


def gelu_slope(pre_act):
    normal_cdf = 0.5 * (1.0 + lax.erf(pre_act * 0.7071067811865476))
    return normal_cdf + pre_act * jnp.exp(-0.5 * pre_act * pre_act) * 0.3989422804014327


def attention_forward(query_all, key_all, value_all, block_rows):
    block_count = query_all.shape[0] // block_rows
    query_blocks = query_all.reshape((block_count, block_rows) + query_all.shape[1:])

    def one_block(query_block):
        scores = (
            jnp.einsum("qshd,kshd->shqk", query_block, key_all, preferred_element_type=jnp.float32)
            * 0.125
        )
        row_max = jnp.max(scores, axis=-1, keepdims=True)
        powers = jnp.exp(scores - row_max)
        exp_total = jnp.sum(powers, axis=-1, keepdims=True)
        attn_weights = (powers / exp_total).astype(jnp.bfloat16)
        attended = jnp.einsum(
            "shqk,kshd->qshd", attn_weights, value_all, preferred_element_type=jnp.float32
        )
        return (attended.astype(jnp.bfloat16), (row_max + jnp.log(exp_total))[..., 0])

    attended, log_total = lax.map(one_block, query_blocks)
    return (attended.reshape(query_all.shape), log_total)


def attention_backward(query_all, key_all, value_all, grad_attended, log_total, block_rows):
    block_count = query_all.shape[0] // block_rows
    query_blocks = query_all.reshape((block_count, block_rows) + query_all.shape[1:])
    grad_blocks = grad_attended.reshape((block_count, block_rows) + query_all.shape[1:])

    def one_block(running, sliced):
        key_grad, value_grad = running
        query_block, grad_block, log_block = sliced
        scores = (
            jnp.einsum("qshd,kshd->shqk", query_block, key_all, preferred_element_type=jnp.float32)
            * 0.125
        )
        attn_weights = jnp.exp(scores - log_block[..., None])
        weight_low = attn_weights.astype(jnp.bfloat16)
        grad_weights = jnp.einsum(
            "qshd,kshd->shqk", grad_block, value_all, preferred_element_type=jnp.float32
        )
        inner = jnp.sum(attn_weights * grad_weights, axis=-1, keepdims=True)
        grad_scores = (attn_weights * (grad_weights - inner)).astype(jnp.bfloat16)
        query_grad = (
            jnp.einsum("shqk,kshd->qshd", grad_scores, key_all, preferred_element_type=jnp.float32)
            * 0.125
        )
        key_grad = (
            key_grad
            + jnp.einsum(
                "shqk,qshd->kshd", grad_scores, query_block, preferred_element_type=jnp.float32
            )
            * 0.125
        )
        value_grad = value_grad + jnp.einsum(
            "shqk,qshd->kshd", weight_low, grad_block, preferred_element_type=jnp.float32
        )
        return ((key_grad, value_grad), query_grad.astype(jnp.bfloat16))

    zero_grad = jnp.zeros(key_all.shape, jnp.float32)
    (key_grad, value_grad), query_grad = lax.scan(
        one_block, (zero_grad, zero_grad), (query_blocks, grad_blocks, log_total)
    )
    return (
        query_grad.reshape(query_all.shape),
        key_grad.astype(jnp.bfloat16),
        value_grad.astype(jnp.bfloat16),
    )


def body(
    tokens,
    cotangent,
    buckets,
    counts,
    lead_table,
    norm1_gain,
    norm1_shift,
    w_qkv,
    qv_bias,
    w_out,
    out_bias,
    norm2_gain,
    norm2_shift,
    w_fc1,
    fc1_bias,
    w_fc2,
    fc2_bias,
):
    samples_here = tokens.shape[0]
    local_rows = tokens.shape[1]
    local_width = w_qkv.shape[2]
    local_heads = local_width // HD
    seq_len = local_rows * lax.axis_size("mp")
    block_rows = min(512, seq_len)
    head_shape = (seq_len, samples_here, local_heads, HD)
    count_f = counts.astype(jnp.float32)
    onehot = (buckets[:, None] == jnp.arange(counts.shape[0], dtype=jnp.int32)[None, :]).astype(
        jnp.float32
    )
    loss_weight = jnp.mean(count_f) / jnp.sum(onehot * count_f[None, :], axis=1)
    lead_rows = jnp.dot(
        onehot,
        lead_table.astype(jnp.float32),
        precision=lax.Precision.HIGHEST,
        preferred_element_type=jnp.float32,
    )
    shifted = jnp.swapaxes(tokens, 0, 1).astype(jnp.float32) + lead_rows[None]
    normed_one, scaled_one, inverse_one = norm_forward(
        shifted, norm1_gain.astype(jnp.float32), norm1_shift.astype(jnp.float32)
    )
    normed_one = normed_one.astype(jnp.bfloat16)
    normed_full = lax.all_gather(normed_one, "mp", axis=0, tiled=True)
    project = jnp.einsum("tsd,dcf->tscf", normed_full, w_qkv, preferred_element_type=jnp.float32)
    bias_f = qv_bias.astype(jnp.float32)
    query_all = (project[:, :, 0] + bias_f[0]).astype(jnp.bfloat16).reshape(head_shape)
    key_all = project[:, :, 1].astype(jnp.bfloat16).reshape(head_shape)
    value_all = (project[:, :, 2] + bias_f[1]).astype(jnp.bfloat16).reshape(head_shape)
    attended, log_total = attention_forward(query_all, key_all, value_all, block_rows)
    attended_flat = attended.reshape(seq_len, samples_here, local_width)
    picked = attended_flat
    branch = lax.psum_scatter(
        jnp.einsum("tsf,fd->tsd", picked, w_out, preferred_element_type=jnp.float32),
        "mp",
        scatter_dimension=0,
        tiled=True,
    )
    middle = shifted + branch + out_bias.astype(jnp.float32)
    gain_two = norm2_gain.astype(jnp.float32)
    normed_two, scaled_two, inverse_two = norm_forward(
        middle, gain_two, norm2_shift.astype(jnp.float32)
    )
    normed_two = normed_two.astype(jnp.bfloat16)
    grad_top = jnp.swapaxes(cotangent, 0, 1).astype(jnp.float32) * loss_weight[None, :, None]
    grad_low = grad_top.astype(jnp.bfloat16)
    fc1_full, fc1_bias_full, fc2_full = (
        lax.all_gather(w_fc1, "mp", axis=1, tiled=True),
        lax.all_gather(fc1_bias, "mp", axis=0, tiled=True),
        lax.all_gather(w_fc2, "mp", axis=0, tiled=True),
    )
    pre_act = jnp.einsum(
        "tsd,df->tsf", normed_two, fc1_full, preferred_element_type=jnp.float32
    ) + fc1_bias_full.astype(jnp.float32)
    hidden = jax.nn.gelu(pre_act, approximate=False).astype(jnp.bfloat16)
    mlp_branch = jnp.einsum("tsf,fd->tsd", hidden, fc2_full, preferred_element_type=jnp.float32)
    output = middle + mlp_branch + fc2_bias.astype(jnp.float32)
    grad_hidden = jnp.einsum("tsd,fd->tsf", grad_low, fc2_full, preferred_element_type=jnp.float32)
    grad_pre = (grad_hidden * gelu_slope(pre_act)).astype(jnp.bfloat16)
    grad_normed_two = jnp.einsum(
        "tsf,df->tsd", grad_pre, fc1_full, preferred_element_type=jnp.float32
    )
    fc1_part = jnp.einsum("tsd,tsf->df", normed_two, grad_pre, preferred_element_type=jnp.float32)
    fc1_bias_part = jnp.sum(grad_pre.astype(jnp.float32), axis=(0, 1))
    fc2_part = jnp.einsum("tsf,tsd->fd", hidden, grad_low, preferred_element_type=jnp.float32)
    fc1_grad, fc1_bias_grad, fc2_grad = (
        lax.psum_scatter(
            fc1_part.astype(jnp.bfloat16), "mp", scatter_dimension=1, tiled=True
        ).astype(jnp.float32),
        lax.psum_scatter(
            fc1_bias_part.astype(jnp.bfloat16), "mp", scatter_dimension=0, tiled=True
        ).astype(jnp.float32),
        lax.psum_scatter(
            fc2_part.astype(jnp.bfloat16), "mp", scatter_dimension=0, tiled=True
        ).astype(jnp.float32),
    )
    fc2_bias_grad = jnp.sum(grad_top, axis=(0, 1))
    grad_from_norm, gain_two_grad, shift_two_grad = norm_backward(
        grad_normed_two, scaled_two, inverse_two, gain_two
    )
    grad_middle = grad_top + grad_from_norm
    out_bias_grad = jnp.sum(grad_middle, axis=(0, 1))
    grad_branch = grad_middle.astype(jnp.bfloat16)
    grad_branch_full = lax.all_gather(grad_branch, "mp", axis=0, tiled=True)
    out_grad = jnp.einsum(
        "tsf,tsd->fd", attended_flat, grad_branch_full, preferred_element_type=jnp.float32
    )
    grad_attended = jnp.einsum(
        "tsd,fd->tsf", grad_branch_full, w_out, preferred_element_type=jnp.float32
    ).astype(jnp.bfloat16)
    query_grad, key_grad, value_grad = attention_backward(
        query_all, key_all, value_all, grad_attended.reshape(head_shape), log_total, block_rows
    )
    grad_project = jnp.stack([query_grad, key_grad, value_grad], axis=2).reshape(
        seq_len, samples_here, 3, local_width
    )
    qkv_grad = jnp.einsum(
        "tsd,tscf->dcf", normed_full, grad_project, preferred_element_type=jnp.float32
    )
    query_bias_grad = jnp.sum(query_grad.astype(jnp.float32), axis=(0, 1)).reshape(local_width)
    value_bias_grad = jnp.sum(value_grad.astype(jnp.float32), axis=(0, 1)).reshape(local_width)
    qv_bias_grad = jnp.stack([query_bias_grad, value_bias_grad])
    picked = grad_project
    grad_normed_one = lax.psum_scatter(
        jnp.einsum("tscf,dcf->tsd", picked, w_qkv, preferred_element_type=jnp.float32).astype(
            jnp.bfloat16
        ),
        "mp",
        scatter_dimension=0,
        tiled=True,
    ).astype(jnp.float32)
    grad_in_one, gain_one_grad, shift_one_grad = norm_backward(
        grad_normed_one, scaled_one, inverse_one, norm1_gain.astype(jnp.float32)
    )
    grad_shifted = grad_middle + grad_in_one
    lead_grad = jnp.dot(
        onehot.T,
        jnp.sum(grad_shifted, axis=0),
        precision=lax.Precision.HIGHEST,
        preferred_element_type=jnp.float32,
    )
    small_grads = jnp.stack(
        [gain_one_grad, shift_one_grad, out_bias_grad, gain_two_grad, shift_two_grad, fc2_bias_grad]
    )
    lead_grad, small_grads = lax.psum((lead_grad, small_grads), ("dp", "mp"))
    qkv_grad, qv_bias_grad, out_grad, fc1_grad, fc1_bias_grad, fc2_grad = (
        lax.psum(qkv_grad.astype(jnp.bfloat16), "dp").astype(jnp.float32),
        lax.psum(qv_bias_grad.astype(jnp.bfloat16), "dp").astype(jnp.float32),
        lax.psum(out_grad.astype(jnp.bfloat16), "dp").astype(jnp.float32),
        lax.psum(fc1_grad.astype(jnp.bfloat16), "dp").astype(jnp.float32),
        lax.psum(fc1_bias_grad.astype(jnp.bfloat16), "dp").astype(jnp.float32),
        lax.psum(fc2_grad.astype(jnp.bfloat16), "dp").astype(jnp.float32),
    )
    block_output = jnp.swapaxes(output, 0, 1).astype(jnp.bfloat16)
    input_grad = jnp.swapaxes(grad_shifted, 0, 1)
    return (
        block_output,
        input_grad,
        lead_grad,
        small_grads[0],
        small_grads[1],
        qkv_grad,
        qv_bias_grad,
        out_grad,
        small_grads[2],
        small_grads[3],
        small_grads[4],
        fc1_grad,
        fc1_bias_grad,
        fc2_grad,
        small_grads[5],
    )


F32 = jnp.float32
BF16 = jnp.bfloat16
NN = (((1,), (0,)), ((), ()))
NT = (((1,), (1,)), ((), ()))
TN = (((0,), (0,)), ((), ()))
MIB = 1 << 20


def dot(left, right, dims):
    return lax.dot_general(left, right, dims, preferred_element_type=F32)


def whole(array):
    return pl.BlockSpec(array.shape, lambda *_: (0,) * array.ndim, pipeline_mode=pl.Buffered(1))


def kernel_call(body, name, grid, scalars, ins, outs, scratch=(), vmem=32, time=6, pinned=()):
    spec = pltpu.PrefetchScalarGridSpec(
        num_scalar_prefetch=len(scalars),
        grid=grid,
        in_specs=[spec for _, spec in ins],
        out_specs=[spec for _, spec in outs],
        scratch_shapes=list(scratch),
    )
    return pl.pallas_call(
        body,
        out_shape=[shape for shape, _ in outs],
        grid_spec=spec,
        compiler_params=pltpu.CompilerParams(vmem_limit_bytes=vmem * MIB),
        cost_estimate=pl.CostEstimate(flops=MIB, transcendentals=0, bytes_accessed=int(time * 2 * MIB)),
        name=name,
    )(
        *scalars,
        *[
            pltpu.with_memory_space_constraint(array, pltpu.HBM) if k in pinned else array
            for k, (array, _) in enumerate(ins)
        ],
    )


def struct(shape, dtype=BF16):
    return jax.ShapeDtypeStruct(shape, dtype)


def centred(values):
    center = values - jnp.mean(values, axis=-1, keepdims=True)
    inverse = lax.rsqrt(jnp.mean(center * center, axis=-1, keepdims=True) + EPS)
    return center * inverse, inverse


def norm_input_grad(grad_out, scaled, inverse, gain):
    grad_scaled = grad_out * gain
    grad_mean = jnp.mean(grad_scaled, axis=-1, keepdims=True)
    cross_mean = jnp.mean(grad_scaled * scaled, axis=-1, keepdims=True)
    return inverse * (grad_scaled - grad_mean - scaled * cross_mean)


def column_sum(values):
    return jnp.sum(values, axis=0, keepdims=True)


def chunk_of(nat_ref, index, size):
    return pl.ds(pl.multiple_of(nat_ref[index] * size, size), size)


def attention_forward_kernel(qkv_ref, out_ref, power_ref, inverse_ref):
    outs = []
    for head in range(2):
        lanes = slice(HD * head, HD * head + HD)
        query = qkv_ref[0, :, lanes] * BF16(0.125)
        scores = dot(qkv_ref[1, :, lanes], query, NT)
        powers = jnp.exp(scores - jnp.max(scores, axis=0, keepdims=True))
        inverse = 1.0 / jnp.sum(powers, axis=0, keepdims=True)
        power_low = powers.astype(BF16)
        power_ref[head] = power_low
        inverse_ref[0, head : head + 1, :] = inverse
        outs.append(dot(qkv_ref[2, :, lanes], power_low, TN) * inverse)
    out_ref[...] = jnp.concatenate(outs, axis=0).T.astype(BF16)


def attend(qkv):
    _, rows, width = qkv.shape
    pairs = width // (2 * HD)
    return kernel_call(
        attention_forward_kernel,
        "attention_forward",
        (pairs,),
        [],
        [(qkv, pl.BlockSpec((3, rows, 2 * HD), lambda j: (0, 0, j)))],
        [
            (struct((rows, width)), pl.BlockSpec((rows, 2 * HD), lambda j: (0, j))),
            (pltpu.HBM((2 * pairs, rows, rows), BF16), pl.BlockSpec((2, rows, rows), lambda j: (j, 0, 0))),
            (struct((pairs, 2, rows), F32), pl.BlockSpec((1, 2, rows), lambda j: (j, 0, 0))),
        ],
        vmem=48,
        time=4 * pairs,
        pinned=[0],
    )


def attention_backward_kernel(block, qkv_ref, power_ref, inverse_ref, out_ref, grad_ref, dqkv_ref, sums_ref):
    rows_all = qkv_ref.shape[1]
    out_t = out_ref[...].astype(F32).T
    grad_t = grad_ref[...].astype(F32).T
    for head in range(2):
        lanes = slice(HD * head, HD * head + HD)
        inverse = inverse_ref[0, head : head + 1, :]
        grad_head = grad_t[lanes]
        inner = jnp.sum(grad_head * out_t[lanes], axis=0, keepdims=True) * inverse
        grad_scaled = grad_head * inverse
        grad_low_t = grad_scaled.astype(BF16)
        grad_low = grad_scaled.T.astype(BF16)
        query = qkv_ref[0, :, lanes] * BF16(0.125)
        key = qkv_ref[1, :, lanes]
        value = qkv_ref[2, :, lanes]
        key_t = key.T
        key_grad = value_grad = None
        query_grads = []
        for start in range(0, rows_all, block):
            rows = slice(start, start + block)
            power = power_ref[head, :, rows]
            grad_power = dot(value, grad_low_t[:, rows], NN) - inner[:, rows]
            grad_scores = (power.astype(F32) * grad_power).astype(BF16)
            key_part = dot(grad_scores, query[rows], NN)
            value_part = dot(power, grad_low[rows], NN)
            key_grad = key_part if key_grad is None else key_grad + key_part
            value_grad = value_part if value_grad is None else value_grad + value_part
            query_grads.append(dot(key_t, grad_scores, NN))
        sums_ref[0, :, lanes] = jnp.concatenate(query_grads, axis=1).T * 0.125
        sums_ref[1, :, lanes] = key_grad
        sums_ref[2, :, lanes] = value_grad
    dqkv_ref[...] = sums_ref[...].astype(BF16)


def attend_back(first, count, qkv, powers, inverse, attended, grad_attended):
    _, rows, width = qkv.shape
    block = (3, rows, 2 * HD)
    flat = pl.BlockSpec((rows, 2 * HD), lambda j: (0, j + first))
    return kernel_call(
        functools.partial(attention_backward_kernel, min(512, rows)),
        "attention_backward",
        (count,),
        [],
        [
            (qkv, pl.BlockSpec(block, lambda j: (0, 0, j + first))),
            (powers, pl.BlockSpec((2, rows, rows), lambda j: (j + first, 0, 0))),
            (inverse, pl.BlockSpec((1, 2, rows), lambda j: (j + first, 0, 0))),
            (attended, flat),
            (grad_attended, flat),
        ],
        [(struct((3, rows, 2 * HD * count)), pl.BlockSpec(block, lambda j: (0, 0, j)))],
        [pltpu.VMEM(block, F32)],
        vmem=40,
        time=5.5 * count,
        pinned=range(5),
    )[0]


def project_own_kernel(at_ref, tokens_ref, recv_ref, lead_ref, gain_ref, shift_ref, weight_ref, bias_ref, rows_ref, normed_ref, heads_ref):
    own = pl.program_id(0) < pl.num_programs(0) // 2
    tokens = jnp.where(own, tokens_ref[0].astype(F32), recv_ref[...].astype(F32))
    rows_ref[...] = tokens.astype(BF16)
    scaled, _ = centred(tokens + lead_ref[...])
    normed = (scaled * gain_ref[...] + shift_ref[...]).astype(BF16)
    normed_ref[...] = normed
    for c in range(3):
        heads_ref[c] = (dot(normed, weight_ref[c], NN) + bias_ref[c : c + 1]).astype(BF16)


def project_own(at, tokens, recv, lead, gain, shift, weight, bias, chunk):
    half, width = tokens.shape[1:]
    heads = weight.shape[2]
    steps = half // chunk
    row = pl.BlockSpec((chunk, width), lambda j, at: (j, 0))
    return kernel_call(
        project_own_kernel,
        "project_own",
        (2 * steps,),
        [at],
        [
            (tokens, pl.BlockSpec((1, chunk, width), lambda j, at: (at[0], jnp.minimum(j, steps - 1), 0))),
            (recv, pl.BlockSpec((chunk, width), lambda j, at: (jnp.maximum(j - steps, 0), 0))),
            *[(v, whole(v)) for v in (lead, gain, shift, weight, bias)],
        ],
        [
            (struct((2 * half, width)), row),
            (struct((2 * half, width)), row),
            (struct((3, 2 * half, heads)), pl.BlockSpec((3, chunk, heads), lambda j, at: (0, j, 0))),
        ],
        pinned=[0, 1, 5],
    )


def project_far_kernel(nat_ref, normed_ref, bias_ref, *refs):
    *pieces, heads_ref = refs
    size = pieces[0].shape[1]
    total = bias_ref[0]
    for k, piece in enumerate(pieces):
        total = total + dot(normed_ref[:, chunk_of(nat_ref, k, size)], piece[0], NN)
    heads_ref[0] = total.astype(BF16)


def project_far(nat, normed, bias, pieces):
    rows = normed.shape[0]
    heads = pieces[0].shape[2]
    first = lambda j, nat: (j, 0, 0)
    return kernel_call(
        project_far_kernel,
        "project_far",
        (3,),
        [nat],
        [
            (normed, whole(normed)),
            (bias[:, None], pl.BlockSpec((1, 1, heads), first)),
            *[(p, pl.BlockSpec((1, *p.shape[1:]), first)) for p in pieces],
        ],
        [(struct((3, rows, heads)), pl.BlockSpec((1, rows, heads), first))],
    )[0]


def middle_kernel(nat_ref, own_ref, far_ref, weight_ref, rows_ref, lead_ref, bias_ref, gain_ref, shift_ref, *refs):
    *pieces, middle_ref, normed_ref = refs
    total = dot(own_ref[...], weight_ref[...], NN)
    for k, piece in enumerate(pieces):
        total = total + dot(far_ref[:, chunk_of(nat_ref, k, piece.shape[0])], piece[...], NN)
    middle = rows_ref[...].astype(F32) + lead_ref[...] + total + bias_ref[...]
    middle_ref[...] = middle
    scaled, _ = centred(middle)
    normed_ref[...] = (scaled * gain_ref[...] + shift_ref[...]).astype(BF16)


def middle_layer(nat, own, far, weight, pieces, rows, lead, bias, gain, shift, chunk):
    count, width = rows.shape
    row = pl.BlockSpec((chunk, width), lambda j, nat: (j, 0))
    heads = pl.BlockSpec((chunk, own.shape[1]), lambda j, nat: (j, 0))
    return kernel_call(
        middle_kernel,
        "middle_layer",
        (count // chunk,),
        [nat],
        [(own, heads), (far, heads), (weight, whole(weight)), (rows, row)]
        + [(v, whole(v)) for v in (lead, bias, gain, shift, *pieces)],
        [(pltpu.HBM((count, width), F32), row), (struct((count, width)), row)],
        pinned=[2, 3],
    )


def gelu_store(pre_act, rows, hidden_ref, slope_ref):
    cdf = 0.5 * (1.0 + lax.erf(pre_act * 0.7071067811865476))
    hidden_ref[rows] = (pre_act * cdf).astype(BF16)
    density = jnp.exp(-0.5 * pre_act * pre_act) * 0.3989422804014327
    slope_ref[rows] = (cdf + pre_act * density).astype(BF16)


def hidden_kernel(block, nat_ref, normed_ref, bias_ref, *refs):
    *pieces, hidden_ref, slope_ref = refs
    size = pieces[0].shape[0]
    for start in range(0, normed_ref.shape[0], block):
        rows = slice(start, start + block)
        pre_act = bias_ref[...]
        for k, piece in enumerate(pieces):
            lanes = slice(None) if len(pieces) == 1 else chunk_of(nat_ref, k, size)
            pre_act = pre_act + dot(normed_ref[rows, lanes], piece[...], NN)
        gelu_store(pre_act, rows, hidden_ref, slope_ref)


def hidden_layer(nat, normed, bias, pieces, chunk):
    rows = normed.shape[0]
    units = pieces[0].shape[1]
    tile = min(512, units)
    column = lambda j, nat: (0, j)
    return kernel_call(
        functools.partial(hidden_kernel, chunk),
        "hidden_layer",
        (units // tile,),
        [nat],
        [(normed, whole(normed)), (bias, pl.BlockSpec((1, tile), column))]
        + [(p, pl.BlockSpec((p.shape[0], tile), column)) for p in pieces],
        [(struct((rows, units)), pl.BlockSpec((rows, tile), column))] * 2,
        vmem=24,
        time=10,
        pinned=range(2, 2 + len(pieces)),
    )


def product_kernel(_, left_ref, right_ref, *refs):
    *add, out_ref = refs
    stacked = len(right_ref.shape) == 3
    value = dot(left_ref[...], right_ref[0] if stacked else right_ref[...], TN)
    if add:
        value = value + (add[0][0] if stacked else add[0][...]).astype(F32)
    if stacked:
        out_ref[0] = value.astype(BF16)
    else:
        out_ref[...] = value.astype(BF16)


def grad_right_half(half, left, right, *add):
    rows, columns = left.shape
    kept = right.shape[1] // 2
    tile = min(1024, columns)
    out_spec = pl.BlockSpec((tile, kept), lambda j, half: (j, 0))
    return kernel_call(
        product_kernel,
        "grad_right_half",
        (columns // tile,),
        [half],
        [
            (left, pl.BlockSpec((rows, tile), lambda j, half: (0, j))),
            (right, pl.BlockSpec((rows, kept), lambda j, half: (0, half[0]))),
        ]
        + [(a, out_spec) for a in add],
        [(struct((columns, kept)), out_spec)],
        vmem=20,
        time=3,
    )[0]


def grad_left_half(half, left, right, *add):
    rows = left.shape[0]
    kept = left.shape[1] // 2
    columns = right.shape[-1]
    tile = min(1024, columns)
    left_spec = pl.BlockSpec((rows, kept), lambda j, half: (0, half[0]))
    if right.ndim == 3:
        grid, out_shape = (right.shape[0],), (right.shape[0], kept, columns)
        right_spec = pl.BlockSpec((1, rows, columns), lambda j, half: (j, 0, 0))
        out_spec = pl.BlockSpec((1, kept, columns), lambda j, half: (j, 0, 0))
    else:
        grid, out_shape = (columns // tile,), (kept, columns)
        right_spec = pl.BlockSpec((rows, tile), lambda j, half: (0, j))
        out_spec = pl.BlockSpec((kept, tile), lambda j, half: (0, j))
    return kernel_call(
        product_kernel,
        "grad_left_half",
        grid,
        [half],
        [(left, left_spec), (right, right_spec)] + [(a, out_spec) for a in add],
        [(struct(out_shape), out_spec)],
        vmem=20,
        time=3,
    )[0]


def pre_grad_store(grad, slope_ref, pre_ref, sum_ref):
    pre = (grad * slope_ref[...].astype(F32)).astype(BF16)
    pre_ref[...] = pre
    sum_ref[...] = column_sum(pre.astype(F32))


def pre_grad_own_kernel(low_ref, weight_ref, slope_ref, pre_ref, sum_ref):
    pre_grad_store(dot(low_ref[...], weight_ref[...], NT), slope_ref, pre_ref, sum_ref)


def pre_grad_own(low, weight, slope):
    rows, width = low.shape
    units = weight.shape[0]
    tile = min(512, units)
    column = lambda j: (0, j)
    return kernel_call(
        pre_grad_own_kernel,
        "pre_grad_own",
        (units // tile,),
        [],
        [
            (low, whole(low)),
            (weight, pl.BlockSpec((tile, width), lambda j: (j, 0))),
            (slope, pl.BlockSpec((rows, tile), column)),
        ],
        [
            (struct((rows, units)), pl.BlockSpec((rows, tile), column)),
            (struct((1, units), F32), pl.BlockSpec((1, tile), column)),
        ],
        vmem=24,
        pinned=[1],
    )


def pre_grad_far_kernel(per, nat_ref, low_ref, slope_ref, *refs):
    *pieces, pre_ref, sum_ref = refs
    for k, piece in enumerate(pieces):

        @pl.when(pl.program_id(0) // per == k)
        def _(piece=piece):
            pre_grad_store(dot(low_ref[...], piece[...], NT), slope_ref, pre_ref, sum_ref)


def pre_grad_far(nat, low, pieces, slope):
    rows, width = low.shape
    size = pieces[0].shape[0]
    tile = min(512, size)
    per = size // tile
    units = size * len(pieces)
    column = lambda j, nat: (0, nat[j // per] * per + j % per)

    def piece_spec(k):
        return pl.BlockSpec((tile, width), lambda j, nat: (jnp.clip(j - k * per, 0, per - 1), 0))

    return kernel_call(
        functools.partial(pre_grad_far_kernel, per),
        "pre_grad_far",
        (len(pieces) * per,),
        [nat],
        [(low, whole(low)), (slope, pl.BlockSpec((rows, tile), column))]
        + [(p, piece_spec(k)) for k, p in enumerate(pieces)],
        [
            (struct((rows, units)), pl.BlockSpec((rows, tile), column)),
            (struct((1, units), F32), pl.BlockSpec((1, tile), column)),
        ],
        vmem=24,
        time=8,
        pinned=range(2, 2 + len(pieces)),
    )


def add_sums(sums_ref, rows):
    @pl.when(pl.program_id(0) == 0)
    def _():
        sums_ref[...] = jnp.zeros_like(sums_ref)

    for k, row in enumerate(rows):
        sums_ref[k : k + 1, :] += row


def middle_grad_kernel(nat_ref, own_ref, far_ref, weight_ref, middle_ref, cot_ref, loss_ref, gain_ref, *refs):
    *pieces, grad_ref, low_ref, sums_ref, total_ref = refs
    total_ref[...] = dot(own_ref[...], weight_ref[...], NT)
    for k, piece in enumerate(pieces):
        total_ref[:, chunk_of(nat_ref, k, piece.shape[0])] += dot(far_ref[...], piece[...], NT)
    grad = total_ref[...]
    scaled, inverse = centred(middle_ref[...])
    top = cot_ref[...].astype(F32) * loss_ref[...]
    grad_middle = top + norm_input_grad(grad, scaled, inverse, gain_ref[...])
    grad_ref[...] = grad_middle
    low_ref[...] = grad_middle.astype(BF16)
    add_sums(
        sums_ref,
        [column_sum(grad * scaled), column_sum(grad), column_sum(grad_middle), column_sum(top)],
    )


def middle_grad(nat, own, far, weight, pieces, middle, cot, loss, gain, chunk):
    count, width = middle.shape
    row = pl.BlockSpec((chunk, width), lambda j, nat: (j, 0))
    units = pl.BlockSpec((chunk, own.shape[1]), lambda j, nat: (j, 0))
    return kernel_call(
        middle_grad_kernel,
        "middle_grad",
        (count // chunk,),
        [nat],
        [(own, units), (far, units), (weight, whole(weight)), (middle, row), (cot, row)]
        + [(v, whole(v)) for v in (loss, gain, *pieces)],
        [
            (struct((count, width), F32), row),
            (struct((count, width)), row),
            (struct((8, width), F32), pl.BlockSpec((8, width), lambda j, nat: (0, 0))),
        ],
        [pltpu.VMEM((chunk, width), F32)],
        time=14,
        pinned=[2, 3, 4, *range(7, 7 + len(pieces))],
    )


def attended_grad_kernel(nat_ref, low_ref, weight_ref, *refs):
    *pieces, own_ref, far_ref = refs
    own_ref[...] = dot(low_ref[...], weight_ref[...], NT).astype(BF16)
    for k, piece in enumerate(pieces):
        far_ref[:, chunk_of(nat_ref, k, piece.shape[0])] = dot(low_ref[...], piece[...], NT).astype(BF16)


def attended_grad(nat, low, weight, pieces, chunk):
    count, width = low.shape
    heads = weight.shape[0]
    out = (struct((count, heads)), pl.BlockSpec((chunk, heads), lambda j, nat: (j, 0)))
    return kernel_call(
        attended_grad_kernel,
        "attended_grad",
        (count // chunk,),
        [nat],
        [(low, pl.BlockSpec((chunk, width), lambda j, nat: (j, 0)))] + [(v, whole(v)) for v in (weight, *pieces)],
        [out, out],
        pinned=range(1, 2 + len(pieces)),
    )


def output_own_kernel(own_ref, weight_ref, out_ref):
    out_ref[...] = dot(own_ref[...], weight_ref[...], NN)


def output_own(own, weight, chunk):
    count, units = own.shape
    width = weight.shape[1]
    return kernel_call(
        output_own_kernel,
        "output_own",
        (count // chunk,),
        [],
        [(own, pl.BlockSpec((chunk, units), lambda j: (j, 0))), (weight, whole(weight))],
        [(struct((count, width), F32), pl.BlockSpec((chunk, width), lambda j: (j, 0)))],
        vmem=20,
        time=6,
    )[0]


def output_kernel(nat_ref, far_ref, own_ref, middle_ref, bias_ref, *refs):
    *pieces, out_ref = refs
    total = own_ref[...]
    for k, piece in enumerate(pieces):
        total = total + dot(far_ref[:, chunk_of(nat_ref, k, piece.shape[0])], piece[...], NN)
    out_ref[...] = (middle_ref[...] + total + bias_ref[...]).astype(BF16)


def output_layer(nat, first, count, far, own, pieces, middle, bias, chunk):
    width = middle.shape[1]
    row = pl.BlockSpec((chunk, width), lambda j, nat: (j + first, 0))
    return kernel_call(
        output_kernel,
        "output_layer",
        (count,),
        [nat],
        [(far, pl.BlockSpec((chunk, far.shape[1]), lambda j, nat: (j + first, 0))), (own, row), (middle, row)]
        + [(v, whole(v)) for v in (bias, *pieces)],
        [(struct((count * chunk, width)), pl.BlockSpec((chunk, width), lambda j, nat: (j, 0)))],
        vmem=24,
        time=6,
        pinned=range(4 + len(pieces)),
    )[0]


def input_grad_kernel(own_count, nat_ref, far_ref, weight_ref, rows_ref, lead_ref, grad_ref, gain_ref, *refs):
    owns, refs = refs[:own_count], refs[own_count:]
    *pieces, out_ref, low_ref, sums_ref, total_ref = refs
    total = None
    at = 0
    for own in owns:
        size = own.shape[2]
        for c in range(3):
            part = dot(own[c], weight_ref[c, :, at : at + size], NT)
            total = part if total is None else total + part
        at += size
    total_ref[...] = total
    for k, piece in enumerate(pieces):
        part = dot(far_ref[0], piece[0], NT) + dot(far_ref[1], piece[1], NT) + dot(far_ref[2], piece[2], NT)
        total_ref[:, chunk_of(nat_ref, k, piece.shape[1])] += part
    grad = total_ref[...]
    scaled, inverse = centred(rows_ref[...].astype(F32) + lead_ref[...])
    grad_shifted = grad_ref[...] + norm_input_grad(grad, scaled, inverse, gain_ref[...])
    out_ref[...] = grad_shifted
    low_ref[...] = grad_shifted.astype(BF16)
    bias_rows = [
        jnp.concatenate([column_sum(d[c].astype(F32)) for d in (*owns, far_ref)], axis=1) for c in (0, 2)
    ]
    add_sums(
        sums_ref, [column_sum(grad * scaled), column_sum(grad), column_sum(grad_shifted), *bias_rows]
    )


def input_grads(nat, owns, far, weight, pieces, rows, lead, grad_middle, gain, chunk):
    count, width = rows.shape
    row = pl.BlockSpec((chunk, width), lambda j, nat: (j, 0))
    heads = lambda d: pl.BlockSpec((3, chunk, d.shape[2]), lambda j, nat: (0, j, 0))
    steps = count // chunk
    half = pl.BlockSpec((chunk, width), lambda j, nat: (jnp.maximum(j - steps // 2, 0), 0))
    return kernel_call(
        functools.partial(input_grad_kernel, len(owns)),
        "input_grads",
        (steps,),
        [nat],
        [
            (far, heads(far)),
            (weight, whole(weight)),
            (rows, row),
            (lead, whole(lead)),
            (grad_middle, row),
            (gain, whole(gain)),
        ]
        + [(d, heads(d)) for d in owns]
        + [(p, whole(p)) for p in pieces],
        [
            (struct((count, width), F32), row),
            (struct((count // 2, width)), half),
            (struct((8, width), F32), pl.BlockSpec((8, width), lambda j, nat: (0, 0))),
        ],
        [pltpu.VMEM((chunk, width), F32)],
        time=14,
        pinned=[1, 2, 4, *range(6 + len(owns), 6 + len(owns) + len(pieces))],
    )


def finish_kernel(turned, at_ref, mine_ref, theirs_ref, out_ref):
    value = jnp.where(pl.program_id(0) == 0, mine_ref[...].astype(F32), theirs_ref[...].astype(F32))
    out_ref[...] = (value.T if turned else value).reshape(out_ref.shape)


def finish(at, mine, theirs, block, out_shape, target, turned=False):
    grid = [size // unit for size, unit in zip(mine.shape, block)]
    steps = math.prod(grid)
    out_block = [block[-1], block[-2]] if turned else [1] * (len(out_shape) - 2) + list(block[-2:])

    def split(step):
        places = []
        for size in reversed(grid):
            places.insert(0, step % size)
            step = step // size
        return tuple(places)

    def source(which):
        idle = 0 if which else steps - 1
        return pl.BlockSpec(block, lambda s, j, at: split(jnp.where(s == which, j, idle)))

    return kernel_call(
        functools.partial(finish_kernel, turned),
        "finish",
        (2, steps),
        [at],
        [(mine, source(0)), (theirs, source(1))],
        [(struct(out_shape, F32), pl.BlockSpec(tuple(out_block), lambda s, j, at: target(at[s], split(j))))],
        vmem=16,
        time=4,
    )[0]


def hold(*values):
    return lax.optimization_barrier(values)


def fast_body(
    tokens,
    cotangent,
    buckets,
    counts,
    lead_table,
    norm1_gain,
    norm1_shift,
    w_qkv,
    qv_bias,
    w_out,
    out_bias,
    norm2_gain,
    norm2_shift,
    w_fc1,
    fc1_bias,
    w_fc2,
    fc2_bias,
):
    replicas = lax.axis_size("dp")
    levels = replicas.bit_length() - 1
    dp_at, mp_at = lax.axis_index("dp"), lax.axis_index("mp")
    bits = [(dp_at >> level) & 1 for level in range(levels)]

    def over_x(value):
        return lax.ppermute(value, "mp", [(0, 1), (1, 0)])

    def over(level, value):
        return lax.ppermute(value, "dp", [(i, i ^ (1 << level)) for i in range(replicas)])

    def joined(bit, mine, theirs, axis=0):
        return jnp.where(
            bit == 0,
            jnp.concatenate([mine, theirs], axis),
            jnp.concatenate([theirs, mine], axis),
        )

    def part(value, index, count, axis=0):
        size = value.shape[axis] // count
        return lax.dynamic_slice_in_dim(value, index * size, size, axis)

    half_rows, width = tokens.shape[1:]
    heads_width = w_qkv.shape[2]
    units = w_fc1.shape[1]
    chunk = 256
    core, side = bits[0], bits[1]
    at = jnp.stack([mp_at, core, 1 - core]).astype(jnp.int32)
    mine = core * 2 + side
    shared_nat = jnp.stack([mine, mine ^ 1, mine ^ 2, mine ^ 3]).astype(jnp.int32)

    def row_of(vector):
        return vector.astype(F32)[None]

    small = jnp.concatenate([qv_bias.reshape(-1), fc1_bias])
    small_rows = -(-small.shape[0] // width)
    small_rows_padded = -(-small_rows // 16) * 16
    small = jnp.pad(small, (0, small_rows_padded * width - small.shape[0])).reshape(-1, width)
    token_recv = over_x(jnp.concatenate([part(tokens, 1 - mp_at, 2)[0], small]))

    bucket = lax.dynamic_index_in_dim(buckets, mp_at, 0, keepdims=False)
    count_f = counts.astype(F32)
    loss_weight = jnp.mean(count_f) / lax.dynamic_index_in_dim(count_f, bucket, 0, keepdims=False)
    loss_row = jnp.broadcast_to(loss_weight, (1, width))
    lead = lax.dynamic_index_in_dim(lead_table, bucket, 0).astype(F32)
    own_qkv = jnp.transpose(w_qkv, (1, 0, 2))

    def bias_three(bias):
        bias_f = bias.astype(F32)
        return jnp.stack([bias_f[0], jnp.zeros_like(bias_f[0]), bias_f[1]])

    (
        token_recv, qkv_send, out_send, fc1_send, cot_send, fc2_send, at, shared_nat, loss_row, loss_weight, lead,
        gain_one, gain_two, shift_one, shift_two, out_row, fc1_row, fc2_row, own_bias,
    ) = hold(
        token_recv,
        part(own_qkv, mine, 4, 1),
        part(w_out, core, 2),
        part(w_fc1, mine, 4),
        part(cotangent, 1 - mp_at, 2)[0],
        part(w_fc2, core, 2),
        at,
        shared_nat,
        loss_row,
        loss_weight,
        lead,
        row_of(norm1_gain),
        row_of(norm2_gain),
        row_of(norm1_shift),
        row_of(norm2_shift),
        row_of(out_bias),
        row_of(fc1_bias),
        row_of(fc2_bias),
        bias_three(qv_bias),
    )
    keep_half, send_half, pair_nat = at[1:2], at[2:3], at[1:3]
    far_small = token_recv[half_rows:].reshape(-1)
    far_bias = bias_three(far_small[: 2 * heads_width].reshape(2, heads_width))
    far_fc1_bias = row_of(far_small[2 * heads_width : 2 * heads_width + units])

    qkv_x = over_x(qkv_send)
    rows, normed_one, own_heads = project_own(
        at[:1], tokens, token_recv, lead, gain_one, shift_one, own_qkv, own_bias, chunk
    )
    own_heads, qkv_x, out_send, fc1_send, far_bias, far_fc1_bias = hold(
        own_heads, qkv_x, out_send, fc1_send, far_bias, far_fc1_bias
    )

    qkv_y = over(1, qkv_x)
    out_x = over_x(out_send)
    fc1_x = over_x(fc1_send)
    own_attended, own_powers, own_inverse = attend(own_heads)
    own_attended, qkv_x, qkv_y, out_x = hold(own_attended, qkv_x, qkv_y, out_x)

    far_qkv = [qkv_x, qkv_y, over(0, qkv_x), over(0, qkv_y)]
    far_out = [out_x, over(0, out_x)]
    far_heads = project_far(shared_nat, normed_one, far_bias, far_qkv)
    far_heads, fc1_x, cot_send = hold(far_heads, fc1_x, cot_send)

    fc1_y = over(1, fc1_x)
    cot_recv = over_x(cot_send)
    far_attended, far_powers, far_inverse = attend(far_heads)
    middle, normed_two = middle_layer(
        pair_nat, own_attended, far_attended, w_out, far_out, rows, lead,
        out_row, gain_two, shift_two, chunk,
    )
    normed_two, fc1_x, fc1_y, cot_recv, fc2_send = hold(
        normed_two, fc1_x, fc1_y, cot_recv, fc2_send
    )

    def total(values):
        return sum(v.astype(F32) for v in values)

    def low(values):
        return total(values).astype(BF16)

    def cut(terms, size):
        return low([lax.dynamic_slice_in_dim(a, at, size, a.ndim - 2) for a, at in terms])

    def moved(terms, offset):
        return [(a, at + offset) for a, at in terms]

    def fresh(*arrays):
        return [(a, 0) for a in arrays]

    def spread(terms, size, level):
        half = size // 2
        return moved(terms, bits[level] * half), over(level, cut(moved(terms, (1 - bits[level]) * half), half))

    def first_steps(own, far, size):
        half, quarter = size // 2, size // 4
        kept, sent = half + side * quarter, half + (1 - side) * quarter
        recv_x = over_x(cut(far, half))
        recv_y = over(1, jnp.concatenate([cut(moved(own, sent), quarter), cut(moved(far, sent), quarter)]))
        return moved(own, kept), moved(far, kept), recv_x, recv_y

    def second_steps(own, own_down, far_down, recv_x, recv_y, size):
        half, quarter = size // 2, size // 4
        up, recv_up = spread(own + fresh(recv_x), half, 1)
        recv_down = over_x(cut(far_down + [(recv_y, quarter)], quarter))
        return up, own_down + fresh(recv_y), recv_up, recv_down


    fc2_x = over_x(fc2_send)
    far_fc1 = [fc1_x, fc1_y, over(0, fc1_x), over(0, fc1_y)]
    cot_rows = jnp.concatenate([part(cotangent, mp_at, 2)[0], cot_recv])
    grad_low = (cot_rows.astype(F32) * loss_weight).astype(BF16)
    own_hidden, own_slope = hidden_layer(shared_nat, normed_two, fc1_row, [w_fc1], chunk)
    far_hidden, far_slope = hidden_layer(shared_nat, normed_two, far_fc1_bias, far_fc1, chunk)
    far_send = grad_right_half(send_half, far_hidden, grad_low)
    own_send = grad_right_half(send_half, own_hidden, grad_low)
    far_send, own_send, fc2_x, grad_low, far_hidden = hold(far_send, own_send, fc2_x, grad_low, far_hidden)

    far_recv, own_recv, fc2_core = over(0, far_send), over(0, own_send), over(0, fc2_x)
    own_pre, own_fc1_bias = pre_grad_own(grad_low, w_fc2, own_slope)
    fc1_own_send = grad_left_half(send_half, normed_two, own_pre)
    far_sum = grad_right_half(keep_half, far_hidden, grad_low, far_recv)
    own_sum = grad_right_half(keep_half, own_hidden, grad_low, own_recv)
    own_pre, fc1_own_send, far_sum, own_sum, fc2_core, grad_low = hold(
        own_pre, fc1_own_send, far_sum, own_sum, fc2_core, grad_low
    )

    half_width = width // 2
    fc2_own = fresh(own_sum)
    fc2_own_down, fc2_far_down, recv_x, recv_y = first_steps(fc2_own, fresh(far_sum), units)
    fc1_own_recv = over(0, fc1_own_send)
    far_fc2 = [fc2_x, fc2_core]
    far_pre, far_fc1_bias_sum = pre_grad_far(pair_nat, grad_low, far_fc2, far_slope)
    fc1_far_send = grad_left_half(send_half, normed_two, far_pre)
    fc1_own_sum = grad_left_half(keep_half, normed_two, own_pre, fc1_own_recv)
    mlp_own = output_own(own_hidden, w_fc2, chunk)
    fc1_far_send, fc1_own_sum, recv_x, recv_y, far_pre, mlp_own = hold(
        fc1_far_send, fc1_own_sum, recv_x, recv_y, far_pre, mlp_own
    )

    fc2_up, fc2_down, recv_up, recv_down = second_steps(fc2_own, fc2_own_down, fc2_far_down, recv_x, recv_y, units)
    fc1_far_recv = over(0, fc1_far_send)
    grad_middle, grad_branch, sums_two = middle_grad(
        shared_nat, own_pre, far_pre, w_fc1, far_fc1, middle, cot_rows, loss_row, gain_two, chunk
    )
    own_grad_att, far_grad_att = attended_grad(pair_nat, grad_branch, w_out, far_out, chunk)
    fc1_far_sum = grad_left_half(keep_half, normed_two, far_pre, fc1_far_recv)
    far_grad_att, own_grad_att, grad_branch, recv_up, recv_down, fc1_far_sum = hold(
        far_grad_att, own_grad_att, grad_branch, recv_up, recv_down, fc1_far_sum
    )

    quarter_rows = units // 4
    fc2_both = jnp.stack([cut(fc2_up + fresh(recv_up), quarter_rows), cut(fc2_down + fresh(recv_down), quarter_rows)])
    fc2_terms, fc2_recv = spread(fresh(fc2_both), quarter_rows, 2)
    fc1_own = fresh(fc1_own_sum)
    fc1_own_down, fc1_far_down, recv_x, recv_y = first_steps(fc1_own, fresh(fc1_far_sum), half_width)
    out_far_recv = over(0, grad_left_half(send_half, grad_branch, far_attended))
    out_own_recv = over(0, grad_left_half(send_half, grad_branch, own_attended))
    pairs = heads_width // (2 * HD)
    far_dqkv = attend_back(0, pairs, far_heads, far_powers, far_inverse, far_attended, far_grad_att)
    out_far_sum = grad_left_half(keep_half, grad_branch, far_attended, out_far_recv)
    out_own_sum = grad_left_half(keep_half, grad_branch, own_attended, out_own_recv)
    far_dqkv, own_grad_att, recv_x, recv_y, fc2_recv, out_far_sum, out_own_sum = hold(
        far_dqkv, own_grad_att, recv_x, recv_y, fc2_recv, out_far_sum, out_own_sum
    )

    fc1_up, fc1_down, recv_up, recv_down = second_steps(fc1_own, fc1_own_down, fc1_far_down, recv_x, recv_y, half_width)
    fc2_terms, fc2_recv = spread(fc2_terms + fresh(fc2_recv), quarter_rows // 2, 3)
    out_recv = over_x(out_far_sum)
    qkv_far_recv = over(0, grad_left_half(send_half, normed_one, far_dqkv))
    qkv_far_keep = grad_left_half(keep_half, normed_one, far_dqkv)
    own_a = attend_back(0, pairs // 2, own_heads, own_powers, own_inverse, own_attended, own_grad_att)
    own_a_send = grad_left_half(send_half, normed_one, own_a)
    own_a_send, own_grad_att, recv_up, recv_down, fc2_recv, out_recv, qkv_far_recv, qkv_far_keep = hold(
        own_a_send, own_grad_att, recv_up, recv_down, fc2_recv, out_recv, qkv_far_recv, qkv_far_keep
    )

    side_a = heads_width // 2
    own_a_recv = over(0, own_a_send)
    qkv_first = over_x(low([qkv_far_keep[..., :side_a], qkv_far_recv[..., :side_a]]))
    fc2_size = quarter_rows // 4
    fc2_terms = fc2_terms + fresh(fc2_recv)
    for level in range(4, levels):
        fc2_terms, fc2_recv = spread(fc2_terms, fc2_size, level)
        fc2_terms, fc2_size = fc2_terms + fresh(fc2_recv), fc2_size // 2
    fc2_mine = cut(fc2_terms, fc2_size)
    fc2_recv = over(levels - 1, fc2_mine)
    fc1_rows = half_width // 4
    fc1_both = jnp.stack([cut(fc1_up + fresh(recv_up), fc1_rows), cut(fc1_down + fresh(recv_down), fc1_rows)])
    fc1_terms, fc1_recv = spread(fresh(fc1_both), fc1_rows, 2)
    out_terms, out_y = spread(fresh(out_own_sum, out_recv), half_width, 1)
    own_b = attend_back(pairs // 2, pairs - pairs // 2, own_heads, own_powers, own_inverse, own_attended, own_grad_att)
    own_a_sum = grad_left_half(keep_half, normed_one, own_a, own_a_recv)
    own_b_send = grad_left_half(send_half, normed_one, own_b)
    own_b, own_b_send, own_a_sum, fc1_recv, fc2_recv, out_y, qkv_first, qkv_far_keep, qkv_far_recv = hold(
        own_b, own_b_send, own_a_sum, fc1_recv, fc2_recv, out_y, qkv_first, qkv_far_keep, qkv_far_recv
    )

    def joined_rows(level, pair):
        return joined(bits[level], *pair, pair[0].ndim - 2)

    own_b_recv = over(0, own_b_send)
    qkv_second = over_x(low([qkv_far_keep[..., side_a:], qkv_far_recv[..., side_a:]]))
    a_terms, a_y = spread(fresh(own_a_sum, qkv_first), half_width, 1)
    fc1_terms, fc1_recv = spread(fc1_terms + fresh(fc1_recv), fc1_rows // 2, 3)
    fc2_pair = (fc2_mine, fc2_recv)
    for level in range(levels - 2, 1, -1):
        fc2_mine = joined_rows(level + 1, fc2_pair)
        fc2_pair = (fc2_mine, over(level, fc2_mine))
    out_mine = cut(out_terms + fresh(out_y), half_width // 2)
    out_z = over(2, out_mine)
    grad_shifted, grad_send, sums_one = input_grads(
        shared_nat, [own_a, own_b], far_dqkv, own_qkv, far_qkv, rows, lead, grad_middle, gain_one, chunk
    )
    own_b_sum = grad_left_half(keep_half, normed_one, own_b, own_b_recv)
    grad_shifted, grad_send, sums_one, a_y, fc1_recv, qkv_second, own_b_sum, out_z, *fc2_pair = hold(
        grad_shifted, grad_send, sums_one, a_y, fc1_recv, qkv_second, own_b_sum, out_z, *fc2_pair
    )

    b_terms, b_y = spread(fresh(own_b_sum, qkv_second), half_width, 1)
    fc1_size = fc1_rows // 4
    fc1_terms = fc1_terms + fresh(fc1_recv)
    for level in range(4, levels):
        fc1_terms, fc1_recv = spread(fc1_terms, fc1_size, level)
        fc1_terms, fc1_size = fc1_terms + fresh(fc1_recv), fc1_size // 2
    fc1_mine = cut(fc1_terms, fc1_size)
    fc1_pair = (fc1_mine, over(levels - 1, fc1_mine))
    bucket_rows = jnp.arange(counts.shape[0], dtype=jnp.int32)[:, None] == bucket
    bias_sums = jnp.concatenate([own_fc1_bias, far_fc1_bias_sum], 0)
    vectors = jnp.concatenate(
        [
            jnp.where(bucket_rows, sums_one[2:3], 0.0),
            sums_one[:2],
            sums_two[:4],
            jnp.where(mp_at == 0, sums_one[3:5], jnp.roll(sums_one[3:5], heads_width, 1)),
            jnp.where(mp_at == 0, bias_sums, bias_sums[::-1]).reshape(-1, width),
        ]
    )
    vectors_recv = over(1, vectors)
    out_mine = low([out_mine, out_z])
    out_z = over(3, out_mine)
    fc2_mine = joined_rows(2, fc2_pair)
    b_y, vectors_recv, out_z, *fc1_pair, fc2_mine, far_hidden = hold(
        b_y, vectors_recv, out_z, *fc1_pair, fc2_mine, far_hidden
    )

    rows_two = half_width // 2
    qkv_both = jnp.stack([cut(a_terms + fresh(a_y), rows_two), cut(b_terms + fresh(b_y), rows_two)])
    qkv_terms, qkv_recv = spread(fresh(qkv_both), rows_two, 2)
    vectors = vectors + vectors_recv
    vectors_recv = over_x(vectors)
    fc2_y = over(1, fc2_mine)
    chunks = half_rows // chunk
    output_low = output_layer(pair_nat, chunks, chunks, far_hidden, mlp_own, far_fc2, middle, fc2_row, chunk)
    qkv_recv, vectors_recv, output_low, far_hidden = hold(qkv_recv, vectors_recv, output_low, far_hidden)

    qkv_terms, qkv_recv = spread(qkv_terms + fresh(qkv_recv), rows_two // 2, 3)
    vectors = vectors + vectors_recv
    vectors_recv = over(3, vectors)
    for level in range(levels - 2, 1, -1):
        fc1_mine = joined_rows(level + 1, fc1_pair)
        fc1_pair = (fc1_mine, over(level, fc1_mine))
    output_high = output_layer(pair_nat, 0, chunks, far_hidden, mlp_own, far_fc2, middle, fc2_row, chunk)
    qkv_recv, vectors_recv, output_high, fc2_y, *fc1_pair = hold(qkv_recv, vectors_recv, output_high, fc2_y, *fc1_pair)

    vectors = vectors + vectors_recv
    vectors_recv = over(2, vectors)
    qkv_size = rows_two // 4
    qkv_terms = qkv_terms + fresh(qkv_recv)
    out_mine = low([out_mine, out_z])
    for level in range(4, levels):
        qkv_terms, qkv_recv = spread(qkv_terms, qkv_size, level)
        qkv_terms, qkv_size = qkv_terms + fresh(qkv_recv), qkv_size // 2
        vectors = vectors + over(level, vectors)
        out_mine = low([out_mine, over(level, out_mine)])
    qkv_mine = cut(qkv_terms, qkv_size)
    qkv_pair = (qkv_mine, over(levels - 1, qkv_mine))
    fc1_mine = joined_rows(2, fc1_pair)
    fc1_y = over(1, fc1_mine)
    grad_recv = over_x(grad_send)
    fc2_half = joined(side, fc2_mine, fc2_y, 1).reshape(units, -1)
    fc2_core = over(0, fc2_half)
    vectors_recv, fc2_core, output_low, *qkv_pair = hold(vectors_recv, fc2_core, output_low, *qkv_pair)

    for level in range(levels - 2, 1, -1):
        qkv_mine = joined_rows(level + 1, qkv_pair)
        qkv_pair = (qkv_mine, over(level, qkv_mine))
    vectors = vectors + vectors_recv
    vectors_recv = over(0, vectors)
    output_recv = over_x(output_low)
    out_pair = (out_mine, over(1, out_mine))
    tile = min(512, half_width)
    fc2_grad = finish(
        pair_nat, fc2_half, fc2_core, (tile, half_width), (units, width), lambda at, place: (place[0], at)
    )
    vectors_recv, fc2_grad, grad_recv, fc1_y, *qkv_pair, out_low, out_high = hold(
        vectors_recv, fc2_grad, grad_recv, fc1_y, *qkv_pair, *out_pair
    )

    qkv_mine = joined_rows(2, qkv_pair)
    qkv_pair = (qkv_mine, over(1, qkv_mine))
    fc1_half = joined(side, fc1_mine, fc1_y, 1).reshape(-1, units)
    fc1_core = over(0, fc1_half)
    out_half = joined(side, out_low, out_high)
    out_core = over(0, out_half)
    input_grad = joined(mp_at, grad_shifted[None, :half_rows], grad_recv[None].astype(F32))
    out_grad = finish(
        pair_nat, out_half, out_core, out_half.shape, (heads_width, width), lambda at, place: (0, at), True
    )
    steps = 4
    fc1_grad = finish(
        pair_nat,
        fc1_half,
        fc1_core,
        (half_width // steps, units),
        (width, units),
        lambda at, place: (at * steps + place[0], 0),
    )
    block_output = joined(mp_at, output_high[None], output_recv[None])
    fc1_grad, out_grad, block_output, input_grad, *qkv_pair = hold(fc1_grad, out_grad, block_output, input_grad, *qkv_pair)

    qkv_half = joined_rows(1, qkv_pair)
    qkv_grad = finish(
        pair_nat,
        qkv_half,
        over(0, qkv_half),
        (1, 1, half_width, side_a),
        (3, width, heads_width),
        lambda at, place: (place[1], at, place[0]),
    )
    qkv_grad = jnp.transpose(qkv_grad, (1, 0, 2))
    vectors = vectors + vectors_recv

    table = counts.shape[0]
    lead_grad, singles, rest = vectors[:table], vectors[table : table + 6], vectors[table + 6 :]
    qv_bias_grad = part(rest[:2], mp_at, 2, 1)
    fc1_bias_grad = part(rest[2:].reshape(-1), mp_at, 2)
    return (
        block_output,
        input_grad,
        lead_grad,
        singles[0],
        singles[1],
        qkv_grad,
        qv_bias_grad,
        out_grad,
        singles[4],
        singles[2],
        singles[3],
        fc1_grad,
        fc1_bias_grad,
        fc2_grad,
        singles[5],
    )


def solution(mesh):
    in_specs = (
        P("dp", "mp", None),
        P("dp", "mp", None),
        P("dp"),
        P(),
        P(),
        P(),
        P(),
        P(None, None, "mp"),
        P(None, "mp"),
        P("mp", None),
        P(),
        P(),
        P(),
        P(None, "mp"),
        P("mp"),
        P("mp", None),
        P(),
    )
    out_specs = (
        P("dp", "mp", None),
        P("dp", "mp", None),
        P(),
        P(),
        P(),
        P(None, None, "mp"),
        P(None, "mp"),
        P("mp", None),
        P(),
        P(),
        P(),
        P(None, "mp"),
        P("mp"),
        P("mp", None),
        P(),
    )
    def local(*args):
        replicas = lax.axis_size("dp")
        samples, half_rows, width = args[0].shape
        heads_width, units = args[7].shape[2], args[13].shape[1]
        fits = samples == 2 and lax.axis_size("mp") == 2 and replicas >= 16 and replicas & (replicas - 1) == 0
        even = half_rows % 256 == 0 and width == 2 * heads_width == 1024 and units == 2 * width
        return (fast_body if fits and even else body)(*args)

    return jax.shard_map(local, mesh=mesh, in_specs=in_specs, out_specs=out_specs, check_vma=False)
```

```python
import functools
import math

import jax
import jax.numpy as jnp
from jax import lax
from jax.experimental import pallas as pl
from jax.experimental.pallas import tpu as pltpu
from jax.sharding import PartitionSpec as P

HD = 64


EPS = 1e-05


def norm_forward(values, norm_gain, norm_shift):
    center = values - jnp.mean(values, axis=-1, keepdims=True)
    inverse = lax.rsqrt(jnp.mean(center * center, axis=-1, keepdims=True) + EPS)
    scaled = center * inverse
    return (scaled * norm_gain + norm_shift, scaled, inverse)


def norm_backward(grad_out, scaled, inverse, norm_gain):
    grad_scaled = grad_out * norm_gain
    grad_mean = jnp.mean(grad_scaled, axis=-1, keepdims=True)
    cross_mean = jnp.mean(grad_scaled * scaled, axis=-1, keepdims=True)
    grad_in = inverse * (grad_scaled - grad_mean - scaled * cross_mean)
    gain_grad = jnp.sum(grad_out * scaled, axis=(0, 1))
    shift_grad = jnp.sum(grad_out, axis=(0, 1))
    return (grad_in, gain_grad, shift_grad)


def gelu_slope(pre_act):
    normal_cdf = 0.5 * (1.0 + lax.erf(pre_act * 0.7071067811865476))
    return normal_cdf + pre_act * jnp.exp(-0.5 * pre_act * pre_act) * 0.3989422804014327


def attention_forward(query_all, key_all, value_all, block_rows):
    block_count = query_all.shape[0] // block_rows
    query_blocks = query_all.reshape((block_count, block_rows) + query_all.shape[1:])

    def one_block(query_block):
        scores = (
            jnp.einsum("qshd,kshd->shqk", query_block, key_all, preferred_element_type=jnp.float32)
            * 0.125
        )
        row_max = jnp.max(scores, axis=-1, keepdims=True)
        powers = jnp.exp(scores - row_max)
        exp_total = jnp.sum(powers, axis=-1, keepdims=True)
        attn_weights = (powers / exp_total).astype(jnp.bfloat16)
        attended = jnp.einsum(
            "shqk,kshd->qshd", attn_weights, value_all, preferred_element_type=jnp.float32
        )
        return (attended.astype(jnp.bfloat16), (row_max + jnp.log(exp_total))[..., 0])

    attended, log_total = lax.map(one_block, query_blocks)
    return (attended.reshape(query_all.shape), log_total)


def attention_backward(query_all, key_all, value_all, grad_attended, log_total, block_rows):
    block_count = query_all.shape[0] // block_rows
    query_blocks = query_all.reshape((block_count, block_rows) + query_all.shape[1:])
    grad_blocks = grad_attended.reshape((block_count, block_rows) + query_all.shape[1:])

    def one_block(running, sliced):
        key_grad, value_grad = running
        query_block, grad_block, log_block = sliced
        scores = (
            jnp.einsum("qshd,kshd->shqk", query_block, key_all, preferred_element_type=jnp.float32)
            * 0.125
        )
        attn_weights = jnp.exp(scores - log_block[..., None])
        weight_low = attn_weights.astype(jnp.bfloat16)
        grad_weights = jnp.einsum(
            "qshd,kshd->shqk", grad_block, value_all, preferred_element_type=jnp.float32
        )
        inner = jnp.sum(attn_weights * grad_weights, axis=-1, keepdims=True)
        grad_scores = (attn_weights * (grad_weights - inner)).astype(jnp.bfloat16)
        query_grad = (
            jnp.einsum("shqk,kshd->qshd", grad_scores, key_all, preferred_element_type=jnp.float32)
            * 0.125
        )
        key_grad = (
            key_grad
            + jnp.einsum(
                "shqk,qshd->kshd", grad_scores, query_block, preferred_element_type=jnp.float32
            )
            * 0.125
        )
        value_grad = value_grad + jnp.einsum(
            "shqk,qshd->kshd", weight_low, grad_block, preferred_element_type=jnp.float32
        )
        return ((key_grad, value_grad), query_grad.astype(jnp.bfloat16))

    zero_grad = jnp.zeros(key_all.shape, jnp.float32)
    (key_grad, value_grad), query_grad = lax.scan(
        one_block, (zero_grad, zero_grad), (query_blocks, grad_blocks, log_total)
    )
    return (
        query_grad.reshape(query_all.shape),
        key_grad.astype(jnp.bfloat16),
        value_grad.astype(jnp.bfloat16),
    )


def body(
    tokens,
    cotangent,
    buckets,
    counts,
    lead_table,
    norm1_gain,
    norm1_shift,
    w_qkv,
    qv_bias,
    w_out,
    out_bias,
    norm2_gain,
    norm2_shift,
    w_fc1,
    fc1_bias,
    w_fc2,
    fc2_bias,
):
    samples_here = tokens.shape[0]
    local_rows = tokens.shape[1]
    local_width = w_qkv.shape[2]
    local_heads = local_width // HD
    seq_len = local_rows * lax.axis_size("mp")
    block_rows = min(512, seq_len)
    head_shape = (seq_len, samples_here, local_heads, HD)
    count_f = counts.astype(jnp.float32)
    onehot = (buckets[:, None] == jnp.arange(counts.shape[0], dtype=jnp.int32)[None, :]).astype(
        jnp.float32
    )
    loss_weight = jnp.mean(count_f) / jnp.sum(onehot * count_f[None, :], axis=1)
    lead_rows = jnp.dot(
        onehot,
        lead_table.astype(jnp.float32),
        precision=lax.Precision.HIGHEST,
        preferred_element_type=jnp.float32,
    )
    shifted = jnp.swapaxes(tokens, 0, 1).astype(jnp.float32) + lead_rows[None]
    normed_one, scaled_one, inverse_one = norm_forward(
        shifted, norm1_gain.astype(jnp.float32), norm1_shift.astype(jnp.float32)
    )
    normed_one = normed_one.astype(jnp.bfloat16)
    normed_full = lax.all_gather(normed_one, "mp", axis=0, tiled=True)
    project = jnp.einsum("tsd,dcf->tscf", normed_full, w_qkv, preferred_element_type=jnp.float32)
    bias_f = qv_bias.astype(jnp.float32)
    query_all = (project[:, :, 0] + bias_f[0]).astype(jnp.bfloat16).reshape(head_shape)
    key_all = project[:, :, 1].astype(jnp.bfloat16).reshape(head_shape)
    value_all = (project[:, :, 2] + bias_f[1]).astype(jnp.bfloat16).reshape(head_shape)
    attended, log_total = attention_forward(query_all, key_all, value_all, block_rows)
    attended_flat = attended.reshape(seq_len, samples_here, local_width)
    picked = attended_flat
    branch = lax.psum_scatter(
        jnp.einsum("tsf,fd->tsd", picked, w_out, preferred_element_type=jnp.float32),
        "mp",
        scatter_dimension=0,
        tiled=True,
    )
    middle = shifted + branch + out_bias.astype(jnp.float32)
    gain_two = norm2_gain.astype(jnp.float32)
    normed_two, scaled_two, inverse_two = norm_forward(
        middle, gain_two, norm2_shift.astype(jnp.float32)
    )
    normed_two = normed_two.astype(jnp.bfloat16)
    grad_top = jnp.swapaxes(cotangent, 0, 1).astype(jnp.float32) * loss_weight[None, :, None]
    grad_low = grad_top.astype(jnp.bfloat16)
    fc1_full, fc1_bias_full, fc2_full = (
        lax.all_gather(w_fc1, "mp", axis=1, tiled=True),
        lax.all_gather(fc1_bias, "mp", axis=0, tiled=True),
        lax.all_gather(w_fc2, "mp", axis=0, tiled=True),
    )
    pre_act = jnp.einsum(
        "tsd,df->tsf", normed_two, fc1_full, preferred_element_type=jnp.float32
    ) + fc1_bias_full.astype(jnp.float32)
    hidden = jax.nn.gelu(pre_act, approximate=False).astype(jnp.bfloat16)
    mlp_branch = jnp.einsum("tsf,fd->tsd", hidden, fc2_full, preferred_element_type=jnp.float32)
    output = middle + mlp_branch + fc2_bias.astype(jnp.float32)
    grad_hidden = jnp.einsum("tsd,fd->tsf", grad_low, fc2_full, preferred_element_type=jnp.float32)
    grad_pre = (grad_hidden * gelu_slope(pre_act)).astype(jnp.bfloat16)
    grad_normed_two = jnp.einsum(
        "tsf,df->tsd", grad_pre, fc1_full, preferred_element_type=jnp.float32
    )
    fc1_part = jnp.einsum("tsd,tsf->df", normed_two, grad_pre, preferred_element_type=jnp.float32)
    fc1_bias_part = jnp.sum(grad_pre.astype(jnp.float32), axis=(0, 1))
    fc2_part = jnp.einsum("tsf,tsd->fd", hidden, grad_low, preferred_element_type=jnp.float32)
    fc1_grad, fc1_bias_grad, fc2_grad = (
        lax.psum_scatter(
            fc1_part.astype(jnp.bfloat16), "mp", scatter_dimension=1, tiled=True
        ).astype(jnp.float32),
        lax.psum_scatter(
            fc1_bias_part.astype(jnp.bfloat16), "mp", scatter_dimension=0, tiled=True
        ).astype(jnp.float32),
        lax.psum_scatter(
            fc2_part.astype(jnp.bfloat16), "mp", scatter_dimension=0, tiled=True
        ).astype(jnp.float32),
    )
    fc2_bias_grad = jnp.sum(grad_top, axis=(0, 1))
    grad_from_norm, gain_two_grad, shift_two_grad = norm_backward(
        grad_normed_two, scaled_two, inverse_two, gain_two
    )
    grad_middle = grad_top + grad_from_norm
    out_bias_grad = jnp.sum(grad_middle, axis=(0, 1))
    grad_branch = grad_middle.astype(jnp.bfloat16)
    grad_branch_full = lax.all_gather(grad_branch, "mp", axis=0, tiled=True)
    out_grad = jnp.einsum(
        "tsf,tsd->fd", attended_flat, grad_branch_full, preferred_element_type=jnp.float32
    )
    grad_attended = jnp.einsum(
        "tsd,fd->tsf", grad_branch_full, w_out, preferred_element_type=jnp.float32
    ).astype(jnp.bfloat16)
    query_grad, key_grad, value_grad = attention_backward(
        query_all, key_all, value_all, grad_attended.reshape(head_shape), log_total, block_rows
    )
    grad_project = jnp.stack([query_grad, key_grad, value_grad], axis=2).reshape(
        seq_len, samples_here, 3, local_width
    )
    qkv_grad = jnp.einsum(
        "tsd,tscf->dcf", normed_full, grad_project, preferred_element_type=jnp.float32
    )
    query_bias_grad = jnp.sum(query_grad.astype(jnp.float32), axis=(0, 1)).reshape(local_width)
    value_bias_grad = jnp.sum(value_grad.astype(jnp.float32), axis=(0, 1)).reshape(local_width)
    qv_bias_grad = jnp.stack([query_bias_grad, value_bias_grad])
    picked = grad_project
    grad_normed_one = lax.psum_scatter(
        jnp.einsum("tscf,dcf->tsd", picked, w_qkv, preferred_element_type=jnp.float32).astype(
            jnp.bfloat16
        ),
        "mp",
        scatter_dimension=0,
        tiled=True,
    ).astype(jnp.float32)
    grad_in_one, gain_one_grad, shift_one_grad = norm_backward(
        grad_normed_one, scaled_one, inverse_one, norm1_gain.astype(jnp.float32)
    )
    grad_shifted = grad_middle + grad_in_one
    lead_grad = jnp.dot(
        onehot.T,
        jnp.sum(grad_shifted, axis=0),
        precision=lax.Precision.HIGHEST,
        preferred_element_type=jnp.float32,
    )
    small_grads = jnp.stack(
        [gain_one_grad, shift_one_grad, out_bias_grad, gain_two_grad, shift_two_grad, fc2_bias_grad]
    )
    lead_grad, small_grads = lax.psum((lead_grad, small_grads), ("dp", "mp"))
    qkv_grad, qv_bias_grad, out_grad, fc1_grad, fc1_bias_grad, fc2_grad = (
        lax.psum(qkv_grad.astype(jnp.bfloat16), "dp").astype(jnp.float32),
        lax.psum(qv_bias_grad.astype(jnp.bfloat16), "dp").astype(jnp.float32),
        lax.psum(out_grad.astype(jnp.bfloat16), "dp").astype(jnp.float32),
        lax.psum(fc1_grad.astype(jnp.bfloat16), "dp").astype(jnp.float32),
        lax.psum(fc1_bias_grad.astype(jnp.bfloat16), "dp").astype(jnp.float32),
        lax.psum(fc2_grad.astype(jnp.bfloat16), "dp").astype(jnp.float32),
    )
    block_output = jnp.swapaxes(output, 0, 1).astype(jnp.bfloat16)
    input_grad = jnp.swapaxes(grad_shifted, 0, 1)
    return (
        block_output,
        input_grad,
        lead_grad,
        small_grads[0],
        small_grads[1],
        qkv_grad,
        qv_bias_grad,
        out_grad,
        small_grads[2],
        small_grads[3],
        small_grads[4],
        fc1_grad,
        fc1_bias_grad,
        fc2_grad,
        small_grads[5],
    )


F32 = jnp.float32
BF16 = jnp.bfloat16
NN = (((1,), (0,)), ((), ()))
NT = (((1,), (1,)), ((), ()))
TN = (((0,), (0,)), ((), ()))
MIB = 1 << 20


def dot(left, right, dims):
    return lax.dot_general(left, right, dims, preferred_element_type=F32)


def whole(array):
    return pl.BlockSpec(array.shape, lambda *_: (0,) * array.ndim, pipeline_mode=pl.Buffered(1))


def kernel_call(body, name, grid, scalars, ins, outs, scratch=(), vmem=32, time=6, pinned=()):
    spec = pltpu.PrefetchScalarGridSpec(
        num_scalar_prefetch=len(scalars),
        grid=grid,
        in_specs=[spec for _, spec in ins],
        out_specs=[spec for _, spec in outs],
        scratch_shapes=list(scratch),
    )
    return pl.pallas_call(
        body,
        out_shape=[shape for shape, _ in outs],
        grid_spec=spec,
        compiler_params=pltpu.CompilerParams(vmem_limit_bytes=vmem * MIB),
        cost_estimate=pl.CostEstimate(flops=MIB, transcendentals=0, bytes_accessed=int(time * 2 * MIB)),
        name=name,
    )(
        *scalars,
        *[
            pltpu.with_memory_space_constraint(array, pltpu.HBM) if k in pinned else array
            for k, (array, _) in enumerate(ins)
        ],
    )


def struct(shape, dtype=BF16):
    return jax.ShapeDtypeStruct(shape, dtype)


def centred(values):
    center = values - jnp.mean(values, axis=-1, keepdims=True)
    inverse = lax.rsqrt(jnp.mean(center * center, axis=-1, keepdims=True) + EPS)
    return center * inverse, inverse


def norm_input_grad(grad_out, scaled, inverse, gain):
    grad_scaled = grad_out * gain
    grad_mean = jnp.mean(grad_scaled, axis=-1, keepdims=True)
    cross_mean = jnp.mean(grad_scaled * scaled, axis=-1, keepdims=True)
    return inverse * (grad_scaled - grad_mean - scaled * cross_mean)


def column_sum(values):
    return jnp.sum(values, axis=0, keepdims=True)


def chunk_of(nat_ref, index, size):
    return pl.ds(pl.multiple_of(nat_ref[index] * size, size), size)


def attention_forward_kernel(qkv_ref, out_ref, power_ref, inverse_ref):
    outs = []
    for head in range(2):
        lanes = slice(HD * head, HD * head + HD)
        query = qkv_ref[0, :, lanes] * BF16(0.125)
        scores = dot(qkv_ref[1, :, lanes], query, NT)
        powers = jnp.exp(scores - jnp.max(scores, axis=0, keepdims=True))
        inverse = 1.0 / jnp.sum(powers, axis=0, keepdims=True)
        power_low = powers.astype(BF16)
        power_ref[head] = power_low
        inverse_ref[0, head : head + 1, :] = inverse
        outs.append(dot(qkv_ref[2, :, lanes], power_low, TN) * inverse)
    out_ref[...] = jnp.concatenate(outs, axis=0).T.astype(BF16)


def attend(qkv):
    _, rows, width = qkv.shape
    pairs = width // (2 * HD)
    return kernel_call(
        attention_forward_kernel,
        "attention_forward",
        (pairs,),
        [],
        [(qkv, pl.BlockSpec((3, rows, 2 * HD), lambda j: (0, 0, j)))],
        [
            (struct((rows, width)), pl.BlockSpec((rows, 2 * HD), lambda j: (0, j))),
            (pltpu.HBM((2 * pairs, rows, rows), BF16), pl.BlockSpec((2, rows, rows), lambda j: (j, 0, 0))),
            (struct((pairs, 2, rows), F32), pl.BlockSpec((1, 2, rows), lambda j: (j, 0, 0))),
        ],
        vmem=48,
        time=4 * pairs,
        pinned=[0],
    )


def attention_backward_kernel(block, qkv_ref, power_ref, inverse_ref, out_ref, grad_ref, dqkv_ref, sums_ref):
    rows_all = qkv_ref.shape[1]
    out_t = out_ref[...].astype(F32).T
    grad_t = grad_ref[...].astype(F32).T
    for head in range(2):
        lanes = slice(HD * head, HD * head + HD)
        inverse = inverse_ref[0, head : head + 1, :]
        grad_head = grad_t[lanes]
        inner = jnp.sum(grad_head * out_t[lanes], axis=0, keepdims=True) * inverse
        grad_scaled = grad_head * inverse
        grad_low_t = grad_scaled.astype(BF16)
        grad_low = grad_scaled.T.astype(BF16)
        query = qkv_ref[0, :, lanes] * BF16(0.125)
        key = qkv_ref[1, :, lanes]
        value = qkv_ref[2, :, lanes]
        key_t = key.T
        key_grad = value_grad = None
        query_grads = []
        for start in range(0, rows_all, block):
            rows = slice(start, start + block)
            power = power_ref[head, :, rows]
            grad_power = dot(value, grad_low_t[:, rows], NN) - inner[:, rows]
            grad_scores = (power.astype(F32) * grad_power).astype(BF16)
            key_part = dot(grad_scores, query[rows], NN)
            value_part = dot(power, grad_low[rows], NN)
            key_grad = key_part if key_grad is None else key_grad + key_part
            value_grad = value_part if value_grad is None else value_grad + value_part
            query_grads.append(dot(key_t, grad_scores, NN))
        sums_ref[0, :, lanes] = jnp.concatenate(query_grads, axis=1).T * 0.125
        sums_ref[1, :, lanes] = key_grad
        sums_ref[2, :, lanes] = value_grad
    dqkv_ref[...] = sums_ref[...].astype(BF16)


def attend_back(first, count, qkv, powers, inverse, attended, grad_attended):
    _, rows, width = qkv.shape
    block = (3, rows, 2 * HD)
    flat = pl.BlockSpec((rows, 2 * HD), lambda j: (0, j + first))
    return kernel_call(
        functools.partial(attention_backward_kernel, min(512, rows)),
        "attention_backward",
        (count,),
        [],
        [
            (qkv, pl.BlockSpec(block, lambda j: (0, 0, j + first))),
            (powers, pl.BlockSpec((2, rows, rows), lambda j: (j + first, 0, 0))),
            (inverse, pl.BlockSpec((1, 2, rows), lambda j: (j + first, 0, 0))),
            (attended, flat),
            (grad_attended, flat),
        ],
        [(struct((3, rows, 2 * HD * count)), pl.BlockSpec(block, lambda j: (0, 0, j)))],
        [pltpu.VMEM(block, F32)],
        vmem=40,
        time=5.5 * count,
        pinned=range(5),
    )[0]


def project_own_kernel(at_ref, tokens_ref, recv_ref, lead_ref, gain_ref, shift_ref, weight_ref, bias_ref, rows_ref, normed_ref, heads_ref):
    own = pl.program_id(0) < pl.num_programs(0) // 2
    tokens = jnp.where(own, tokens_ref[0].astype(F32), recv_ref[...].astype(F32))
    rows_ref[...] = tokens.astype(BF16)
    scaled, _ = centred(tokens + lead_ref[...])
    normed = (scaled * gain_ref[...] + shift_ref[...]).astype(BF16)
    normed_ref[...] = normed
    for c in range(3):
        heads_ref[c] = (dot(normed, weight_ref[c], NN) + bias_ref[c : c + 1]).astype(BF16)


def project_own(at, tokens, recv, lead, gain, shift, weight, bias, chunk):
    half, width = tokens.shape[1:]
    heads = weight.shape[2]
    steps = half // chunk
    row = pl.BlockSpec((chunk, width), lambda j, at: (j, 0))
    return kernel_call(
        project_own_kernel,
        "project_own",
        (2 * steps,),
        [at],
        [
            (tokens, pl.BlockSpec((1, chunk, width), lambda j, at: (at[0], jnp.minimum(j, steps - 1), 0))),
            (recv, pl.BlockSpec((chunk, width), lambda j, at: (jnp.maximum(j - steps, 0), 0))),
            *[(v, whole(v)) for v in (lead, gain, shift, weight, bias)],
        ],
        [
            (struct((2 * half, width)), row),
            (struct((2 * half, width)), row),
            (struct((3, 2 * half, heads)), pl.BlockSpec((3, chunk, heads), lambda j, at: (0, j, 0))),
        ],
        pinned=[0, 1, 5],
    )


def project_far_kernel(nat_ref, normed_ref, bias_ref, *refs):
    *pieces, heads_ref = refs
    size = pieces[0].shape[1]
    total = bias_ref[0]
    for k, piece in enumerate(pieces):
        total = total + dot(normed_ref[:, chunk_of(nat_ref, k, size)], piece[0], NN)
    heads_ref[0] = total.astype(BF16)


def project_far(nat, normed, bias, pieces):
    rows = normed.shape[0]
    heads = pieces[0].shape[2]
    first = lambda j, nat: (j, 0, 0)
    return kernel_call(
        project_far_kernel,
        "project_far",
        (3,),
        [nat],
        [
            (normed, whole(normed)),
            (bias[:, None], pl.BlockSpec((1, 1, heads), first)),
            *[(p, pl.BlockSpec((1, *p.shape[1:]), first)) for p in pieces],
        ],
        [(struct((3, rows, heads)), pl.BlockSpec((1, rows, heads), first))],
    )[0]


def middle_kernel(nat_ref, own_ref, far_ref, weight_ref, rows_ref, lead_ref, bias_ref, gain_ref, shift_ref, *refs):
    *pieces, middle_ref, normed_ref = refs
    total = dot(own_ref[...], weight_ref[...], NN)
    for k, piece in enumerate(pieces):
        total = total + dot(far_ref[:, chunk_of(nat_ref, k, piece.shape[0])], piece[...], NN)
    middle = rows_ref[...].astype(F32) + lead_ref[...] + total + bias_ref[...]
    middle_ref[...] = middle
    scaled, _ = centred(middle)
    normed_ref[...] = (scaled * gain_ref[...] + shift_ref[...]).astype(BF16)


def middle_layer(nat, own, far, weight, pieces, rows, lead, bias, gain, shift, chunk):
    count, width = rows.shape
    row = pl.BlockSpec((chunk, width), lambda j, nat: (j, 0))
    heads = pl.BlockSpec((chunk, own.shape[1]), lambda j, nat: (j, 0))
    return kernel_call(
        middle_kernel,
        "middle_layer",
        (count // chunk,),
        [nat],
        [(own, heads), (far, heads), (weight, whole(weight)), (rows, row)]
        + [(v, whole(v)) for v in (lead, bias, gain, shift, *pieces)],
        [(pltpu.HBM((count, width), F32), row), (struct((count, width)), row)],
        pinned=[2, 3],
    )


def gelu_store(pre_act, rows, hidden_ref, slope_ref):
    cdf = 0.5 * (1.0 + lax.erf(pre_act * 0.7071067811865476))
    hidden_ref[rows] = (pre_act * cdf).astype(BF16)
    density = jnp.exp(-0.5 * pre_act * pre_act) * 0.3989422804014327
    slope_ref[rows] = (cdf + pre_act * density).astype(BF16)


def hidden_kernel(block, nat_ref, normed_ref, bias_ref, *refs):
    *pieces, hidden_ref, slope_ref = refs
    size = pieces[0].shape[0]
    for start in range(0, normed_ref.shape[0], block):
        rows = slice(start, start + block)
        pre_act = bias_ref[...]
        for k, piece in enumerate(pieces):
            lanes = slice(None) if len(pieces) == 1 else chunk_of(nat_ref, k, size)
            pre_act = pre_act + dot(normed_ref[rows, lanes], piece[...], NN)
        gelu_store(pre_act, rows, hidden_ref, slope_ref)


def hidden_layer(nat, normed, bias, pieces, chunk):
    rows = normed.shape[0]
    units = pieces[0].shape[1]
    tile = min(512, units)
    column = lambda j, nat: (0, j)
    return kernel_call(
        functools.partial(hidden_kernel, chunk),
        "hidden_layer",
        (units // tile,),
        [nat],
        [(normed, whole(normed)), (bias, pl.BlockSpec((1, tile), column))]
        + [(p, pl.BlockSpec((p.shape[0], tile), column)) for p in pieces],
        [(struct((rows, units)), pl.BlockSpec((rows, tile), column))] * 2,
        vmem=24,
        time=10,
        pinned=range(2, 2 + len(pieces)),
    )


def product_kernel(outs, add_count, by_step, _, left_ref, right_ref, *refs):
    adds, out_refs = refs[:add_count], refs[add_count:]
    stacked = len(right_ref.shape) == 3
    value = dot(left_ref[...], right_ref[0] if stacked else right_ref[...], TN)
    for add in adds:
        value = value + (add[0] if stacked else add[...]).astype(F32)
    value = value.astype(BF16)
    if stacked:
        out_refs[0][0] = value
    elif outs == 1:
        out_refs[0][...] = value
    elif by_step:
        for k, out_ref in enumerate(out_refs):

            @pl.when(pl.program_id(0) == k)
            def _(out_ref=out_ref):
                out_ref[...] = value
    else:
        size = value.shape[0] // outs
        for k, out_ref in enumerate(out_refs):
            out_ref[...] = value[k * size : (k + 1) * size]


def grad_right_half(half, left, right, *add):
    rows, columns = left.shape
    kept = right.shape[1] // 2
    tile = columns // 2
    out_spec = pl.BlockSpec((tile, kept), lambda j, half: (j, 0))
    outs = 2 if add else 1
    split = [(struct((tile, kept)), pl.BlockSpec((tile, kept), lambda j, half: (0, 0)))] * 2
    result = kernel_call(
        functools.partial(product_kernel, outs, len(add), True),
        "grad_right_half",
        (2,),
        [half],
        [
            (left, pl.BlockSpec((rows, tile), lambda j, half: (0, j))),
            (right, pl.BlockSpec((rows, kept), lambda j, half: (0, half[0]))),
        ]
        + [(a, out_spec) for a in add],
        split if add else [(struct((columns, kept)), out_spec)],
        vmem=20,
        time=3,
    )
    return result if add else result[0]


def grad_left_half(half, left, right, *add, split=False):
    rows = left.shape[0]
    kept = left.shape[1] // 2
    columns = right.shape[-1]
    tile = min(1024, columns)
    outs = 2 if split else 1
    left_spec = pl.BlockSpec((rows, kept), lambda j, half: (0, half[0]))
    if right.ndim == 3:
        grid, out_shape = (right.shape[0],), (right.shape[0], kept, columns)
        right_spec = pl.BlockSpec((1, rows, columns), lambda j, half: (j, 0, 0))
        add_spec = out_spec = pl.BlockSpec((1, kept, columns), lambda j, half: (j, 0, 0))
    else:
        grid, out_shape = (columns // tile,), (kept // outs, columns)
        right_spec = pl.BlockSpec((rows, tile), lambda j, half: (0, j))
        add_spec = pl.BlockSpec((kept, tile), lambda j, half: (0, j))
        out_spec = pl.BlockSpec((kept // outs, tile), lambda j, half: (0, j))
    result = kernel_call(
        functools.partial(product_kernel, outs, len(add), False),
        "grad_left_half",
        grid,
        [half],
        [(left, left_spec), (right, right_spec)] + [(a, add_spec) for a in add],
        [(struct(out_shape), out_spec)] * outs,
        vmem=20,
        time=3,
    )
    return result if split else result[0]


def term(array, at=None, size=None, column=None):
    block, index = list(array.shape), [None] * array.ndim
    if size is not None:
        block[-2], index[-2] = size, at
    if column is not None:
        block[-1], index[-1] = array.shape[-1] // 2, lambda _: column

    def index_map(_, flags):
        return tuple(0 if f is None else f(flags) for f in index)

    return array, pl.BlockSpec(tuple(block), index_map)


def combine_kernel(plan, flags_ref, *refs):
    count = sum(terms for parts in plan for _, _, terms in parts)
    ins, outs = list(refs[:count]), refs[count:]
    for parts, out_ref in zip(plan, outs):
        for lead, row, terms in parts:
            value = None
            for ref in ins[:terms]:
                part = ref[...] if terms == 1 else ref[...].astype(F32)
                value = part if value is None else value + part
            ins = ins[terms:]
            value = value.astype(BF16)
            if lead is not None:
                out_ref[lead] = value
            elif row is not None:
                size = value.shape[-2]
                start = row if isinstance(row, int) else pl.multiple_of(row(flags_ref) * size, size)
                where = (slice(None),) * (value.ndim - 2) + (pl.ds(start, size), slice(None))
                out_ref[where] = value
            else:
                out_ref[...] = value


def combine(flags, *outs):
    ins = [t for _, parts in outs for _, _, terms in parts for t in terms]
    plan = [[(lead, row, len(terms)) for lead, row, terms in parts] for _, parts in outs]

    def full(shape):
        return pl.BlockSpec(shape, lambda *_: (0,) * len(shape))

    return kernel_call(
        functools.partial(combine_kernel, plan),
        "combine",
        (1,),
        [flags],
        ins,
        [(struct(shape), full(shape)) for shape, _ in outs],
        vmem=32,
        time=3,
    )


def summed(shape, *terms):
    return shape, [(None, None, terms)]


def pre_grad_store(grad, slope_ref, pre_ref, sum_ref):
    pre = (grad * slope_ref[...].astype(F32)).astype(BF16)
    pre_ref[...] = pre
    sum_ref[...] = column_sum(pre.astype(F32))


def pre_grad_own_kernel(low_ref, weight_ref, slope_ref, pre_ref, sum_ref):
    pre_grad_store(dot(low_ref[...], weight_ref[...], NT), slope_ref, pre_ref, sum_ref)


def pre_grad_own(low, weight, slope):
    rows, width = low.shape
    units = weight.shape[0]
    tile = min(512, units)
    column = lambda j: (0, j)
    return kernel_call(
        pre_grad_own_kernel,
        "pre_grad_own",
        (units // tile,),
        [],
        [
            (low, whole(low)),
            (weight, pl.BlockSpec((tile, width), lambda j: (j, 0))),
            (slope, pl.BlockSpec((rows, tile), column)),
        ],
        [
            (struct((rows, units)), pl.BlockSpec((rows, tile), column)),
            (struct((1, units), F32), pl.BlockSpec((1, tile), column)),
        ],
        vmem=24,
        pinned=[1],
    )


def pre_grad_far_kernel(per, nat_ref, low_ref, slope_ref, *refs):
    *pieces, pre_ref, sum_ref = refs
    for k, piece in enumerate(pieces):

        @pl.when(pl.program_id(0) // per == k)
        def _(piece=piece):
            pre_grad_store(dot(low_ref[...], piece[...], NT), slope_ref, pre_ref, sum_ref)


def pre_grad_far(nat, low, pieces, slope):
    rows, width = low.shape
    size = pieces[0].shape[0]
    tile = min(512, size)
    per = size // tile
    units = size * len(pieces)
    column = lambda j, nat: (0, nat[j // per] * per + j % per)

    def piece_spec(k):
        return pl.BlockSpec((tile, width), lambda j, nat: (jnp.clip(j - k * per, 0, per - 1), 0))

    return kernel_call(
        functools.partial(pre_grad_far_kernel, per),
        "pre_grad_far",
        (len(pieces) * per,),
        [nat],
        [(low, whole(low)), (slope, pl.BlockSpec((rows, tile), column))]
        + [(p, piece_spec(k)) for k, p in enumerate(pieces)],
        [
            (struct((rows, units)), pl.BlockSpec((rows, tile), column)),
            (struct((1, units), F32), pl.BlockSpec((1, tile), column)),
        ],
        vmem=24,
        time=8,
        pinned=range(2, 2 + len(pieces)),
    )


def add_sums(sums_ref, rows):
    @pl.when(pl.program_id(0) == 0)
    def _():
        sums_ref[...] = jnp.zeros_like(sums_ref)

    for k, row in enumerate(rows):
        sums_ref[k : k + 1, :] += row


def middle_grad_kernel(
    nat_ref, at_ref, own_ref, far_ref, weight_ref, middle_ref, cot_ref, recv_ref, loss_ref, gain_ref, *refs
):
    *pieces, grad_ref, low_ref, sums_ref, total_ref = refs
    total_ref[...] = dot(own_ref[...], weight_ref[...], NT)
    for k, piece in enumerate(pieces):
        total_ref[:, chunk_of(nat_ref, k, piece.shape[0])] += dot(far_ref[...], piece[...], NT)
    grad = total_ref[...]
    scaled, inverse = centred(middle_ref[...])
    mine = pl.program_id(0) < pl.num_programs(0) // 2
    top = jnp.where(mine, cot_ref[0].astype(F32), recv_ref[...].astype(F32)) * loss_ref[...]
    grad_middle = top + norm_input_grad(grad, scaled, inverse, gain_ref[...])
    grad_ref[...] = grad_middle
    low_ref[...] = grad_middle.astype(BF16)
    add_sums(
        sums_ref,
        [column_sum(grad * scaled), column_sum(grad), column_sum(grad_middle), column_sum(top)],
    )


def middle_grad(nat, at, own, far, weight, pieces, middle, cot, recv, loss, gain, chunk):
    count, width = middle.shape
    row = pl.BlockSpec((chunk, width), lambda j, *_: (j, 0))
    units = pl.BlockSpec((chunk, own.shape[1]), lambda j, *_: (j, 0))
    steps = count // chunk // 2
    return kernel_call(
        middle_grad_kernel,
        "middle_grad",
        (count // chunk,),
        [nat, at],
        [
            (own, units),
            (far, units),
            (weight, whole(weight)),
            (middle, row),
            (cot, pl.BlockSpec((1, chunk, width), lambda j, nat, at: (at[0], jnp.minimum(j, steps - 1), 0))),
            (recv, pl.BlockSpec((chunk, width), lambda j, *_: (jnp.maximum(j - steps, 0), 0))),
        ]
        + [(v, whole(v)) for v in (loss, gain, *pieces)],
        [
            (struct((count, width), F32), row),
            (struct((count, width)), row),
            (struct((8, width), F32), pl.BlockSpec((8, width), lambda j, *_: (0, 0))),
        ],
        [pltpu.VMEM((chunk, width), F32)],
        time=14,
        pinned=[2, 3, 4, 5, *range(8, 8 + len(pieces))],
    )


def attended_grad_kernel(nat_ref, low_ref, weight_ref, *refs):
    *pieces, own_ref, far_ref = refs
    own_ref[...] = dot(low_ref[...], weight_ref[...], NT).astype(BF16)
    for k, piece in enumerate(pieces):
        far_ref[:, chunk_of(nat_ref, k, piece.shape[0])] = dot(low_ref[...], piece[...], NT).astype(BF16)


def attended_grad(nat, low, weight, pieces, chunk):
    count, width = low.shape
    heads = weight.shape[0]
    out = (struct((count, heads)), pl.BlockSpec((chunk, heads), lambda j, nat: (j, 0)))
    return kernel_call(
        attended_grad_kernel,
        "attended_grad",
        (count // chunk,),
        [nat],
        [(low, pl.BlockSpec((chunk, width), lambda j, nat: (j, 0)))] + [(v, whole(v)) for v in (weight, *pieces)],
        [out, out],
        pinned=range(1, 2 + len(pieces)),
    )


def output_own_kernel(own_ref, weight_ref, out_ref):
    out_ref[...] = dot(own_ref[...], weight_ref[...], NN)


def output_own(own, weight, chunk):
    count, units = own.shape
    width = weight.shape[1]
    return kernel_call(
        output_own_kernel,
        "output_own",
        (count // chunk,),
        [],
        [(own, pl.BlockSpec((chunk, units), lambda j: (j, 0))), (weight, whole(weight))],
        [(struct((count, width), F32), pl.BlockSpec((chunk, width), lambda j: (j, 0)))],
        vmem=20,
        time=6,
        pinned=range(2),
    )[0]


def output_kernel(nat_ref, far_ref, own_ref, middle_ref, bias_ref, *refs):
    *pieces, out_ref = refs
    total = own_ref[...]
    for k, piece in enumerate(pieces):
        total = total + dot(far_ref[:, chunk_of(nat_ref, k, piece.shape[0])], piece[...], NN)
    out_ref[...] = (middle_ref[...] + total + bias_ref[...]).astype(BF16)


def output_layer(nat, first, count, far, own, pieces, middle, bias, chunk):
    width = middle.shape[1]
    row = pl.BlockSpec((chunk, width), lambda j, nat: (j + first, 0))
    return kernel_call(
        output_kernel,
        "output_layer",
        (count,),
        [nat],
        [(far, pl.BlockSpec((chunk, far.shape[1]), lambda j, nat: (j + first, 0))), (own, row), (middle, row)]
        + [(v, whole(v)) for v in (bias, *pieces)],
        [(struct((count * chunk, width)), pl.BlockSpec((chunk, width), lambda j, nat: (j, 0)))],
        vmem=24,
        time=6,
        pinned=range(4 + len(pieces)),
    )[0]


def input_grad_kernel(own_count, nat_ref, far_ref, weight_ref, rows_ref, lead_ref, grad_ref, gain_ref, *refs):
    owns, refs = refs[:own_count], refs[own_count:]
    *pieces, out_ref, low_ref, sums_ref, total_ref = refs
    total = None
    at = 0
    for own in owns:
        size = own.shape[2]
        for c in range(3):
            part = dot(own[c], weight_ref[c, :, at : at + size], NT)
            total = part if total is None else total + part
        at += size
    total_ref[...] = total
    for k, piece in enumerate(pieces):
        part = dot(far_ref[0], piece[0], NT) + dot(far_ref[1], piece[1], NT) + dot(far_ref[2], piece[2], NT)
        total_ref[:, chunk_of(nat_ref, k, piece.shape[1])] += part
    grad = total_ref[...]
    scaled, inverse = centred(rows_ref[...].astype(F32) + lead_ref[...])
    grad_shifted = grad_ref[...] + norm_input_grad(grad, scaled, inverse, gain_ref[...])
    out_ref[...] = grad_shifted
    low_ref[...] = grad_shifted.astype(BF16)
    bias_rows = [
        jnp.concatenate([column_sum(d[c].astype(F32)) for d in (*owns, far_ref)], axis=1) for c in (0, 2)
    ]
    add_sums(
        sums_ref, [column_sum(grad * scaled), column_sum(grad), column_sum(grad_shifted), *bias_rows]
    )


def input_grads(nat, owns, far, weight, pieces, rows, lead, grad_middle, gain, chunk):
    count, width = rows.shape
    row = pl.BlockSpec((chunk, width), lambda j, nat: (j, 0))
    heads = lambda d: pl.BlockSpec((3, chunk, d.shape[2]), lambda j, nat: (0, j, 0))
    steps = count // chunk
    half = pl.BlockSpec((chunk, width), lambda j, nat: (jnp.maximum(j - steps // 2, 0), 0))
    return kernel_call(
        functools.partial(input_grad_kernel, len(owns)),
        "input_grads",
        (steps,),
        [nat],
        [
            (far, heads(far)),
            (weight, whole(weight)),
            (rows, row),
            (lead, whole(lead)),
            (grad_middle, row),
            (gain, whole(gain)),
        ]
        + [(d, heads(d)) for d in owns]
        + [(p, whole(p)) for p in pieces],
        [
            (struct((count, width), F32), row),
            (struct((count // 2, width)), half),
            (struct((8, width), F32), pl.BlockSpec((8, width), lambda j, nat: (0, 0))),
        ],
        [pltpu.VMEM((chunk, width), F32)],
        time=14,
        pinned=[1, 2, 4, *range(6 + len(owns), 6 + len(owns) + len(pieces))],
    )


def finish_turned_kernel(_, mine_ref, theirs_ref, out_ref):
    value = jnp.where(pl.program_id(0) == 0, mine_ref[...].astype(F32), theirs_ref[...].astype(F32))
    out_ref[...] = value.T


def finish_turned(at, mine, theirs):
    rows, columns = mine.shape
    return kernel_call(
        finish_turned_kernel,
        "finish",
        (2,),
        [at],
        [(mine, whole(mine)), (theirs, whole(theirs))],
        [(struct((columns, 2 * rows), F32), pl.BlockSpec((columns, rows), lambda s, at: (0, at[s])))],
        vmem=16,
        time=2,
    )[0]


def source_spec(block, which, steps, place):
    def index(s, j, *_):
        return place(jnp.where(s == which, j, jnp.where(s < which, 0, steps - 1)))

    return pl.BlockSpec(block, index)


def finish_rows_kernel(_, *refs):
    *pieces, out_ref = refs
    for k, piece in enumerate(pieces):

        @pl.when(pl.program_id(0) == k)
        def _(piece=piece):
            out_ref[...] = piece[0].astype(F32)


def finish_rows(nat, pieces):
    halves, rows, columns = pieces[0].shape
    block = (1, rows, columns)
    return kernel_call(
        finish_rows_kernel,
        "finish",
        (4, halves),
        [nat],
        [(p, source_spec(block, k, halves, lambda j: (j, 0, 0))) for k, p in enumerate(pieces)],
        [
            (
                struct((4 * halves * rows, columns), F32),
                pl.BlockSpec((rows, columns), lambda s, j, nat: (nat[s] // 2 * 2 * halves + j * 2 + nat[s] % 2, 0)),
            )
        ],
        vmem=16,
        time=4,
        pinned=range(4),
    )[0]


def finish_columns_kernel(at_ref, *refs):
    *pieces, out_ref = refs
    first = at_ref[0] == 0
    for k in range(2):
        mine, theirs = pieces[k], pieces[k + 2]

        @pl.when(pl.program_id(0) == k)
        def _(mine=mine, theirs=theirs):
            one, two = mine[0].astype(F32), theirs[0].astype(F32)
            columns = one.shape[1]
            out_ref[:, :columns] = jnp.where(first, one, two)
            out_ref[:, columns:] = jnp.where(first, two, one)


def finish_columns(at, pieces):
    halves, rows, columns = pieces[0].shape
    block = (1, rows, columns)
    return kernel_call(
        finish_columns_kernel,
        "finish",
        (2, halves),
        [at],
        [(p, source_spec(block, k % 2, halves, lambda j: (j, 0, 0))) for k, p in enumerate(pieces)],
        [
            (
                struct((2 * halves * rows, 2 * columns), F32),
                pl.BlockSpec((rows, 2 * columns), lambda s, j, at: (j * 2 + at[2 + s], 0)),
            )
        ],
        vmem=24,
        time=4,
        pinned=range(4),
    )[0]


def finish_stack_kernel(_, *refs):
    *pieces, out_ref = refs
    for k, piece in enumerate(pieces):

        @pl.when(pl.program_id(0) == k)
        def _(piece=piece):
            out_ref[0] = jnp.concatenate([piece[0, 0].astype(F32), piece[1, 0].astype(F32)], axis=1)


def finish_stack(nat, pieces):
    _, stack, rows, columns = pieces[0].shape
    block = (2, 1, rows, columns)
    return kernel_call(
        finish_stack_kernel,
        "finish",
        (4, stack),
        [nat],
        [(p, source_spec(block, k, stack, lambda j: (0, j, 0, 0))) for k, p in enumerate(pieces)],
        [
            (
                struct((stack, 4 * rows, 2 * columns), F32),
                pl.BlockSpec((1, rows, 2 * columns), lambda s, j, nat: (j, nat[s], 0)),
            )
        ],
        vmem=16,
        time=4,
        pinned=range(4),
    )[0]


def hold(*values):
    return lax.optimization_barrier(values)


def fast_body(
    tokens,
    cotangent,
    buckets,
    counts,
    lead_table,
    norm1_gain,
    norm1_shift,
    w_qkv,
    qv_bias,
    w_out,
    out_bias,
    norm2_gain,
    norm2_shift,
    w_fc1,
    fc1_bias,
    w_fc2,
    fc2_bias,
):
    replicas = lax.axis_size("dp")
    levels = replicas.bit_length() - 1
    dp_at, mp_at = lax.axis_index("dp"), lax.axis_index("mp")
    bits = [(dp_at >> level) & 1 for level in range(levels)]

    def over_x(value):
        return lax.ppermute(value, "mp", [(0, 1), (1, 0)])

    def over(level, value):
        return over_mask(1 << level, value)

    def over_mask(mask, value):
        return lax.ppermute(value, "dp", [(i, i ^ mask) for i in range(replicas)])

    def joined(bit, mine, theirs, axis=0):
        return jnp.where(
            bit == 0,
            jnp.concatenate([mine, theirs], axis),
            jnp.concatenate([theirs, mine], axis),
        )

    def part(value, index, count, axis=0):
        size = value.shape[axis] // count
        return lax.dynamic_slice_in_dim(value, index * size, size, axis)

    half_rows, width = tokens.shape[1:]
    heads_width = w_qkv.shape[2]
    units = w_fc1.shape[1]
    chunk = 256
    core, side = bits[0], bits[1]
    at = jnp.stack([mp_at, core, 1 - core, side, 1 - side, bits[2], bits[3]]).astype(jnp.int32)
    mine = core * 2 + side
    shared_nat = jnp.stack([mine, mine ^ 1, mine ^ 2, mine ^ 3]).astype(jnp.int32)

    def row_of(vector):
        return vector.astype(F32)[None]

    small = jnp.concatenate([qv_bias.reshape(-1), fc1_bias])
    small_rows = -(-small.shape[0] // width)
    small_rows_padded = -(-small_rows // 16) * 16
    small = jnp.pad(small, (0, small_rows_padded * width - small.shape[0])).reshape(-1, width)
    token_recv = over_x(jnp.concatenate([part(tokens, 1 - mp_at, 2)[0], small]))

    bucket = lax.dynamic_index_in_dim(buckets, mp_at, 0, keepdims=False)
    count_f = counts.astype(F32)
    loss_weight = jnp.mean(count_f) / lax.dynamic_index_in_dim(count_f, bucket, 0, keepdims=False)
    loss_row = jnp.broadcast_to(loss_weight, (1, width))
    lead = lax.dynamic_index_in_dim(lead_table, bucket, 0).astype(F32)
    own_qkv = jnp.transpose(w_qkv, (1, 0, 2))

    def bias_three(bias):
        bias_f = bias.astype(F32)
        return jnp.stack([bias_f[0], jnp.zeros_like(bias_f[0]), bias_f[1]])

    (
        token_recv, qkv_send, out_send, fc1_send, cot_send, fc2_send, at, shared_nat, loss_row, loss_weight, lead,
        gain_one, gain_two, shift_one, shift_two, out_row, fc1_row, fc2_row, own_bias,
    ) = hold(
        token_recv,
        part(own_qkv, mine, 4, 1),
        part(w_out, core, 2),
        part(w_fc1, mine, 4),
        part(cotangent, 1 - mp_at, 2)[0],
        part(w_fc2, core, 2),
        at,
        shared_nat,
        loss_row,
        loss_weight,
        lead,
        row_of(norm1_gain),
        row_of(norm2_gain),
        row_of(norm1_shift),
        row_of(norm2_shift),
        row_of(out_bias),
        row_of(fc1_bias),
        row_of(fc2_bias),
        bias_three(qv_bias),
    )
    keep_half, send_half, pair_nat = at[1:2], at[2:3], at[1:3]
    far_small = token_recv[half_rows:].reshape(-1)
    far_bias = bias_three(far_small[: 2 * heads_width].reshape(2, heads_width))
    far_fc1_bias = row_of(far_small[2 * heads_width : 2 * heads_width + units])

    qkv_x = over_x(qkv_send)
    rows, normed_one, own_heads = project_own(
        at[:1], tokens, token_recv, lead, gain_one, shift_one, own_qkv, own_bias, chunk
    )
    own_heads, qkv_x, out_send, fc1_send, far_bias, far_fc1_bias = hold(
        own_heads, qkv_x, out_send, fc1_send, far_bias, far_fc1_bias
    )

    qkv_y = over(1, qkv_x)
    out_x = over_x(out_send)
    fc1_x = over_x(fc1_send)
    own_attended, own_powers, own_inverse = attend(own_heads)
    own_attended, qkv_x, qkv_y, out_x = hold(own_attended, qkv_x, qkv_y, out_x)

    far_qkv = [qkv_x, qkv_y, over(0, qkv_x), over(0, qkv_y)]
    far_out = [out_x, over(0, out_x)]
    far_heads = project_far(shared_nat, normed_one, far_bias, far_qkv)
    far_heads, fc1_x, cot_send = hold(far_heads, fc1_x, cot_send)

    fc1_y = over(1, fc1_x)
    cot_recv = over_x(cot_send)
    far_attended, far_powers, far_inverse = attend(far_heads)
    middle, normed_two = middle_layer(
        pair_nat, own_attended, far_attended, w_out, far_out, rows, lead,
        out_row, gain_two, shift_two, chunk,
    )
    normed_two, fc1_x, fc1_y, cot_recv, fc2_send = hold(
        normed_two, fc1_x, fc1_y, cot_recv, fc2_send
    )

    def mine_y(flags):
        return flags[3]

    def theirs_y(flags):
        return flags[4]

    def mine_z(flags):
        return flags[5]

    def theirs_z(flags):
        return 1 - flags[5]

    def zero(_):
        return 0

    def one(_):
        return 1

    def first_y(own_down, far_down):
        size = own_down.shape[0] // 2
        return (2 * size, own_down.shape[1]), [
            (None, 0, [term(own_down, theirs_y, size)]),
            (None, size, [term(far_down, theirs_y, size)]),
        ]

    def second_y(own_up, recv_x):
        size = own_up.shape[0] // 2
        return summed((size, own_up.shape[1]), term(own_up, theirs_y, size), term(recv_x, theirs_y, size))

    def second_x(far_down, recv_y):
        size = far_down.shape[0] // 2
        return summed((size, far_down.shape[1]), term(far_down, mine_y, size), term(recv_y, one, size))

    def z_half(which, own_up, recv_x, recv_up, own_down, recv_y, recv_down):
        size = own_up.shape[0] // 4

        def within(side_of, start=0):
            return lambda flags: (start + side_of(flags)) * 2 + which(flags)

        upper = [term(own_up, within(mine_y), size), term(recv_x, within(mine_y), size), term(recv_up, which, size)]
        lower = [term(own_down, within(mine_y), size), term(recv_y, within(zero), size), term(recv_down, which, size)]
        return (2, size, own_up.shape[1]), [(0, None, upper), (1, None, lower)]

    def z_sides(mine, recv):
        shape = list(mine.shape)
        shape[-2] *= 2
        return tuple(shape), [(None, mine_z, [term(mine)]), (None, theirs_z, [term(recv)])]

    masks = {1: 8, 2: 4, 3: 12}

    def quarter_z(k):
        def index(flags):
            first = 1 - flags[5] if k & 2 else flags[5]
            second = 1 - flags[6] if k & 1 else flags[6]
            return first * 2 + second

        return index

    fc2_x = over_x(fc2_send)
    far_fc1 = [fc1_x, fc1_y, over(0, fc1_x), over(0, fc1_y)]
    cot_rows = jnp.concatenate([part(cotangent, mp_at, 2)[0], cot_recv])
    grad_low = (cot_rows.astype(F32) * loss_weight).astype(BF16)
    own_hidden, own_slope = hidden_layer(shared_nat, normed_two, fc1_row, [w_fc1], chunk)
    far_hidden, far_slope = hidden_layer(shared_nat, normed_two, far_fc1_bias, far_fc1, chunk)
    far_send = grad_right_half(send_half, far_hidden, grad_low)
    own_send = grad_right_half(send_half, own_hidden, grad_low)
    own_pre, own_fc1_bias = pre_grad_own(grad_low, w_fc2, own_slope)
    fc1_own_send = grad_left_half(send_half, normed_two, own_pre)
    far_send, own_send, fc2_x, grad_low, far_hidden, own_pre, fc1_own_send = hold(
        far_send, own_send, fc2_x, grad_low, far_hidden, own_pre, fc1_own_send
    )

    far_recv, own_recv, fc2_core, fc1_own_recv = over(0, far_send), over(0, own_send), over(0, fc2_x), over(0, fc1_own_send)
    far_up, far_down = grad_right_half(keep_half, far_hidden, grad_low, far_recv)
    own_up, own_down = grad_right_half(keep_half, own_hidden, grad_low, own_recv)
    far_up, far_down, own_up, own_down, fc2_core, fc1_own_recv = hold(
        far_up, far_down, own_up, own_down, fc2_core, fc1_own_recv
    )

    half_width = width // 2
    fc2_x1 = over_x(far_up)
    fc2_y1 = over(1, combine(at, first_y(own_down, far_down))[0])
    far_fc2 = [fc2_x, fc2_core]
    far_pre, far_fc1_bias_sum = pre_grad_far(pair_nat, grad_low, far_fc2, far_slope)
    fc1_far_send = grad_left_half(send_half, normed_two, far_pre)
    fc1_own_up, fc1_own_down = grad_left_half(keep_half, normed_two, own_pre, fc1_own_recv, split=True)
    fc1_far_send, fc1_own_up, fc1_own_down, fc2_x1, fc2_y1, far_pre = hold(
        fc1_far_send, fc1_own_up, fc1_own_down, fc2_x1, fc2_y1, far_pre
    )

    send_y, send_x = combine(at, second_y(own_up, fc2_x1), second_x(far_down, fc2_y1))
    fc2_y2, fc2_x2 = over(1, send_y), over_x(send_x)
    fc1_far_recv = over(0, fc1_far_send)
    grad_middle, grad_branch, sums_two = middle_grad(
        shared_nat, at[:1], own_pre, far_pre, w_fc1, far_fc1, middle, cotangent, cot_recv, loss_row, gain_two, chunk
    )
    own_grad_att, far_grad_att = attended_grad(pair_nat, grad_branch, w_out, far_out, chunk)
    out_far_send = grad_left_half(send_half, grad_branch, far_attended)
    out_own_send = grad_left_half(send_half, grad_branch, own_attended)
    fc1_far_up, fc1_far_down = grad_left_half(keep_half, normed_two, far_pre, fc1_far_recv, split=True)
    far_grad_att, own_grad_att, grad_branch, fc2_y2, fc2_x2, fc1_far_up, fc1_far_down, out_far_send, out_own_send = hold(
        far_grad_att, own_grad_att, grad_branch, fc2_y2, fc2_x2, fc1_far_up, fc1_far_down, out_far_send, out_own_send
    )

    fc2_terms = (own_up, fc2_x1, fc2_y2, own_down, fc2_y1, fc2_x2)
    fc2_send, fc2_mine, send_y = combine(
        at, z_half(theirs_z, *fc2_terms), z_half(mine_z, *fc2_terms), first_y(fc1_own_down, fc1_far_down)
    )
    fc1_x1, fc1_y1, fc2_recv = over_x(fc1_far_up), over(1, send_y), over(2, fc2_send)
    out_far_recv, out_own_recv = over(0, out_far_send), over(0, out_own_send)
    out_far_sum = grad_left_half(keep_half, grad_branch, far_attended, out_far_recv)
    out_own_sum = grad_left_half(keep_half, grad_branch, own_attended, out_own_recv)
    out_recv = over_x(out_far_sum)
    pairs = heads_width // (2 * HD)
    far_dqkv = attend_back(0, pairs, far_heads, far_powers, far_inverse, far_attended, far_grad_att)
    far_dqkv, own_grad_att, fc1_x1, fc1_y1, out_recv, out_own_sum, fc2_recv = hold(
        far_dqkv, own_grad_att, fc1_x1, fc1_y1, out_recv, out_own_sum, fc2_recv
    )

    half_rows_out = half_width // 2
    out_shape = (half_rows_out, heads_width)
    send_y, send_x, fc2_mine, out_send = combine(
        at,
        second_y(fc1_own_up, fc1_x1),
        second_x(fc1_far_down, fc1_y1),
        summed(fc2_mine.shape, term(fc2_mine), term(fc2_recv)),
        summed(out_shape, term(out_own_sum, theirs_y, half_rows_out), term(out_recv, theirs_y, half_rows_out)),
    )
    fc1_y2, fc1_x2, fc2_recv, out_y = over(1, send_y), over_x(send_x), over(3, fc2_mine), over(1, out_send)
    qkv_far_recv = over(0, grad_left_half(send_half, normed_one, far_dqkv))
    qkv_far_keep = grad_left_half(keep_half, normed_one, far_dqkv)
    own_a = attend_back(0, pairs // 2, own_heads, own_powers, own_inverse, own_attended, own_grad_att)
    own_a_send = grad_left_half(send_half, normed_one, own_a)
    own_a_send, own_grad_att, fc1_y2, fc1_x2, out_y, qkv_far_recv, qkv_far_keep, fc2_recv = hold(
        own_a_send, own_grad_att, fc1_y2, fc1_x2, out_y, qkv_far_recv, qkv_far_keep, fc2_recv
    )

    side_a = heads_width // 2
    own_a_recv = over(0, own_a_send)
    fc1_terms = (fc1_own_up, fc1_x1, fc1_y2, fc1_own_down, fc1_y1, fc1_x2)
    qkv_send, fc1_send, fc1_mine, fc2_mine, out_mine = combine(
        at,
        summed((3, half_width, side_a), term(qkv_far_keep, column=0), term(qkv_far_recv, column=0)),
        z_half(theirs_z, *fc1_terms),
        z_half(mine_z, *fc1_terms),
        summed(fc2_mine.shape, term(fc2_mine), term(fc2_recv)),
        summed(
            out_shape,
            term(out_own_sum, mine_y, half_rows_out),
            term(out_recv, mine_y, half_rows_out),
            term(out_y),
        ),
    )
    qkv_first, fc1_recv, fc2_recv, out_z = over_x(qkv_send), over(2, fc1_send), over(2, fc2_mine), over(2, out_mine)
    own_b = attend_back(pairs // 2, pairs - pairs // 2, own_heads, own_powers, own_inverse, own_attended, own_grad_att)
    own_a_sum = grad_left_half(keep_half, normed_one, own_a, own_a_recv)
    own_b_send = grad_left_half(send_half, normed_one, own_b)
    own_b, own_b_send, own_a_sum, fc2_recv, out_z, qkv_first, qkv_far_keep, qkv_far_recv, fc1_recv = hold(
        own_b, own_b_send, own_a_sum, fc2_recv, out_z, qkv_first, qkv_far_keep, qkv_far_recv, fc1_recv
    )

    own_b_recv = over(0, own_b_send)
    a_shape = (3, half_rows_out, side_a)
    qkv_send, fc1_mine, a_send, out_mine, fc2_mine = combine(
        at,
        summed((3, half_width, side_a), term(qkv_far_keep, column=1), term(qkv_far_recv, column=1)),
        summed(fc1_mine.shape, term(fc1_mine), term(fc1_recv)),
        summed(a_shape, term(own_a_sum, theirs_y, half_rows_out), term(qkv_first, theirs_y, half_rows_out)),
        summed(out_shape, term(out_mine), term(out_z)),
        z_sides(fc2_mine, fc2_recv),
    )
    qkv_second, fc1_recv, a_y, out_z, fc2_y = over_x(qkv_send), over(3, fc1_mine), over(1, a_send), over(3, out_mine), over(1, fc2_mine)
    grad_shifted, grad_send, sums_one = input_grads(
        shared_nat, [own_a, own_b], far_dqkv, own_qkv, far_qkv, rows, lead, grad_middle, gain_one, chunk
    )
    own_b_sum = grad_left_half(keep_half, normed_one, own_b, own_b_recv)
    grad_shifted, grad_send, sums_one, a_y, qkv_second, own_b_sum, out_z, fc2_mine, fc2_y, fc1_recv, own_hidden = hold(
        grad_shifted, grad_send, sums_one, a_y, qkv_second, own_b_sum, out_z, fc2_mine, fc2_y, fc1_recv, own_hidden
    )

    b_send, fc1_mine, out_mine, grad_part = combine(
        at,
        summed(a_shape, term(own_b_sum, theirs_y, half_rows_out), term(qkv_second, theirs_y, half_rows_out)),
        summed(fc1_mine.shape, term(fc1_mine), term(fc1_recv)),
        summed(out_shape, term(out_mine), term(out_z)),
        summed((half_rows // 2, width), term(grad_send, zero, half_rows // 2)),
    )
    b_y, fc1_recv, out_y, grad_first = over(1, b_send), over(2, fc1_mine), over(1, out_mine), over_x(grad_part)
    bucket_rows = jnp.arange(counts.shape[0], dtype=jnp.int32)[:, None] == bucket
    bias_sums = jnp.concatenate([own_fc1_bias, far_fc1_bias_sum], 0)
    vectors = jnp.concatenate(
        [
            jnp.where(bucket_rows, sums_one[2:3], 0.0),
            sums_one[:2],
            sums_two[:4],
            jnp.where(mp_at == 0, sums_one[3:5], jnp.roll(sums_one[3:5], heads_width, 1)),
            jnp.where(mp_at == 0, bias_sums, bias_sums[::-1]).reshape(-1, width),
        ]
    )
    vectors_recv = over(0, vectors)
    b_y, vectors_recv, fc1_mine, fc1_recv, out_mine, out_y, grad_first, grad_send, own_hidden, fc2_mine, fc2_y = hold(
        b_y, vectors_recv, fc1_mine, fc1_recv, out_mine, out_y, grad_first, grad_send, own_hidden, fc2_mine, fc2_y
    )

    z_rows = half_rows_out // 4

    def qkv_quarter(k):
        def within(flags):
            return mine_y(flags) * 4 + quarter_z(k)(flags)

        parts = [
            (side_k, None, [term(total, within, z_rows), term(recv, within, z_rows), term(recv_y, quarter_z(k), z_rows)])
            for side_k, (total, recv, recv_y) in enumerate(((own_a_sum, qkv_first, a_y), (own_b_sum, qkv_second, b_y)))
        ]
        return (2, 3, z_rows, side_a), parts

    *qkv_sends, qkv_mine, fc1_mine, grad_part = combine(
        at,
        *[qkv_quarter(k) for k in masks],
        qkv_quarter(0),
        z_sides(fc1_mine, fc1_recv),
        summed((half_rows // 2, width), term(grad_send, one, half_rows // 2)),
    )
    qkv_recv = [over_mask(mask, sent) for mask, sent in zip(masks.values(), qkv_sends)]
    fc1_y = over(1, fc1_mine)
    grad_second = over_x(grad_part)
    vectors = vectors + vectors_recv
    mlp_own = output_own(own_hidden, w_fc2, chunk)
    chunks = half_rows // chunk
    output_low = output_layer(pair_nat, chunks, chunks, far_hidden, mlp_own, far_fc2, middle, fc2_row, chunk)
    output_low, far_hidden, grad_second, vectors, fc2_mine, fc2_y, *qkv_recv = hold(
        output_low, far_hidden, grad_second, vectors, fc2_mine, fc2_y, *qkv_recv
    )

    qkv_mine, output_part = combine(
        at,
        summed(qkv_mine.shape, *[term(v) for v in (qkv_mine, *qkv_recv)]),
        summed((half_rows // 2, width), term(output_low, zero, half_rows // 2)),
    )
    qkv_parts = [qkv_mine] + [over_mask(mask, qkv_mine) for mask in masks.values()]
    output_first = over_x(output_part)
    vectors_recv = over_x(vectors)
    output_high = output_layer(pair_nat, 0, chunks, far_hidden, mlp_own, far_fc2, middle, fc2_row, chunk)
    output_high, vectors_recv, output_first, output_low, fc1_y, fc2_mine, fc2_y, *qkv_parts = hold(
        output_high, vectors_recv, output_first, output_low, fc1_y, fc2_mine, fc2_y, *qkv_parts
    )

    qkv_mine, out_half, output_part = combine(
        at,
        (
            (2, 3, half_rows_out, side_a),
            [(None, quarter_z(k), [term(v)]) for k, v in zip((0, *masks), qkv_parts)],
        ),
        ((half_width, heads_width), [(None, mine_y, [term(out_mine)]), (None, theirs_y, [term(out_y)])]),
        summed((half_rows // 2, width), term(output_low, one, half_rows // 2)),
    )
    qkv_y = over(1, qkv_mine)
    qkv_core = over(0, qkv_mine)
    output_second = over_x(output_part)
    vectors = vectors + vectors_recv
    vectors_recv = over(2, vectors)
    fc1_pieces = [fc1_mine, fc1_y, over(0, fc1_mine), over(0, fc1_y)]
    fc2_pieces = [fc2_mine, fc2_y, over(0, fc2_mine), over(0, fc2_y)]
    out_core = over(0, out_half)
    grad_recv = jnp.concatenate([grad_first, grad_second]).astype(F32)
    input_grad = joined(mp_at, grad_shifted[None, :half_rows], grad_recv[None])
    out_grad = finish_turned(pair_nat, out_half, out_core)
    fc1_grad = finish_rows(shared_nat, fc1_pieces)
    fc2_grad = finish_columns(at[1:5], fc2_pieces)
    qkv_mine, qkv_y, qkv_core, vectors_recv, output_second, fc1_grad, fc2_grad, out_grad, input_grad = hold(
        qkv_mine, qkv_y, qkv_core, vectors_recv, output_second, fc1_grad, fc2_grad, out_grad, input_grad
    )

    qkv_last = over(0, qkv_y)
    vectors = vectors + vectors_recv
    vectors_recv = over(3, vectors)
    output_recv = jnp.concatenate([output_first, output_second])
    block_output = joined(mp_at, output_high[None], output_recv[None])
    qkv_last, vectors_recv, block_output = hold(qkv_last, vectors_recv, block_output)

    vectors = vectors + vectors_recv
    vectors = vectors + over(1, vectors)
    qkv_grad = finish_stack(shared_nat, [qkv_mine, qkv_y, qkv_core, qkv_last])
    qkv_grad = jnp.transpose(qkv_grad, (1, 0, 2))

    table = counts.shape[0]
    lead_grad, singles, rest = vectors[:table], vectors[table : table + 6], vectors[table + 6 :]
    qv_bias_grad = part(rest[:2], mp_at, 2, 1)
    fc1_bias_grad = part(rest[2:].reshape(-1), mp_at, 2)
    return (
        block_output,
        input_grad,
        lead_grad,
        singles[0],
        singles[1],
        qkv_grad,
        qv_bias_grad,
        out_grad,
        singles[4],
        singles[2],
        singles[3],
        fc1_grad,
        fc1_bias_grad,
        fc2_grad,
        singles[5],
    )


def solution(mesh):
    in_specs = (
        P("dp", "mp", None),
        P("dp", "mp", None),
        P("dp"),
        P(),
        P(),
        P(),
        P(),
        P(None, None, "mp"),
        P(None, "mp"),
        P("mp", None),
        P(),
        P(),
        P(),
        P(None, "mp"),
        P("mp"),
        P("mp", None),
        P(),
    )
    out_specs = (
        P("dp", "mp", None),
        P("dp", "mp", None),
        P(),
        P(),
        P(),
        P(None, None, "mp"),
        P(None, "mp"),
        P("mp", None),
        P(),
        P(),
        P(),
        P(None, "mp"),
        P("mp"),
        P("mp", None),
        P(),
    )
    def local(*args):
        replicas = lax.axis_size("dp")
        samples, half_rows, width = args[0].shape
        heads_width, units = args[7].shape[2], args[13].shape[1]
        fits = samples == 2 and lax.axis_size("mp") == 2 and replicas == 16
        even = half_rows % 256 == 0 and width == 2 * heads_width == 1024 and units == 2 * width
        return (fast_body if fits and even else body)(*args)

    return jax.shard_map(local, mesh=mesh, in_specs=in_specs, out_specs=out_specs, check_vma=False)
```

```python
import functools
import math

import jax
import jax.numpy as jnp
from jax import lax
from jax.experimental import pallas as pl
from jax.experimental.pallas import tpu as pltpu
from jax.sharding import PartitionSpec as P

HD = 64


EPS = 1e-05


def norm_forward(values, norm_gain, norm_shift):
    center = values - jnp.mean(values, axis=-1, keepdims=True)
    inverse = lax.rsqrt(jnp.mean(center * center, axis=-1, keepdims=True) + EPS)
    scaled = center * inverse
    return (scaled * norm_gain + norm_shift, scaled, inverse)


def norm_backward(grad_out, scaled, inverse, norm_gain):
    grad_scaled = grad_out * norm_gain
    grad_mean = jnp.mean(grad_scaled, axis=-1, keepdims=True)
    cross_mean = jnp.mean(grad_scaled * scaled, axis=-1, keepdims=True)
    grad_in = inverse * (grad_scaled - grad_mean - scaled * cross_mean)
    gain_grad = jnp.sum(grad_out * scaled, axis=(0, 1))
    shift_grad = jnp.sum(grad_out, axis=(0, 1))
    return (grad_in, gain_grad, shift_grad)


def gelu_slope(pre_act):
    normal_cdf = 0.5 * (1.0 + lax.erf(pre_act * 0.7071067811865476))
    return normal_cdf + pre_act * jnp.exp(-0.5 * pre_act * pre_act) * 0.3989422804014327


def attention_forward(query_all, key_all, value_all, block_rows):
    block_count = query_all.shape[0] // block_rows
    query_blocks = query_all.reshape((block_count, block_rows) + query_all.shape[1:])

    def one_block(query_block):
        scores = (
            jnp.einsum("qshd,kshd->shqk", query_block, key_all, preferred_element_type=jnp.float32)
            * 0.125
        )
        row_max = jnp.max(scores, axis=-1, keepdims=True)
        powers = jnp.exp(scores - row_max)
        exp_total = jnp.sum(powers, axis=-1, keepdims=True)
        attn_weights = (powers / exp_total).astype(jnp.bfloat16)
        attended = jnp.einsum(
            "shqk,kshd->qshd", attn_weights, value_all, preferred_element_type=jnp.float32
        )
        return (attended.astype(jnp.bfloat16), (row_max + jnp.log(exp_total))[..., 0])

    attended, log_total = lax.map(one_block, query_blocks)
    return (attended.reshape(query_all.shape), log_total)


def attention_backward(query_all, key_all, value_all, grad_attended, log_total, block_rows):
    block_count = query_all.shape[0] // block_rows
    query_blocks = query_all.reshape((block_count, block_rows) + query_all.shape[1:])
    grad_blocks = grad_attended.reshape((block_count, block_rows) + query_all.shape[1:])

    def one_block(running, sliced):
        key_grad, value_grad = running
        query_block, grad_block, log_block = sliced
        scores = (
            jnp.einsum("qshd,kshd->shqk", query_block, key_all, preferred_element_type=jnp.float32)
            * 0.125
        )
        attn_weights = jnp.exp(scores - log_block[..., None])
        weight_low = attn_weights.astype(jnp.bfloat16)
        grad_weights = jnp.einsum(
            "qshd,kshd->shqk", grad_block, value_all, preferred_element_type=jnp.float32
        )
        inner = jnp.sum(attn_weights * grad_weights, axis=-1, keepdims=True)
        grad_scores = (attn_weights * (grad_weights - inner)).astype(jnp.bfloat16)
        query_grad = (
            jnp.einsum("shqk,kshd->qshd", grad_scores, key_all, preferred_element_type=jnp.float32)
            * 0.125
        )
        key_grad = (
            key_grad
            + jnp.einsum(
                "shqk,qshd->kshd", grad_scores, query_block, preferred_element_type=jnp.float32
            )
            * 0.125
        )
        value_grad = value_grad + jnp.einsum(
            "shqk,qshd->kshd", weight_low, grad_block, preferred_element_type=jnp.float32
        )
        return ((key_grad, value_grad), query_grad.astype(jnp.bfloat16))

    zero_grad = jnp.zeros(key_all.shape, jnp.float32)
    (key_grad, value_grad), query_grad = lax.scan(
        one_block, (zero_grad, zero_grad), (query_blocks, grad_blocks, log_total)
    )
    return (
        query_grad.reshape(query_all.shape),
        key_grad.astype(jnp.bfloat16),
        value_grad.astype(jnp.bfloat16),
    )


def body(
    tokens,
    cotangent,
    buckets,
    counts,
    lead_table,
    norm1_gain,
    norm1_shift,
    w_qkv,
    qv_bias,
    w_out,
    out_bias,
    norm2_gain,
    norm2_shift,
    w_fc1,
    fc1_bias,
    w_fc2,
    fc2_bias,
):
    samples_here = tokens.shape[0]
    local_rows = tokens.shape[1]
    local_width = w_qkv.shape[2]
    local_heads = local_width // HD
    seq_len = local_rows * lax.axis_size("mp")
    block_rows = min(512, seq_len)
    head_shape = (seq_len, samples_here, local_heads, HD)
    count_f = counts.astype(jnp.float32)
    onehot = (buckets[:, None] == jnp.arange(counts.shape[0], dtype=jnp.int32)[None, :]).astype(
        jnp.float32
    )
    loss_weight = jnp.mean(count_f) / jnp.sum(onehot * count_f[None, :], axis=1)
    lead_rows = jnp.dot(
        onehot,
        lead_table.astype(jnp.float32),
        precision=lax.Precision.HIGHEST,
        preferred_element_type=jnp.float32,
    )
    shifted = jnp.swapaxes(tokens, 0, 1).astype(jnp.float32) + lead_rows[None]
    normed_one, scaled_one, inverse_one = norm_forward(
        shifted, norm1_gain.astype(jnp.float32), norm1_shift.astype(jnp.float32)
    )
    normed_one = normed_one.astype(jnp.bfloat16)
    normed_full = lax.all_gather(normed_one, "mp", axis=0, tiled=True)
    project = jnp.einsum("tsd,dcf->tscf", normed_full, w_qkv, preferred_element_type=jnp.float32)
    bias_f = qv_bias.astype(jnp.float32)
    query_all = (project[:, :, 0] + bias_f[0]).astype(jnp.bfloat16).reshape(head_shape)
    key_all = project[:, :, 1].astype(jnp.bfloat16).reshape(head_shape)
    value_all = (project[:, :, 2] + bias_f[1]).astype(jnp.bfloat16).reshape(head_shape)
    attended, log_total = attention_forward(query_all, key_all, value_all, block_rows)
    attended_flat = attended.reshape(seq_len, samples_here, local_width)
    picked = attended_flat
    branch = lax.psum_scatter(
        jnp.einsum("tsf,fd->tsd", picked, w_out, preferred_element_type=jnp.float32),
        "mp",
        scatter_dimension=0,
        tiled=True,
    )
    middle = shifted + branch + out_bias.astype(jnp.float32)
    gain_two = norm2_gain.astype(jnp.float32)
    normed_two, scaled_two, inverse_two = norm_forward(
        middle, gain_two, norm2_shift.astype(jnp.float32)
    )
    normed_two = normed_two.astype(jnp.bfloat16)
    grad_top = jnp.swapaxes(cotangent, 0, 1).astype(jnp.float32) * loss_weight[None, :, None]
    grad_low = grad_top.astype(jnp.bfloat16)
    fc1_full, fc1_bias_full, fc2_full = (
        lax.all_gather(w_fc1, "mp", axis=1, tiled=True),
        lax.all_gather(fc1_bias, "mp", axis=0, tiled=True),
        lax.all_gather(w_fc2, "mp", axis=0, tiled=True),
    )
    pre_act = jnp.einsum(
        "tsd,df->tsf", normed_two, fc1_full, preferred_element_type=jnp.float32
    ) + fc1_bias_full.astype(jnp.float32)
    hidden = jax.nn.gelu(pre_act, approximate=False).astype(jnp.bfloat16)
    mlp_branch = jnp.einsum("tsf,fd->tsd", hidden, fc2_full, preferred_element_type=jnp.float32)
    output = middle + mlp_branch + fc2_bias.astype(jnp.float32)
    grad_hidden = jnp.einsum("tsd,fd->tsf", grad_low, fc2_full, preferred_element_type=jnp.float32)
    grad_pre = (grad_hidden * gelu_slope(pre_act)).astype(jnp.bfloat16)
    grad_normed_two = jnp.einsum(
        "tsf,df->tsd", grad_pre, fc1_full, preferred_element_type=jnp.float32
    )
    fc1_part = jnp.einsum("tsd,tsf->df", normed_two, grad_pre, preferred_element_type=jnp.float32)
    fc1_bias_part = jnp.sum(grad_pre.astype(jnp.float32), axis=(0, 1))
    fc2_part = jnp.einsum("tsf,tsd->fd", hidden, grad_low, preferred_element_type=jnp.float32)
    fc1_grad, fc1_bias_grad, fc2_grad = (
        lax.psum_scatter(
            fc1_part.astype(jnp.bfloat16), "mp", scatter_dimension=1, tiled=True
        ).astype(jnp.float32),
        lax.psum_scatter(
            fc1_bias_part.astype(jnp.bfloat16), "mp", scatter_dimension=0, tiled=True
        ).astype(jnp.float32),
        lax.psum_scatter(
            fc2_part.astype(jnp.bfloat16), "mp", scatter_dimension=0, tiled=True
        ).astype(jnp.float32),
    )
    fc2_bias_grad = jnp.sum(grad_top, axis=(0, 1))
    grad_from_norm, gain_two_grad, shift_two_grad = norm_backward(
        grad_normed_two, scaled_two, inverse_two, gain_two
    )
    grad_middle = grad_top + grad_from_norm
    out_bias_grad = jnp.sum(grad_middle, axis=(0, 1))
    grad_branch = grad_middle.astype(jnp.bfloat16)
    grad_branch_full = lax.all_gather(grad_branch, "mp", axis=0, tiled=True)
    out_grad = jnp.einsum(
        "tsf,tsd->fd", attended_flat, grad_branch_full, preferred_element_type=jnp.float32
    )
    grad_attended = jnp.einsum(
        "tsd,fd->tsf", grad_branch_full, w_out, preferred_element_type=jnp.float32
    ).astype(jnp.bfloat16)
    query_grad, key_grad, value_grad = attention_backward(
        query_all, key_all, value_all, grad_attended.reshape(head_shape), log_total, block_rows
    )
    grad_project = jnp.stack([query_grad, key_grad, value_grad], axis=2).reshape(
        seq_len, samples_here, 3, local_width
    )
    qkv_grad = jnp.einsum(
        "tsd,tscf->dcf", normed_full, grad_project, preferred_element_type=jnp.float32
    )
    query_bias_grad = jnp.sum(query_grad.astype(jnp.float32), axis=(0, 1)).reshape(local_width)
    value_bias_grad = jnp.sum(value_grad.astype(jnp.float32), axis=(0, 1)).reshape(local_width)
    qv_bias_grad = jnp.stack([query_bias_grad, value_bias_grad])
    picked = grad_project
    grad_normed_one = lax.psum_scatter(
        jnp.einsum("tscf,dcf->tsd", picked, w_qkv, preferred_element_type=jnp.float32).astype(
            jnp.bfloat16
        ),
        "mp",
        scatter_dimension=0,
        tiled=True,
    ).astype(jnp.float32)
    grad_in_one, gain_one_grad, shift_one_grad = norm_backward(
        grad_normed_one, scaled_one, inverse_one, norm1_gain.astype(jnp.float32)
    )
    grad_shifted = grad_middle + grad_in_one
    lead_grad = jnp.dot(
        onehot.T,
        jnp.sum(grad_shifted, axis=0),
        precision=lax.Precision.HIGHEST,
        preferred_element_type=jnp.float32,
    )
    small_grads = jnp.stack(
        [gain_one_grad, shift_one_grad, out_bias_grad, gain_two_grad, shift_two_grad, fc2_bias_grad]
    )
    lead_grad, small_grads = lax.psum((lead_grad, small_grads), ("dp", "mp"))
    qkv_grad, qv_bias_grad, out_grad, fc1_grad, fc1_bias_grad, fc2_grad = (
        lax.psum(qkv_grad.astype(jnp.bfloat16), "dp").astype(jnp.float32),
        lax.psum(qv_bias_grad.astype(jnp.bfloat16), "dp").astype(jnp.float32),
        lax.psum(out_grad.astype(jnp.bfloat16), "dp").astype(jnp.float32),
        lax.psum(fc1_grad.astype(jnp.bfloat16), "dp").astype(jnp.float32),
        lax.psum(fc1_bias_grad.astype(jnp.bfloat16), "dp").astype(jnp.float32),
        lax.psum(fc2_grad.astype(jnp.bfloat16), "dp").astype(jnp.float32),
    )
    block_output = jnp.swapaxes(output, 0, 1).astype(jnp.bfloat16)
    input_grad = jnp.swapaxes(grad_shifted, 0, 1)
    return (
        block_output,
        input_grad,
        lead_grad,
        small_grads[0],
        small_grads[1],
        qkv_grad,
        qv_bias_grad,
        out_grad,
        small_grads[2],
        small_grads[3],
        small_grads[4],
        fc1_grad,
        fc1_bias_grad,
        fc2_grad,
        small_grads[5],
    )


F32 = jnp.float32
BF16 = jnp.bfloat16
NN = (((1,), (0,)), ((), ()))
NT = (((1,), (1,)), ((), ()))
TN = (((0,), (0,)), ((), ()))
MIB = 1 << 20


def dot(left, right, dims):
    return lax.dot_general(left, right, dims, preferred_element_type=F32)


def whole(array):
    return pl.BlockSpec(array.shape, lambda *_: (0,) * array.ndim, pipeline_mode=pl.Buffered(1))


def kernel_call(body, name, grid, scalars, ins, outs, scratch=(), vmem=32, time=6, pinned=(), alias=None):
    spec = pltpu.PrefetchScalarGridSpec(
        num_scalar_prefetch=len(scalars),
        grid=grid,
        in_specs=[spec for _, spec in ins],
        out_specs=[spec for _, spec in outs],
        scratch_shapes=list(scratch),
    )
    return pl.pallas_call(
        body,
        out_shape=[shape for shape, _ in outs],
        grid_spec=spec,
        compiler_params=pltpu.CompilerParams(vmem_limit_bytes=vmem * MIB),
        input_output_aliases={} if alias is None else {len(scalars) + alias: 0},
        cost_estimate=pl.CostEstimate(flops=MIB, transcendentals=0, bytes_accessed=int(time * 2 * MIB)),
        name=name,
    )(
        *scalars,
        *[
            pltpu.with_memory_space_constraint(array, pltpu.HBM) if k in pinned else array
            for k, (array, _) in enumerate(ins)
        ],
    )


def struct(shape, dtype=BF16):
    return jax.ShapeDtypeStruct(shape, dtype)


def centred(values):
    center = values - jnp.mean(values, axis=-1, keepdims=True)
    inverse = lax.rsqrt(jnp.mean(center * center, axis=-1, keepdims=True) + EPS)
    return center * inverse, inverse


def norm_input_grad(grad_out, scaled, inverse, gain):
    grad_scaled = grad_out * gain
    grad_mean = jnp.mean(grad_scaled, axis=-1, keepdims=True)
    cross_mean = jnp.mean(grad_scaled * scaled, axis=-1, keepdims=True)
    return inverse * (grad_scaled - grad_mean - scaled * cross_mean)


def column_sum(values):
    return jnp.sum(values, axis=0, keepdims=True)


def chunk_of(nat_ref, index, size):
    return pl.ds(pl.multiple_of(nat_ref[index] * size, size), size)


def attention_forward_kernel(block, qkv_ref, out_ref, power_ref, inverse_ref):
    rows_all = qkv_ref.shape[1]
    steps = [(head, start) for head in range(2) for start in range(0, rows_all, block)]

    def scores_of(head, start):
        lanes = slice(HD * head, HD * head + HD)
        query = qkv_ref[0, start : start + block, lanes] * BF16(0.125)
        return dot(qkv_ref[1, :, lanes], query, NT)

    outs = [[], []]
    ahead = scores_of(*steps[0])
    for k, (head, start) in enumerate(steps):
        scores = ahead
        if k + 1 < len(steps):
            ahead = scores_of(*steps[k + 1])
        lanes = slice(HD * head, HD * head + HD)
        rows = slice(start, start + block)
        powers = jnp.exp2((scores - jnp.max(scores, axis=0, keepdims=True)) * 1.4426950408889634)
        inverse = 1.0 / jnp.sum(powers, axis=0, keepdims=True)
        power_low = powers.astype(BF16)
        power_ref[head, :, rows] = power_low
        inverse_ref[0, head : head + 1, rows] = inverse
        outs[head].append(dot(qkv_ref[2, :, lanes], power_low, TN) * inverse)
    heads = [jnp.concatenate(parts, axis=1) for parts in outs]
    out_ref[...] = jnp.concatenate(heads, axis=0).T.astype(BF16)


def attend(qkv):
    _, rows, width = qkv.shape
    pairs = width // (2 * HD)
    return kernel_call(
        functools.partial(attention_forward_kernel, min(512, rows)),
        "attention_forward",
        (pairs,),
        [],
        [(qkv, pl.BlockSpec((3, rows, 2 * HD), lambda j: (0, 0, j)))],
        [
            (struct((rows, width)), pl.BlockSpec((rows, 2 * HD), lambda j: (0, j))),
            (pltpu.HBM((2 * pairs, rows, rows), BF16), pl.BlockSpec((2, rows, rows), lambda j: (j, 0, 0))),
            (struct((pairs, 2, rows), F32), pl.BlockSpec((1, 2, rows), lambda j: (j, 0, 0))),
        ],
        vmem=48,
        time=4 * pairs,
        pinned=[0],
    )


def attention_backward_kernel(block, qkv_ref, power_ref, inverse_ref, out_ref, grad_ref, dqkv_ref, sums_ref):
    rows_all = qkv_ref.shape[1]
    out_t = out_ref[...].astype(F32).T
    grad_t = grad_ref[...].astype(F32).T
    for head in range(2):
        lanes = slice(HD * head, HD * head + HD)
        inverse = inverse_ref[0, head : head + 1, :]
        grad_head = grad_t[lanes]
        inner = jnp.sum(grad_head * out_t[lanes], axis=0, keepdims=True) * inverse
        grad_scaled = grad_head * inverse
        grad_low_t = grad_scaled.astype(BF16)
        grad_low = grad_scaled.T.astype(BF16)
        query = qkv_ref[0, :, lanes] * BF16(0.125)
        key = qkv_ref[1, :, lanes]
        value = qkv_ref[2, :, lanes]
        key_t = key.T
        key_grad = value_grad = None
        query_grads = []
        for start in range(0, rows_all, block):
            rows = slice(start, start + block)
            power = power_ref[head, :, rows]
            grad_power = dot(value, grad_low_t[:, rows], NN) - inner[:, rows]
            grad_scores = (power.astype(F32) * grad_power).astype(BF16)
            key_part = dot(grad_scores, query[rows], NN)
            value_part = dot(power, grad_low[rows], NN)
            key_grad = key_part if key_grad is None else key_grad + key_part
            value_grad = value_part if value_grad is None else value_grad + value_part
            query_grads.append(dot(key_t, grad_scores, NN))
        sums_ref[0, :, lanes] = jnp.concatenate(query_grads, axis=1).T * 0.125
        sums_ref[1, :, lanes] = key_grad
        sums_ref[2, :, lanes] = value_grad
    dqkv_ref[...] = sums_ref[...].astype(BF16)


def attend_back(first, count, qkv, powers, inverse, attended, grad_attended):
    _, rows, width = qkv.shape
    block = (3, rows, 2 * HD)
    flat = pl.BlockSpec((rows, 2 * HD), lambda j: (0, j + first))
    return kernel_call(
        functools.partial(attention_backward_kernel, min(512, rows)),
        "attention_backward",
        (count,),
        [],
        [
            (qkv, pl.BlockSpec(block, lambda j: (0, 0, j + first))),
            (powers, pl.BlockSpec((2, rows, rows), lambda j: (j + first, 0, 0))),
            (inverse, pl.BlockSpec((1, 2, rows), lambda j: (j + first, 0, 0))),
            (attended, flat),
            (grad_attended, flat),
        ],
        [(struct((3, rows, 2 * HD * count)), pl.BlockSpec(block, lambda j: (0, 0, j)))],
        [pltpu.VMEM(block, F32)],
        vmem=40,
        time=5.5 * count,
        pinned=range(5),
    )[0]


def project_own_kernel(at_ref, tokens_ref, recv_ref, lead_ref, gain_ref, shift_ref, weight_ref, bias_ref, rows_ref, normed_ref, heads_ref):
    own = pl.program_id(0) < pl.num_programs(0) // 2
    tokens = jnp.where(own, tokens_ref[0].astype(F32), recv_ref[...].astype(F32))
    rows_ref[...] = tokens.astype(BF16)
    scaled, _ = centred(tokens + lead_ref[...])
    normed = (scaled * gain_ref[...] + shift_ref[...]).astype(BF16)
    normed_ref[...] = normed
    for c in range(3):
        heads_ref[c] = (dot(normed, weight_ref[c], NN) + bias_ref[c : c + 1]).astype(BF16)


def project_own(at, tokens, recv, lead, gain, shift, weight, bias, chunk):
    half, width = tokens.shape[1:]
    heads = weight.shape[2]
    steps = half // chunk
    row = pl.BlockSpec((chunk, width), lambda j, at: (j, 0))
    return kernel_call(
        project_own_kernel,
        "project_own",
        (2 * steps,),
        [at],
        [
            (tokens, pl.BlockSpec((1, chunk, width), lambda j, at: (at[0], jnp.minimum(j, steps - 1), 0))),
            (recv, pl.BlockSpec((chunk, width), lambda j, at: (jnp.maximum(j - steps, 0), 0))),
            *[(v, whole(v)) for v in (lead, gain, shift, weight, bias)],
        ],
        [
            (struct((2 * half, width)), row),
            (struct((2 * half, width)), row),
            (struct((3, 2 * half, heads)), pl.BlockSpec((3, chunk, heads), lambda j, at: (0, j, 0))),
        ],
        pinned=[0, 1, 5],
    )


def project_far_kernel(nat_ref, normed_ref, bias_ref, *refs):
    *pieces, heads_ref = refs
    size = pieces[0].shape[1]
    total = bias_ref[0]
    for k, piece in enumerate(pieces):
        total = total + dot(normed_ref[:, chunk_of(nat_ref, k, size)], piece[0], NN)
    heads_ref[0] = total.astype(BF16)


def project_far(nat, normed, bias, pieces):
    rows = normed.shape[0]
    heads = pieces[0].shape[2]
    first = lambda j, nat: (j, 0, 0)
    return kernel_call(
        project_far_kernel,
        "project_far",
        (3,),
        [nat],
        [
            (normed, whole(normed)),
            (bias[:, None], pl.BlockSpec((1, 1, heads), first)),
            *[(p, pl.BlockSpec((1, *p.shape[1:]), first)) for p in pieces],
        ],
        [(struct((3, rows, heads)), pl.BlockSpec((1, rows, heads), first))],
    )[0]


def middle_kernel(nat_ref, own_ref, far_ref, weight_ref, rows_ref, lead_ref, bias_ref, gain_ref, shift_ref, *refs):
    *pieces, middle_ref, normed_ref = refs
    total = dot(own_ref[...], weight_ref[...], NN)
    for k, piece in enumerate(pieces):
        total = total + dot(far_ref[:, chunk_of(nat_ref, k, piece.shape[0])], piece[...], NN)
    middle = rows_ref[...].astype(F32) + lead_ref[...] + total + bias_ref[...]
    middle_ref[...] = middle
    scaled, _ = centred(middle)
    normed_ref[...] = (scaled * gain_ref[...] + shift_ref[...]).astype(BF16)


def middle_layer(nat, own, far, weight, pieces, rows, lead, bias, gain, shift, chunk):
    count, width = rows.shape
    row = pl.BlockSpec((chunk, width), lambda j, nat: (j, 0))
    heads = pl.BlockSpec((chunk, own.shape[1]), lambda j, nat: (j, 0))
    return kernel_call(
        middle_kernel,
        "middle_layer",
        (count // chunk,),
        [nat],
        [(own, heads), (far, heads), (weight, whole(weight)), (rows, row)]
        + [(v, whole(v)) for v in (lead, bias, gain, shift, *pieces)],
        [(pltpu.HBM((count, width), F32), row), (struct((count, width)), row)],
        pinned=[2, 3],
    )


def gelu_store(pre_act, rows, hidden_ref, slope_ref):
    cdf = 0.5 * (1.0 + lax.erf(pre_act * 0.7071067811865476))
    hidden_ref[rows] = (pre_act * cdf).astype(BF16)
    density = jnp.exp(-0.5 * pre_act * pre_act) * 0.3989422804014327
    slope_ref[rows] = (cdf + pre_act * density).astype(BF16)


def hidden_kernel(block, nat_ref, normed_ref, bias_ref, *refs):
    *pieces, hidden_ref, slope_ref = refs
    size = pieces[0].shape[0]
    for start in range(0, normed_ref.shape[0], block):
        rows = slice(start, start + block)
        pre_act = bias_ref[...]
        for k, piece in enumerate(pieces):
            lanes = slice(None) if len(pieces) == 1 else chunk_of(nat_ref, k, size)
            pre_act = pre_act + dot(normed_ref[rows, lanes], piece[...], NN)
        gelu_store(pre_act, rows, hidden_ref, slope_ref)


def hidden_layer(nat, normed, bias, pieces, chunk):
    rows = normed.shape[0]
    units = pieces[0].shape[1]
    tile = min(512, units)
    column = lambda j, nat: (0, j)
    return kernel_call(
        functools.partial(hidden_kernel, chunk),
        "hidden_layer",
        (units // tile,),
        [nat],
        [(normed, whole(normed)), (bias, pl.BlockSpec((1, tile), column))]
        + [(p, pl.BlockSpec((p.shape[0], tile), column)) for p in pieces],
        [(struct((rows, units)), pl.BlockSpec((rows, tile), column))] * 2,
        vmem=24,
        time=10,
        pinned=range(2, 2 + len(pieces)),
    )


def product_kernel(outs, add_count, by_step, _, left_ref, right_ref, *refs):
    adds, out_refs = refs[:add_count], refs[add_count:]
    stacked = len(right_ref.shape) == 3
    value = dot(left_ref[...], right_ref[0] if stacked else right_ref[...], TN)
    for add in adds:
        value = value + (add[0] if stacked else add[...]).astype(F32)
    value = value.astype(BF16)
    if stacked:
        out_refs[0][0] = value
    elif outs == 1:
        out_refs[0][...] = value
    elif by_step:
        for k, out_ref in enumerate(out_refs):

            @pl.when(pl.program_id(0) == k)
            def _(out_ref=out_ref):
                out_ref[...] = value
    else:
        size = value.shape[0] // outs
        for k, out_ref in enumerate(out_refs):
            out_ref[...] = value[k * size : (k + 1) * size]


def grad_right_half(half, left, right, *add):
    rows, columns = left.shape
    kept = right.shape[1] // 2
    tile = columns // 2
    out_spec = pl.BlockSpec((tile, kept), lambda j, half: (j, 0))
    outs = 2 if add else 1
    split = [(struct((tile, kept)), pl.BlockSpec((tile, kept), lambda j, half: (0, 0)))] * 2
    result = kernel_call(
        functools.partial(product_kernel, outs, len(add), True),
        "grad_right_half",
        (2,),
        [half],
        [
            (left, pl.BlockSpec((rows, tile), lambda j, half: (0, j))),
            (right, pl.BlockSpec((rows, kept), lambda j, half: (0, half[0]))),
        ]
        + [(a, out_spec) for a in add],
        split if add else [(struct((columns, kept)), out_spec)],
        vmem=20,
        time=3,
    )
    return result if add else result[0]


def grad_left_half(half, left, right, *add, split=False):
    rows = left.shape[0]
    kept = left.shape[1] // 2
    columns = right.shape[-1]
    tile = min(1024, columns)
    outs = 2 if split else 1
    left_spec = pl.BlockSpec((rows, kept), lambda j, half: (0, half[0]))
    if right.ndim == 3:
        grid, out_shape = (right.shape[0],), (right.shape[0], kept, columns)
        right_spec = pl.BlockSpec((1, rows, columns), lambda j, half: (j, 0, 0))
        add_spec = out_spec = pl.BlockSpec((1, kept, columns), lambda j, half: (j, 0, 0))
    else:
        grid, out_shape = (columns // tile,), (kept // outs, columns)
        right_spec = pl.BlockSpec((rows, tile), lambda j, half: (0, j))
        add_spec = pl.BlockSpec((kept, tile), lambda j, half: (0, j))
        out_spec = pl.BlockSpec((kept // outs, tile), lambda j, half: (0, j))
    result = kernel_call(
        functools.partial(product_kernel, outs, len(add), False),
        "grad_left_half",
        grid,
        [half],
        [(left, left_spec), (right, right_spec)] + [(a, add_spec) for a in add],
        [(struct(out_shape), out_spec)] * outs,
        vmem=20,
        time=3,
    )
    return result if split else result[0]


def term(array, at=None, size=None, column=None):
    block, index = list(array.shape), [None] * array.ndim
    if size is not None:
        block[-2], index[-2] = size, at
    if column is not None:
        block[-1], index[-1] = array.shape[-1] // 2, lambda _: column

    def index_map(_, flags):
        return tuple(0 if f is None else f(flags) for f in index)

    return array, pl.BlockSpec(tuple(block), index_map)


def combine_kernel(plan, flags_ref, *refs):
    count = sum(terms for parts in plan for _, _, terms in parts)
    ins, outs = list(refs[:count]), refs[count:]
    for parts, out_ref in zip(plan, outs):
        for lead, row, terms in parts:
            value = None
            for ref in ins[:terms]:
                part = ref[...] if terms == 1 else ref[...].astype(F32)
                value = part if value is None else value + part
            ins = ins[terms:]
            value = value.astype(BF16)
            if lead is not None:
                out_ref[lead] = value
            elif row is not None:
                size = value.shape[-2]
                start = row if isinstance(row, int) else pl.multiple_of(row(flags_ref) * size, size)
                where = (slice(None),) * (value.ndim - 2) + (pl.ds(start, size), slice(None))
                out_ref[where] = value
            else:
                out_ref[...] = value


def combine(flags, *outs):
    ins = [t for _, parts in outs for _, _, terms in parts for t in terms]
    plan = [[(lead, row, len(terms)) for lead, row, terms in parts] for _, parts in outs]

    def full(shape):
        return pl.BlockSpec(shape, lambda *_: (0,) * len(shape))

    return kernel_call(
        functools.partial(combine_kernel, plan),
        "combine",
        (1,),
        [flags],
        ins,
        [(struct(shape), full(shape)) for shape, _ in outs],
        vmem=32,
        time=3,
    )


def summed(shape, *terms):
    return shape, [(None, None, terms)]


def pre_grad_store(grad, slope_ref, pre_ref, sum_ref):
    pre = (grad * slope_ref[...].astype(F32)).astype(BF16)
    pre_ref[...] = pre
    sum_ref[...] = column_sum(pre.astype(F32))


def pre_grad_own_kernel(low_ref, weight_ref, slope_ref, pre_ref, sum_ref):
    pre_grad_store(dot(low_ref[...], weight_ref[...], NT), slope_ref, pre_ref, sum_ref)


def pre_grad_own(low, weight, slope):
    rows, width = low.shape
    units = weight.shape[0]
    tile = min(512, units)
    column = lambda j: (0, j)
    return kernel_call(
        pre_grad_own_kernel,
        "pre_grad_own",
        (units // tile,),
        [],
        [
            (low, whole(low)),
            (weight, pl.BlockSpec((tile, width), lambda j: (j, 0))),
            (slope, pl.BlockSpec((rows, tile), column)),
        ],
        [
            (struct((rows, units)), pl.BlockSpec((rows, tile), column)),
            (struct((1, units), F32), pl.BlockSpec((1, tile), column)),
        ],
        vmem=24,
        pinned=[1],
    )


def pre_grad_far_kernel(per, nat_ref, low_ref, slope_ref, *refs):
    *pieces, pre_ref, sum_ref = refs
    for k, piece in enumerate(pieces):

        @pl.when(pl.program_id(0) // per == k)
        def _(piece=piece):
            pre_grad_store(dot(low_ref[...], piece[...], NT), slope_ref, pre_ref, sum_ref)


def pre_grad_far(nat, low, pieces, slope):
    rows, width = low.shape
    size = pieces[0].shape[0]
    tile = min(512, size)
    per = size // tile
    units = size * len(pieces)
    column = lambda j, nat: (0, nat[j // per] * per + j % per)

    def piece_spec(k):
        return pl.BlockSpec((tile, width), lambda j, nat: (jnp.clip(j - k * per, 0, per - 1), 0))

    return kernel_call(
        functools.partial(pre_grad_far_kernel, per),
        "pre_grad_far",
        (len(pieces) * per,),
        [nat],
        [(low, whole(low)), (slope, pl.BlockSpec((rows, tile), column))]
        + [(p, piece_spec(k)) for k, p in enumerate(pieces)],
        [
            (struct((rows, units)), pl.BlockSpec((rows, tile), column)),
            (struct((1, units), F32), pl.BlockSpec((1, tile), column)),
        ],
        vmem=24,
        time=8,
        pinned=range(2, 2 + len(pieces)),
    )


def add_sums(sums_ref, rows):
    @pl.when(pl.program_id(0) == 0)
    def _():
        sums_ref[...] = jnp.zeros_like(sums_ref)

    for k, row in enumerate(rows):
        sums_ref[k : k + 1, :] += row


def middle_grad_kernel(
    nat_ref, at_ref, own_ref, far_ref, weight_ref, middle_ref, cot_ref, recv_ref, loss_ref, gain_ref, *refs
):
    *pieces, grad_ref, low_ref, sums_ref, total_ref = refs
    total_ref[...] = dot(own_ref[...], weight_ref[...], NT)
    for k, piece in enumerate(pieces):
        total_ref[:, chunk_of(nat_ref, k, piece.shape[0])] += dot(far_ref[...], piece[...], NT)
    grad = total_ref[...]
    scaled, inverse = centred(middle_ref[...])
    mine = pl.program_id(0) < pl.num_programs(0) // 2
    top = jnp.where(mine, cot_ref[0].astype(F32), recv_ref[...].astype(F32)) * loss_ref[...]
    grad_middle = top + norm_input_grad(grad, scaled, inverse, gain_ref[...])
    grad_ref[...] = grad_middle
    low_ref[...] = grad_middle.astype(BF16)
    add_sums(
        sums_ref,
        [column_sum(grad * scaled), column_sum(grad), column_sum(grad_middle), column_sum(top)],
    )


def middle_grad(nat, at, own, far, weight, pieces, middle, cot, recv, loss, gain, chunk):
    count, width = middle.shape
    row = pl.BlockSpec((chunk, width), lambda j, *_: (j, 0))
    units = pl.BlockSpec((chunk, own.shape[1]), lambda j, *_: (j, 0))
    steps = count // chunk // 2
    return kernel_call(
        middle_grad_kernel,
        "middle_grad",
        (count // chunk,),
        [nat, at],
        [
            (own, units),
            (far, units),
            (weight, whole(weight)),
            (middle, row),
            (cot, pl.BlockSpec((1, chunk, width), lambda j, nat, at: (at[0], jnp.minimum(j, steps - 1), 0))),
            (recv, pl.BlockSpec((chunk, width), lambda j, *_: (jnp.maximum(j - steps, 0), 0))),
        ]
        + [(v, whole(v)) for v in (loss, gain, *pieces)],
        [
            (struct((count, width), F32), row),
            (struct((count, width)), row),
            (struct((8, width), F32), pl.BlockSpec((8, width), lambda j, *_: (0, 0))),
        ],
        [pltpu.VMEM((chunk, width), F32)],
        time=14,
        pinned=[2, 3, 4, 5, *range(8, 8 + len(pieces))],
    )


def attended_grad_kernel(nat_ref, low_ref, weight_ref, *refs):
    *pieces, own_ref, far_ref = refs
    own_ref[...] = dot(low_ref[...], weight_ref[...], NT).astype(BF16)
    for k, piece in enumerate(pieces):
        far_ref[:, chunk_of(nat_ref, k, piece.shape[0])] = dot(low_ref[...], piece[...], NT).astype(BF16)


def attended_grad(nat, low, weight, pieces, chunk):
    count, width = low.shape
    heads = weight.shape[0]
    out = (struct((count, heads)), pl.BlockSpec((chunk, heads), lambda j, nat: (j, 0)))
    return kernel_call(
        attended_grad_kernel,
        "attended_grad",
        (count // chunk,),
        [nat],
        [(low, pl.BlockSpec((chunk, width), lambda j, nat: (j, 0)))] + [(v, whole(v)) for v in (weight, *pieces)],
        [out, out],
        pinned=range(1, 2 + len(pieces)),
    )


def output_own_kernel(own_ref, weight_ref, out_ref):
    out_ref[...] = dot(own_ref[...], weight_ref[...], NN)


def output_own(own, weight, chunk):
    count, units = own.shape
    width = weight.shape[1]
    return kernel_call(
        output_own_kernel,
        "output_own",
        (count // chunk,),
        [],
        [(own, pl.BlockSpec((chunk, units), lambda j: (j, 0))), (weight, whole(weight))],
        [(struct((count, width), F32), pl.BlockSpec((chunk, width), lambda j: (j, 0)))],
        vmem=20,
        time=6,
        pinned=range(2),
    )[0]


def output_kernel(nat_ref, far_ref, own_ref, middle_ref, bias_ref, *refs):
    *pieces, out_ref = refs
    total = own_ref[...]
    for k, piece in enumerate(pieces):
        total = total + dot(far_ref[:, chunk_of(nat_ref, k, piece.shape[0])], piece[...], NN)
    out_ref[...] = (middle_ref[...] + total + bias_ref[...]).astype(BF16)


def output_layer(nat, first, count, far, own, pieces, middle, bias, chunk):
    width = middle.shape[1]
    row = pl.BlockSpec((chunk, width), lambda j, nat: (j + first, 0))
    return kernel_call(
        output_kernel,
        "output_layer",
        (count,),
        [nat],
        [(far, pl.BlockSpec((chunk, far.shape[1]), lambda j, nat: (j + first, 0))), (own, row), (middle, row)]
        + [(v, whole(v)) for v in (bias, *pieces)],
        [(struct((count * chunk, width)), pl.BlockSpec((chunk, width), lambda j, nat: (j, 0)))],
        vmem=24,
        time=6,
        pinned=range(4 + len(pieces)),
    )[0]


def input_grad_kernel(own_count, nat_ref, far_ref, weight_ref, rows_ref, lead_ref, grad_ref, gain_ref, *refs):
    owns, refs = refs[:own_count], refs[own_count:]
    *pieces, out_ref, low_ref, sums_ref, total_ref = refs
    total = None
    at = 0
    for own in owns:
        size = own.shape[2]
        for c in range(3):
            part = dot(own[c], weight_ref[c, :, at : at + size], NT)
            total = part if total is None else total + part
        at += size
    total_ref[...] = total
    for k, piece in enumerate(pieces):
        part = dot(far_ref[0], piece[0], NT) + dot(far_ref[1], piece[1], NT) + dot(far_ref[2], piece[2], NT)
        total_ref[:, chunk_of(nat_ref, k, piece.shape[1])] += part
    grad = total_ref[...]
    scaled, inverse = centred(rows_ref[...].astype(F32) + lead_ref[...])
    grad_shifted = grad_ref[...] + norm_input_grad(grad, scaled, inverse, gain_ref[...])
    out_ref[...] = grad_shifted
    low_ref[...] = grad_shifted.astype(BF16)
    bias_rows = [
        jnp.concatenate([column_sum(d[c].astype(F32)) for d in (*owns, far_ref)], axis=1) for c in (0, 2)
    ]
    add_sums(
        sums_ref, [column_sum(grad * scaled), column_sum(grad), column_sum(grad_shifted), *bias_rows]
    )


def input_grads(nat, owns, far, weight, pieces, rows, lead, grad_middle, gain, chunk):
    count, width = rows.shape
    row = pl.BlockSpec((chunk, width), lambda j, nat: (j, 0))
    heads = lambda d: pl.BlockSpec((3, chunk, d.shape[2]), lambda j, nat: (0, j, 0))
    steps = count // chunk
    half = pl.BlockSpec((chunk, width), lambda j, nat: (jnp.maximum(j - steps // 2, 0), 0))
    return kernel_call(
        functools.partial(input_grad_kernel, len(owns)),
        "input_grads",
        (steps,),
        [nat],
        [
            (far, heads(far)),
            (weight, whole(weight)),
            (rows, row),
            (lead, whole(lead)),
            (grad_middle, row),
            (gain, whole(gain)),
        ]
        + [(d, heads(d)) for d in owns]
        + [(p, whole(p)) for p in pieces],
        [
            (struct((count, width), F32), row),
            (struct((count // 2, width)), half),
            (struct((8, width), F32), pl.BlockSpec((8, width), lambda j, nat: (0, 0))),
        ],
        [pltpu.VMEM((chunk, width), F32)],
        time=14,
        pinned=[0, 1, 2, 4, *range(6, 6 + len(owns) + len(pieces))],
    )


def pack_kernel(buckets, flags_ref, one_ref, two_ref, own_ref, far_ref, out_ref):
    width = one_ref.shape[1]
    half = width // 2
    first = flags_ref[0] == 0
    rows = lax.broadcasted_iota(jnp.int32, (buckets, width), 0)
    out_ref[:buckets] = jnp.where(rows == flags_ref[7], one_ref[2:3], 0.0)
    out_ref[buckets : buckets + 2] = one_ref[:2]
    out_ref[buckets + 2 : buckets + 6] = two_ref[:4]
    bias = one_ref[3:5]
    swapped = jnp.concatenate([bias[:, half:], bias[:, :half]], axis=1)
    out_ref[buckets + 6 : buckets + 8] = jnp.where(first, bias, swapped)
    own, far = own_ref[...], far_ref[...]
    count = own.shape[1] // width
    for k in range(count):
        columns = slice(k * width, (k + 1) * width)
        low, high = own[:, columns], far[:, columns]
        out_ref[buckets + 8 + k : buckets + 9 + k] = jnp.where(first, low, high)
        out_ref[buckets + 8 + count + k : buckets + 9 + count + k] = jnp.where(first, high, low)


def pack_vectors(flags, buckets, one, two, own, far):
    width = one.shape[1]
    rows = buckets + 8 + 2 * own.shape[1] // width
    return kernel_call(
        functools.partial(pack_kernel, buckets),
        "pack_vectors",
        (1,),
        [flags],
        [(v, whole(v)) for v in (one, two, own, far)],
        [(struct((rows, width), F32), pl.BlockSpec((rows, width), lambda *_: (0, 0)))],
        vmem=8,
        time=1,
    )[0]


def finish_turned_kernel(_, *refs):
    *pieces, out_ref = refs
    for k, piece in enumerate(pieces):

        @pl.when(pl.program_id(0) == k)
        def _(piece=piece):
            out_ref[...] = piece[...].astype(F32).T


def finish_turned(nat, pieces):
    rows, columns = pieces[0].shape
    return kernel_call(
        finish_turned_kernel,
        "finish",
        (4,),
        [nat],
        [(p, whole(p)) for p in pieces],
        [(struct((columns, 4 * rows), F32), pl.BlockSpec((columns, rows), lambda s, nat: (0, nat[s])))],
        vmem=16,
        time=2,
    )[0]


def source_spec(block, which, steps, place):
    def index(s, j, *_):
        return place(jnp.where(s == which, j, jnp.where(s < which, 0, steps - 1)))

    return pl.BlockSpec(block, index)


def finish_rows_kernel(_, *refs):
    *pieces, out_ref = refs
    for k, piece in enumerate(pieces):

        @pl.when(pl.program_id(0) == k)
        def _(piece=piece):
            out_ref[...] = piece[0].astype(F32)


def finish_rows(at, pieces):
    halves, rows, columns = pieces[0].shape
    block = (1, rows, columns)
    return kernel_call(
        finish_rows_kernel,
        "finish",
        (2, halves),
        [at],
        [(p, source_spec(block, k, halves, lambda j: (j, 0, 0))) for k, p in enumerate(pieces)],
        [
            (
                struct((2 * halves * rows, columns), F32),
                pl.BlockSpec((rows, columns), lambda s, j, at: (at[s] * halves + j, 0)),
            )
        ],
        vmem=20,
        time=5,
    )[0]


def finish_columns_kernel(at_ref, mine_ref, theirs_ref, out_ref):
    first = at_ref[0] == 0
    one, two = mine_ref[0].astype(F32), theirs_ref[0].astype(F32)
    columns = one.shape[1]
    out_ref[:, :columns] = jnp.where(first, one, two)
    out_ref[:, columns:] = jnp.where(first, two, one)


def finish_columns(at, pieces):
    halves, rows, columns = pieces[0].shape
    tile = min(512, rows)
    per = rows // tile
    spec = pl.BlockSpec((1, tile, columns), lambda j, at: (j // per, j % per, 0))
    return kernel_call(
        finish_columns_kernel,
        "finish",
        (halves * per,),
        [at],
        [(p, spec) for p in pieces],
        [(struct((halves * rows, 2 * columns), F32), pl.BlockSpec((tile, 2 * columns), lambda j, at: (j, 0)))],
        vmem=20,
        time=5,
    )[0]


def finish_stack_kernel(count, at_ref, *refs):
    pieces, out_ref = refs[:count], refs[-1]
    for k, piece in enumerate(pieces):

        @pl.when(pl.program_id(0) == k)
        def _(piece=piece):
            out_ref[0] = jnp.concatenate([piece[0, 0].astype(F32), piece[1, 0].astype(F32)], axis=1)


def finish_stack(nat, first, pieces, *so_far):
    _, stack, rows, columns = pieces[0].shape
    block = (2, 1, rows, columns)
    count = len(pieces)
    return kernel_call(
        functools.partial(finish_stack_kernel, count),
        "finish",
        (count, stack),
        [nat],
        [(p, source_spec(block, k, stack, lambda j: (0, j, 0, 0))) for k, p in enumerate(pieces)]
        + [(v, pl.BlockSpec(memory_space=pl.ANY)) for v in so_far],
        [
            (
                struct((stack, 4 * rows, 2 * columns), F32),
                pl.BlockSpec((1, rows, 2 * columns), lambda s, j, nat: (j, nat[first + s], 0)),
            )
        ],
        vmem=16,
        time=3,
        alias=count if so_far else None,
    )[0]


def hold(*values):
    return lax.optimization_barrier(values)


def fast_body(
    tokens,
    cotangent,
    buckets,
    counts,
    lead_table,
    norm1_gain,
    norm1_shift,
    w_qkv,
    qv_bias,
    w_out,
    out_bias,
    norm2_gain,
    norm2_shift,
    w_fc1,
    fc1_bias,
    w_fc2,
    fc2_bias,
):
    replicas = lax.axis_size("dp")
    levels = replicas.bit_length() - 1
    dp_at, mp_at = lax.axis_index("dp"), lax.axis_index("mp")
    bits = [(dp_at >> level) & 1 for level in range(levels)]

    def over_x(value):
        return lax.ppermute(value, "mp", [(0, 1), (1, 0)])

    def over(level, value):
        return over_mask(1 << level, value)

    def over_mask(mask, value):
        return lax.ppermute(value, "dp", [(i, i ^ mask) for i in range(replicas)])

    def joined(bit, mine, theirs, axis=0):
        return jnp.where(
            bit == 0,
            jnp.concatenate([mine, theirs], axis),
            jnp.concatenate([theirs, mine], axis),
        )

    def part(value, index, count, axis=0):
        size = value.shape[axis] // count
        return lax.dynamic_slice_in_dim(value, index * size, size, axis)

    half_rows, width = tokens.shape[1:]
    heads_width = w_qkv.shape[2]
    units = w_fc1.shape[1]
    chunk = 256
    core, side = bits[0], bits[1]
    bucket = lax.dynamic_index_in_dim(buckets, mp_at, 0, keepdims=False)
    at = jnp.stack([mp_at, core, 1 - core, side, 1 - side, bits[2], bits[3], bucket]).astype(jnp.int32)
    mine = core * 2 + side
    shared_nat = jnp.stack([mine, mine ^ 1, mine ^ 2, mine ^ 3]).astype(jnp.int32)
    core_first_nat = jnp.stack([mine, mine ^ 2, mine ^ 1, mine ^ 3]).astype(jnp.int32)

    def row_of(vector):
        return vector.astype(F32)[None]

    small = jnp.concatenate([qv_bias.reshape(-1), fc1_bias])
    small_rows = -(-small.shape[0] // width)
    small_rows_padded = -(-small_rows // 16) * 16
    small = jnp.pad(small, (0, small_rows_padded * width - small.shape[0])).reshape(-1, width)
    token_recv = over_x(jnp.concatenate([part(tokens, 1 - mp_at, 2)[0], small]))

    count_f = counts.astype(F32)
    loss_weight = jnp.mean(count_f) / lax.dynamic_index_in_dim(count_f, bucket, 0, keepdims=False)
    loss_row = jnp.broadcast_to(loss_weight, (1, width))
    lead = lax.dynamic_index_in_dim(lead_table, bucket, 0).astype(F32)
    own_qkv = jnp.transpose(w_qkv, (1, 0, 2))

    def bias_three(bias):
        bias_f = bias.astype(F32)
        return jnp.stack([bias_f[0], jnp.zeros_like(bias_f[0]), bias_f[1]])

    (
        token_recv, qkv_send, out_send, fc1_send, cot_send, fc2_send, at, shared_nat, core_first_nat, loss_row, loss_weight, lead,
        gain_one, gain_two, shift_one, shift_two, out_row, fc1_row, fc2_row, own_bias,
    ) = hold(
        token_recv,
        part(own_qkv, mine, 4, 1),
        part(w_out, core, 2),
        part(w_fc1, mine, 4),
        part(cotangent, 1 - mp_at, 2)[0],
        part(w_fc2, core, 2),
        at,
        shared_nat,
        core_first_nat,
        loss_row,
        loss_weight,
        lead,
        row_of(norm1_gain),
        row_of(norm2_gain),
        row_of(norm1_shift),
        row_of(norm2_shift),
        row_of(out_bias),
        row_of(fc1_bias),
        row_of(fc2_bias),
        bias_three(qv_bias),
    )
    keep_half, send_half, pair_nat = at[1:2], at[2:3], at[1:3]
    far_small = token_recv[half_rows:].reshape(-1)
    far_bias = bias_three(far_small[: 2 * heads_width].reshape(2, heads_width))
    far_fc1_bias = row_of(far_small[2 * heads_width : 2 * heads_width + units])

    qkv_x = over_x(qkv_send)
    rows, normed_one, own_heads = project_own(
        at[:1], tokens, token_recv, lead, gain_one, shift_one, own_qkv, own_bias, chunk
    )
    own_heads, qkv_x, out_send, fc1_send, far_bias, far_fc1_bias = hold(
        own_heads, qkv_x, out_send, fc1_send, far_bias, far_fc1_bias
    )

    qkv_y = over(1, qkv_x)
    out_x = over_x(out_send)
    fc1_x = over_x(fc1_send)
    own_attended, own_powers, own_inverse = attend(own_heads)
    own_attended, qkv_x, qkv_y, out_x = hold(own_attended, qkv_x, qkv_y, out_x)

    far_qkv = [qkv_x, qkv_y, over(0, qkv_x), over(0, qkv_y)]
    far_out = [out_x, over(0, out_x)]
    far_heads = project_far(shared_nat, normed_one, far_bias, far_qkv)
    far_heads, fc1_x, cot_send = hold(far_heads, fc1_x, cot_send)

    fc1_y = over(1, fc1_x)
    cot_recv = over_x(cot_send)
    far_attended, far_powers, far_inverse = attend(far_heads)
    middle, normed_two = middle_layer(
        pair_nat, own_attended, far_attended, w_out, far_out, rows, lead,
        out_row, gain_two, shift_two, chunk,
    )
    normed_two, fc1_x, fc1_y, cot_recv, fc2_send = hold(
        normed_two, fc1_x, fc1_y, cot_recv, fc2_send
    )

    def mine_y(flags):
        return flags[3]

    def theirs_y(flags):
        return flags[4]

    def mine_z(flags):
        return flags[5]

    def theirs_z(flags):
        return 1 - flags[5]

    def zero(_):
        return 0

    def one(_):
        return 1

    def first_y(own_down, far_down):
        size = own_down.shape[0] // 2
        return (2 * size, own_down.shape[1]), [
            (None, 0, [term(own_down, theirs_y, size)]),
            (None, size, [term(far_down, theirs_y, size)]),
        ]

    def second_y(own_up, recv_x):
        size = own_up.shape[0] // 2
        return summed((size, own_up.shape[1]), term(own_up, theirs_y, size), term(recv_x, theirs_y, size))

    def second_x(far_down, recv_y):
        size = far_down.shape[0] // 2
        return summed((size, far_down.shape[1]), term(far_down, mine_y, size), term(recv_y, one, size))

    def z_half(which, own_up, recv_x, recv_up, own_down, recv_y, recv_down):
        size = own_up.shape[0] // 4

        def within(side_of, start=0):
            return lambda flags: (start + side_of(flags)) * 2 + which(flags)

        upper = [term(own_up, within(mine_y), size), term(recv_x, within(mine_y), size), term(recv_up, which, size)]
        lower = [term(own_down, within(mine_y), size), term(recv_y, within(zero), size), term(recv_down, which, size)]
        return (2, size, own_up.shape[1]), [(0, None, upper), (1, None, lower)]

    def z_sides(mine, recv):
        shape = list(mine.shape)
        shape[-2] *= 2
        return tuple(shape), [(None, mine_z, [term(mine)]), (None, theirs_z, [term(recv)])]

    def y_sides(mine, recv):
        shape = list(mine.shape)
        shape[-2] *= 2
        return tuple(shape), [(None, mine_y, [term(mine)]), (None, theirs_y, [term(recv)])]

    masks = {1: 8, 2: 4, 3: 12}

    def quarter_z(k):
        def index(flags):
            first = 1 - flags[5] if k & 2 else flags[5]
            second = 1 - flags[6] if k & 1 else flags[6]
            return first * 2 + second

        return index

    fc2_x = over_x(fc2_send)
    far_fc1 = [fc1_x, fc1_y, over(0, fc1_x), over(0, fc1_y)]
    cot_rows = jnp.concatenate([part(cotangent, mp_at, 2)[0], cot_recv])
    grad_low = (cot_rows.astype(F32) * loss_weight).astype(BF16)
    own_hidden, own_slope = hidden_layer(shared_nat, normed_two, fc1_row, [w_fc1], chunk)
    far_hidden, far_slope = hidden_layer(shared_nat, normed_two, far_fc1_bias, far_fc1, chunk)
    far_send = grad_right_half(send_half, far_hidden, grad_low)
    own_send = grad_right_half(send_half, own_hidden, grad_low)
    own_pre, own_fc1_bias = pre_grad_own(grad_low, w_fc2, own_slope)
    fc1_own_send = grad_left_half(send_half, normed_two, own_pre)
    far_send, own_send, fc2_x, grad_low, far_hidden, own_pre, fc1_own_send = hold(
        far_send, own_send, fc2_x, grad_low, far_hidden, own_pre, fc1_own_send
    )

    far_recv, own_recv, fc2_core, fc1_own_recv = over(0, far_send), over(0, own_send), over(0, fc2_x), over(0, fc1_own_send)
    far_up, far_down = grad_right_half(keep_half, far_hidden, grad_low, far_recv)
    own_up, own_down = grad_right_half(keep_half, own_hidden, grad_low, own_recv)
    far_up, far_down, own_up, own_down, fc2_core, fc1_own_recv = hold(
        far_up, far_down, own_up, own_down, fc2_core, fc1_own_recv
    )

    half_width = width // 2
    fc2_x1 = over_x(far_up)
    fc2_y1 = over(1, combine(at, first_y(own_down, far_down))[0])
    far_fc2 = [fc2_x, fc2_core]
    far_pre, far_fc1_bias_sum = pre_grad_far(pair_nat, grad_low, far_fc2, far_slope)
    fc1_far_send = grad_left_half(send_half, normed_two, far_pre)
    fc1_own_up, fc1_own_down = grad_left_half(keep_half, normed_two, own_pre, fc1_own_recv, split=True)
    mlp_own = output_own(own_hidden, w_fc2, chunk)
    fc1_far_send, fc1_own_up, fc1_own_down, fc2_x1, fc2_y1, far_pre, mlp_own = hold(
        fc1_far_send, fc1_own_up, fc1_own_down, fc2_x1, fc2_y1, far_pre, mlp_own
    )

    send_y, send_x = combine(at, second_y(own_up, fc2_x1), second_x(far_down, fc2_y1))
    fc2_y2, fc2_x2 = over(1, send_y), over_x(send_x)
    fc1_far_recv = over(0, fc1_far_send)
    grad_middle, grad_branch, sums_two = middle_grad(
        shared_nat, at[:1], own_pre, far_pre, w_fc1, far_fc1, middle, cotangent, cot_recv, loss_row, gain_two, chunk
    )
    own_grad_att, far_grad_att = attended_grad(pair_nat, grad_branch, w_out, far_out, chunk)
    out_far_send = grad_left_half(send_half, grad_branch, far_attended)
    out_own_send = grad_left_half(send_half, grad_branch, own_attended)
    fc1_far_up, fc1_far_down = grad_left_half(keep_half, normed_two, far_pre, fc1_far_recv, split=True)
    out_far_recv, out_own_recv = over(0, out_far_send), over(0, out_own_send)
    out_far_sum = grad_left_half(keep_half, grad_branch, far_attended, out_far_recv)
    out_own_sum = grad_left_half(keep_half, grad_branch, own_attended, out_own_recv)
    far_grad_att, own_grad_att, fc2_y2, fc2_x2, fc1_far_up, fc1_far_down, out_far_sum, out_own_sum = hold(
        far_grad_att, own_grad_att, fc2_y2, fc2_x2, fc1_far_up, fc1_far_down, out_far_sum, out_own_sum
    )

    fc2_terms = (own_up, fc2_x1, fc2_y2, own_down, fc2_y1, fc2_x2)
    fc2_send, fc2_mine, send_y = combine(
        at, z_half(theirs_z, *fc2_terms), z_half(mine_z, *fc2_terms), first_y(fc1_own_down, fc1_far_down)
    )
    fc1_x1, fc1_y1, fc2_recv = over_x(fc1_far_up), over(1, send_y), over(2, fc2_send)
    pairs = heads_width // (2 * HD)
    far_dqkv = attend_back(0, pairs, far_heads, far_powers, far_inverse, far_attended, far_grad_att)
    far_dqkv, own_grad_att, fc1_x1, fc1_y1, out_far_sum, fc2_recv = hold(
        far_dqkv, own_grad_att, fc1_x1, fc1_y1, out_far_sum, fc2_recv
    )

    half_rows_out = half_width // 2
    out_shape = (half_rows_out, heads_width)
    send_y, send_x, fc2_mine = combine(
        at,
        second_y(fc1_own_up, fc1_x1),
        second_x(fc1_far_down, fc1_y1),
        summed(fc2_mine.shape, term(fc2_mine), term(fc2_recv)),
    )
    fc1_y2, fc1_x2, fc2_recv, out_recv = over(1, send_y), over_x(send_x), over(3, fc2_mine), over_x(out_far_sum)
    qkv_far_recv = over(0, grad_left_half(send_half, normed_one, far_dqkv))
    qkv_far_keep = grad_left_half(keep_half, normed_one, far_dqkv)
    own_a = attend_back(0, pairs // 2, own_heads, own_powers, own_inverse, own_attended, own_grad_att)
    own_a_send = grad_left_half(send_half, normed_one, own_a)
    own_a_send, own_grad_att, fc1_y2, fc1_x2, out_recv, qkv_far_recv, qkv_far_keep, fc2_recv = hold(
        own_a_send, own_grad_att, fc1_y2, fc1_x2, out_recv, qkv_far_recv, qkv_far_keep, fc2_recv
    )

    side_a = heads_width // 2
    own_a_recv = over(0, own_a_send)
    fc1_terms = (fc1_own_up, fc1_x1, fc1_y2, fc1_own_down, fc1_y1, fc1_x2)
    qkv_send, fc1_send, fc1_mine, fc2_mine, out_send = combine(
        at,
        summed((3, half_width, side_a), term(qkv_far_keep, column=0), term(qkv_far_recv, column=0)),
        z_half(theirs_z, *fc1_terms),
        z_half(mine_z, *fc1_terms),
        summed(fc2_mine.shape, term(fc2_mine), term(fc2_recv)),
        summed(out_shape, term(out_own_sum, theirs_y, half_rows_out), term(out_recv, theirs_y, half_rows_out)),
    )
    qkv_first, fc1_recv, fc2_recv, out_y = over_x(qkv_send), over(2, fc1_send), over(2, fc2_mine), over(1, out_send)
    own_b = attend_back(pairs // 2, pairs - pairs // 2, own_heads, own_powers, own_inverse, own_attended, own_grad_att)
    own_a_sum = grad_left_half(keep_half, normed_one, own_a, own_a_recv)
    own_b_send = grad_left_half(send_half, normed_one, own_b)
    own_b, own_b_send, own_a_sum, fc2_recv, out_y, qkv_first, qkv_far_keep, qkv_far_recv, fc1_recv = hold(
        own_b, own_b_send, own_a_sum, fc2_recv, out_y, qkv_first, qkv_far_keep, qkv_far_recv, fc1_recv
    )

    own_b_recv = over(0, own_b_send)
    a_shape = (3, half_rows_out, side_a)
    qkv_send, fc1_mine, a_send, out_mine, fc2_mine = combine(
        at,
        summed((3, half_width, side_a), term(qkv_far_keep, column=1), term(qkv_far_recv, column=1)),
        summed(fc1_mine.shape, term(fc1_mine), term(fc1_recv)),
        summed(a_shape, term(own_a_sum, theirs_y, half_rows_out), term(qkv_first, theirs_y, half_rows_out)),
        summed(
            out_shape,
            term(out_own_sum, mine_y, half_rows_out),
            term(out_recv, mine_y, half_rows_out),
            term(out_y),
        ),
        z_sides(fc2_mine, fc2_recv),
    )
    qkv_second, fc1_recv, a_y, out_z = over_x(qkv_send), over(3, fc1_mine), over(1, a_send), over(2, out_mine)
    grad_shifted, grad_send, sums_one = input_grads(
        shared_nat, [own_a, own_b], far_dqkv, own_qkv, far_qkv, rows, lead, grad_middle, gain_one, chunk
    )
    own_b_sum = grad_left_half(keep_half, normed_one, own_b, own_b_recv)
    grad_shifted, grad_send, sums_one, a_y, qkv_second, own_b_sum, out_z, fc2_mine, fc1_recv, far_hidden = hold(
        grad_shifted, grad_send, sums_one, a_y, qkv_second, own_b_sum, out_z, fc2_mine, fc1_recv, far_hidden
    )

    b_send, fc1_mine, out_mine = combine(
        at,
        summed(a_shape, term(own_b_sum, theirs_y, half_rows_out), term(qkv_second, theirs_y, half_rows_out)),
        summed(fc1_mine.shape, term(fc1_mine), term(fc1_recv)),
        summed(out_shape, term(out_mine), term(out_z)),
    )
    b_y, fc1_recv, out_z = over(1, b_send), over(2, fc1_mine), over(3, out_mine)
    grad_recv = over_x(grad_send)
    chunks = half_rows // chunk
    output_low = output_layer(pair_nat, chunks, chunks, far_hidden, mlp_own, far_fc2, middle, fc2_row, chunk)
    vectors = pack_vectors(at, counts.shape[0], sums_one, sums_two, own_fc1_bias, far_fc1_bias_sum)
    vectors_recv = over(1, vectors)
    b_y, vectors_recv, fc1_mine, fc1_recv, out_mine, out_z, output_low, far_hidden, fc2_mine = hold(
        b_y, vectors_recv, fc1_mine, fc1_recv, out_mine, out_z, output_low, far_hidden, fc2_mine
    )

    z_rows = half_rows_out // 4

    def qkv_quarter(k):
        def within(flags):
            return mine_y(flags) * 4 + quarter_z(k)(flags)

        parts = [
            (side_k, None, [term(total, within, z_rows), term(recv, within, z_rows), term(recv_y, quarter_z(k), z_rows)])
            for side_k, (total, recv, recv_y) in enumerate(((own_a_sum, qkv_first, a_y), (own_b_sum, qkv_second, b_y)))
        ]
        return (2, 3, z_rows, side_a), parts

    *qkv_sends, qkv_mine, fc1_mine, out_mine = combine(
        at,
        *[qkv_quarter(k) for k in masks],
        qkv_quarter(0),
        z_sides(fc1_mine, fc1_recv),
        summed(out_shape, term(out_mine), term(out_z)),
    )
    qkv_recv = [over_mask(mask, sent) for mask, sent in zip(masks.values(), qkv_sends)]
    fc2_y = over(1, fc2_mine)
    vectors = vectors + vectors_recv
    vectors_recv = over(2, vectors)
    output_high = output_layer(pair_nat, 0, chunks, far_hidden, mlp_own, far_fc2, middle, fc2_row, chunk)
    output_high, output_low, grad_recv, vectors_recv, fc1_mine, out_mine, fc2_mine, fc2_y, *qkv_recv = hold(
        output_high, output_low, grad_recv, vectors_recv, fc1_mine, out_mine, fc2_mine, fc2_y, *qkv_recv
    )

    qkv_mine, fc2_half = combine(
        at, summed(qkv_mine.shape, *[term(v) for v in (qkv_mine, *qkv_recv)]), y_sides(fc2_mine, fc2_y)
    )
    qkv_parts = [qkv_mine] + [over_mask(mask, qkv_mine) for mask in masks.values()]
    fc1_y = over(1, fc1_mine)
    output_recv = over_x(output_low)
    vectors = vectors + vectors_recv
    vectors, fc1_y, fc2_half, out_mine, grad_recv, output_recv, *qkv_parts = hold(
        vectors, fc1_y, fc2_half, out_mine, grad_recv, output_recv, *qkv_parts
    )

    qkv_mine, fc1_half = combine(
        at,
        (
            (2, 3, half_rows_out, side_a),
            [(None, quarter_z(k), [term(v)]) for k, v in zip((0, *masks), qkv_parts)],
        ),
        y_sides(fc1_mine, fc1_y),
    )
    qkv_y, qkv_core = over(1, qkv_mine), over(0, qkv_mine)
    fc1_core, fc2_core = over(0, fc1_half), over(0, fc2_half)
    vectors_recv = over_x(vectors)
    input_grad = joined(mp_at, grad_shifted[None, :half_rows], grad_recv[None].astype(F32))
    fc2_grad = finish_columns(pair_nat, [fc2_half, fc2_core])
    fc1_grad = finish_rows(pair_nat, [fc1_half, fc1_core])
    qkv_mine, qkv_y, qkv_core, vectors_recv, fc1_grad, fc2_grad, out_mine, input_grad = hold(
        qkv_mine, qkv_y, qkv_core, vectors_recv, fc1_grad, fc2_grad, out_mine, input_grad
    )

    qkv_last = over(0, qkv_y)
    out_y, out_core = over(1, out_mine), over(0, out_mine)
    qkv_grad = finish_stack(core_first_nat, 0, [qkv_mine, qkv_core, qkv_y])
    block_output = joined(mp_at, output_high[None], output_recv[None])
    vectors = vectors + vectors_recv
    vectors_recv = over(3, vectors)
    qkv_last, qkv_grad, vectors_recv, out_y, out_core, block_output = hold(
        qkv_last, qkv_grad, vectors_recv, out_y, out_core, block_output
    )

    vectors = vectors + vectors_recv
    vectors = vectors + over(0, vectors)
    out_grad = finish_turned(core_first_nat, [out_mine, out_core, out_y, over(0, out_y)])
    qkv_grad = finish_stack(core_first_nat, 3, [qkv_last], qkv_grad)
    qkv_grad = jnp.transpose(qkv_grad, (1, 0, 2))

    table = counts.shape[0]
    lead_grad, singles, rest = vectors[:table], vectors[table : table + 6], vectors[table + 6 :]
    qv_bias_grad = part(rest[:2], mp_at, 2, 1)
    fc1_bias_grad = part(rest[2:].reshape(-1), mp_at, 2)
    return (
        block_output,
        input_grad,
        lead_grad,
        singles[0],
        singles[1],
        qkv_grad,
        qv_bias_grad,
        out_grad,
        singles[4],
        singles[2],
        singles[3],
        fc1_grad,
        fc1_bias_grad,
        fc2_grad,
        singles[5],
    )


def solution(mesh):
    in_specs = (
        P("dp", "mp", None),
        P("dp", "mp", None),
        P("dp"),
        P(),
        P(),
        P(),
        P(),
        P(None, None, "mp"),
        P(None, "mp"),
        P("mp", None),
        P(),
        P(),
        P(),
        P(None, "mp"),
        P("mp"),
        P("mp", None),
        P(),
    )
    out_specs = (
        P("dp", "mp", None),
        P("dp", "mp", None),
        P(),
        P(),
        P(),
        P(None, None, "mp"),
        P(None, "mp"),
        P("mp", None),
        P(),
        P(),
        P(),
        P(None, "mp"),
        P("mp"),
        P("mp", None),
        P(),
    )
    def local(*args):
        replicas = lax.axis_size("dp")
        samples, half_rows, width = args[0].shape
        heads_width, units = args[7].shape[2], args[13].shape[1]
        fits = samples == 2 and lax.axis_size("mp") == 2 and replicas == 16
        even = half_rows % 256 == 0 and width == 2 * heads_width == 1024 and units == 2 * width
        return (fast_body if fits and even else body)(*args)

    return jax.shard_map(local, mesh=mesh, in_specs=in_specs, out_specs=out_specs, check_vma=False)
```

```python
import functools
import math

import jax
import jax.numpy as jnp
from jax import lax
from jax.experimental import pallas as pl
from jax.experimental.pallas import tpu as pltpu
from jax.sharding import PartitionSpec as P

HD = 64


EPS = 1e-05


def norm_forward(values, norm_gain, norm_shift):
    center = values - jnp.mean(values, axis=-1, keepdims=True)
    inverse = lax.rsqrt(jnp.mean(center * center, axis=-1, keepdims=True) + EPS)
    scaled = center * inverse
    return (scaled * norm_gain + norm_shift, scaled, inverse)


def norm_backward(grad_out, scaled, inverse, norm_gain):
    grad_scaled = grad_out * norm_gain
    grad_mean = jnp.mean(grad_scaled, axis=-1, keepdims=True)
    cross_mean = jnp.mean(grad_scaled * scaled, axis=-1, keepdims=True)
    grad_in = inverse * (grad_scaled - grad_mean - scaled * cross_mean)
    gain_grad = jnp.sum(grad_out * scaled, axis=(0, 1))
    shift_grad = jnp.sum(grad_out, axis=(0, 1))
    return (grad_in, gain_grad, shift_grad)


def gelu_slope(pre_act):
    normal_cdf = 0.5 * (1.0 + lax.erf(pre_act * 0.7071067811865476))
    return normal_cdf + pre_act * jnp.exp(-0.5 * pre_act * pre_act) * 0.3989422804014327


def attention_forward(query_all, key_all, value_all, block_rows):
    block_count = query_all.shape[0] // block_rows
    query_blocks = query_all.reshape((block_count, block_rows) + query_all.shape[1:])

    def one_block(query_block):
        scores = (
            jnp.einsum("qshd,kshd->shqk", query_block, key_all, preferred_element_type=jnp.float32)
            * 0.125
        )
        row_max = jnp.max(scores, axis=-1, keepdims=True)
        powers = jnp.exp(scores - row_max)
        exp_total = jnp.sum(powers, axis=-1, keepdims=True)
        attn_weights = (powers / exp_total).astype(jnp.bfloat16)
        attended = jnp.einsum(
            "shqk,kshd->qshd", attn_weights, value_all, preferred_element_type=jnp.float32
        )
        return (attended.astype(jnp.bfloat16), (row_max + jnp.log(exp_total))[..., 0])

    attended, log_total = lax.map(one_block, query_blocks)
    return (attended.reshape(query_all.shape), log_total)


def attention_backward(query_all, key_all, value_all, grad_attended, log_total, block_rows):
    block_count = query_all.shape[0] // block_rows
    query_blocks = query_all.reshape((block_count, block_rows) + query_all.shape[1:])
    grad_blocks = grad_attended.reshape((block_count, block_rows) + query_all.shape[1:])

    def one_block(running, sliced):
        key_grad, value_grad = running
        query_block, grad_block, log_block = sliced
        scores = (
            jnp.einsum("qshd,kshd->shqk", query_block, key_all, preferred_element_type=jnp.float32)
            * 0.125
        )
        attn_weights = jnp.exp(scores - log_block[..., None])
        weight_low = attn_weights.astype(jnp.bfloat16)
        grad_weights = jnp.einsum(
            "qshd,kshd->shqk", grad_block, value_all, preferred_element_type=jnp.float32
        )
        inner = jnp.sum(attn_weights * grad_weights, axis=-1, keepdims=True)
        grad_scores = (attn_weights * (grad_weights - inner)).astype(jnp.bfloat16)
        query_grad = (
            jnp.einsum("shqk,kshd->qshd", grad_scores, key_all, preferred_element_type=jnp.float32)
            * 0.125
        )
        key_grad = (
            key_grad
            + jnp.einsum(
                "shqk,qshd->kshd", grad_scores, query_block, preferred_element_type=jnp.float32
            )
            * 0.125
        )
        value_grad = value_grad + jnp.einsum(
            "shqk,qshd->kshd", weight_low, grad_block, preferred_element_type=jnp.float32
        )
        return ((key_grad, value_grad), query_grad.astype(jnp.bfloat16))

    zero_grad = jnp.zeros(key_all.shape, jnp.float32)
    (key_grad, value_grad), query_grad = lax.scan(
        one_block, (zero_grad, zero_grad), (query_blocks, grad_blocks, log_total)
    )
    return (
        query_grad.reshape(query_all.shape),
        key_grad.astype(jnp.bfloat16),
        value_grad.astype(jnp.bfloat16),
    )


def body(
    tokens,
    cotangent,
    buckets,
    counts,
    lead_table,
    norm1_gain,
    norm1_shift,
    w_qkv,
    qv_bias,
    w_out,
    out_bias,
    norm2_gain,
    norm2_shift,
    w_fc1,
    fc1_bias,
    w_fc2,
    fc2_bias,
):
    samples_here = tokens.shape[0]
    local_rows = tokens.shape[1]
    local_width = w_qkv.shape[2]
    local_heads = local_width // HD
    seq_len = local_rows * lax.axis_size("mp")
    block_rows = min(512, seq_len)
    head_shape = (seq_len, samples_here, local_heads, HD)
    count_f = counts.astype(jnp.float32)
    onehot = (buckets[:, None] == jnp.arange(counts.shape[0], dtype=jnp.int32)[None, :]).astype(
        jnp.float32
    )
    loss_weight = jnp.mean(count_f) / jnp.sum(onehot * count_f[None, :], axis=1)
    lead_rows = jnp.dot(
        onehot,
        lead_table.astype(jnp.float32),
        precision=lax.Precision.HIGHEST,
        preferred_element_type=jnp.float32,
    )
    shifted = jnp.swapaxes(tokens, 0, 1).astype(jnp.float32) + lead_rows[None]
    normed_one, scaled_one, inverse_one = norm_forward(
        shifted, norm1_gain.astype(jnp.float32), norm1_shift.astype(jnp.float32)
    )
    normed_one = normed_one.astype(jnp.bfloat16)
    normed_full = lax.all_gather(normed_one, "mp", axis=0, tiled=True)
    project = jnp.einsum("tsd,dcf->tscf", normed_full, w_qkv, preferred_element_type=jnp.float32)
    bias_f = qv_bias.astype(jnp.float32)
    query_all = (project[:, :, 0] + bias_f[0]).astype(jnp.bfloat16).reshape(head_shape)
    key_all = project[:, :, 1].astype(jnp.bfloat16).reshape(head_shape)
    value_all = (project[:, :, 2] + bias_f[1]).astype(jnp.bfloat16).reshape(head_shape)
    attended, log_total = attention_forward(query_all, key_all, value_all, block_rows)
    attended_flat = attended.reshape(seq_len, samples_here, local_width)
    picked = attended_flat
    branch = lax.psum_scatter(
        jnp.einsum("tsf,fd->tsd", picked, w_out, preferred_element_type=jnp.float32),
        "mp",
        scatter_dimension=0,
        tiled=True,
    )
    middle = shifted + branch + out_bias.astype(jnp.float32)
    gain_two = norm2_gain.astype(jnp.float32)
    normed_two, scaled_two, inverse_two = norm_forward(
        middle, gain_two, norm2_shift.astype(jnp.float32)
    )
    normed_two = normed_two.astype(jnp.bfloat16)
    grad_top = jnp.swapaxes(cotangent, 0, 1).astype(jnp.float32) * loss_weight[None, :, None]
    grad_low = grad_top.astype(jnp.bfloat16)
    fc1_full, fc1_bias_full, fc2_full = (
        lax.all_gather(w_fc1, "mp", axis=1, tiled=True),
        lax.all_gather(fc1_bias, "mp", axis=0, tiled=True),
        lax.all_gather(w_fc2, "mp", axis=0, tiled=True),
    )
    pre_act = jnp.einsum(
        "tsd,df->tsf", normed_two, fc1_full, preferred_element_type=jnp.float32
    ) + fc1_bias_full.astype(jnp.float32)
    hidden = jax.nn.gelu(pre_act, approximate=False).astype(jnp.bfloat16)
    mlp_branch = jnp.einsum("tsf,fd->tsd", hidden, fc2_full, preferred_element_type=jnp.float32)
    output = middle + mlp_branch + fc2_bias.astype(jnp.float32)
    grad_hidden = jnp.einsum("tsd,fd->tsf", grad_low, fc2_full, preferred_element_type=jnp.float32)
    grad_pre = (grad_hidden * gelu_slope(pre_act)).astype(jnp.bfloat16)
    grad_normed_two = jnp.einsum(
        "tsf,df->tsd", grad_pre, fc1_full, preferred_element_type=jnp.float32
    )
    fc1_part = jnp.einsum("tsd,tsf->df", normed_two, grad_pre, preferred_element_type=jnp.float32)
    fc1_bias_part = jnp.sum(grad_pre.astype(jnp.float32), axis=(0, 1))
    fc2_part = jnp.einsum("tsf,tsd->fd", hidden, grad_low, preferred_element_type=jnp.float32)
    fc1_grad, fc1_bias_grad, fc2_grad = (
        lax.psum_scatter(
            fc1_part.astype(jnp.bfloat16), "mp", scatter_dimension=1, tiled=True
        ).astype(jnp.float32),
        lax.psum_scatter(
            fc1_bias_part.astype(jnp.bfloat16), "mp", scatter_dimension=0, tiled=True
        ).astype(jnp.float32),
        lax.psum_scatter(
            fc2_part.astype(jnp.bfloat16), "mp", scatter_dimension=0, tiled=True
        ).astype(jnp.float32),
    )
    fc2_bias_grad = jnp.sum(grad_top, axis=(0, 1))
    grad_from_norm, gain_two_grad, shift_two_grad = norm_backward(
        grad_normed_two, scaled_two, inverse_two, gain_two
    )
    grad_middle = grad_top + grad_from_norm
    out_bias_grad = jnp.sum(grad_middle, axis=(0, 1))
    grad_branch = grad_middle.astype(jnp.bfloat16)
    grad_branch_full = lax.all_gather(grad_branch, "mp", axis=0, tiled=True)
    out_grad = jnp.einsum(
        "tsf,tsd->fd", attended_flat, grad_branch_full, preferred_element_type=jnp.float32
    )
    grad_attended = jnp.einsum(
        "tsd,fd->tsf", grad_branch_full, w_out, preferred_element_type=jnp.float32
    ).astype(jnp.bfloat16)
    query_grad, key_grad, value_grad = attention_backward(
        query_all, key_all, value_all, grad_attended.reshape(head_shape), log_total, block_rows
    )
    grad_project = jnp.stack([query_grad, key_grad, value_grad], axis=2).reshape(
        seq_len, samples_here, 3, local_width
    )
    qkv_grad = jnp.einsum(
        "tsd,tscf->dcf", normed_full, grad_project, preferred_element_type=jnp.float32
    )
    query_bias_grad = jnp.sum(query_grad.astype(jnp.float32), axis=(0, 1)).reshape(local_width)
    value_bias_grad = jnp.sum(value_grad.astype(jnp.float32), axis=(0, 1)).reshape(local_width)
    qv_bias_grad = jnp.stack([query_bias_grad, value_bias_grad])
    picked = grad_project
    grad_normed_one = lax.psum_scatter(
        jnp.einsum("tscf,dcf->tsd", picked, w_qkv, preferred_element_type=jnp.float32).astype(
            jnp.bfloat16
        ),
        "mp",
        scatter_dimension=0,
        tiled=True,
    ).astype(jnp.float32)
    grad_in_one, gain_one_grad, shift_one_grad = norm_backward(
        grad_normed_one, scaled_one, inverse_one, norm1_gain.astype(jnp.float32)
    )
    grad_shifted = grad_middle + grad_in_one
    lead_grad = jnp.dot(
        onehot.T,
        jnp.sum(grad_shifted, axis=0),
        precision=lax.Precision.HIGHEST,
        preferred_element_type=jnp.float32,
    )
    small_grads = jnp.stack(
        [gain_one_grad, shift_one_grad, out_bias_grad, gain_two_grad, shift_two_grad, fc2_bias_grad]
    )
    lead_grad, small_grads = lax.psum((lead_grad, small_grads), ("dp", "mp"))
    qkv_grad, qv_bias_grad, out_grad, fc1_grad, fc1_bias_grad, fc2_grad = (
        lax.psum(qkv_grad.astype(jnp.bfloat16), "dp").astype(jnp.float32),
        lax.psum(qv_bias_grad.astype(jnp.bfloat16), "dp").astype(jnp.float32),
        lax.psum(out_grad.astype(jnp.bfloat16), "dp").astype(jnp.float32),
        lax.psum(fc1_grad.astype(jnp.bfloat16), "dp").astype(jnp.float32),
        lax.psum(fc1_bias_grad.astype(jnp.bfloat16), "dp").astype(jnp.float32),
        lax.psum(fc2_grad.astype(jnp.bfloat16), "dp").astype(jnp.float32),
    )
    block_output = jnp.swapaxes(output, 0, 1).astype(jnp.bfloat16)
    input_grad = jnp.swapaxes(grad_shifted, 0, 1)
    return (
        block_output,
        input_grad,
        lead_grad,
        small_grads[0],
        small_grads[1],
        qkv_grad,
        qv_bias_grad,
        out_grad,
        small_grads[2],
        small_grads[3],
        small_grads[4],
        fc1_grad,
        fc1_bias_grad,
        fc2_grad,
        small_grads[5],
    )


F32 = jnp.float32
BF16 = jnp.bfloat16
NN = (((1,), (0,)), ((), ()))
NT = (((1,), (1,)), ((), ()))
TN = (((0,), (0,)), ((), ()))
MIB = 1 << 20


def dot(left, right, dims):
    return lax.dot_general(left, right, dims, preferred_element_type=F32)


def whole(array):
    return pl.BlockSpec(array.shape, lambda *_: (0,) * array.ndim, pipeline_mode=pl.Buffered(1))


def kernel_call(body, name, grid, scalars, ins, outs, scratch=(), vmem=32, time=6, pinned=(), alias=None):
    spec = pltpu.PrefetchScalarGridSpec(
        num_scalar_prefetch=len(scalars),
        grid=grid,
        in_specs=[spec for _, spec in ins],
        out_specs=[spec for _, spec in outs],
        scratch_shapes=list(scratch),
    )
    return pl.pallas_call(
        body,
        out_shape=[shape for shape, _ in outs],
        grid_spec=spec,
        compiler_params=pltpu.CompilerParams(vmem_limit_bytes=vmem * MIB),
        input_output_aliases={} if alias is None else {len(scalars) + alias: 0},
        cost_estimate=pl.CostEstimate(flops=MIB, transcendentals=0, bytes_accessed=int(time * 2 * MIB)),
        name=name,
    )(
        *scalars,
        *[
            pltpu.with_memory_space_constraint(array, pltpu.HBM) if k in pinned else array
            for k, (array, _) in enumerate(ins)
        ],
    )


def struct(shape, dtype=BF16):
    return jax.ShapeDtypeStruct(shape, dtype)


def centred(values):
    center = values - jnp.mean(values, axis=-1, keepdims=True)
    inverse = lax.rsqrt(jnp.mean(center * center, axis=-1, keepdims=True) + EPS)
    return center * inverse, inverse


def norm_input_grad(grad_out, scaled, inverse, gain):
    grad_scaled = grad_out * gain
    grad_mean = jnp.mean(grad_scaled, axis=-1, keepdims=True)
    cross_mean = jnp.mean(grad_scaled * scaled, axis=-1, keepdims=True)
    return inverse * (grad_scaled - grad_mean - scaled * cross_mean)


def column_sum(values):
    return jnp.sum(values, axis=0, keepdims=True)


def chunk_of(nat_ref, index, size):
    return pl.ds(pl.multiple_of(nat_ref[index] * size, size), size)


def attention_forward_kernel(block, qkv_ref, out_ref, power_ref, inverse_ref):
    rows_all = qkv_ref.shape[1]
    steps = [(head, start) for head in range(2) for start in range(0, rows_all, block)]

    def scores_of(head, start):
        lanes = slice(HD * head, HD * head + HD)
        query = qkv_ref[0, start : start + block, lanes] * BF16(0.125)
        return dot(qkv_ref[1, :, lanes], query, NT)

    outs = [[], []]
    ahead = scores_of(*steps[0])
    for k, (head, start) in enumerate(steps):
        scores = ahead
        if k + 1 < len(steps):
            ahead = scores_of(*steps[k + 1])
        lanes = slice(HD * head, HD * head + HD)
        rows = slice(start, start + block)
        powers = jnp.exp2((scores - jnp.max(scores, axis=0, keepdims=True)) * 1.4426950408889634)
        inverse = 1.0 / jnp.sum(powers, axis=0, keepdims=True)
        power_low = powers.astype(BF16)
        power_ref[head, :, rows] = power_low
        inverse_ref[0, head : head + 1, rows] = inverse
        outs[head].append(dot(qkv_ref[2, :, lanes], power_low, TN) * inverse)
    heads = [jnp.concatenate(parts, axis=1) for parts in outs]
    out_ref[...] = jnp.concatenate(heads, axis=0).T.astype(BF16)


def attend(qkv):
    _, rows, width = qkv.shape
    pairs = width // (2 * HD)
    return kernel_call(
        functools.partial(attention_forward_kernel, min(512, rows)),
        "attention_forward",
        (pairs,),
        [],
        [(qkv, pl.BlockSpec((3, rows, 2 * HD), lambda j: (0, 0, j)))],
        [
            (struct((rows, width)), pl.BlockSpec((rows, 2 * HD), lambda j: (0, j))),
            (pltpu.HBM((2 * pairs, rows, rows), BF16), pl.BlockSpec((2, rows, rows), lambda j: (j, 0, 0))),
            (struct((pairs, 2, rows), F32), pl.BlockSpec((1, 2, rows), lambda j: (j, 0, 0))),
        ],
        vmem=48,
        time=4 * pairs,
        pinned=[0],
    )


def attention_backward_kernel(block, qkv_ref, power_ref, inverse_ref, out_ref, grad_ref, dqkv_ref, sums_ref):
    rows_all = qkv_ref.shape[1]
    out_t = out_ref[...].astype(F32).T
    grad_t = grad_ref[...].astype(F32).T
    for head in range(2):
        lanes = slice(HD * head, HD * head + HD)
        inverse = inverse_ref[0, head : head + 1, :]
        grad_head = grad_t[lanes]
        inner = jnp.sum(grad_head * out_t[lanes], axis=0, keepdims=True) * inverse
        grad_scaled = grad_head * inverse
        grad_low_t = grad_scaled.astype(BF16)
        grad_low = grad_scaled.T.astype(BF16)
        query = qkv_ref[0, :, lanes] * BF16(0.125)
        key = qkv_ref[1, :, lanes]
        value = qkv_ref[2, :, lanes]
        key_t = key.T
        key_grad = value_grad = None
        query_grads = []
        for start in range(0, rows_all, block):
            rows = slice(start, start + block)
            power = power_ref[head, :, rows]
            grad_power = dot(value, grad_low_t[:, rows], NN) - inner[:, rows]
            grad_scores = (power.astype(F32) * grad_power).astype(BF16)
            key_part = dot(grad_scores, query[rows], NN)
            value_part = dot(power, grad_low[rows], NN)
            key_grad = key_part if key_grad is None else key_grad + key_part
            value_grad = value_part if value_grad is None else value_grad + value_part
            query_grads.append(dot(key_t, grad_scores, NN))
        sums_ref[0, :, lanes] = jnp.concatenate(query_grads, axis=1).T * 0.125
        sums_ref[1, :, lanes] = key_grad
        sums_ref[2, :, lanes] = value_grad
    dqkv_ref[...] = sums_ref[...].astype(BF16)


def attend_back(first, count, qkv, powers, inverse, attended, grad_attended):
    _, rows, width = qkv.shape
    block = (3, rows, 2 * HD)
    flat = pl.BlockSpec((rows, 2 * HD), lambda j: (0, j + first))
    return kernel_call(
        functools.partial(attention_backward_kernel, min(512, rows)),
        "attention_backward",
        (count,),
        [],
        [
            (qkv, pl.BlockSpec(block, lambda j: (0, 0, j + first))),
            (powers, pl.BlockSpec((2, rows, rows), lambda j: (j + first, 0, 0))),
            (inverse, pl.BlockSpec((1, 2, rows), lambda j: (j + first, 0, 0))),
            (attended, flat),
            (grad_attended, flat),
        ],
        [(struct((3, rows, 2 * HD * count)), pl.BlockSpec(block, lambda j: (0, 0, j)))],
        [pltpu.VMEM(block, F32)],
        vmem=40,
        time=5.5 * count,
        pinned=range(5),
    )[0]


def project_own_kernel(at_ref, tokens_ref, recv_ref, lead_ref, gain_ref, shift_ref, weight_ref, bias_ref, rows_ref, normed_ref, heads_ref):
    own = pl.program_id(0) < pl.num_programs(0) // 2
    tokens = jnp.where(own, tokens_ref[0].astype(F32), recv_ref[...].astype(F32))
    rows_ref[...] = tokens.astype(BF16)
    scaled, _ = centred(tokens + lead_ref[...])
    normed = (scaled * gain_ref[...] + shift_ref[...]).astype(BF16)
    normed_ref[...] = normed
    for c in range(3):
        heads_ref[c] = (dot(normed, weight_ref[c], NN) + bias_ref[c : c + 1]).astype(BF16)


def project_own(at, tokens, recv, lead, gain, shift, weight, bias, chunk):
    half, width = tokens.shape[1:]
    heads = weight.shape[2]
    steps = half // chunk
    row = pl.BlockSpec((chunk, width), lambda j, at: (j, 0))
    return kernel_call(
        project_own_kernel,
        "project_own",
        (2 * steps,),
        [at],
        [
            (tokens, pl.BlockSpec((1, chunk, width), lambda j, at: (at[0], jnp.minimum(j, steps - 1), 0))),
            (recv, pl.BlockSpec((chunk, width), lambda j, at: (jnp.maximum(j - steps, 0), 0))),
            *[(v, whole(v)) for v in (lead, gain, shift, weight, bias)],
        ],
        [
            (struct((2 * half, width)), row),
            (struct((2 * half, width)), row),
            (struct((3, 2 * half, heads)), pl.BlockSpec((3, chunk, heads), lambda j, at: (0, j, 0))),
        ],
        pinned=[0, 1, 5],
    )


def project_far_kernel(nat_ref, normed_ref, bias_ref, *refs):
    *pieces, heads_ref = refs
    size = pieces[0].shape[1]
    total = bias_ref[0]
    for k, piece in enumerate(pieces):
        total = total + dot(normed_ref[:, chunk_of(nat_ref, k, size)], piece[0], NN)
    heads_ref[0] = total.astype(BF16)


def project_far(nat, normed, bias, pieces):
    rows = normed.shape[0]
    heads = pieces[0].shape[2]
    first = lambda j, nat: (j, 0, 0)
    return kernel_call(
        project_far_kernel,
        "project_far",
        (3,),
        [nat],
        [
            (normed, whole(normed)),
            (bias[:, None], pl.BlockSpec((1, 1, heads), first)),
            *[(p, pl.BlockSpec((1, *p.shape[1:]), first)) for p in pieces],
        ],
        [(struct((3, rows, heads)), pl.BlockSpec((1, rows, heads), first))],
    )[0]


def middle_kernel(nat_ref, own_ref, far_ref, weight_ref, rows_ref, lead_ref, bias_ref, gain_ref, shift_ref, *refs):
    *pieces, middle_ref, normed_ref = refs
    total = dot(own_ref[...], weight_ref[...], NN)
    for k, piece in enumerate(pieces):
        total = total + dot(far_ref[:, chunk_of(nat_ref, k, piece.shape[0])], piece[...], NN)
    middle = rows_ref[...].astype(F32) + lead_ref[...] + total + bias_ref[...]
    middle_ref[...] = middle
    scaled, _ = centred(middle)
    normed_ref[...] = (scaled * gain_ref[...] + shift_ref[...]).astype(BF16)


def middle_layer(nat, own, far, weight, pieces, rows, lead, bias, gain, shift, chunk):
    count, width = rows.shape
    row = pl.BlockSpec((chunk, width), lambda j, nat: (j, 0))
    heads = pl.BlockSpec((chunk, own.shape[1]), lambda j, nat: (j, 0))
    return kernel_call(
        middle_kernel,
        "middle_layer",
        (count // chunk,),
        [nat],
        [(own, heads), (far, heads), (weight, whole(weight)), (rows, row)]
        + [(v, whole(v)) for v in (lead, bias, gain, shift, *pieces)],
        [(pltpu.HBM((count, width), F32), row), (struct((count, width)), row)],
        pinned=[2, 3],
    )


def gelu_store(pre_act, rows, hidden_ref, slope_ref):
    cdf = 0.5 * (1.0 + lax.erf(pre_act * 0.7071067811865476))
    hidden_ref[rows] = (pre_act * cdf).astype(BF16)
    density = jnp.exp(-0.5 * pre_act * pre_act) * 0.3989422804014327
    slope_ref[rows] = (cdf + pre_act * density).astype(BF16)


def hidden_kernel(block, nat_ref, normed_ref, bias_ref, *refs):
    *pieces, hidden_ref, slope_ref = refs
    size = pieces[0].shape[0]
    for start in range(0, normed_ref.shape[0], block):
        rows = slice(start, start + block)
        pre_act = bias_ref[...]
        for k, piece in enumerate(pieces):
            lanes = slice(None) if len(pieces) == 1 else chunk_of(nat_ref, k, size)
            pre_act = pre_act + dot(normed_ref[rows, lanes], piece[...], NN)
        gelu_store(pre_act, rows, hidden_ref, slope_ref)


def hidden_layer(nat, normed, bias, pieces, chunk):
    rows = normed.shape[0]
    units = pieces[0].shape[1]
    tile = min(512, units)
    column = lambda j, nat: (0, j)
    return kernel_call(
        functools.partial(hidden_kernel, chunk),
        "hidden_layer",
        (units // tile,),
        [nat],
        [(normed, whole(normed)), (bias, pl.BlockSpec((1, tile), column))]
        + [(p, pl.BlockSpec((p.shape[0], tile), column)) for p in pieces],
        [(struct((rows, units)), pl.BlockSpec((rows, tile), column))] * 2,
        vmem=24,
        time=10,
        pinned=range(2, 2 + len(pieces)),
    )


def product_kernel(outs, add_count, by_step, _, left_ref, right_ref, *refs):
    adds, out_refs = refs[:add_count], refs[add_count:]
    stacked = len(right_ref.shape) == 3
    value = dot(left_ref[...], right_ref[0] if stacked else right_ref[...], TN)
    for add in adds:
        value = value + (add[0] if stacked else add[...]).astype(F32)
    value = value.astype(BF16)
    if stacked:
        out_refs[0][0] = value
    elif outs == 1:
        out_refs[0][...] = value
    elif by_step:
        for k, out_ref in enumerate(out_refs):

            @pl.when(pl.program_id(0) == k)
            def _(out_ref=out_ref):
                out_ref[...] = value
    else:
        size = value.shape[0] // outs
        for k, out_ref in enumerate(out_refs):
            out_ref[...] = value[k * size : (k + 1) * size]


def grad_right_half(half, left, right, *add):
    rows, columns = left.shape
    kept = right.shape[1] // 2
    tile = columns // 2
    out_spec = pl.BlockSpec((tile, kept), lambda j, half: (j, 0))
    outs = 2 if add else 1
    split = [(struct((tile, kept)), pl.BlockSpec((tile, kept), lambda j, half: (0, 0)))] * 2
    result = kernel_call(
        functools.partial(product_kernel, outs, len(add), True),
        "grad_right_half",
        (2,),
        [half],
        [
            (left, pl.BlockSpec((rows, tile), lambda j, half: (0, j))),
            (right, pl.BlockSpec((rows, kept), lambda j, half: (0, half[0]))),
        ]
        + [(a, out_spec) for a in add],
        split if add else [(struct((columns, kept)), out_spec)],
        vmem=20,
        time=3,
    )
    return result if add else result[0]


def grad_left_half(half, left, right, *add, split=False):
    rows = left.shape[0]
    kept = left.shape[1] // 2
    columns = right.shape[-1]
    tile = min(1024, columns)
    outs = 2 if split else 1
    left_spec = pl.BlockSpec((rows, kept), lambda j, half: (0, half[0]))
    if right.ndim == 3:
        grid, out_shape = (right.shape[0],), (right.shape[0], kept, columns)
        right_spec = pl.BlockSpec((1, rows, columns), lambda j, half: (j, 0, 0))
        add_spec = out_spec = pl.BlockSpec((1, kept, columns), lambda j, half: (j, 0, 0))
    else:
        grid, out_shape = (columns // tile,), (kept // outs, columns)
        right_spec = pl.BlockSpec((rows, tile), lambda j, half: (0, j))
        add_spec = pl.BlockSpec((kept, tile), lambda j, half: (0, j))
        out_spec = pl.BlockSpec((kept // outs, tile), lambda j, half: (0, j))
    result = kernel_call(
        functools.partial(product_kernel, outs, len(add), False),
        "grad_left_half",
        grid,
        [half],
        [(left, left_spec), (right, right_spec)] + [(a, add_spec) for a in add],
        [(struct(out_shape), out_spec)] * outs,
        vmem=20,
        time=3,
    )
    return result if split else result[0]


def term(array, at=None, size=None, column=None):
    block, index = list(array.shape), [None] * array.ndim
    if size is not None:
        block[-2], index[-2] = size, at
    if column is not None:
        block[-1], index[-1] = array.shape[-1] // 2, lambda _: column

    def index_map(_, flags):
        return tuple(0 if f is None else f(flags) for f in index)

    return array, pl.BlockSpec(tuple(block), index_map)


def combine_kernel(plan, flags_ref, *refs):
    count = sum(terms for parts in plan for _, _, terms in parts)
    ins, outs = list(refs[:count]), refs[count:]
    for parts, out_ref in zip(plan, outs):
        for lead, row, terms in parts:
            value = None
            for ref in ins[:terms]:
                part = ref[...] if terms == 1 else ref[...].astype(F32)
                value = part if value is None else value + part
            ins = ins[terms:]
            value = value.astype(BF16)
            if lead is not None:
                out_ref[lead] = value
            elif row is not None:
                size = value.shape[-2]
                start = row if isinstance(row, int) else pl.multiple_of(row(flags_ref) * size, size)
                where = (slice(None),) * (value.ndim - 2) + (pl.ds(start, size), slice(None))
                out_ref[where] = value
            else:
                out_ref[...] = value


def combine(flags, *outs):
    ins = [t for _, parts in outs for _, _, terms in parts for t in terms]
    plan = [[(lead, row, len(terms)) for lead, row, terms in parts] for _, parts in outs]

    def full(shape):
        return pl.BlockSpec(shape, lambda *_: (0,) * len(shape))

    return kernel_call(
        functools.partial(combine_kernel, plan),
        "combine",
        (1,),
        [flags],
        ins,
        [(struct(shape), full(shape)) for shape, _ in outs],
        vmem=32,
        time=3,
    )


def summed(shape, *terms):
    return shape, [(None, None, terms)]


def pre_grad_store(grad, slope_ref, pre_ref, sum_ref):
    pre = (grad * slope_ref[...].astype(F32)).astype(BF16)
    pre_ref[...] = pre
    sum_ref[...] = column_sum(pre.astype(F32))


def pre_grad_own_kernel(low_ref, weight_ref, slope_ref, pre_ref, sum_ref):
    pre_grad_store(dot(low_ref[...], weight_ref[...], NT), slope_ref, pre_ref, sum_ref)


def pre_grad_own(low, weight, slope):
    rows, width = low.shape
    units = weight.shape[0]
    tile = min(512, units)
    column = lambda j: (0, j)
    return kernel_call(
        pre_grad_own_kernel,
        "pre_grad_own",
        (units // tile,),
        [],
        [
            (low, whole(low)),
            (weight, pl.BlockSpec((tile, width), lambda j: (j, 0))),
            (slope, pl.BlockSpec((rows, tile), column)),
        ],
        [
            (struct((rows, units)), pl.BlockSpec((rows, tile), column)),
            (struct((1, units), F32), pl.BlockSpec((1, tile), column)),
        ],
        vmem=24,
        pinned=[1],
    )


def pre_grad_far_kernel(per, nat_ref, low_ref, slope_ref, *refs):
    *pieces, pre_ref, sum_ref = refs
    for k, piece in enumerate(pieces):

        @pl.when(pl.program_id(0) // per == k)
        def _(piece=piece):
            pre_grad_store(dot(low_ref[...], piece[...], NT), slope_ref, pre_ref, sum_ref)


def pre_grad_far(nat, low, pieces, slope):
    rows, width = low.shape
    size = pieces[0].shape[0]
    tile = min(512, size)
    per = size // tile
    units = size * len(pieces)
    column = lambda j, nat: (0, nat[j // per] * per + j % per)

    def piece_spec(k):
        return pl.BlockSpec((tile, width), lambda j, nat: (jnp.clip(j - k * per, 0, per - 1), 0))

    return kernel_call(
        functools.partial(pre_grad_far_kernel, per),
        "pre_grad_far",
        (len(pieces) * per,),
        [nat],
        [(low, whole(low)), (slope, pl.BlockSpec((rows, tile), column))]
        + [(p, piece_spec(k)) for k, p in enumerate(pieces)],
        [
            (struct((rows, units)), pl.BlockSpec((rows, tile), column)),
            (struct((1, units), F32), pl.BlockSpec((1, tile), column)),
        ],
        vmem=24,
        time=8,
        pinned=range(2, 2 + len(pieces)),
    )


def add_sums(sums_ref, rows):
    @pl.when(pl.program_id(0) == 0)
    def _():
        sums_ref[...] = jnp.zeros_like(sums_ref)

    for k, row in enumerate(rows):
        sums_ref[k : k + 1, :] += row


def middle_grad_kernel(
    nat_ref, at_ref, own_ref, far_ref, weight_ref, middle_ref, cot_ref, recv_ref, loss_ref, gain_ref, *refs
):
    *pieces, grad_ref, low_ref, sums_ref, total_ref = refs
    total_ref[...] = dot(own_ref[...], weight_ref[...], NT)
    for k, piece in enumerate(pieces):
        total_ref[:, chunk_of(nat_ref, k, piece.shape[0])] += dot(far_ref[...], piece[...], NT)
    grad = total_ref[...]
    scaled, inverse = centred(middle_ref[...])
    mine = pl.program_id(0) < pl.num_programs(0) // 2
    top = jnp.where(mine, cot_ref[0].astype(F32), recv_ref[...].astype(F32)) * loss_ref[...]
    grad_middle = top + norm_input_grad(grad, scaled, inverse, gain_ref[...])
    grad_ref[...] = grad_middle
    low_ref[...] = grad_middle.astype(BF16)
    add_sums(
        sums_ref,
        [column_sum(grad * scaled), column_sum(grad), column_sum(grad_middle), column_sum(top)],
    )


def middle_grad(nat, at, own, far, weight, pieces, middle, cot, recv, loss, gain, chunk):
    count, width = middle.shape
    row = pl.BlockSpec((chunk, width), lambda j, *_: (j, 0))
    units = pl.BlockSpec((chunk, own.shape[1]), lambda j, *_: (j, 0))
    steps = count // chunk // 2
    return kernel_call(
        middle_grad_kernel,
        "middle_grad",
        (count // chunk,),
        [nat, at],
        [
            (own, units),
            (far, units),
            (weight, whole(weight)),
            (middle, row),
            (cot, pl.BlockSpec((1, chunk, width), lambda j, nat, at: (at[0], jnp.minimum(j, steps - 1), 0))),
            (recv, pl.BlockSpec((chunk, width), lambda j, *_: (jnp.maximum(j - steps, 0), 0))),
        ]
        + [(v, whole(v)) for v in (loss, gain, *pieces)],
        [
            (struct((count, width), F32), row),
            (struct((count, width)), row),
            (struct((8, width), F32), pl.BlockSpec((8, width), lambda j, *_: (0, 0))),
        ],
        [pltpu.VMEM((chunk, width), F32)],
        time=14,
        pinned=[2, 3, 4, 5, *range(8, 8 + len(pieces))],
    )


def attended_grad_kernel(nat_ref, low_ref, weight_ref, *refs):
    *pieces, own_ref, far_ref = refs
    own_ref[...] = dot(low_ref[...], weight_ref[...], NT).astype(BF16)
    for k, piece in enumerate(pieces):
        far_ref[:, chunk_of(nat_ref, k, piece.shape[0])] = dot(low_ref[...], piece[...], NT).astype(BF16)


def attended_grad(nat, low, weight, pieces, chunk):
    count, width = low.shape
    heads = weight.shape[0]
    out = (struct((count, heads)), pl.BlockSpec((chunk, heads), lambda j, nat: (j, 0)))
    return kernel_call(
        attended_grad_kernel,
        "attended_grad",
        (count // chunk,),
        [nat],
        [(low, pl.BlockSpec((chunk, width), lambda j, nat: (j, 0)))] + [(v, whole(v)) for v in (weight, *pieces)],
        [out, out],
        pinned=range(1, 2 + len(pieces)),
    )


def output_own_kernel(own_ref, weight_ref, out_ref):
    out_ref[...] = dot(own_ref[...], weight_ref[...], NN)


def output_own(first, count, own, weight, chunk):
    units = own.shape[1]
    width = weight.shape[1]
    return kernel_call(
        output_own_kernel,
        "output_own",
        (count,),
        [],
        [(own, pl.BlockSpec((chunk, units), lambda j: (j + first, 0))), (weight, whole(weight))],
        [(struct((count * chunk, width), F32), pl.BlockSpec((chunk, width), lambda j: (j, 0)))],
        vmem=20,
        time=4,
        pinned=range(2),
    )[0]


def output_kernel(nat_ref, far_ref, own_ref, middle_ref, bias_ref, *refs):
    *pieces, out_ref = refs
    total = own_ref[...]
    for k, piece in enumerate(pieces):
        total = total + dot(far_ref[:, chunk_of(nat_ref, k, piece.shape[0])], piece[...], NN)
    out_ref[...] = (middle_ref[...] + total + bias_ref[...]).astype(BF16)


def output_layer(nat, first, count, far, own, pieces, middle, bias, chunk):
    width = middle.shape[1]
    row = pl.BlockSpec((chunk, width), lambda j, nat: (j + first, 0))
    here = pl.BlockSpec((chunk, width), lambda j, nat: (j, 0))
    return kernel_call(
        output_kernel,
        "output_layer",
        (count,),
        [nat],
        [(far, pl.BlockSpec((chunk, far.shape[1]), lambda j, nat: (j + first, 0))), (own, here), (middle, row)]
        + [(v, whole(v)) for v in (bias, *pieces)],
        [(struct((count * chunk, width)), pl.BlockSpec((chunk, width), lambda j, nat: (j, 0)))],
        vmem=24,
        time=6,
        pinned=range(4 + len(pieces)),
    )[0]


def input_grad_kernel(own_count, nat_ref, far_ref, weight_ref, rows_ref, lead_ref, grad_ref, gain_ref, *refs):
    owns, refs = refs[:own_count], refs[own_count:]
    *pieces, out_ref, low_ref, sums_ref, total_ref = refs
    total = None
    at = 0
    for own in owns:
        size = own.shape[2]
        for c in range(3):
            part = dot(own[c], weight_ref[c, :, at : at + size], NT)
            total = part if total is None else total + part
        at += size
    total_ref[...] = total
    for k, piece in enumerate(pieces):
        part = dot(far_ref[0], piece[0], NT) + dot(far_ref[1], piece[1], NT) + dot(far_ref[2], piece[2], NT)
        total_ref[:, chunk_of(nat_ref, k, piece.shape[1])] += part
    grad = total_ref[...]
    scaled, inverse = centred(rows_ref[...].astype(F32) + lead_ref[...])
    grad_shifted = grad_ref[...] + norm_input_grad(grad, scaled, inverse, gain_ref[...])
    out_ref[...] = grad_shifted
    low_ref[...] = grad_shifted.astype(BF16)
    bias_rows = [
        jnp.concatenate([column_sum(d[c].astype(F32)) for d in (*owns, far_ref)], axis=1) for c in (0, 2)
    ]
    add_sums(
        sums_ref, [column_sum(grad * scaled), column_sum(grad), column_sum(grad_shifted), *bias_rows]
    )


def input_grads(nat, owns, far, weight, pieces, rows, lead, grad_middle, gain, chunk):
    count, width = rows.shape
    row = pl.BlockSpec((chunk, width), lambda j, nat: (j, 0))
    heads = lambda d: pl.BlockSpec((3, chunk, d.shape[2]), lambda j, nat: (0, j, 0))
    steps = count // chunk
    half = pl.BlockSpec((chunk, width), lambda j, nat: (jnp.maximum(j - steps // 2, 0), 0))
    return kernel_call(
        functools.partial(input_grad_kernel, len(owns)),
        "input_grads",
        (steps,),
        [nat],
        [
            (far, heads(far)),
            (weight, whole(weight)),
            (rows, row),
            (lead, whole(lead)),
            (grad_middle, row),
            (gain, whole(gain)),
        ]
        + [(d, heads(d)) for d in owns]
        + [(p, whole(p)) for p in pieces],
        [
            (struct((count, width), F32), row),
            (struct((count // 2, width)), half),
            (struct((8, width), F32), pl.BlockSpec((8, width), lambda j, nat: (0, 0))),
        ],
        [pltpu.VMEM((chunk, width), F32)],
        time=14,
        pinned=[0, 1, 2, 4, *range(6, 6 + len(owns) + len(pieces))],
    )


def pack_kernel(buckets, flags_ref, one_ref, two_ref, own_ref, far_ref, out_ref):
    width = one_ref.shape[1]
    half = width // 2
    first = flags_ref[0] == 0
    rows = lax.broadcasted_iota(jnp.int32, (buckets, width), 0)
    out_ref[:buckets] = jnp.where(rows == flags_ref[7], one_ref[2:3], 0.0)
    out_ref[buckets : buckets + 2] = one_ref[:2]
    out_ref[buckets + 2 : buckets + 6] = two_ref[:4]
    bias = one_ref[3:5]
    swapped = jnp.concatenate([bias[:, half:], bias[:, :half]], axis=1)
    out_ref[buckets + 6 : buckets + 8] = jnp.where(first, bias, swapped)
    own, far = own_ref[...], far_ref[...]
    count = own.shape[1] // width
    for k in range(count):
        columns = slice(k * width, (k + 1) * width)
        low, high = own[:, columns], far[:, columns]
        out_ref[buckets + 8 + k : buckets + 9 + k] = jnp.where(first, low, high)
        out_ref[buckets + 8 + count + k : buckets + 9 + count + k] = jnp.where(first, high, low)


def pack_vectors(flags, buckets, one, two, own, far):
    width = one.shape[1]
    rows = buckets + 8 + 2 * own.shape[1] // width
    return kernel_call(
        functools.partial(pack_kernel, buckets),
        "pack_vectors",
        (1,),
        [flags],
        [(v, whole(v)) for v in (one, two, own, far)],
        [(struct((rows, width), F32), pl.BlockSpec((rows, width), lambda *_: (0, 0)))],
        vmem=8,
        time=1,
    )[0]


def finish_turned_kernel(_, *refs):
    *pieces, out_ref = refs
    for k, piece in enumerate(pieces):

        @pl.when(pl.program_id(0) == k)
        def _(piece=piece):
            out_ref[...] = piece[...].astype(F32).T


def finish_turned(nat, pieces):
    rows, columns = pieces[0].shape
    return kernel_call(
        finish_turned_kernel,
        "finish",
        (4,),
        [nat],
        [(p, whole(p)) for p in pieces],
        [(struct((columns, 4 * rows), F32), pl.BlockSpec((columns, rows), lambda s, nat: (0, nat[s])))],
        vmem=16,
        time=2,
    )[0]


def source_spec(block, which, steps, place):
    def index(s, j, *_):
        return place(jnp.where(s == which, j, jnp.where(s < which, 0, steps - 1)))

    return pl.BlockSpec(block, index)


def finish_rows_kernel(_, *refs):
    *pieces, out_ref = refs
    for k, piece in enumerate(pieces):

        @pl.when(pl.program_id(0) == k)
        def _(piece=piece):
            out_ref[...] = piece[0].astype(F32)


def finish_rows(at, pieces):
    halves, rows, columns = pieces[0].shape
    block = (1, rows, columns)
    return kernel_call(
        finish_rows_kernel,
        "finish",
        (2, halves),
        [at],
        [(p, source_spec(block, k, halves, lambda j: (j, 0, 0))) for k, p in enumerate(pieces)],
        [
            (
                struct((2 * halves * rows, columns), F32),
                pl.BlockSpec((rows, columns), lambda s, j, at: (at[s] * halves + j, 0)),
            )
        ],
        vmem=20,
        time=5,
    )[0]


def finish_columns_kernel(at_ref, mine_ref, theirs_ref, out_ref):
    first = at_ref[0] == 0
    one, two = mine_ref[0].astype(F32), theirs_ref[0].astype(F32)
    columns = one.shape[1]
    out_ref[:, :columns] = jnp.where(first, one, two)
    out_ref[:, columns:] = jnp.where(first, two, one)


def finish_columns(at, pieces):
    halves, rows, columns = pieces[0].shape
    tile = min(512, rows)
    per = rows // tile
    spec = pl.BlockSpec((1, tile, columns), lambda j, at: (j // per, j % per, 0))
    return kernel_call(
        finish_columns_kernel,
        "finish",
        (halves * per,),
        [at],
        [(p, spec) for p in pieces],
        [(struct((halves * rows, 2 * columns), F32), pl.BlockSpec((tile, 2 * columns), lambda j, at: (j, 0)))],
        vmem=20,
        time=5,
    )[0]


def finish_stack_kernel(count, at_ref, *refs):
    pieces, out_ref = refs[:count], refs[-1]
    for k, piece in enumerate(pieces):

        @pl.when(pl.program_id(0) == k)
        def _(piece=piece):
            out_ref[0] = jnp.concatenate([piece[0, 0].astype(F32), piece[1, 0].astype(F32)], axis=1)


def finish_stack(nat, first, pieces, *so_far):
    _, stack, rows, columns = pieces[0].shape
    block = (2, 1, rows, columns)
    count = len(pieces)
    return kernel_call(
        functools.partial(finish_stack_kernel, count),
        "finish",
        (count, stack),
        [nat],
        [(p, source_spec(block, k, stack, lambda j: (0, j, 0, 0))) for k, p in enumerate(pieces)]
        + [(v, pl.BlockSpec(memory_space=pl.ANY)) for v in so_far],
        [
            (
                struct((stack, 4 * rows, 2 * columns), F32),
                pl.BlockSpec((1, rows, 2 * columns), lambda s, j, nat: (j, nat[first + s], 0)),
            )
        ],
        vmem=16,
        time=3,
        alias=count if so_far else None,
    )[0]


def hold(*values):
    return lax.optimization_barrier(values)


def fast_body(
    tokens,
    cotangent,
    buckets,
    counts,
    lead_table,
    norm1_gain,
    norm1_shift,
    w_qkv,
    qv_bias,
    w_out,
    out_bias,
    norm2_gain,
    norm2_shift,
    w_fc1,
    fc1_bias,
    w_fc2,
    fc2_bias,
):
    replicas = lax.axis_size("dp")
    levels = replicas.bit_length() - 1
    dp_at, mp_at = lax.axis_index("dp"), lax.axis_index("mp")
    bits = [(dp_at >> level) & 1 for level in range(levels)]

    def over_x(value):
        return lax.ppermute(value, "mp", [(0, 1), (1, 0)])

    def over(level, value):
        return over_mask(1 << level, value)

    def over_mask(mask, value):
        return lax.ppermute(value, "dp", [(i, i ^ mask) for i in range(replicas)])

    def joined(bit, mine, theirs, axis=0):
        return jnp.where(
            bit == 0,
            jnp.concatenate([mine, theirs], axis),
            jnp.concatenate([theirs, mine], axis),
        )

    def part(value, index, count, axis=0):
        size = value.shape[axis] // count
        return lax.dynamic_slice_in_dim(value, index * size, size, axis)

    half_rows, width = tokens.shape[1:]
    heads_width = w_qkv.shape[2]
    units = w_fc1.shape[1]
    chunk = 256
    core, side = bits[0], bits[1]
    bucket = lax.dynamic_index_in_dim(buckets, mp_at, 0, keepdims=False)
    at = jnp.stack([mp_at, core, 1 - core, side, 1 - side, bits[2], bits[3], bucket]).astype(jnp.int32)
    mine = core * 2 + side
    shared_nat = jnp.stack([mine, mine ^ 1, mine ^ 2, mine ^ 3]).astype(jnp.int32)
    core_first_nat = jnp.stack([mine, mine ^ 2, mine ^ 1, mine ^ 3]).astype(jnp.int32)

    def row_of(vector):
        return vector.astype(F32)[None]

    small = jnp.concatenate([qv_bias.reshape(-1), fc1_bias])
    small_rows = -(-small.shape[0] // width)
    small_rows_padded = -(-small_rows // 16) * 16
    small = jnp.pad(small, (0, small_rows_padded * width - small.shape[0])).reshape(-1, width)
    token_recv = over_x(jnp.concatenate([part(tokens, 1 - mp_at, 2)[0], small]))

    count_f = counts.astype(F32)
    loss_weight = jnp.mean(count_f) / lax.dynamic_index_in_dim(count_f, bucket, 0, keepdims=False)
    loss_row = jnp.broadcast_to(loss_weight, (1, width))
    lead = lax.dynamic_index_in_dim(lead_table, bucket, 0).astype(F32)
    own_qkv = jnp.transpose(w_qkv, (1, 0, 2))

    def bias_three(bias):
        bias_f = bias.astype(F32)
        return jnp.stack([bias_f[0], jnp.zeros_like(bias_f[0]), bias_f[1]])

    (
        token_recv, qkv_send, out_send, fc1_send, cot_send, fc2_send, at, shared_nat, core_first_nat, loss_row, loss_weight, lead,
        gain_one, gain_two, shift_one, shift_two, out_row, fc1_row, fc2_row, own_bias,
    ) = hold(
        token_recv,
        part(own_qkv, mine, 4, 1),
        part(w_out, core, 2),
        part(w_fc1, mine, 4),
        part(cotangent, 1 - mp_at, 2)[0],
        part(w_fc2, core, 2),
        at,
        shared_nat,
        core_first_nat,
        loss_row,
        loss_weight,
        lead,
        row_of(norm1_gain),
        row_of(norm2_gain),
        row_of(norm1_shift),
        row_of(norm2_shift),
        row_of(out_bias),
        row_of(fc1_bias),
        row_of(fc2_bias),
        bias_three(qv_bias),
    )
    keep_half, send_half, pair_nat = at[1:2], at[2:3], at[1:3]
    far_small = token_recv[half_rows:].reshape(-1)
    far_bias = bias_three(far_small[: 2 * heads_width].reshape(2, heads_width))
    far_fc1_bias = row_of(far_small[2 * heads_width : 2 * heads_width + units])

    qkv_x = over_x(qkv_send)
    rows, normed_one, own_heads = project_own(
        at[:1], tokens, token_recv, lead, gain_one, shift_one, own_qkv, own_bias, chunk
    )
    own_heads, qkv_x, out_send, fc1_send, far_bias, far_fc1_bias = hold(
        own_heads, qkv_x, out_send, fc1_send, far_bias, far_fc1_bias
    )

    qkv_y = over(1, qkv_x)
    out_x = over_x(out_send)
    fc1_x = over_x(fc1_send)
    own_attended, own_powers, own_inverse = attend(own_heads)
    own_attended, qkv_x, qkv_y, out_x = hold(own_attended, qkv_x, qkv_y, out_x)

    far_qkv = [qkv_x, qkv_y, over(0, qkv_x), over(0, qkv_y)]
    far_out = [out_x, over(0, out_x)]
    far_heads = project_far(shared_nat, normed_one, far_bias, far_qkv)
    far_heads, fc1_x, cot_send = hold(far_heads, fc1_x, cot_send)

    fc1_y = over(1, fc1_x)
    cot_recv = over_x(cot_send)
    far_attended, far_powers, far_inverse = attend(far_heads)
    middle, normed_two = middle_layer(
        pair_nat, own_attended, far_attended, w_out, far_out, rows, lead,
        out_row, gain_two, shift_two, chunk,
    )
    normed_two, fc1_x, fc1_y, cot_recv, fc2_send = hold(
        normed_two, fc1_x, fc1_y, cot_recv, fc2_send
    )

    def mine_y(flags):
        return flags[3]

    def theirs_y(flags):
        return flags[4]

    def mine_z(flags):
        return flags[5]

    def theirs_z(flags):
        return 1 - flags[5]

    def mine_z2(flags):
        return flags[6]

    def theirs_z2(flags):
        return 1 - flags[6]

    def zero(_):
        return 0

    def one(_):
        return 1

    def first_y(own_down, far_down):
        size = own_down.shape[0] // 2
        return (2 * size, own_down.shape[1]), [
            (None, 0, [term(own_down, theirs_y, size)]),
            (None, size, [term(far_down, theirs_y, size)]),
        ]

    def second_y(own_up, recv_x):
        size = own_up.shape[0] // 2
        return summed((size, own_up.shape[1]), term(own_up, theirs_y, size), term(recv_x, theirs_y, size))

    def second_x(far_down, recv_y):
        size = far_down.shape[0] // 2
        return summed((size, far_down.shape[1]), term(far_down, mine_y, size), term(recv_y, one, size))

    def z_half(which, own_up, recv_x, recv_up, own_down, recv_y, recv_down):
        size = own_up.shape[0] // 4

        def within(side_of, start=0):
            return lambda flags: (start + side_of(flags)) * 2 + which(flags)

        upper = [term(own_up, within(mine_y), size), term(recv_x, within(mine_y), size), term(recv_up, which, size)]
        lower = [term(own_down, within(mine_y), size), term(recv_y, within(zero), size), term(recv_down, which, size)]
        return (2, size, own_up.shape[1]), [(0, None, upper), (1, None, lower)]

    def z_sides(mine, recv):
        shape = list(mine.shape)
        shape[-2] *= 2
        return tuple(shape), [(None, mine_z, [term(mine)]), (None, theirs_z, [term(recv)])]

    def y_sides(mine, recv):
        shape = list(mine.shape)
        shape[-2] *= 2
        return tuple(shape), [(None, mine_y, [term(mine)]), (None, theirs_y, [term(recv)])]

    masks = {1: 8, 2: 4, 3: 12}

    def quarter_z(k):
        def index(flags):
            first = 1 - flags[5] if k & 2 else flags[5]
            second = 1 - flags[6] if k & 1 else flags[6]
            return first * 2 + second

        return index

    fc2_x = over_x(fc2_send)
    far_fc1 = [fc1_x, fc1_y, over(0, fc1_x), over(0, fc1_y)]
    cot_rows = jnp.concatenate([part(cotangent, mp_at, 2)[0], cot_recv])
    grad_low = (cot_rows.astype(F32) * loss_weight).astype(BF16)
    own_hidden, own_slope = hidden_layer(shared_nat, normed_two, fc1_row, [w_fc1], chunk)
    far_hidden, far_slope = hidden_layer(shared_nat, normed_two, far_fc1_bias, far_fc1, chunk)
    far_send = grad_right_half(send_half, far_hidden, grad_low)
    own_send = grad_right_half(send_half, own_hidden, grad_low)
    own_pre, own_fc1_bias = pre_grad_own(grad_low, w_fc2, own_slope)
    fc1_own_send = grad_left_half(send_half, normed_two, own_pre)
    far_send, own_send, fc2_x, grad_low, far_hidden, own_pre, fc1_own_send = hold(
        far_send, own_send, fc2_x, grad_low, far_hidden, own_pre, fc1_own_send
    )

    far_recv, own_recv, fc2_core, fc1_own_recv = over(0, far_send), over(0, own_send), over(0, fc2_x), over(0, fc1_own_send)
    far_up, far_down = grad_right_half(keep_half, far_hidden, grad_low, far_recv)
    own_up, own_down = grad_right_half(keep_half, own_hidden, grad_low, own_recv)
    far_up, far_down, own_up, own_down, fc2_core, fc1_own_recv = hold(
        far_up, far_down, own_up, own_down, fc2_core, fc1_own_recv
    )

    half_width = width // 2
    fc2_x1 = over_x(far_up)
    fc2_y1 = over(1, combine(at, first_y(own_down, far_down))[0])
    far_fc2 = [fc2_x, fc2_core]
    far_pre, far_fc1_bias_sum = pre_grad_far(pair_nat, grad_low, far_fc2, far_slope)
    fc1_far_send = grad_left_half(send_half, normed_two, far_pre)
    fc1_own_up, fc1_own_down = grad_left_half(keep_half, normed_two, own_pre, fc1_own_recv, split=True)
    chunks = half_rows // chunk
    mlp_low = output_own(chunks, chunks, own_hidden, w_fc2, chunk)
    fc1_far_send, fc1_own_up, fc1_own_down, fc2_x1, fc2_y1, far_pre, mlp_low = hold(
        fc1_far_send, fc1_own_up, fc1_own_down, fc2_x1, fc2_y1, far_pre, mlp_low
    )

    send_y, send_x = combine(at, second_y(own_up, fc2_x1), second_x(far_down, fc2_y1))
    fc2_y2, fc2_x2 = over(1, send_y), over_x(send_x)
    fc1_far_recv = over(0, fc1_far_send)
    grad_middle, grad_branch, sums_two = middle_grad(
        shared_nat, at[:1], own_pre, far_pre, w_fc1, far_fc1, middle, cotangent, cot_recv, loss_row, gain_two, chunk
    )
    own_grad_att, far_grad_att = attended_grad(pair_nat, grad_branch, w_out, far_out, chunk)
    out_far_send = grad_left_half(send_half, grad_branch, far_attended)
    out_own_send = grad_left_half(send_half, grad_branch, own_attended)
    fc1_far_up, fc1_far_down = grad_left_half(keep_half, normed_two, far_pre, fc1_far_recv, split=True)
    out_far_recv, out_own_recv = over(0, out_far_send), over(0, out_own_send)
    out_far_sum = grad_left_half(keep_half, grad_branch, far_attended, out_far_recv)
    out_own_sum = grad_left_half(keep_half, grad_branch, own_attended, out_own_recv)
    far_grad_att, own_grad_att, fc2_y2, fc2_x2, fc1_far_up, fc1_far_down, out_far_sum, out_own_sum = hold(
        far_grad_att, own_grad_att, fc2_y2, fc2_x2, fc1_far_up, fc1_far_down, out_far_sum, out_own_sum
    )

    fc2_terms = (own_up, fc2_x1, fc2_y2, own_down, fc2_y1, fc2_x2)
    fc2_send, fc2_mine, send_y = combine(
        at, z_half(theirs_z, *fc2_terms), z_half(mine_z, *fc2_terms), first_y(fc1_own_down, fc1_far_down)
    )
    fc1_x1, fc1_y1, fc2_recv = over_x(fc1_far_up), over(1, send_y), over(2, fc2_send)
    pairs = heads_width // (2 * HD)
    far_dqkv = attend_back(0, pairs, far_heads, far_powers, far_inverse, far_attended, far_grad_att)
    far_dqkv, own_grad_att, fc1_x1, fc1_y1, out_far_sum, fc2_recv = hold(
        far_dqkv, own_grad_att, fc1_x1, fc1_y1, out_far_sum, fc2_recv
    )

    half_rows_out = half_width // 2
    out_shape = (half_rows_out, heads_width)
    z_shape = (2, fc2_mine.shape[1] // 2, fc2_mine.shape[2])
    send_y, send_x, fc2_send, fc2_mine = combine(
        at,
        second_y(fc1_own_up, fc1_x1),
        second_x(fc1_far_down, fc1_y1),
        summed(z_shape, term(fc2_mine, theirs_z2, z_shape[1]), term(fc2_recv, theirs_z2, z_shape[1])),
        summed(z_shape, term(fc2_mine, mine_z2, z_shape[1]), term(fc2_recv, mine_z2, z_shape[1])),
    )
    fc1_y2, fc1_x2, fc2_recv, out_recv = over(1, send_y), over_x(send_x), over(3, fc2_send), over_x(out_far_sum)
    qkv_far_recv = over(0, grad_left_half(send_half, normed_one, far_dqkv))
    qkv_far_keep = grad_left_half(keep_half, normed_one, far_dqkv)
    own_a = attend_back(0, pairs // 2, own_heads, own_powers, own_inverse, own_attended, own_grad_att)
    own_a_send = grad_left_half(send_half, normed_one, own_a)
    own_a_send, own_grad_att, fc1_y2, fc1_x2, out_recv, qkv_far_recv, qkv_far_keep, fc2_recv = hold(
        own_a_send, own_grad_att, fc1_y2, fc1_x2, out_recv, qkv_far_recv, qkv_far_keep, fc2_recv
    )

    side_a = heads_width // 2
    own_a_recv = over(0, own_a_send)
    fc1_terms = (fc1_own_up, fc1_x1, fc1_y2, fc1_own_down, fc1_y1, fc1_x2)
    qkv_send, fc1_send, fc1_mine, fc2_mine, out_send = combine(
        at,
        summed((3, half_width, side_a), term(qkv_far_keep, column=0), term(qkv_far_recv, column=0)),
        z_half(theirs_z, *fc1_terms),
        z_half(mine_z, *fc1_terms),
        summed(fc2_mine.shape, term(fc2_mine), term(fc2_recv)),
        summed(out_shape, term(out_own_sum, theirs_y, half_rows_out), term(out_recv, theirs_y, half_rows_out)),
    )
    qkv_first, fc1_recv, fc2_recv, out_y = over_x(qkv_send), over(2, fc1_send), over(3, fc2_mine), over(1, out_send)
    own_b = attend_back(pairs // 2, pairs - pairs // 2, own_heads, own_powers, own_inverse, own_attended, own_grad_att)
    own_a_sum = grad_left_half(keep_half, normed_one, own_a, own_a_recv)
    own_b_send = grad_left_half(send_half, normed_one, own_b)
    own_b, own_b_send, own_a_sum, fc2_recv, out_y, qkv_first, qkv_far_keep, qkv_far_recv, fc1_recv = hold(
        own_b, own_b_send, own_a_sum, fc2_recv, out_y, qkv_first, qkv_far_keep, qkv_far_recv, fc1_recv
    )

    own_b_recv = over(0, own_b_send)
    a_shape = (3, half_rows_out, side_a)
    qkv_send, fc1_mine, a_send, out_mine, fc2_mine = combine(
        at,
        summed((3, half_width, side_a), term(qkv_far_keep, column=1), term(qkv_far_recv, column=1)),
        summed(fc1_mine.shape, term(fc1_mine), term(fc1_recv)),
        summed(a_shape, term(own_a_sum, theirs_y, half_rows_out), term(qkv_first, theirs_y, half_rows_out)),
        summed(
            out_shape,
            term(out_own_sum, mine_y, half_rows_out),
            term(out_recv, mine_y, half_rows_out),
            term(out_y),
        ),
        ((2, 2 * z_shape[1], z_shape[2]), [(None, mine_z2, [term(fc2_mine)]), (None, theirs_z2, [term(fc2_recv)])]),
    )
    qkv_second, fc1_recv, a_y = over_x(qkv_send), over(3, fc1_mine), over(1, a_send)
    fc2_recv = over(2, fc2_mine)
    grad_shifted, grad_send, sums_one = input_grads(
        shared_nat, [own_a, own_b], far_dqkv, own_qkv, far_qkv, rows, lead, grad_middle, gain_one, chunk
    )
    own_b_sum = grad_left_half(keep_half, normed_one, own_b, own_b_recv)
    grad_shifted, grad_send, sums_one, a_y, qkv_second, own_b_sum, out_mine, fc2_mine, fc2_recv, fc1_recv, own_hidden, far_hidden = hold(
        grad_shifted, grad_send, sums_one, a_y, qkv_second, own_b_sum, out_mine, fc2_mine, fc2_recv, fc1_recv, own_hidden, far_hidden
    )

    b_send, fc2_mine, fc1_mine = combine(
        at,
        summed(a_shape, term(own_b_sum, theirs_y, half_rows_out), term(qkv_second, theirs_y, half_rows_out)),
        z_sides(fc2_mine, fc2_recv),
        summed(fc1_mine.shape, term(fc1_mine), term(fc1_recv)),
    )
    b_y, fc1_recv = over(1, b_send), over(2, fc1_mine)
    grad_recv = over_x(grad_send)
    vectors = pack_vectors(at, counts.shape[0], sums_one, sums_two, own_fc1_bias, far_fc1_bias_sum)
    vectors_recv = over(1, vectors)
    b_y, vectors_recv, fc1_mine, fc1_recv, own_hidden, fc2_mine = hold(
        b_y, vectors_recv, fc1_mine, fc1_recv, own_hidden, fc2_mine
    )

    z_rows = half_rows_out // 4

    def qkv_quarter(k):
        def within(flags):
            return mine_y(flags) * 4 + quarter_z(k)(flags)

        parts = [
            (side_k, None, [term(total, within, z_rows), term(recv, within, z_rows), term(recv_y, quarter_z(k), z_rows)])
            for side_k, (total, recv, recv_y) in enumerate(((own_a_sum, qkv_first, a_y), (own_b_sum, qkv_second, b_y)))
        ]
        return (2, 3, z_rows, side_a), parts

    *qkv_sends, qkv_mine, fc1_mine = combine(
        at,
        *[qkv_quarter(k) for k in masks],
        qkv_quarter(0),
        z_sides(fc1_mine, fc1_recv),
    )
    qkv_recv = [over_mask(mask, sent) for mask, sent in zip(masks.values(), qkv_sends)]
    fc2_y = over(1, fc2_mine)
    vectors = vectors + vectors_recv
    output_low = output_layer(pair_nat, chunks, chunks, far_hidden, mlp_low, far_fc2, middle, fc2_row, chunk)
    mlp_high = output_own(0, chunks, own_hidden, w_fc2, chunk)
    mlp_high, output_low, grad_recv, vectors, fc1_mine, fc2_mine, fc2_y, *qkv_recv = hold(
        mlp_high, output_low, grad_recv, vectors, fc1_mine, fc2_mine, fc2_y, *qkv_recv
    )

    qkv_mine, fc2_half = combine(
        at,
        summed(qkv_mine.shape, *[term(v) for v in (qkv_mine, *qkv_recv)]),
        y_sides(fc2_mine, fc2_y),
    )
    qkv_parts = [qkv_mine] + [over_mask(mask, qkv_mine) for mask in masks.values()]
    fc1_y = over(1, fc1_mine)
    output_recv = over_x(output_low)
    output_high = output_layer(pair_nat, 0, chunks, far_hidden, mlp_high, far_fc2, middle, fc2_row, chunk)
    fc2_grad = finish_columns(pair_nat, [fc2_half, over(0, fc2_half)])
    vectors, fc1_y, fc2_grad, out_mine, grad_recv, output_recv, output_high, *qkv_parts = hold(
        vectors, fc1_y, fc2_grad, out_mine, grad_recv, output_recv, output_high, *qkv_parts
    )

    qkv_mine, fc1_half = combine(
        at,
        (
            (2, 3, half_rows_out, side_a),
            [(None, quarter_z(k), [term(v)]) for k, v in zip((0, *masks), qkv_parts)],
        ),
        y_sides(fc1_mine, fc1_y),
    )
    qkv_y, qkv_core = over(1, qkv_mine), over(0, qkv_mine)
    fc1_core = over(0, fc1_half)
    out_mine = combine(at, summed(out_shape, term(out_mine), term(over(2, out_mine))))[0]
    out_z = over(3, out_mine)
    vectors = vectors + over_x(vectors)
    vectors_recv = over(2, vectors)
    input_grad = joined(mp_at, grad_shifted[None, :half_rows], grad_recv[None].astype(F32))
    fc1_grad = finish_rows(pair_nat, [fc1_half, fc1_core])
    qkv_mine, qkv_y, qkv_core, vectors_recv, fc1_grad, out_mine, out_z, input_grad = hold(
        qkv_mine, qkv_y, qkv_core, vectors_recv, fc1_grad, out_mine, out_z, input_grad
    )

    qkv_last = over(0, qkv_y)
    out_mine = combine(at, summed(out_shape, term(out_mine), term(out_z)))[0]
    out_y, out_core = over(1, out_mine), over(0, out_mine)
    qkv_grad = finish_stack(core_first_nat, 0, [qkv_mine, qkv_core])
    block_output = joined(mp_at, output_high[None], output_recv[None])
    vectors = vectors + vectors_recv
    vectors_recv = over(3, vectors)
    qkv_last, qkv_grad, vectors_recv, out_y, out_core, block_output = hold(
        qkv_last, qkv_grad, vectors_recv, out_y, out_core, block_output
    )

    vectors = vectors + vectors_recv
    vectors = vectors + over(0, vectors)
    out_grad = finish_turned(core_first_nat, [out_mine, out_core, out_y, over(0, out_y)])
    qkv_grad = finish_stack(core_first_nat, 2, [qkv_y, qkv_last], qkv_grad)
    qkv_grad = jnp.transpose(qkv_grad, (1, 0, 2))

    table = counts.shape[0]
    lead_grad, singles, rest = vectors[:table], vectors[table : table + 6], vectors[table + 6 :]
    qv_bias_grad = part(rest[:2], mp_at, 2, 1)
    fc1_bias_grad = part(rest[2:].reshape(-1), mp_at, 2)
    return (
        block_output,
        input_grad,
        lead_grad,
        singles[0],
        singles[1],
        qkv_grad,
        qv_bias_grad,
        out_grad,
        singles[4],
        singles[2],
        singles[3],
        fc1_grad,
        fc1_bias_grad,
        fc2_grad,
        singles[5],
    )


def solution(mesh):
    in_specs = (
        P("dp", "mp", None),
        P("dp", "mp", None),
        P("dp"),
        P(),
        P(),
        P(),
        P(),
        P(None, None, "mp"),
        P(None, "mp"),
        P("mp", None),
        P(),
        P(),
        P(),
        P(None, "mp"),
        P("mp"),
        P("mp", None),
        P(),
    )
    out_specs = (
        P("dp", "mp", None),
        P("dp", "mp", None),
        P(),
        P(),
        P(),
        P(None, None, "mp"),
        P(None, "mp"),
        P("mp", None),
        P(),
        P(),
        P(),
        P(None, "mp"),
        P("mp"),
        P("mp", None),
        P(),
    )
    def local(*args):
        replicas = lax.axis_size("dp")
        samples, half_rows, width = args[0].shape
        heads_width, units = args[7].shape[2], args[13].shape[1]
        fits = samples == 2 and lax.axis_size("mp") == 2 and replicas == 16
        even = half_rows % 256 == 0 and width == 2 * heads_width == 1024 and units == 2 * width
        return (fast_body if fits and even else body)(*args)

    return jax.shard_map(local, mesh=mesh, in_specs=in_specs, out_specs=out_specs, check_vma=False)
```

```python
import functools
import math

import jax
import jax.numpy as jnp
from jax import lax
from jax.experimental import pallas as pl
from jax.experimental.pallas import tpu as pltpu
from jax.sharding import PartitionSpec as P

HD = 64


EPS = 1e-05


def norm_forward(values, norm_gain, norm_shift):
    center = values - jnp.mean(values, axis=-1, keepdims=True)
    inverse = lax.rsqrt(jnp.mean(center * center, axis=-1, keepdims=True) + EPS)
    scaled = center * inverse
    return (scaled * norm_gain + norm_shift, scaled, inverse)


def norm_backward(grad_out, scaled, inverse, norm_gain):
    grad_scaled = grad_out * norm_gain
    grad_mean = jnp.mean(grad_scaled, axis=-1, keepdims=True)
    cross_mean = jnp.mean(grad_scaled * scaled, axis=-1, keepdims=True)
    grad_in = inverse * (grad_scaled - grad_mean - scaled * cross_mean)
    gain_grad = jnp.sum(grad_out * scaled, axis=(0, 1))
    shift_grad = jnp.sum(grad_out, axis=(0, 1))
    return (grad_in, gain_grad, shift_grad)


def gelu_slope(pre_act):
    normal_cdf = 0.5 * (1.0 + lax.erf(pre_act * 0.7071067811865476))
    return normal_cdf + pre_act * jnp.exp(-0.5 * pre_act * pre_act) * 0.3989422804014327


def attention_forward(query_all, key_all, value_all, block_rows):
    block_count = query_all.shape[0] // block_rows
    query_blocks = query_all.reshape((block_count, block_rows) + query_all.shape[1:])

    def one_block(query_block):
        scores = (
            jnp.einsum("qshd,kshd->shqk", query_block, key_all, preferred_element_type=jnp.float32)
            * 0.125
        )
        row_max = jnp.max(scores, axis=-1, keepdims=True)
        powers = jnp.exp(scores - row_max)
        exp_total = jnp.sum(powers, axis=-1, keepdims=True)
        attn_weights = (powers / exp_total).astype(jnp.bfloat16)
        attended = jnp.einsum(
            "shqk,kshd->qshd", attn_weights, value_all, preferred_element_type=jnp.float32
        )
        return (attended.astype(jnp.bfloat16), (row_max + jnp.log(exp_total))[..., 0])

    attended, log_total = lax.map(one_block, query_blocks)
    return (attended.reshape(query_all.shape), log_total)


def attention_backward(query_all, key_all, value_all, grad_attended, log_total, block_rows):
    block_count = query_all.shape[0] // block_rows
    query_blocks = query_all.reshape((block_count, block_rows) + query_all.shape[1:])
    grad_blocks = grad_attended.reshape((block_count, block_rows) + query_all.shape[1:])

    def one_block(running, sliced):
        key_grad, value_grad = running
        query_block, grad_block, log_block = sliced
        scores = (
            jnp.einsum("qshd,kshd->shqk", query_block, key_all, preferred_element_type=jnp.float32)
            * 0.125
        )
        attn_weights = jnp.exp(scores - log_block[..., None])
        weight_low = attn_weights.astype(jnp.bfloat16)
        grad_weights = jnp.einsum(
            "qshd,kshd->shqk", grad_block, value_all, preferred_element_type=jnp.float32
        )
        inner = jnp.sum(attn_weights * grad_weights, axis=-1, keepdims=True)
        grad_scores = (attn_weights * (grad_weights - inner)).astype(jnp.bfloat16)
        query_grad = (
            jnp.einsum("shqk,kshd->qshd", grad_scores, key_all, preferred_element_type=jnp.float32)
            * 0.125
        )
        key_grad = (
            key_grad
            + jnp.einsum(
                "shqk,qshd->kshd", grad_scores, query_block, preferred_element_type=jnp.float32
            )
            * 0.125
        )
        value_grad = value_grad + jnp.einsum(
            "shqk,qshd->kshd", weight_low, grad_block, preferred_element_type=jnp.float32
        )
        return ((key_grad, value_grad), query_grad.astype(jnp.bfloat16))

    zero_grad = jnp.zeros(key_all.shape, jnp.float32)
    (key_grad, value_grad), query_grad = lax.scan(
        one_block, (zero_grad, zero_grad), (query_blocks, grad_blocks, log_total)
    )
    return (
        query_grad.reshape(query_all.shape),
        key_grad.astype(jnp.bfloat16),
        value_grad.astype(jnp.bfloat16),
    )


def body(
    tokens,
    cotangent,
    buckets,
    counts,
    lead_table,
    norm1_gain,
    norm1_shift,
    w_qkv,
    qv_bias,
    w_out,
    out_bias,
    norm2_gain,
    norm2_shift,
    w_fc1,
    fc1_bias,
    w_fc2,
    fc2_bias,
):
    samples_here = tokens.shape[0]
    local_rows = tokens.shape[1]
    local_width = w_qkv.shape[2]
    local_heads = local_width // HD
    seq_len = local_rows * lax.axis_size("mp")
    block_rows = min(512, seq_len)
    head_shape = (seq_len, samples_here, local_heads, HD)
    count_f = counts.astype(jnp.float32)
    onehot = (buckets[:, None] == jnp.arange(counts.shape[0], dtype=jnp.int32)[None, :]).astype(
        jnp.float32
    )
    loss_weight = jnp.mean(count_f) / jnp.sum(onehot * count_f[None, :], axis=1)
    lead_rows = jnp.dot(
        onehot,
        lead_table.astype(jnp.float32),
        precision=lax.Precision.HIGHEST,
        preferred_element_type=jnp.float32,
    )
    shifted = jnp.swapaxes(tokens, 0, 1).astype(jnp.float32) + lead_rows[None]
    normed_one, scaled_one, inverse_one = norm_forward(
        shifted, norm1_gain.astype(jnp.float32), norm1_shift.astype(jnp.float32)
    )
    normed_one = normed_one.astype(jnp.bfloat16)
    normed_full = lax.all_gather(normed_one, "mp", axis=0, tiled=True)
    project = jnp.einsum("tsd,dcf->tscf", normed_full, w_qkv, preferred_element_type=jnp.float32)
    bias_f = qv_bias.astype(jnp.float32)
    query_all = (project[:, :, 0] + bias_f[0]).astype(jnp.bfloat16).reshape(head_shape)
    key_all = project[:, :, 1].astype(jnp.bfloat16).reshape(head_shape)
    value_all = (project[:, :, 2] + bias_f[1]).astype(jnp.bfloat16).reshape(head_shape)
    attended, log_total = attention_forward(query_all, key_all, value_all, block_rows)
    attended_flat = attended.reshape(seq_len, samples_here, local_width)
    picked = attended_flat
    branch = lax.psum_scatter(
        jnp.einsum("tsf,fd->tsd", picked, w_out, preferred_element_type=jnp.float32),
        "mp",
        scatter_dimension=0,
        tiled=True,
    )
    middle = shifted + branch + out_bias.astype(jnp.float32)
    gain_two = norm2_gain.astype(jnp.float32)
    normed_two, scaled_two, inverse_two = norm_forward(
        middle, gain_two, norm2_shift.astype(jnp.float32)
    )
    normed_two = normed_two.astype(jnp.bfloat16)
    grad_top = jnp.swapaxes(cotangent, 0, 1).astype(jnp.float32) * loss_weight[None, :, None]
    grad_low = grad_top.astype(jnp.bfloat16)
    fc1_full, fc1_bias_full, fc2_full = (
        lax.all_gather(w_fc1, "mp", axis=1, tiled=True),
        lax.all_gather(fc1_bias, "mp", axis=0, tiled=True),
        lax.all_gather(w_fc2, "mp", axis=0, tiled=True),
    )
    pre_act = jnp.einsum(
        "tsd,df->tsf", normed_two, fc1_full, preferred_element_type=jnp.float32
    ) + fc1_bias_full.astype(jnp.float32)
    hidden = jax.nn.gelu(pre_act, approximate=False).astype(jnp.bfloat16)
    mlp_branch = jnp.einsum("tsf,fd->tsd", hidden, fc2_full, preferred_element_type=jnp.float32)
    output = middle + mlp_branch + fc2_bias.astype(jnp.float32)
    grad_hidden = jnp.einsum("tsd,fd->tsf", grad_low, fc2_full, preferred_element_type=jnp.float32)
    grad_pre = (grad_hidden * gelu_slope(pre_act)).astype(jnp.bfloat16)
    grad_normed_two = jnp.einsum(
        "tsf,df->tsd", grad_pre, fc1_full, preferred_element_type=jnp.float32
    )
    fc1_part = jnp.einsum("tsd,tsf->df", normed_two, grad_pre, preferred_element_type=jnp.float32)
    fc1_bias_part = jnp.sum(grad_pre.astype(jnp.float32), axis=(0, 1))
    fc2_part = jnp.einsum("tsf,tsd->fd", hidden, grad_low, preferred_element_type=jnp.float32)
    fc1_grad, fc1_bias_grad, fc2_grad = (
        lax.psum_scatter(
            fc1_part.astype(jnp.bfloat16), "mp", scatter_dimension=1, tiled=True
        ).astype(jnp.float32),
        lax.psum_scatter(
            fc1_bias_part.astype(jnp.bfloat16), "mp", scatter_dimension=0, tiled=True
        ).astype(jnp.float32),
        lax.psum_scatter(
            fc2_part.astype(jnp.bfloat16), "mp", scatter_dimension=0, tiled=True
        ).astype(jnp.float32),
    )
    fc2_bias_grad = jnp.sum(grad_top, axis=(0, 1))
    grad_from_norm, gain_two_grad, shift_two_grad = norm_backward(
        grad_normed_two, scaled_two, inverse_two, gain_two
    )
    grad_middle = grad_top + grad_from_norm
    out_bias_grad = jnp.sum(grad_middle, axis=(0, 1))
    grad_branch = grad_middle.astype(jnp.bfloat16)
    grad_branch_full = lax.all_gather(grad_branch, "mp", axis=0, tiled=True)
    out_grad = jnp.einsum(
        "tsf,tsd->fd", attended_flat, grad_branch_full, preferred_element_type=jnp.float32
    )
    grad_attended = jnp.einsum(
        "tsd,fd->tsf", grad_branch_full, w_out, preferred_element_type=jnp.float32
    ).astype(jnp.bfloat16)
    query_grad, key_grad, value_grad = attention_backward(
        query_all, key_all, value_all, grad_attended.reshape(head_shape), log_total, block_rows
    )
    grad_project = jnp.stack([query_grad, key_grad, value_grad], axis=2).reshape(
        seq_len, samples_here, 3, local_width
    )
    qkv_grad = jnp.einsum(
        "tsd,tscf->dcf", normed_full, grad_project, preferred_element_type=jnp.float32
    )
    query_bias_grad = jnp.sum(query_grad.astype(jnp.float32), axis=(0, 1)).reshape(local_width)
    value_bias_grad = jnp.sum(value_grad.astype(jnp.float32), axis=(0, 1)).reshape(local_width)
    qv_bias_grad = jnp.stack([query_bias_grad, value_bias_grad])
    picked = grad_project
    grad_normed_one = lax.psum_scatter(
        jnp.einsum("tscf,dcf->tsd", picked, w_qkv, preferred_element_type=jnp.float32).astype(
            jnp.bfloat16
        ),
        "mp",
        scatter_dimension=0,
        tiled=True,
    ).astype(jnp.float32)
    grad_in_one, gain_one_grad, shift_one_grad = norm_backward(
        grad_normed_one, scaled_one, inverse_one, norm1_gain.astype(jnp.float32)
    )
    grad_shifted = grad_middle + grad_in_one
    lead_grad = jnp.dot(
        onehot.T,
        jnp.sum(grad_shifted, axis=0),
        precision=lax.Precision.HIGHEST,
        preferred_element_type=jnp.float32,
    )
    small_grads = jnp.stack(
        [gain_one_grad, shift_one_grad, out_bias_grad, gain_two_grad, shift_two_grad, fc2_bias_grad]
    )
    lead_grad, small_grads = lax.psum((lead_grad, small_grads), ("dp", "mp"))
    qkv_grad, qv_bias_grad, out_grad, fc1_grad, fc1_bias_grad, fc2_grad = (
        lax.psum(qkv_grad.astype(jnp.bfloat16), "dp").astype(jnp.float32),
        lax.psum(qv_bias_grad.astype(jnp.bfloat16), "dp").astype(jnp.float32),
        lax.psum(out_grad.astype(jnp.bfloat16), "dp").astype(jnp.float32),
        lax.psum(fc1_grad.astype(jnp.bfloat16), "dp").astype(jnp.float32),
        lax.psum(fc1_bias_grad.astype(jnp.bfloat16), "dp").astype(jnp.float32),
        lax.psum(fc2_grad.astype(jnp.bfloat16), "dp").astype(jnp.float32),
    )
    block_output = jnp.swapaxes(output, 0, 1).astype(jnp.bfloat16)
    input_grad = jnp.swapaxes(grad_shifted, 0, 1)
    return (
        block_output,
        input_grad,
        lead_grad,
        small_grads[0],
        small_grads[1],
        qkv_grad,
        qv_bias_grad,
        out_grad,
        small_grads[2],
        small_grads[3],
        small_grads[4],
        fc1_grad,
        fc1_bias_grad,
        fc2_grad,
        small_grads[5],
    )


F32 = jnp.float32
BF16 = jnp.bfloat16
NN = (((1,), (0,)), ((), ()))
NT = (((1,), (1,)), ((), ()))
TN = (((0,), (0,)), ((), ()))
MIB = 1 << 20


def dot(left, right, dims):
    return lax.dot_general(left, right, dims, preferred_element_type=F32)


def whole(array):
    return pl.BlockSpec(array.shape, lambda *_: (0,) * array.ndim, pipeline_mode=pl.Buffered(1))


def kernel_call(body, name, grid, scalars, ins, outs, scratch=(), vmem=32, time=6, pinned=(), alias=None):
    spec = pltpu.PrefetchScalarGridSpec(
        num_scalar_prefetch=len(scalars),
        grid=grid,
        in_specs=[spec for _, spec in ins],
        out_specs=[spec for _, spec in outs],
        scratch_shapes=list(scratch),
    )
    return pl.pallas_call(
        body,
        out_shape=[shape for shape, _ in outs],
        grid_spec=spec,
        compiler_params=pltpu.CompilerParams(vmem_limit_bytes=vmem * MIB),
        input_output_aliases={} if alias is None else {len(scalars) + alias: 0},
        cost_estimate=pl.CostEstimate(flops=MIB, transcendentals=0, bytes_accessed=int(time * 2 * MIB)),
        name=name,
    )(
        *scalars,
        *[
            pltpu.with_memory_space_constraint(array, pltpu.HBM) if k in pinned else array
            for k, (array, _) in enumerate(ins)
        ],
    )


def struct(shape, dtype=BF16):
    return jax.ShapeDtypeStruct(shape, dtype)


def centred(values):
    center = values - jnp.mean(values, axis=-1, keepdims=True)
    inverse = lax.rsqrt(jnp.mean(center * center, axis=-1, keepdims=True) + EPS)
    return center * inverse, inverse


def norm_input_grad(grad_out, scaled, inverse, gain):
    grad_scaled = grad_out * gain
    grad_mean = jnp.mean(grad_scaled, axis=-1, keepdims=True)
    cross_mean = jnp.mean(grad_scaled * scaled, axis=-1, keepdims=True)
    return inverse * (grad_scaled - grad_mean - scaled * cross_mean)


def column_sum(values):
    return jnp.sum(values, axis=0, keepdims=True)


def chunk_of(nat_ref, index, size):
    return pl.ds(pl.multiple_of(nat_ref[index] * size, size), size)


def attention_forward_kernel(block, qkv_ref, out_ref, power_ref, inverse_ref):
    rows_all = qkv_ref.shape[1]
    steps = [(head, start) for head in range(2) for start in range(0, rows_all, block)]

    def scores_of(head, start):
        lanes = slice(HD * head, HD * head + HD)
        query = qkv_ref[0, start : start + block, lanes] * BF16(0.125)
        return dot(qkv_ref[1, :, lanes], query, NT)

    outs = [[], []]
    ahead = scores_of(*steps[0])
    for k, (head, start) in enumerate(steps):
        scores = ahead
        if k + 1 < len(steps):
            ahead = scores_of(*steps[k + 1])
        lanes = slice(HD * head, HD * head + HD)
        rows = slice(start, start + block)
        powers = jnp.exp2((scores - jnp.max(scores, axis=0, keepdims=True)) * 1.4426950408889634)
        inverse = 1.0 / jnp.sum(powers, axis=0, keepdims=True)
        power_low = powers.astype(BF16)
        power_ref[head, :, rows] = power_low
        inverse_ref[0, head : head + 1, rows] = inverse
        outs[head].append(dot(qkv_ref[2, :, lanes], power_low, TN) * inverse)
    heads = [jnp.concatenate(parts, axis=1) for parts in outs]
    out_ref[...] = jnp.concatenate(heads, axis=0).T.astype(BF16)


def attend(qkv):
    _, rows, width = qkv.shape
    pairs = width // (2 * HD)
    return kernel_call(
        functools.partial(attention_forward_kernel, min(512, rows)),
        "attention_forward",
        (pairs,),
        [],
        [(qkv, pl.BlockSpec((3, rows, 2 * HD), lambda j: (0, 0, j)))],
        [
            (struct((rows, width)), pl.BlockSpec((rows, 2 * HD), lambda j: (0, j))),
            (pltpu.HBM((2 * pairs, rows, rows), BF16), pl.BlockSpec((2, rows, rows), lambda j: (j, 0, 0))),
            (struct((pairs, 2, rows), F32), pl.BlockSpec((1, 2, rows), lambda j: (j, 0, 0))),
        ],
        vmem=28,
        time=4 * pairs,
        pinned=[0],
    )


def attention_backward_kernel(block, qkv_ref, power_ref, inverse_ref, out_ref, grad_ref, dqkv_ref, sums_ref):
    rows_all = qkv_ref.shape[1]
    out_t = out_ref[...].astype(F32).T
    grad_t = grad_ref[...].astype(F32).T
    for head in range(2):
        lanes = slice(HD * head, HD * head + HD)
        inverse = inverse_ref[0, head : head + 1, :]
        grad_head = grad_t[lanes]
        inner = jnp.sum(grad_head * out_t[lanes], axis=0, keepdims=True) * inverse
        grad_scaled = grad_head * inverse
        grad_low_t = grad_scaled.astype(BF16)
        grad_low = grad_scaled.T.astype(BF16)
        query = qkv_ref[0, :, lanes] * BF16(0.125)
        key = qkv_ref[1, :, lanes]
        value = qkv_ref[2, :, lanes]
        key_t = key.T
        key_grad = value_grad = None
        query_grads = []
        for start in range(0, rows_all, block):
            rows = slice(start, start + block)
            power = power_ref[head, :, rows]
            grad_power = dot(value, grad_low_t[:, rows], NN) - inner[:, rows]
            grad_scores = (power.astype(F32) * grad_power).astype(BF16)
            key_part = dot(grad_scores, query[rows], NN)
            value_part = dot(power, grad_low[rows], NN)
            key_grad = key_part if key_grad is None else key_grad + key_part
            value_grad = value_part if value_grad is None else value_grad + value_part
            query_grads.append(dot(key_t, grad_scores, NN))
        sums_ref[0, :, lanes] = jnp.concatenate(query_grads, axis=1).T * 0.125
        sums_ref[1, :, lanes] = key_grad
        sums_ref[2, :, lanes] = value_grad
    dqkv_ref[...] = sums_ref[...].astype(BF16)


def attend_back(first, count, qkv, powers, inverse, attended, grad_attended):
    _, rows, width = qkv.shape
    block = (3, rows, 2 * HD)
    flat = pl.BlockSpec((rows, 2 * HD), lambda j: (0, j + first))
    return kernel_call(
        functools.partial(attention_backward_kernel, min(512, rows)),
        "attention_backward",
        (count,),
        [],
        [
            (qkv, pl.BlockSpec(block, lambda j: (0, 0, j + first))),
            (powers, pl.BlockSpec((2, rows, rows), lambda j: (j + first, 0, 0))),
            (inverse, pl.BlockSpec((1, 2, rows), lambda j: (j + first, 0, 0))),
            (attended, flat),
            (grad_attended, flat),
        ],
        [(struct((3, rows, 2 * HD * count)), pl.BlockSpec(block, lambda j: (0, 0, j)))],
        [pltpu.VMEM(block, F32)],
        vmem=28,
        time=5.5 * count,
        pinned=range(5),
    )[0]


def project_own_kernel(at_ref, tokens_ref, recv_ref, lead_ref, gain_ref, shift_ref, weight_ref, bias_ref, rows_ref, normed_ref, heads_ref):
    own = pl.program_id(0) < pl.num_programs(0) // 2
    tokens = jnp.where(own, tokens_ref[0].astype(F32), recv_ref[...].astype(F32))
    rows_ref[...] = tokens.astype(BF16)
    scaled, _ = centred(tokens + lead_ref[...])
    normed = (scaled * gain_ref[...] + shift_ref[...]).astype(BF16)
    normed_ref[...] = normed
    for c in range(3):
        heads_ref[c] = (dot(normed, weight_ref[c], NN) + bias_ref[c : c + 1]).astype(BF16)


def project_own(at, tokens, recv, lead, gain, shift, weight, bias, chunk):
    half, width = tokens.shape[1:]
    heads = weight.shape[2]
    steps = half // chunk
    row = pl.BlockSpec((chunk, width), lambda j, at: (j, 0))
    return kernel_call(
        project_own_kernel,
        "project_own",
        (2 * steps,),
        [at],
        [
            (tokens, pl.BlockSpec((1, chunk, width), lambda j, at: (at[0], jnp.minimum(j, steps - 1), 0))),
            (recv, pl.BlockSpec((chunk, width), lambda j, at: (jnp.maximum(j - steps, 0), 0))),
            *[(v, whole(v)) for v in (lead, gain, shift, weight, bias)],
        ],
        [
            (struct((2 * half, width)), row),
            (struct((2 * half, width)), row),
            (pltpu.HBM((3, 2 * half, heads), BF16), pl.BlockSpec((3, chunk, heads), lambda j, at: (0, j, 0))),
        ],
        pinned=[0, 1, 5],
    )


def project_far_kernel(nat_ref, normed_ref, bias_ref, *refs):
    *pieces, heads_ref = refs
    size = pieces[0].shape[1]
    total = bias_ref[0]
    for k, piece in enumerate(pieces):
        total = total + dot(normed_ref[:, chunk_of(nat_ref, k, size)], piece[0], NN)
    heads_ref[0] = total.astype(BF16)


def project_far(nat, normed, bias, pieces):
    rows = normed.shape[0]
    heads = pieces[0].shape[2]
    first = lambda j, nat: (j, 0, 0)
    return kernel_call(
        project_far_kernel,
        "project_far",
        (3,),
        [nat],
        [
            (normed, whole(normed)),
            (bias[:, None], pl.BlockSpec((1, 1, heads), first)),
            *[(p, pl.BlockSpec((1, *p.shape[1:]), first)) for p in pieces],
        ],
        [(pltpu.HBM((3, rows, heads), BF16), pl.BlockSpec((1, rows, heads), first))],
    )[0]


def middle_kernel(nat_ref, own_ref, far_ref, weight_ref, rows_ref, lead_ref, bias_ref, gain_ref, shift_ref, *refs):
    *pieces, middle_ref, normed_ref = refs
    total = dot(own_ref[...], weight_ref[...], NN)
    for k, piece in enumerate(pieces):
        total = total + dot(far_ref[:, chunk_of(nat_ref, k, piece.shape[0])], piece[...], NN)
    middle = rows_ref[...].astype(F32) + lead_ref[...] + total + bias_ref[...]
    middle_ref[...] = middle
    scaled, _ = centred(middle)
    normed_ref[...] = (scaled * gain_ref[...] + shift_ref[...]).astype(BF16)


def middle_layer(nat, own, far, weight, pieces, rows, lead, bias, gain, shift, chunk):
    count, width = rows.shape
    row = pl.BlockSpec((chunk, width), lambda j, nat: (j, 0))
    heads = pl.BlockSpec((chunk, own.shape[1]), lambda j, nat: (j, 0))
    return kernel_call(
        middle_kernel,
        "middle_layer",
        (count // chunk,),
        [nat],
        [(own, heads), (far, heads), (weight, whole(weight)), (rows, row)]
        + [(v, whole(v)) for v in (lead, bias, gain, shift, *pieces)],
        [(pltpu.HBM((count, width), F32), row), (struct((count, width)), row)],
        pinned=[2, 3],
    )


def gelu_store(pre_act, rows, hidden_ref, slope_ref):
    cdf = 0.5 * (1.0 + lax.erf(pre_act * 0.7071067811865476))
    hidden_ref[rows] = (pre_act * cdf).astype(BF16)
    density = jnp.exp(-0.5 * pre_act * pre_act) * 0.3989422804014327
    slope_ref[rows] = (cdf + pre_act * density).astype(BF16)


def hidden_kernel(block, nat_ref, normed_ref, bias_ref, *refs):
    *pieces, hidden_ref, slope_ref = refs
    size = pieces[0].shape[0]
    for start in range(0, normed_ref.shape[0], block):
        rows = slice(start, start + block)
        pre_act = bias_ref[...]
        for k, piece in enumerate(pieces):
            lanes = slice(None) if len(pieces) == 1 else chunk_of(nat_ref, k, size)
            pre_act = pre_act + dot(normed_ref[rows, lanes], piece[...], NN)
        gelu_store(pre_act, rows, hidden_ref, slope_ref)


def hidden_layer(nat, normed, bias, pieces, chunk):
    rows = normed.shape[0]
    units = pieces[0].shape[1]
    tile = min(512, units)
    column = lambda j, nat: (0, j)
    return kernel_call(
        functools.partial(hidden_kernel, chunk),
        "hidden_layer",
        (units // tile,),
        [nat],
        [(normed, whole(normed)), (bias, pl.BlockSpec((1, tile), column))]
        + [(p, pl.BlockSpec((p.shape[0], tile), column)) for p in pieces],
        [(struct((rows, units)), pl.BlockSpec((rows, tile), column))] * 2,
        vmem=24,
        time=10,
        pinned=range(2, 2 + len(pieces)),
    )


def product_kernel(outs, add_count, by_step, _, left_ref, right_ref, *refs):
    adds, out_refs = refs[:add_count], refs[add_count:]
    stacked = len(right_ref.shape) == 3
    value = dot(left_ref[...], right_ref[0] if stacked else right_ref[...], TN)
    for add in adds:
        value = value + (add[0] if stacked else add[...]).astype(F32)
    value = value.astype(BF16)
    if stacked:
        out_refs[0][0] = value
    elif outs == 1:
        out_refs[0][...] = value
    elif by_step:
        for k, out_ref in enumerate(out_refs):

            @pl.when(pl.program_id(0) == k)
            def _(out_ref=out_ref):
                out_ref[...] = value
    else:
        size = value.shape[0] // outs
        for k, out_ref in enumerate(out_refs):
            out_ref[...] = value[k * size : (k + 1) * size]


def grad_right_half(half, left, right, *add):
    rows, columns = left.shape
    kept = right.shape[1] // 2
    tile = columns // 2
    out_spec = pl.BlockSpec((tile, kept), lambda j, half: (j, 0))
    outs = 2 if add else 1
    split = [(struct((tile, kept)), pl.BlockSpec((tile, kept), lambda j, half: (0, 0)))] * 2
    result = kernel_call(
        functools.partial(product_kernel, outs, len(add), True),
        "grad_right_half",
        (2,),
        [half],
        [
            (left, pl.BlockSpec((rows, tile), lambda j, half: (0, j))),
            (right, pl.BlockSpec((rows, kept), lambda j, half: (0, half[0]))),
        ]
        + [(a, out_spec) for a in add],
        split if add else [(struct((columns, kept)), out_spec)],
        vmem=20,
        time=3,
    )
    return result if add else result[0]


def grad_left_half(half, left, right, *add, split=False):
    rows = left.shape[0]
    kept = left.shape[1] // 2
    columns = right.shape[-1]
    tile = min(1024, columns)
    outs = 2 if split else 1
    left_spec = pl.BlockSpec((rows, kept), lambda j, half: (0, half[0]))
    if right.ndim == 3:
        grid, out_shape = (right.shape[0],), (right.shape[0], kept, columns)
        right_spec = pl.BlockSpec((1, rows, columns), lambda j, half: (j, 0, 0))
        add_spec = out_spec = pl.BlockSpec((1, kept, columns), lambda j, half: (j, 0, 0))
    else:
        grid, out_shape = (columns // tile,), (kept // outs, columns)
        right_spec = pl.BlockSpec((rows, tile), lambda j, half: (0, j))
        add_spec = pl.BlockSpec((kept, tile), lambda j, half: (0, j))
        out_spec = pl.BlockSpec((kept // outs, tile), lambda j, half: (0, j))
    result = kernel_call(
        functools.partial(product_kernel, outs, len(add), False),
        "grad_left_half",
        grid,
        [half],
        [(left, left_spec), (right, right_spec)] + [(a, add_spec) for a in add],
        [(struct(out_shape), out_spec)] * outs,
        vmem=20,
        time=3,
    )
    return result if split else result[0]


def term(array, at=None, size=None, column=None):
    block, index = list(array.shape), [None] * array.ndim
    if size is not None:
        block[-2], index[-2] = size, at
    if column is not None:
        block[-1], index[-1] = array.shape[-1] // 2, lambda _: column

    def index_map(_, flags):
        return tuple(0 if f is None else f(flags) for f in index)

    return array, pl.BlockSpec(tuple(block), index_map)


def combine_kernel(plan, flags_ref, *refs):
    count = sum(terms for parts in plan for _, _, terms in parts)
    ins, outs = list(refs[:count]), refs[count:]
    for parts, out_ref in zip(plan, outs):
        for lead, row, terms in parts:
            value = None
            for ref in ins[:terms]:
                part = ref[...] if terms == 1 else ref[...].astype(F32)
                value = part if value is None else value + part
            ins = ins[terms:]
            value = value.astype(BF16)
            if lead is not None:
                out_ref[lead] = value
            elif row is not None:
                size = value.shape[-2]
                start = row if isinstance(row, int) else pl.multiple_of(row(flags_ref) * size, size)
                where = (slice(None),) * (value.ndim - 2) + (pl.ds(start, size), slice(None))
                out_ref[where] = value
            else:
                out_ref[...] = value


def combine(flags, *outs):
    ins = [t for _, parts in outs for _, _, terms in parts for t in terms]
    plan = [[(lead, row, len(terms)) for lead, row, terms in parts] for _, parts in outs]

    def full(shape):
        return pl.BlockSpec(shape, lambda *_: (0,) * len(shape))

    return kernel_call(
        functools.partial(combine_kernel, plan),
        "combine",
        (1,),
        [flags],
        ins,
        [(struct(shape), full(shape)) for shape, _ in outs],
        vmem=32,
        time=3,
    )


def summed(shape, *terms):
    return shape, [(None, None, terms)]


def pre_grad_store(grad, slope_ref, pre_ref, sum_ref):
    pre = (grad * slope_ref[...].astype(F32)).astype(BF16)
    pre_ref[...] = pre
    sum_ref[...] = column_sum(pre.astype(F32))


def pre_grad_own_kernel(low_ref, weight_ref, slope_ref, pre_ref, sum_ref):
    pre_grad_store(dot(low_ref[...], weight_ref[...], NT), slope_ref, pre_ref, sum_ref)


def pre_grad_own(low, weight, slope):
    rows, width = low.shape
    units = weight.shape[0]
    tile = min(512, units)
    column = lambda j: (0, j)
    return kernel_call(
        pre_grad_own_kernel,
        "pre_grad_own",
        (units // tile,),
        [],
        [
            (low, whole(low)),
            (weight, pl.BlockSpec((tile, width), lambda j: (j, 0))),
            (slope, pl.BlockSpec((rows, tile), column)),
        ],
        [
            (struct((rows, units)), pl.BlockSpec((rows, tile), column)),
            (struct((1, units), F32), pl.BlockSpec((1, tile), column)),
        ],
        vmem=24,
        pinned=[1],
    )


def pre_grad_far_kernel(per, nat_ref, low_ref, slope_ref, *refs):
    *pieces, pre_ref, sum_ref = refs
    for k, piece in enumerate(pieces):

        @pl.when(pl.program_id(0) // per == k)
        def _(piece=piece):
            pre_grad_store(dot(low_ref[...], piece[...], NT), slope_ref, pre_ref, sum_ref)


def pre_grad_far(nat, low, pieces, slope):
    rows, width = low.shape
    size = pieces[0].shape[0]
    tile = min(512, size)
    per = size // tile
    units = size * len(pieces)
    column = lambda j, nat: (0, nat[j // per] * per + j % per)

    def piece_spec(k):
        return pl.BlockSpec((tile, width), lambda j, nat: (jnp.clip(j - k * per, 0, per - 1), 0))

    return kernel_call(
        functools.partial(pre_grad_far_kernel, per),
        "pre_grad_far",
        (len(pieces) * per,),
        [nat],
        [(low, whole(low)), (slope, pl.BlockSpec((rows, tile), column))]
        + [(p, piece_spec(k)) for k, p in enumerate(pieces)],
        [
            (struct((rows, units)), pl.BlockSpec((rows, tile), column)),
            (struct((1, units), F32), pl.BlockSpec((1, tile), column)),
        ],
        vmem=24,
        time=8,
        pinned=range(2, 2 + len(pieces)),
    )


def add_sums(sums_ref, rows):
    @pl.when(pl.program_id(0) == 0)
    def _():
        sums_ref[...] = jnp.zeros_like(sums_ref)

    for k, row in enumerate(rows):
        sums_ref[k : k + 1, :] += row


def middle_grad_kernel(
    nat_ref, at_ref, own_ref, far_ref, weight_ref, middle_ref, cot_ref, recv_ref, loss_ref, gain_ref, *refs
):
    *pieces, grad_ref, low_ref, sums_ref, total_ref = refs
    total_ref[...] = dot(own_ref[...], weight_ref[...], NT)
    for k, piece in enumerate(pieces):
        total_ref[:, chunk_of(nat_ref, k, piece.shape[0])] += dot(far_ref[...], piece[...], NT)
    grad = total_ref[...]
    scaled, inverse = centred(middle_ref[...])
    mine = pl.program_id(0) < pl.num_programs(0) // 2
    top = jnp.where(mine, cot_ref[0].astype(F32), recv_ref[...].astype(F32)) * loss_ref[...]
    grad_middle = top + norm_input_grad(grad, scaled, inverse, gain_ref[...])
    grad_ref[...] = grad_middle
    low_ref[...] = grad_middle.astype(BF16)
    add_sums(
        sums_ref,
        [column_sum(grad * scaled), column_sum(grad), column_sum(grad_middle), column_sum(top)],
    )


def middle_grad(nat, at, own, far, weight, pieces, middle, cot, recv, loss, gain, chunk):
    count, width = middle.shape
    row = pl.BlockSpec((chunk, width), lambda j, *_: (j, 0))
    units = pl.BlockSpec((chunk, own.shape[1]), lambda j, *_: (j, 0))
    steps = count // chunk // 2
    return kernel_call(
        middle_grad_kernel,
        "middle_grad",
        (count // chunk,),
        [nat, at],
        [
            (own, units),
            (far, units),
            (weight, whole(weight)),
            (middle, row),
            (cot, pl.BlockSpec((1, chunk, width), lambda j, nat, at: (at[0], jnp.minimum(j, steps - 1), 0))),
            (recv, pl.BlockSpec((chunk, width), lambda j, *_: (jnp.maximum(j - steps, 0), 0))),
        ]
        + [(v, whole(v)) for v in (loss, gain, *pieces)],
        [
            (struct((count, width), F32), row),
            (struct((count, width)), row),
            (struct((8, width), F32), pl.BlockSpec((8, width), lambda j, *_: (0, 0))),
        ],
        [pltpu.VMEM((chunk, width), F32)],
        time=14,
        pinned=[2, 3, 4, 5, *range(8, 8 + len(pieces))],
    )


def attended_grad_kernel(nat_ref, low_ref, weight_ref, *refs):
    *pieces, own_ref, far_ref = refs
    own_ref[...] = dot(low_ref[...], weight_ref[...], NT).astype(BF16)
    for k, piece in enumerate(pieces):
        far_ref[:, chunk_of(nat_ref, k, piece.shape[0])] = dot(low_ref[...], piece[...], NT).astype(BF16)


def attended_grad(nat, low, weight, pieces, chunk):
    count, width = low.shape
    heads = weight.shape[0]
    out = (struct((count, heads)), pl.BlockSpec((chunk, heads), lambda j, nat: (j, 0)))
    return kernel_call(
        attended_grad_kernel,
        "attended_grad",
        (count // chunk,),
        [nat],
        [(low, pl.BlockSpec((chunk, width), lambda j, nat: (j, 0)))] + [(v, whole(v)) for v in (weight, *pieces)],
        [out, out],
        pinned=range(1, 2 + len(pieces)),
    )


def output_own_kernel(own_ref, weight_ref, out_ref):
    out_ref[...] = dot(own_ref[...], weight_ref[...], NN)


def output_own(first, count, own, weight, chunk):
    units = own.shape[1]
    width = weight.shape[1]
    return kernel_call(
        output_own_kernel,
        "output_own",
        (count,),
        [],
        [(own, pl.BlockSpec((chunk, units), lambda j: (j + first, 0))), (weight, whole(weight))],
        [(struct((count * chunk, width), F32), pl.BlockSpec((chunk, width), lambda j: (j, 0)))],
        vmem=20,
        time=4,
        pinned=range(2),
    )[0]


def output_kernel(nat_ref, far_ref, own_ref, middle_ref, bias_ref, *refs):
    *pieces, out_ref = refs
    total = own_ref[...]
    for k, piece in enumerate(pieces):
        total = total + dot(far_ref[:, chunk_of(nat_ref, k, piece.shape[0])], piece[...], NN)
    out_ref[...] = (middle_ref[...] + total + bias_ref[...]).astype(BF16)


def output_layer(nat, first, count, far, own, pieces, middle, bias, chunk):
    width = middle.shape[1]
    row = pl.BlockSpec((chunk, width), lambda j, nat: (j + first, 0))
    here = pl.BlockSpec((chunk, width), lambda j, nat: (j, 0))
    return kernel_call(
        output_kernel,
        "output_layer",
        (count,),
        [nat],
        [(far, pl.BlockSpec((chunk, far.shape[1]), lambda j, nat: (j + first, 0))), (own, here), (middle, row)]
        + [(v, whole(v)) for v in (bias, *pieces)],
        [(struct((count * chunk, width)), pl.BlockSpec((chunk, width), lambda j, nat: (j, 0)))],
        vmem=24,
        time=6,
        pinned=range(4 + len(pieces)),
    )[0]


def input_grad_kernel(own_count, nat_ref, far_ref, weight_ref, rows_ref, lead_ref, grad_ref, gain_ref, *refs):
    owns, refs = refs[:own_count], refs[own_count:]
    *pieces, out_ref, low_ref, sums_ref, total_ref = refs
    total = None
    at = 0
    for own in owns:
        size = own.shape[2]
        for c in range(3):
            part = dot(own[c], weight_ref[c, :, at : at + size], NT)
            total = part if total is None else total + part
        at += size
    total_ref[...] = total
    for k, piece in enumerate(pieces):
        part = dot(far_ref[0], piece[0], NT) + dot(far_ref[1], piece[1], NT) + dot(far_ref[2], piece[2], NT)
        total_ref[:, chunk_of(nat_ref, k, piece.shape[1])] += part
    grad = total_ref[...]
    scaled, inverse = centred(rows_ref[...].astype(F32) + lead_ref[...])
    grad_shifted = grad_ref[...] + norm_input_grad(grad, scaled, inverse, gain_ref[...])
    out_ref[...] = grad_shifted
    low_ref[...] = grad_shifted.astype(BF16)
    bias_rows = [
        jnp.concatenate([column_sum(d[c].astype(F32)) for d in (*owns, far_ref)], axis=1) for c in (0, 2)
    ]
    add_sums(
        sums_ref, [column_sum(grad * scaled), column_sum(grad), column_sum(grad_shifted), *bias_rows]
    )


def input_grads(nat, owns, far, weight, pieces, rows, lead, grad_middle, gain, chunk):
    count, width = rows.shape
    row = pl.BlockSpec((chunk, width), lambda j, nat: (j, 0))
    heads = lambda d: pl.BlockSpec((3, chunk, d.shape[2]), lambda j, nat: (0, j, 0))
    steps = count // chunk
    half = pl.BlockSpec((chunk, width), lambda j, nat: (jnp.maximum(j - steps // 2, 0), 0))
    return kernel_call(
        functools.partial(input_grad_kernel, len(owns)),
        "input_grads",
        (steps,),
        [nat],
        [
            (far, heads(far)),
            (weight, whole(weight)),
            (rows, row),
            (lead, whole(lead)),
            (grad_middle, row),
            (gain, whole(gain)),
        ]
        + [(d, heads(d)) for d in owns]
        + [(p, whole(p)) for p in pieces],
        [
            (struct((count, width), F32), row),
            (struct((count // 2, width)), half),
            (struct((8, width), F32), pl.BlockSpec((8, width), lambda j, nat: (0, 0))),
        ],
        [pltpu.VMEM((chunk, width), F32)],
        time=14,
        pinned=[0, 1, 2, 4, *range(6, 6 + len(owns) + len(pieces))],
    )


def pack_kernel(buckets, flags_ref, one_ref, two_ref, own_ref, far_ref, out_ref):
    width = one_ref.shape[1]
    half = width // 2
    first = flags_ref[0] == 0
    rows = lax.broadcasted_iota(jnp.int32, (buckets, width), 0)
    out_ref[:buckets] = jnp.where(rows == flags_ref[7], one_ref[2:3], 0.0)
    out_ref[buckets : buckets + 2] = one_ref[:2]
    out_ref[buckets + 2 : buckets + 6] = two_ref[:4]
    bias = one_ref[3:5]
    swapped = jnp.concatenate([bias[:, half:], bias[:, :half]], axis=1)
    out_ref[buckets + 6 : buckets + 8] = jnp.where(first, bias, swapped)
    own, far = own_ref[...], far_ref[...]
    count = own.shape[1] // width
    for k in range(count):
        columns = slice(k * width, (k + 1) * width)
        low, high = own[:, columns], far[:, columns]
        out_ref[buckets + 8 + k : buckets + 9 + k] = jnp.where(first, low, high)
        out_ref[buckets + 8 + count + k : buckets + 9 + count + k] = jnp.where(first, high, low)


def pack_vectors(flags, buckets, one, two, own, far):
    width = one.shape[1]
    rows = buckets + 8 + 2 * own.shape[1] // width
    return kernel_call(
        functools.partial(pack_kernel, buckets),
        "pack_vectors",
        (1,),
        [flags],
        [(v, whole(v)) for v in (one, two, own, far)],
        [(struct((rows, width), F32), pl.BlockSpec((rows, width), lambda *_: (0, 0)))],
        vmem=8,
        time=1,
    )[0]


def finish_turned_kernel(_, *refs):
    *pieces, out_ref = refs
    for k, piece in enumerate(pieces):

        @pl.when(pl.program_id(0) == k)
        def _(piece=piece):
            out_ref[...] = piece[...].astype(F32).T


def finish_turned(nat, pieces):
    rows, columns = pieces[0].shape
    return kernel_call(
        finish_turned_kernel,
        "finish",
        (4,),
        [nat],
        [(p, whole(p)) for p in pieces],
        [(struct((columns, 4 * rows), F32), pl.BlockSpec((columns, rows), lambda s, nat: (0, nat[s])))],
        vmem=16,
        time=2,
    )[0]


def source_spec(block, which, steps, place):
    def index(s, j, *_):
        return place(jnp.where(s == which, j, jnp.where(s < which, 0, steps - 1)))

    return pl.BlockSpec(block, index)


def finish_rows_kernel(_, *refs):
    *pieces, out_ref = refs
    for k, piece in enumerate(pieces):

        @pl.when(pl.program_id(0) == k)
        def _(piece=piece):
            out_ref[...] = piece[0].astype(F32)


def finish_rows(at, pieces):
    halves, rows, columns = pieces[0].shape
    block = (1, rows, columns)
    return kernel_call(
        finish_rows_kernel,
        "finish",
        (2, halves),
        [at],
        [(p, source_spec(block, k, halves, lambda j: (j, 0, 0))) for k, p in enumerate(pieces)],
        [
            (
                struct((2 * halves * rows, columns), F32),
                pl.BlockSpec((rows, columns), lambda s, j, at: (at[s] * halves + j, 0)),
            )
        ],
        vmem=20,
        time=5,
    )[0]


def finish_columns_kernel(at_ref, mine_ref, theirs_ref, out_ref):
    first = at_ref[0] == 0
    one, two = mine_ref[0].astype(F32), theirs_ref[0].astype(F32)
    columns = one.shape[1]
    out_ref[:, :columns] = jnp.where(first, one, two)
    out_ref[:, columns:] = jnp.where(first, two, one)


def finish_columns(at, pieces):
    halves, rows, columns = pieces[0].shape
    tile = min(512, rows)
    per = rows // tile
    spec = pl.BlockSpec((1, tile, columns), lambda j, at: (j // per, j % per, 0))
    return kernel_call(
        finish_columns_kernel,
        "finish",
        (halves * per,),
        [at],
        [(p, spec) for p in pieces],
        [(struct((halves * rows, 2 * columns), F32), pl.BlockSpec((tile, 2 * columns), lambda j, at: (j, 0)))],
        vmem=20,
        time=5,
    )[0]


def finish_stack_kernel(count, at_ref, *refs):
    pieces, out_ref = refs[:count], refs[-1]
    for k, piece in enumerate(pieces):

        @pl.when(pl.program_id(0) == k)
        def _(piece=piece):
            out_ref[0] = jnp.concatenate([piece[0, 0].astype(F32), piece[1, 0].astype(F32)], axis=1)


def finish_stack(nat, first, pieces, *so_far):
    _, stack, rows, columns = pieces[0].shape
    block = (2, 1, rows, columns)
    count = len(pieces)
    return kernel_call(
        functools.partial(finish_stack_kernel, count),
        "finish",
        (count, stack),
        [nat],
        [(p, source_spec(block, k, stack, lambda j: (0, j, 0, 0))) for k, p in enumerate(pieces)]
        + [(v, pl.BlockSpec(memory_space=pl.ANY)) for v in so_far],
        [
            (
                struct((stack, 4 * rows, 2 * columns), F32),
                pl.BlockSpec((1, rows, 2 * columns), lambda s, j, nat: (j, nat[first + s], 0)),
            )
        ],
        vmem=16,
        time=3,
        alias=count if so_far else None,
    )[0]


def hold(*values):
    return lax.optimization_barrier(values)


def fast_body(
    tokens,
    cotangent,
    buckets,
    counts,
    lead_table,
    norm1_gain,
    norm1_shift,
    w_qkv,
    qv_bias,
    w_out,
    out_bias,
    norm2_gain,
    norm2_shift,
    w_fc1,
    fc1_bias,
    w_fc2,
    fc2_bias,
):
    replicas = lax.axis_size("dp")
    levels = replicas.bit_length() - 1
    dp_at, mp_at = lax.axis_index("dp"), lax.axis_index("mp")
    bits = [(dp_at >> level) & 1 for level in range(levels)]

    def over_x(value):
        return lax.ppermute(value, "mp", [(0, 1), (1, 0)])

    def over(level, value):
        return over_mask(1 << level, value)

    def over_mask(mask, value):
        return lax.ppermute(value, "dp", [(i, i ^ mask) for i in range(replicas)])

    def joined(bit, mine, theirs, axis=0):
        return jnp.where(
            bit == 0,
            jnp.concatenate([mine, theirs], axis),
            jnp.concatenate([theirs, mine], axis),
        )

    def part(value, index, count, axis=0):
        size = value.shape[axis] // count
        return lax.dynamic_slice_in_dim(value, index * size, size, axis)

    half_rows, width = tokens.shape[1:]
    heads_width = w_qkv.shape[2]
    units = w_fc1.shape[1]
    chunk = 256
    core, side = bits[0], bits[1]
    bucket = lax.dynamic_index_in_dim(buckets, mp_at, 0, keepdims=False)
    at = jnp.stack([mp_at, core, 1 - core, side, 1 - side, bits[2], bits[3], bucket]).astype(jnp.int32)
    mine = core * 2 + side
    shared_nat = jnp.stack([mine, mine ^ 1, mine ^ 2, mine ^ 3]).astype(jnp.int32)
    core_first_nat = jnp.stack([mine, mine ^ 2, mine ^ 1, mine ^ 3]).astype(jnp.int32)

    def row_of(vector):
        return vector.astype(F32)[None]

    small = jnp.concatenate([qv_bias.reshape(-1), fc1_bias])
    small_rows = -(-small.shape[0] // width)
    small_rows_padded = -(-small_rows // 16) * 16
    small = jnp.pad(small, (0, small_rows_padded * width - small.shape[0])).reshape(-1, width)
    token_recv = over_x(jnp.concatenate([part(tokens, 1 - mp_at, 2)[0], small]))

    count_f = counts.astype(F32)
    loss_weight = jnp.mean(count_f) / lax.dynamic_index_in_dim(count_f, bucket, 0, keepdims=False)
    loss_row = jnp.broadcast_to(loss_weight, (1, width))
    lead = lax.dynamic_index_in_dim(lead_table, bucket, 0).astype(F32)
    own_qkv = jnp.transpose(w_qkv, (1, 0, 2))

    def bias_three(bias):
        bias_f = bias.astype(F32)
        return jnp.stack([bias_f[0], jnp.zeros_like(bias_f[0]), bias_f[1]])

    (
        token_recv, qkv_send, out_send, fc1_send, cot_send, fc2_send, at, shared_nat, core_first_nat, loss_row, loss_weight, lead,
        gain_one, gain_two, shift_one, shift_two, out_row, fc1_row, fc2_row, own_bias,
    ) = hold(
        token_recv,
        part(own_qkv, mine, 4, 1),
        part(w_out, core, 2),
        part(w_fc1, mine, 4),
        part(cotangent, 1 - mp_at, 2)[0],
        part(w_fc2, core, 2),
        at,
        shared_nat,
        core_first_nat,
        loss_row,
        loss_weight,
        lead,
        row_of(norm1_gain),
        row_of(norm2_gain),
        row_of(norm1_shift),
        row_of(norm2_shift),
        row_of(out_bias),
        row_of(fc1_bias),
        row_of(fc2_bias),
        bias_three(qv_bias),
    )
    keep_half, send_half, pair_nat = at[1:2], at[2:3], at[1:3]
    far_small = token_recv[half_rows:].reshape(-1)
    far_bias = bias_three(far_small[: 2 * heads_width].reshape(2, heads_width))
    far_fc1_bias = row_of(far_small[2 * heads_width : 2 * heads_width + units])

    qkv_x = over_x(qkv_send)
    rows, normed_one, own_heads = project_own(
        at[:1], tokens, token_recv, lead, gain_one, shift_one, own_qkv, own_bias, chunk
    )
    own_heads, qkv_x, out_send, fc1_send, far_bias, far_fc1_bias = hold(
        own_heads, qkv_x, out_send, fc1_send, far_bias, far_fc1_bias
    )

    qkv_y = over(1, qkv_x)
    out_x = over_x(out_send)
    fc1_x = over_x(fc1_send)
    own_attended, own_powers, own_inverse = attend(own_heads)
    own_attended, qkv_x, qkv_y, out_x = hold(own_attended, qkv_x, qkv_y, out_x)

    far_qkv = [qkv_x, qkv_y, over(0, qkv_x), over(0, qkv_y)]
    far_out = [out_x, over(0, out_x)]
    far_heads = project_far(shared_nat, normed_one, far_bias, far_qkv)
    far_heads, fc1_x, cot_send = hold(far_heads, fc1_x, cot_send)

    fc1_y = over(1, fc1_x)
    cot_recv = over_x(cot_send)
    far_attended, far_powers, far_inverse = attend(far_heads)
    middle, normed_two = middle_layer(
        pair_nat, own_attended, far_attended, w_out, far_out, rows, lead,
        out_row, gain_two, shift_two, chunk,
    )
    normed_two, fc1_x, fc1_y, cot_recv, fc2_send = hold(
        normed_two, fc1_x, fc1_y, cot_recv, fc2_send
    )

    def mine_y(flags):
        return flags[3]

    def theirs_y(flags):
        return flags[4]

    def mine_z(flags):
        return flags[5]

    def theirs_z(flags):
        return 1 - flags[5]

    def mine_z2(flags):
        return flags[6]

    def theirs_z2(flags):
        return 1 - flags[6]

    def zero(_):
        return 0

    def one(_):
        return 1

    def first_y(own_down, far_down):
        size = own_down.shape[0] // 2
        return (2 * size, own_down.shape[1]), [
            (None, 0, [term(own_down, theirs_y, size)]),
            (None, size, [term(far_down, theirs_y, size)]),
        ]

    def second_y(own_up, recv_x):
        size = own_up.shape[0] // 2
        return summed((size, own_up.shape[1]), term(own_up, theirs_y, size), term(recv_x, theirs_y, size))

    def second_x(far_down, recv_y):
        size = far_down.shape[0] // 2
        return summed((size, far_down.shape[1]), term(far_down, mine_y, size), term(recv_y, one, size))

    def z_half(which, own_up, recv_x, recv_up, own_down, recv_y, recv_down):
        size = own_up.shape[0] // 4

        def within(side_of, start=0):
            return lambda flags: (start + side_of(flags)) * 2 + which(flags)

        upper = [term(own_up, within(mine_y), size), term(recv_x, within(mine_y), size), term(recv_up, which, size)]
        lower = [term(own_down, within(mine_y), size), term(recv_y, within(zero), size), term(recv_down, which, size)]
        return (2, size, own_up.shape[1]), [(0, None, upper), (1, None, lower)]

    def z_sides(mine, recv):
        shape = list(mine.shape)
        shape[-2] *= 2
        return tuple(shape), [(None, mine_z, [term(mine)]), (None, theirs_z, [term(recv)])]

    def y_sides(mine, recv):
        shape = list(mine.shape)
        shape[-2] *= 2
        return tuple(shape), [(None, mine_y, [term(mine)]), (None, theirs_y, [term(recv)])]

    masks = {1: 8, 2: 4, 3: 12}

    def quarter_z(k):
        def index(flags):
            first = 1 - flags[5] if k & 2 else flags[5]
            second = 1 - flags[6] if k & 1 else flags[6]
            return first * 2 + second

        return index

    fc2_x = over_x(fc2_send)
    far_fc1 = [fc1_x, fc1_y, over(0, fc1_x), over(0, fc1_y)]
    cot_rows = jnp.concatenate([part(cotangent, mp_at, 2)[0], cot_recv])
    grad_low = (cot_rows.astype(F32) * loss_weight).astype(BF16)
    own_hidden, own_slope = hidden_layer(shared_nat, normed_two, fc1_row, [w_fc1], chunk)
    far_hidden, far_slope = hidden_layer(shared_nat, normed_two, far_fc1_bias, far_fc1, chunk)
    far_send = grad_right_half(send_half, far_hidden, grad_low)
    own_send = grad_right_half(send_half, own_hidden, grad_low)
    own_pre, own_fc1_bias = pre_grad_own(grad_low, w_fc2, own_slope)
    fc1_own_send = grad_left_half(send_half, normed_two, own_pre)
    far_send, own_send, fc2_x, grad_low, far_hidden, own_pre, fc1_own_send = hold(
        far_send, own_send, fc2_x, grad_low, far_hidden, own_pre, fc1_own_send
    )

    far_recv, own_recv, fc2_core, fc1_own_recv = over(0, far_send), over(0, own_send), over(0, fc2_x), over(0, fc1_own_send)
    far_up, far_down = grad_right_half(keep_half, far_hidden, grad_low, far_recv)
    own_up, own_down = grad_right_half(keep_half, own_hidden, grad_low, own_recv)
    far_up, far_down, own_up, own_down, fc2_core, fc1_own_recv = hold(
        far_up, far_down, own_up, own_down, fc2_core, fc1_own_recv
    )

    half_width = width // 2
    fc2_x1 = over_x(far_up)
    fc2_y1 = over(1, combine(at, first_y(own_down, far_down))[0])
    far_fc2 = [fc2_x, fc2_core]
    far_pre, far_fc1_bias_sum = pre_grad_far(pair_nat, grad_low, far_fc2, far_slope)
    fc1_far_send = grad_left_half(send_half, normed_two, far_pre)
    fc1_own_up, fc1_own_down = grad_left_half(keep_half, normed_two, own_pre, fc1_own_recv, split=True)
    chunks = half_rows // chunk
    mlp_low = output_own(chunks, chunks, own_hidden, w_fc2, chunk)
    fc1_far_send, fc1_own_up, fc1_own_down, fc2_x1, fc2_y1, far_pre, mlp_low = hold(
        fc1_far_send, fc1_own_up, fc1_own_down, fc2_x1, fc2_y1, far_pre, mlp_low
    )

    send_y, send_x = combine(at, second_y(own_up, fc2_x1), second_x(far_down, fc2_y1))
    fc2_y2, fc2_x2 = over(1, send_y), over_x(send_x)
    fc1_far_recv = over(0, fc1_far_send)
    grad_middle, grad_branch, sums_two = middle_grad(
        shared_nat, at[:1], own_pre, far_pre, w_fc1, far_fc1, middle, cotangent, cot_recv, loss_row, gain_two, chunk
    )
    own_grad_att, far_grad_att = attended_grad(pair_nat, grad_branch, w_out, far_out, chunk)
    out_far_send = grad_left_half(send_half, grad_branch, far_attended)
    out_own_send = grad_left_half(send_half, grad_branch, own_attended)
    fc1_far_up, fc1_far_down = grad_left_half(keep_half, normed_two, far_pre, fc1_far_recv, split=True)
    out_far_recv, out_own_recv = over(0, out_far_send), over(0, out_own_send)
    out_far_sum = grad_left_half(keep_half, grad_branch, far_attended, out_far_recv)
    out_own_sum = grad_left_half(keep_half, grad_branch, own_attended, out_own_recv)
    far_grad_att, own_grad_att, fc2_y2, fc2_x2, fc1_far_up, fc1_far_down, out_far_sum, out_own_sum = hold(
        far_grad_att, own_grad_att, fc2_y2, fc2_x2, fc1_far_up, fc1_far_down, out_far_sum, out_own_sum
    )

    fc2_terms = (own_up, fc2_x1, fc2_y2, own_down, fc2_y1, fc2_x2)
    fc2_send, fc2_mine, send_y = combine(
        at, z_half(theirs_z, *fc2_terms), z_half(mine_z, *fc2_terms), first_y(fc1_own_down, fc1_far_down)
    )
    fc1_x1, fc1_y1, fc2_recv = over_x(fc1_far_up), over(1, send_y), over(2, fc2_send)
    pairs = heads_width // (2 * HD)
    far_dqkv = attend_back(0, pairs, far_heads, far_powers, far_inverse, far_attended, far_grad_att)
    far_dqkv, own_grad_att, fc1_x1, fc1_y1, out_far_sum, fc2_recv = hold(
        far_dqkv, own_grad_att, fc1_x1, fc1_y1, out_far_sum, fc2_recv
    )

    half_rows_out = half_width // 2
    out_shape = (half_rows_out, heads_width)
    z_shape = (2, fc2_mine.shape[1] // 2, fc2_mine.shape[2])
    send_y, send_x, fc2_send, fc2_mine = combine(
        at,
        second_y(fc1_own_up, fc1_x1),
        second_x(fc1_far_down, fc1_y1),
        summed(z_shape, term(fc2_mine, theirs_z2, z_shape[1]), term(fc2_recv, theirs_z2, z_shape[1])),
        summed(z_shape, term(fc2_mine, mine_z2, z_shape[1]), term(fc2_recv, mine_z2, z_shape[1])),
    )
    fc1_y2, fc1_x2, fc2_recv, out_recv = over(1, send_y), over_x(send_x), over(3, fc2_send), over_x(out_far_sum)
    qkv_far_recv = over(0, grad_left_half(send_half, normed_one, far_dqkv))
    qkv_far_keep = grad_left_half(keep_half, normed_one, far_dqkv)
    own_a = attend_back(0, pairs // 2, own_heads, own_powers, own_inverse, own_attended, own_grad_att)
    own_a_send = grad_left_half(send_half, normed_one, own_a)
    own_a_send, own_grad_att, fc1_y2, fc1_x2, out_recv, qkv_far_recv, qkv_far_keep, fc2_recv = hold(
        own_a_send, own_grad_att, fc1_y2, fc1_x2, out_recv, qkv_far_recv, qkv_far_keep, fc2_recv
    )

    side_a = heads_width // 2
    own_a_recv = over(0, own_a_send)
    fc1_terms = (fc1_own_up, fc1_x1, fc1_y2, fc1_own_down, fc1_y1, fc1_x2)
    qkv_send, fc1_send, fc1_mine, fc2_mine, out_send = combine(
        at,
        summed((3, half_width, side_a), term(qkv_far_keep, column=0), term(qkv_far_recv, column=0)),
        z_half(theirs_z, *fc1_terms),
        z_half(mine_z, *fc1_terms),
        summed(fc2_mine.shape, term(fc2_mine), term(fc2_recv)),
        summed(out_shape, term(out_own_sum, theirs_y, half_rows_out), term(out_recv, theirs_y, half_rows_out)),
    )
    qkv_first, fc1_recv, fc2_recv, out_y = over_x(qkv_send), over(2, fc1_send), over(3, fc2_mine), over(1, out_send)
    own_b = attend_back(pairs // 2, pairs - pairs // 2, own_heads, own_powers, own_inverse, own_attended, own_grad_att)
    own_a_sum = grad_left_half(keep_half, normed_one, own_a, own_a_recv)
    own_b_send = grad_left_half(send_half, normed_one, own_b)
    own_b, own_b_send, own_a_sum, fc2_recv, out_y, qkv_first, qkv_far_keep, qkv_far_recv, fc1_recv = hold(
        own_b, own_b_send, own_a_sum, fc2_recv, out_y, qkv_first, qkv_far_keep, qkv_far_recv, fc1_recv
    )

    own_b_recv = over(0, own_b_send)
    a_shape = (3, half_rows_out, side_a)
    qkv_send, fc1_mine, a_send, out_mine, fc2_mine = combine(
        at,
        summed((3, half_width, side_a), term(qkv_far_keep, column=1), term(qkv_far_recv, column=1)),
        summed(fc1_mine.shape, term(fc1_mine), term(fc1_recv)),
        summed(a_shape, term(own_a_sum, theirs_y, half_rows_out), term(qkv_first, theirs_y, half_rows_out)),
        summed(
            out_shape,
            term(out_own_sum, mine_y, half_rows_out),
            term(out_recv, mine_y, half_rows_out),
            term(out_y),
        ),
        ((2, 2 * z_shape[1], z_shape[2]), [(None, mine_z2, [term(fc2_mine)]), (None, theirs_z2, [term(fc2_recv)])]),
    )
    qkv_second, fc1_recv, a_y = over_x(qkv_send), over(3, fc1_mine), over(1, a_send)
    fc2_recv = over(2, fc2_mine)
    grad_shifted, grad_send, sums_one = input_grads(
        shared_nat, [own_a, own_b], far_dqkv, own_qkv, far_qkv, rows, lead, grad_middle, gain_one, chunk
    )
    own_b_sum = grad_left_half(keep_half, normed_one, own_b, own_b_recv)
    grad_shifted, grad_send, sums_one, a_y, qkv_second, own_b_sum, out_mine, fc2_mine, fc2_recv, fc1_recv, own_hidden, far_hidden = hold(
        grad_shifted, grad_send, sums_one, a_y, qkv_second, own_b_sum, out_mine, fc2_mine, fc2_recv, fc1_recv, own_hidden, far_hidden
    )

    b_send, fc2_mine, fc1_mine = combine(
        at,
        summed(a_shape, term(own_b_sum, theirs_y, half_rows_out), term(qkv_second, theirs_y, half_rows_out)),
        z_sides(fc2_mine, fc2_recv),
        summed(fc1_mine.shape, term(fc1_mine), term(fc1_recv)),
    )
    b_y, fc1_recv = over(1, b_send), over(2, fc1_mine)
    grad_recv = over_x(grad_send)
    vectors = pack_vectors(at, counts.shape[0], sums_one, sums_two, own_fc1_bias, far_fc1_bias_sum)
    vectors_recv = over(1, vectors)
    b_y, vectors_recv, fc1_mine, fc1_recv, own_hidden, fc2_mine = hold(
        b_y, vectors_recv, fc1_mine, fc1_recv, own_hidden, fc2_mine
    )

    z_rows = half_rows_out // 4

    def qkv_quarter(k):
        def within(flags):
            return mine_y(flags) * 4 + quarter_z(k)(flags)

        parts = [
            (side_k, None, [term(total, within, z_rows), term(recv, within, z_rows), term(recv_y, quarter_z(k), z_rows)])
            for side_k, (total, recv, recv_y) in enumerate(((own_a_sum, qkv_first, a_y), (own_b_sum, qkv_second, b_y)))
        ]
        return (2, 3, z_rows, side_a), parts

    *qkv_sends, qkv_mine, fc1_mine = combine(
        at,
        *[qkv_quarter(k) for k in masks],
        qkv_quarter(0),
        z_sides(fc1_mine, fc1_recv),
    )
    qkv_recv = [over_mask(mask, sent) for mask, sent in zip(masks.values(), qkv_sends)]
    fc2_y = over(1, fc2_mine)
    vectors = vectors + vectors_recv
    output_low = output_layer(pair_nat, chunks, chunks, far_hidden, mlp_low, far_fc2, middle, fc2_row, chunk)
    mlp_high = output_own(0, chunks, own_hidden, w_fc2, chunk)
    mlp_high, output_low, grad_recv, vectors, fc1_mine, fc2_mine, fc2_y, *qkv_recv = hold(
        mlp_high, output_low, grad_recv, vectors, fc1_mine, fc2_mine, fc2_y, *qkv_recv
    )

    qkv_mine, fc2_half = combine(
        at,
        summed(qkv_mine.shape, *[term(v) for v in (qkv_mine, *qkv_recv)]),
        y_sides(fc2_mine, fc2_y),
    )
    qkv_parts = [qkv_mine] + [over_mask(mask, qkv_mine) for mask in masks.values()]
    fc1_y = over(1, fc1_mine)
    output_recv = over_x(output_low)
    output_high = output_layer(pair_nat, 0, chunks, far_hidden, mlp_high, far_fc2, middle, fc2_row, chunk)
    fc2_grad = finish_columns(pair_nat, [fc2_half, over(0, fc2_half)])
    vectors, fc1_y, fc2_grad, out_mine, grad_recv, output_recv, output_high, *qkv_parts = hold(
        vectors, fc1_y, fc2_grad, out_mine, grad_recv, output_recv, output_high, *qkv_parts
    )

    qkv_mine, fc1_half = combine(
        at,
        (
            (2, 3, half_rows_out, side_a),
            [(None, quarter_z(k), [term(v)]) for k, v in zip((0, *masks), qkv_parts)],
        ),
        y_sides(fc1_mine, fc1_y),
    )
    qkv_y, qkv_core = over(1, qkv_mine), over(0, qkv_mine)
    fc1_core = over(0, fc1_half)
    out_mine = combine(at, summed(out_shape, term(out_mine), term(over(2, out_mine))))[0]
    out_z = over(3, out_mine)
    vectors = vectors + over_x(vectors)
    vectors_recv = over(2, vectors)
    input_grad = joined(mp_at, grad_shifted[None, :half_rows], grad_recv[None].astype(F32))
    fc1_grad = finish_rows(pair_nat, [fc1_half, fc1_core])
    qkv_mine, qkv_y, qkv_core, vectors_recv, fc1_grad, out_mine, out_z, input_grad = hold(
        qkv_mine, qkv_y, qkv_core, vectors_recv, fc1_grad, out_mine, out_z, input_grad
    )

    qkv_last = over(0, qkv_y)
    out_mine = combine(at, summed(out_shape, term(out_mine), term(out_z)))[0]
    out_y, out_core = over(1, out_mine), over(0, out_mine)
    qkv_grad = finish_stack(core_first_nat, 0, [qkv_mine, qkv_core])
    block_output = joined(mp_at, output_high[None], output_recv[None])
    vectors = vectors + vectors_recv
    vectors_recv = over(3, vectors)
    qkv_last, qkv_grad, vectors_recv, out_y, out_core, block_output = hold(
        qkv_last, qkv_grad, vectors_recv, out_y, out_core, block_output
    )

    vectors = vectors + vectors_recv
    vectors = vectors + over(0, vectors)
    out_grad = finish_turned(core_first_nat, [out_mine, out_core, out_y, over(0, out_y)])
    qkv_grad = finish_stack(core_first_nat, 2, [qkv_y, qkv_last], qkv_grad)
    qkv_grad = jnp.transpose(qkv_grad, (1, 0, 2))

    table = counts.shape[0]
    lead_grad, singles, rest = vectors[:table], vectors[table : table + 6], vectors[table + 6 :]
    qv_bias_grad = part(rest[:2], mp_at, 2, 1)
    fc1_bias_grad = part(rest[2:].reshape(-1), mp_at, 2)
    return (
        block_output,
        input_grad,
        lead_grad,
        singles[0],
        singles[1],
        qkv_grad,
        qv_bias_grad,
        out_grad,
        singles[4],
        singles[2],
        singles[3],
        fc1_grad,
        fc1_bias_grad,
        fc2_grad,
        singles[5],
    )


def solution(mesh):
    in_specs = (
        P("dp", "mp", None),
        P("dp", "mp", None),
        P("dp"),
        P(),
        P(),
        P(),
        P(),
        P(None, None, "mp"),
        P(None, "mp"),
        P("mp", None),
        P(),
        P(),
        P(),
        P(None, "mp"),
        P("mp"),
        P("mp", None),
        P(),
    )
    out_specs = (
        P("dp", "mp", None),
        P("dp", "mp", None),
        P(),
        P(),
        P(),
        P(None, None, "mp"),
        P(None, "mp"),
        P("mp", None),
        P(),
        P(),
        P(),
        P(None, "mp"),
        P("mp"),
        P("mp", None),
        P(),
    )
    def local(*args):
        replicas = lax.axis_size("dp")
        samples, half_rows, width = args[0].shape
        heads_width, units = args[7].shape[2], args[13].shape[1]
        fits = samples == 2 and lax.axis_size("mp") == 2 and replicas == 16
        even = half_rows % 256 == 0 and width == 2 * heads_width == 1024 and units == 2 * width
        return (fast_body if fits and even else body)(*args)

    return jax.shard_map(local, mesh=mesh, in_specs=in_specs, out_specs=out_specs, check_vma=False)
```

```python
import functools
import math

import jax
import jax.numpy as jnp
from jax import lax
from jax.experimental import pallas as pl
from jax.experimental.pallas import tpu as pltpu
from jax.sharding import PartitionSpec as P

HD = 64


EPS = 1e-05


def norm_forward(values, norm_gain, norm_shift):
    center = values - jnp.mean(values, axis=-1, keepdims=True)
    inverse = lax.rsqrt(jnp.mean(center * center, axis=-1, keepdims=True) + EPS)
    scaled = center * inverse
    return (scaled * norm_gain + norm_shift, scaled, inverse)


def norm_backward(grad_out, scaled, inverse, norm_gain):
    grad_scaled = grad_out * norm_gain
    grad_mean = jnp.mean(grad_scaled, axis=-1, keepdims=True)
    cross_mean = jnp.mean(grad_scaled * scaled, axis=-1, keepdims=True)
    grad_in = inverse * (grad_scaled - grad_mean - scaled * cross_mean)
    gain_grad = jnp.sum(grad_out * scaled, axis=(0, 1))
    shift_grad = jnp.sum(grad_out, axis=(0, 1))
    return (grad_in, gain_grad, shift_grad)


def gelu_slope(pre_act):
    normal_cdf = 0.5 * (1.0 + lax.erf(pre_act * 0.7071067811865476))
    return normal_cdf + pre_act * jnp.exp(-0.5 * pre_act * pre_act) * 0.3989422804014327


def attention_forward(query_all, key_all, value_all, block_rows):
    block_count = query_all.shape[0] // block_rows
    query_blocks = query_all.reshape((block_count, block_rows) + query_all.shape[1:])

    def one_block(query_block):
        scores = (
            jnp.einsum("qshd,kshd->shqk", query_block, key_all, preferred_element_type=jnp.float32)
            * 0.125
        )
        row_max = jnp.max(scores, axis=-1, keepdims=True)
        powers = jnp.exp(scores - row_max)
        exp_total = jnp.sum(powers, axis=-1, keepdims=True)
        attn_weights = (powers / exp_total).astype(jnp.bfloat16)
        attended = jnp.einsum(
            "shqk,kshd->qshd", attn_weights, value_all, preferred_element_type=jnp.float32
        )
        return (attended.astype(jnp.bfloat16), (row_max + jnp.log(exp_total))[..., 0])

    attended, log_total = lax.map(one_block, query_blocks)
    return (attended.reshape(query_all.shape), log_total)


def attention_backward(query_all, key_all, value_all, grad_attended, log_total, block_rows):
    block_count = query_all.shape[0] // block_rows
    query_blocks = query_all.reshape((block_count, block_rows) + query_all.shape[1:])
    grad_blocks = grad_attended.reshape((block_count, block_rows) + query_all.shape[1:])

    def one_block(running, sliced):
        key_grad, value_grad = running
        query_block, grad_block, log_block = sliced
        scores = (
            jnp.einsum("qshd,kshd->shqk", query_block, key_all, preferred_element_type=jnp.float32)
            * 0.125
        )
        attn_weights = jnp.exp(scores - log_block[..., None])
        weight_low = attn_weights.astype(jnp.bfloat16)
        grad_weights = jnp.einsum(
            "qshd,kshd->shqk", grad_block, value_all, preferred_element_type=jnp.float32
        )
        inner = jnp.sum(attn_weights * grad_weights, axis=-1, keepdims=True)
        grad_scores = (attn_weights * (grad_weights - inner)).astype(jnp.bfloat16)
        query_grad = (
            jnp.einsum("shqk,kshd->qshd", grad_scores, key_all, preferred_element_type=jnp.float32)
            * 0.125
        )
        key_grad = (
            key_grad
            + jnp.einsum(
                "shqk,qshd->kshd", grad_scores, query_block, preferred_element_type=jnp.float32
            )
            * 0.125
        )
        value_grad = value_grad + jnp.einsum(
            "shqk,qshd->kshd", weight_low, grad_block, preferred_element_type=jnp.float32
        )
        return ((key_grad, value_grad), query_grad.astype(jnp.bfloat16))

    zero_grad = jnp.zeros(key_all.shape, jnp.float32)
    (key_grad, value_grad), query_grad = lax.scan(
        one_block, (zero_grad, zero_grad), (query_blocks, grad_blocks, log_total)
    )
    return (
        query_grad.reshape(query_all.shape),
        key_grad.astype(jnp.bfloat16),
        value_grad.astype(jnp.bfloat16),
    )


def body(
    tokens,
    cotangent,
    buckets,
    counts,
    lead_table,
    norm1_gain,
    norm1_shift,
    w_qkv,
    qv_bias,
    w_out,
    out_bias,
    norm2_gain,
    norm2_shift,
    w_fc1,
    fc1_bias,
    w_fc2,
    fc2_bias,
):
    samples_here = tokens.shape[0]
    local_rows = tokens.shape[1]
    local_width = w_qkv.shape[2]
    local_heads = local_width // HD
    seq_len = local_rows * lax.axis_size("mp")
    block_rows = min(512, seq_len)
    head_shape = (seq_len, samples_here, local_heads, HD)
    count_f = counts.astype(jnp.float32)
    onehot = (buckets[:, None] == jnp.arange(counts.shape[0], dtype=jnp.int32)[None, :]).astype(
        jnp.float32
    )
    loss_weight = jnp.mean(count_f) / jnp.sum(onehot * count_f[None, :], axis=1)
    lead_rows = jnp.dot(
        onehot,
        lead_table.astype(jnp.float32),
        precision=lax.Precision.HIGHEST,
        preferred_element_type=jnp.float32,
    )
    shifted = jnp.swapaxes(tokens, 0, 1).astype(jnp.float32) + lead_rows[None]
    normed_one, scaled_one, inverse_one = norm_forward(
        shifted, norm1_gain.astype(jnp.float32), norm1_shift.astype(jnp.float32)
    )
    normed_one = normed_one.astype(jnp.bfloat16)
    normed_full = lax.all_gather(normed_one, "mp", axis=0, tiled=True)
    project = jnp.einsum("tsd,dcf->tscf", normed_full, w_qkv, preferred_element_type=jnp.float32)
    bias_f = qv_bias.astype(jnp.float32)
    query_all = (project[:, :, 0] + bias_f[0]).astype(jnp.bfloat16).reshape(head_shape)
    key_all = project[:, :, 1].astype(jnp.bfloat16).reshape(head_shape)
    value_all = (project[:, :, 2] + bias_f[1]).astype(jnp.bfloat16).reshape(head_shape)
    attended, log_total = attention_forward(query_all, key_all, value_all, block_rows)
    attended_flat = attended.reshape(seq_len, samples_here, local_width)
    picked = attended_flat
    branch = lax.psum_scatter(
        jnp.einsum("tsf,fd->tsd", picked, w_out, preferred_element_type=jnp.float32),
        "mp",
        scatter_dimension=0,
        tiled=True,
    )
    middle = shifted + branch + out_bias.astype(jnp.float32)
    gain_two = norm2_gain.astype(jnp.float32)
    normed_two, scaled_two, inverse_two = norm_forward(
        middle, gain_two, norm2_shift.astype(jnp.float32)
    )
    normed_two = normed_two.astype(jnp.bfloat16)
    grad_top = jnp.swapaxes(cotangent, 0, 1).astype(jnp.float32) * loss_weight[None, :, None]
    grad_low = grad_top.astype(jnp.bfloat16)
    fc1_full, fc1_bias_full, fc2_full = (
        lax.all_gather(w_fc1, "mp", axis=1, tiled=True),
        lax.all_gather(fc1_bias, "mp", axis=0, tiled=True),
        lax.all_gather(w_fc2, "mp", axis=0, tiled=True),
    )
    pre_act = jnp.einsum(
        "tsd,df->tsf", normed_two, fc1_full, preferred_element_type=jnp.float32
    ) + fc1_bias_full.astype(jnp.float32)
    hidden = jax.nn.gelu(pre_act, approximate=False).astype(jnp.bfloat16)
    mlp_branch = jnp.einsum("tsf,fd->tsd", hidden, fc2_full, preferred_element_type=jnp.float32)
    output = middle + mlp_branch + fc2_bias.astype(jnp.float32)
    grad_hidden = jnp.einsum("tsd,fd->tsf", grad_low, fc2_full, preferred_element_type=jnp.float32)
    grad_pre = (grad_hidden * gelu_slope(pre_act)).astype(jnp.bfloat16)
    grad_normed_two = jnp.einsum(
        "tsf,df->tsd", grad_pre, fc1_full, preferred_element_type=jnp.float32
    )
    fc1_part = jnp.einsum("tsd,tsf->df", normed_two, grad_pre, preferred_element_type=jnp.float32)
    fc1_bias_part = jnp.sum(grad_pre.astype(jnp.float32), axis=(0, 1))
    fc2_part = jnp.einsum("tsf,tsd->fd", hidden, grad_low, preferred_element_type=jnp.float32)
    fc1_grad, fc1_bias_grad, fc2_grad = (
        lax.psum_scatter(
            fc1_part.astype(jnp.bfloat16), "mp", scatter_dimension=1, tiled=True
        ).astype(jnp.float32),
        lax.psum_scatter(
            fc1_bias_part.astype(jnp.bfloat16), "mp", scatter_dimension=0, tiled=True
        ).astype(jnp.float32),
        lax.psum_scatter(
            fc2_part.astype(jnp.bfloat16), "mp", scatter_dimension=0, tiled=True
        ).astype(jnp.float32),
    )
    fc2_bias_grad = jnp.sum(grad_top, axis=(0, 1))
    grad_from_norm, gain_two_grad, shift_two_grad = norm_backward(
        grad_normed_two, scaled_two, inverse_two, gain_two
    )
    grad_middle = grad_top + grad_from_norm
    out_bias_grad = jnp.sum(grad_middle, axis=(0, 1))
    grad_branch = grad_middle.astype(jnp.bfloat16)
    grad_branch_full = lax.all_gather(grad_branch, "mp", axis=0, tiled=True)
    out_grad = jnp.einsum(
        "tsf,tsd->fd", attended_flat, grad_branch_full, preferred_element_type=jnp.float32
    )
    grad_attended = jnp.einsum(
        "tsd,fd->tsf", grad_branch_full, w_out, preferred_element_type=jnp.float32
    ).astype(jnp.bfloat16)
    query_grad, key_grad, value_grad = attention_backward(
        query_all, key_all, value_all, grad_attended.reshape(head_shape), log_total, block_rows
    )
    grad_project = jnp.stack([query_grad, key_grad, value_grad], axis=2).reshape(
        seq_len, samples_here, 3, local_width
    )
    qkv_grad = jnp.einsum(
        "tsd,tscf->dcf", normed_full, grad_project, preferred_element_type=jnp.float32
    )
    query_bias_grad = jnp.sum(query_grad.astype(jnp.float32), axis=(0, 1)).reshape(local_width)
    value_bias_grad = jnp.sum(value_grad.astype(jnp.float32), axis=(0, 1)).reshape(local_width)
    qv_bias_grad = jnp.stack([query_bias_grad, value_bias_grad])
    picked = grad_project
    grad_normed_one = lax.psum_scatter(
        jnp.einsum("tscf,dcf->tsd", picked, w_qkv, preferred_element_type=jnp.float32).astype(
            jnp.bfloat16
        ),
        "mp",
        scatter_dimension=0,
        tiled=True,
    ).astype(jnp.float32)
    grad_in_one, gain_one_grad, shift_one_grad = norm_backward(
        grad_normed_one, scaled_one, inverse_one, norm1_gain.astype(jnp.float32)
    )
    grad_shifted = grad_middle + grad_in_one
    lead_grad = jnp.dot(
        onehot.T,
        jnp.sum(grad_shifted, axis=0),
        precision=lax.Precision.HIGHEST,
        preferred_element_type=jnp.float32,
    )
    small_grads = jnp.stack(
        [gain_one_grad, shift_one_grad, out_bias_grad, gain_two_grad, shift_two_grad, fc2_bias_grad]
    )
    lead_grad, small_grads = lax.psum((lead_grad, small_grads), ("dp", "mp"))
    qkv_grad, qv_bias_grad, out_grad, fc1_grad, fc1_bias_grad, fc2_grad = (
        lax.psum(qkv_grad.astype(jnp.bfloat16), "dp").astype(jnp.float32),
        lax.psum(qv_bias_grad.astype(jnp.bfloat16), "dp").astype(jnp.float32),
        lax.psum(out_grad.astype(jnp.bfloat16), "dp").astype(jnp.float32),
        lax.psum(fc1_grad.astype(jnp.bfloat16), "dp").astype(jnp.float32),
        lax.psum(fc1_bias_grad.astype(jnp.bfloat16), "dp").astype(jnp.float32),
        lax.psum(fc2_grad.astype(jnp.bfloat16), "dp").astype(jnp.float32),
    )
    block_output = jnp.swapaxes(output, 0, 1).astype(jnp.bfloat16)
    input_grad = jnp.swapaxes(grad_shifted, 0, 1)
    return (
        block_output,
        input_grad,
        lead_grad,
        small_grads[0],
        small_grads[1],
        qkv_grad,
        qv_bias_grad,
        out_grad,
        small_grads[2],
        small_grads[3],
        small_grads[4],
        fc1_grad,
        fc1_bias_grad,
        fc2_grad,
        small_grads[5],
    )


F32 = jnp.float32
BF16 = jnp.bfloat16
NN = (((1,), (0,)), ((), ()))
NT = (((1,), (1,)), ((), ()))
TN = (((0,), (0,)), ((), ()))
MIB = 1 << 20


def dot(left, right, dims):
    return lax.dot_general(left, right, dims, preferred_element_type=F32)


def whole(array):
    return pl.BlockSpec(array.shape, lambda *_: (0,) * array.ndim, pipeline_mode=pl.Buffered(1))


def kernel_call(body, name, grid, scalars, ins, outs, scratch=(), vmem=32, time=6, pinned=(), alias=None):
    spec = pltpu.PrefetchScalarGridSpec(
        num_scalar_prefetch=len(scalars),
        grid=grid,
        in_specs=[spec for _, spec in ins],
        out_specs=[spec for _, spec in outs],
        scratch_shapes=list(scratch),
    )
    return pl.pallas_call(
        body,
        out_shape=[shape for shape, _ in outs],
        grid_spec=spec,
        compiler_params=pltpu.CompilerParams(vmem_limit_bytes=vmem * MIB),
        input_output_aliases={} if alias is None else {len(scalars) + alias: 0},
        cost_estimate=pl.CostEstimate(flops=MIB, transcendentals=0, bytes_accessed=int(time * 2 * MIB)),
        name=name,
    )(
        *scalars,
        *[
            pltpu.with_memory_space_constraint(array, pltpu.HBM) if k in pinned else array
            for k, (array, _) in enumerate(ins)
        ],
    )


def struct(shape, dtype=BF16):
    return jax.ShapeDtypeStruct(shape, dtype)


def centred(values):
    center = values - jnp.mean(values, axis=-1, keepdims=True)
    inverse = lax.rsqrt(jnp.mean(center * center, axis=-1, keepdims=True) + EPS)
    return center * inverse, inverse


def norm_input_grad(grad_out, scaled, inverse, gain):
    grad_scaled = grad_out * gain
    grad_mean = jnp.mean(grad_scaled, axis=-1, keepdims=True)
    cross_mean = jnp.mean(grad_scaled * scaled, axis=-1, keepdims=True)
    return inverse * (grad_scaled - grad_mean - scaled * cross_mean)


def column_sum(values):
    return jnp.sum(values, axis=0, keepdims=True)


def chunk_of(nat_ref, index, size):
    return pl.ds(pl.multiple_of(nat_ref[index] * size, size), size)


def attention_forward_kernel(block, qkv_ref, out_ref, power_ref, inverse_ref):
    rows_all = qkv_ref.shape[1]
    steps = [(head, start) for head in range(2) for start in range(0, rows_all, block)]

    def scores_of(head, start):
        lanes = slice(HD * head, HD * head + HD)
        query = qkv_ref[0, start : start + block, lanes] * BF16(0.125)
        return dot(qkv_ref[1, :, lanes], query, NT)

    outs = [[], []]
    ahead = scores_of(*steps[0])
    for k, (head, start) in enumerate(steps):
        scores = ahead
        if k + 1 < len(steps):
            ahead = scores_of(*steps[k + 1])
        lanes = slice(HD * head, HD * head + HD)
        rows = slice(start, start + block)
        powers = jnp.exp2((scores - jnp.max(scores, axis=0, keepdims=True)) * 1.4426950408889634)
        inverse = 1.0 / jnp.sum(powers, axis=0, keepdims=True)
        power_low = powers.astype(BF16)
        power_ref[head, :, rows] = power_low
        inverse_ref[0, head : head + 1, rows] = inverse
        outs[head].append(dot(qkv_ref[2, :, lanes], power_low, TN) * inverse)
    heads = [jnp.concatenate(parts, axis=1) for parts in outs]
    out_ref[...] = jnp.concatenate(heads, axis=0).T.astype(BF16)


def attend(qkv):
    _, rows, width = qkv.shape
    pairs = width // (2 * HD)
    return kernel_call(
        functools.partial(attention_forward_kernel, min(512, rows)),
        "attention_forward",
        (pairs,),
        [],
        [(qkv, pl.BlockSpec((3, rows, 2 * HD), lambda j: (0, 0, j)))],
        [
            (struct((rows, width)), pl.BlockSpec((rows, 2 * HD), lambda j: (0, j))),
            (pltpu.HBM((2 * pairs, rows, rows), BF16), pl.BlockSpec((2, rows, rows), lambda j: (j, 0, 0))),
            (struct((pairs, 2, rows), F32), pl.BlockSpec((1, 2, rows), lambda j: (j, 0, 0))),
        ],
        vmem=28,
        time=4 * pairs,
        pinned=[0],
    )


def attention_backward_kernel(block, qkv_ref, power_ref, inverse_ref, out_ref, grad_ref, dqkv_ref, sums_ref):
    rows_all = qkv_ref.shape[1]
    out_t = out_ref[...].astype(F32).T
    grad_t = grad_ref[...].astype(F32).T
    for head in range(2):
        lanes = slice(HD * head, HD * head + HD)
        inverse = inverse_ref[0, head : head + 1, :]
        grad_head = grad_t[lanes]
        inner = jnp.sum(grad_head * out_t[lanes], axis=0, keepdims=True) * inverse
        grad_scaled = grad_head * inverse
        grad_low_t = grad_scaled.astype(BF16)
        grad_low = grad_scaled.T.astype(BF16)
        query = qkv_ref[0, :, lanes] * BF16(0.125)
        key = qkv_ref[1, :, lanes]
        value = qkv_ref[2, :, lanes]
        key_t = key.T
        key_grad = value_grad = None
        query_grads = []
        for start in range(0, rows_all, block):
            rows = slice(start, start + block)
            power = power_ref[head, :, rows]
            grad_power = dot(value, grad_low_t[:, rows], NN) - inner[:, rows]
            grad_scores = (power.astype(F32) * grad_power).astype(BF16)
            key_part = dot(grad_scores, query[rows], NN)
            value_part = dot(power, grad_low[rows], NN)
            key_grad = key_part if key_grad is None else key_grad + key_part
            value_grad = value_part if value_grad is None else value_grad + value_part
            query_grads.append(dot(key_t, grad_scores, NN))
        sums_ref[0, :, lanes] = jnp.concatenate(query_grads, axis=1).T * 0.125
        sums_ref[1, :, lanes] = key_grad
        sums_ref[2, :, lanes] = value_grad
    dqkv_ref[...] = sums_ref[...].astype(BF16)


def attend_back(first, count, qkv, powers, inverse, attended, grad_attended):
    _, rows, width = qkv.shape
    block = (3, rows, 2 * HD)
    flat = pl.BlockSpec((rows, 2 * HD), lambda j: (0, j + first))
    return kernel_call(
        functools.partial(attention_backward_kernel, min(512, rows)),
        "attention_backward",
        (count,),
        [],
        [
            (qkv, pl.BlockSpec(block, lambda j: (0, 0, j + first))),
            (powers, pl.BlockSpec((2, rows, rows), lambda j: (j + first, 0, 0))),
            (inverse, pl.BlockSpec((1, 2, rows), lambda j: (j + first, 0, 0))),
            (attended, flat),
            (grad_attended, flat),
        ],
        [(struct((3, rows, 2 * HD * count)), pl.BlockSpec(block, lambda j: (0, 0, j)))],
        [pltpu.VMEM(block, F32)],
        vmem=28,
        time=5.5 * count,
        pinned=range(5),
    )[0]


def project_own_kernel(at_ref, tokens_ref, recv_ref, lead_ref, gain_ref, shift_ref, weight_ref, bias_ref, rows_ref, normed_ref, heads_ref):
    own = pl.program_id(0) < pl.num_programs(0) // 2
    tokens = jnp.where(own, tokens_ref[0].astype(F32), recv_ref[...].astype(F32))
    rows_ref[...] = tokens.astype(BF16)
    scaled, _ = centred(tokens + lead_ref[...])
    normed = (scaled * gain_ref[...] + shift_ref[...]).astype(BF16)
    normed_ref[...] = normed
    for c in range(3):
        heads_ref[c] = (dot(normed, weight_ref[c], NN) + bias_ref[c : c + 1]).astype(BF16)


def project_own(at, tokens, recv, lead, gain, shift, weight, bias, chunk):
    half, width = tokens.shape[1:]
    heads = weight.shape[2]
    steps = half // chunk
    row = pl.BlockSpec((chunk, width), lambda j, at: (j, 0))
    return kernel_call(
        project_own_kernel,
        "project_own",
        (2 * steps,),
        [at],
        [
            (tokens, pl.BlockSpec((1, chunk, width), lambda j, at: (at[0], jnp.minimum(j, steps - 1), 0))),
            (recv, pl.BlockSpec((chunk, width), lambda j, at: (jnp.maximum(j - steps, 0), 0))),
            *[(v, whole(v)) for v in (lead, gain, shift, weight, bias)],
        ],
        [
            (struct((2 * half, width)), row),
            (struct((2 * half, width)), row),
            (pltpu.HBM((3, 2 * half, heads), BF16), pl.BlockSpec((3, chunk, heads), lambda j, at: (0, j, 0))),
        ],
        pinned=[0, 1, 5],
    )


def project_far_kernel(nat_ref, normed_ref, bias_ref, *refs):
    *pieces, heads_ref = refs
    size = pieces[0].shape[1]
    total = bias_ref[0]
    for k, piece in enumerate(pieces):
        total = total + dot(normed_ref[:, chunk_of(nat_ref, k, size)], piece[0], NN)
    heads_ref[0] = total.astype(BF16)


def project_far(nat, normed, bias, pieces):
    rows = normed.shape[0]
    heads = pieces[0].shape[2]
    first = lambda j, nat: (j, 0, 0)
    return kernel_call(
        project_far_kernel,
        "project_far",
        (3,),
        [nat],
        [
            (normed, whole(normed)),
            (bias[:, None], pl.BlockSpec((1, 1, heads), first)),
            *[(p, pl.BlockSpec((1, *p.shape[1:]), first)) for p in pieces],
        ],
        [(pltpu.HBM((3, rows, heads), BF16), pl.BlockSpec((1, rows, heads), first))],
    )[0]


def middle_kernel(nat_ref, own_ref, far_ref, weight_ref, rows_ref, lead_ref, bias_ref, gain_ref, shift_ref, *refs):
    *pieces, middle_ref, normed_ref = refs
    total = dot(own_ref[...], weight_ref[...], NN)
    for k, piece in enumerate(pieces):
        total = total + dot(far_ref[:, chunk_of(nat_ref, k, piece.shape[0])], piece[...], NN)
    middle = rows_ref[...].astype(F32) + lead_ref[...] + total + bias_ref[...]
    middle_ref[...] = middle
    scaled, _ = centred(middle)
    normed_ref[...] = (scaled * gain_ref[...] + shift_ref[...]).astype(BF16)


def middle_layer(nat, own, far, weight, pieces, rows, lead, bias, gain, shift, chunk):
    count, width = rows.shape
    row = pl.BlockSpec((chunk, width), lambda j, nat: (j, 0))
    heads = pl.BlockSpec((chunk, own.shape[1]), lambda j, nat: (j, 0))
    return kernel_call(
        middle_kernel,
        "middle_layer",
        (count // chunk,),
        [nat],
        [(own, heads), (far, heads), (weight, whole(weight)), (rows, row)]
        + [(v, whole(v)) for v in (lead, bias, gain, shift, *pieces)],
        [(pltpu.HBM((count, width), F32), row), (struct((count, width)), row)],
        pinned=[2, 3],
    )


def gelu_store(pre_act, rows, hidden_ref, slope_ref):
    cdf = 0.5 * (1.0 + lax.erf(pre_act * 0.7071067811865476))
    hidden_ref[rows] = (pre_act * cdf).astype(BF16)
    density = jnp.exp(-0.5 * pre_act * pre_act) * 0.3989422804014327
    slope_ref[rows] = (cdf + pre_act * density).astype(BF16)


def hidden_kernel(block, nat_ref, normed_ref, bias_ref, *refs):
    *pieces, hidden_ref, slope_ref = refs
    size = pieces[0].shape[0]
    for start in range(0, normed_ref.shape[0], block):
        rows = slice(start, start + block)
        pre_act = bias_ref[...]
        for k, piece in enumerate(pieces):
            lanes = slice(None) if len(pieces) == 1 else chunk_of(nat_ref, k, size)
            pre_act = pre_act + dot(normed_ref[rows, lanes], piece[...], NN)
        gelu_store(pre_act, rows, hidden_ref, slope_ref)


def hidden_layer(nat, normed, bias, pieces, chunk):
    rows = normed.shape[0]
    units = pieces[0].shape[1]
    tile = min(512, units)
    column = lambda j, nat: (0, j)
    return kernel_call(
        functools.partial(hidden_kernel, chunk),
        "hidden_layer",
        (units // tile,),
        [nat],
        [(normed, whole(normed)), (bias, pl.BlockSpec((1, tile), column))]
        + [(p, pl.BlockSpec((p.shape[0], tile), column)) for p in pieces],
        [(struct((rows, units)), pl.BlockSpec((rows, tile), column))] * 2,
        vmem=24,
        time=10,
        pinned=range(2, 2 + len(pieces)),
    )


def product_kernel(outs, add_count, by_step, _, left_ref, right_ref, *refs):
    adds, out_refs = refs[:add_count], refs[add_count:]
    stacked = len(right_ref.shape) == 3
    value = dot(left_ref[...], right_ref[0] if stacked else right_ref[...], TN)
    for add in adds:
        value = value + (add[0] if stacked else add[...]).astype(F32)
    value = value.astype(BF16)
    if stacked:
        out_refs[0][0] = value
    elif outs == 1:
        out_refs[0][...] = value
    elif by_step:
        for k, out_ref in enumerate(out_refs):

            @pl.when(pl.program_id(0) == k)
            def _(out_ref=out_ref):
                out_ref[...] = value
    else:
        size = value.shape[0] // outs
        for k, out_ref in enumerate(out_refs):
            out_ref[...] = value[k * size : (k + 1) * size]


def grad_right_half(half, left, right, *add):
    rows, columns = left.shape
    kept = right.shape[1] // 2
    tile = columns // 2
    out_spec = pl.BlockSpec((tile, kept), lambda j, half: (j, 0))
    outs = 2 if add else 1
    split = [(struct((tile, kept)), pl.BlockSpec((tile, kept), lambda j, half: (0, 0)))] * 2
    result = kernel_call(
        functools.partial(product_kernel, outs, len(add), True),
        "grad_right_half",
        (2,),
        [half],
        [
            (left, pl.BlockSpec((rows, tile), lambda j, half: (0, j))),
            (right, pl.BlockSpec((rows, kept), lambda j, half: (0, half[0]))),
        ]
        + [(a, out_spec) for a in add],
        split if add else [(struct((columns, kept)), out_spec)],
        vmem=20,
        time=3,
    )
    return result if add else result[0]


def grad_left_half(half, left, right, *add, split=False):
    rows = left.shape[0]
    kept = left.shape[1] // 2
    columns = right.shape[-1]
    tile = min(1024, columns)
    outs = 2 if split else 1
    left_spec = pl.BlockSpec((rows, kept), lambda j, half: (0, half[0]))
    if right.ndim == 3:
        grid, out_shape = (right.shape[0],), (right.shape[0], kept, columns)
        right_spec = pl.BlockSpec((1, rows, columns), lambda j, half: (j, 0, 0))
        add_spec = out_spec = pl.BlockSpec((1, kept, columns), lambda j, half: (j, 0, 0))
    else:
        grid, out_shape = (columns // tile,), (kept // outs, columns)
        right_spec = pl.BlockSpec((rows, tile), lambda j, half: (0, j))
        add_spec = pl.BlockSpec((kept, tile), lambda j, half: (0, j))
        out_spec = pl.BlockSpec((kept // outs, tile), lambda j, half: (0, j))
    result = kernel_call(
        functools.partial(product_kernel, outs, len(add), False),
        "grad_left_half",
        grid,
        [half],
        [(left, left_spec), (right, right_spec)] + [(a, add_spec) for a in add],
        [(struct(out_shape), out_spec)] * outs,
        vmem=20,
        time=3,
    )
    return result if split else result[0]


def term(array, at=None, size=None, column=None):
    block, index = list(array.shape), [None] * array.ndim
    if size is not None:
        block[-2], index[-2] = size, at
    if column is not None:
        block[-1], index[-1] = array.shape[-1] // 2, lambda _: column

    def index_map(_, flags):
        return tuple(0 if f is None else f(flags) for f in index)

    return array, pl.BlockSpec(tuple(block), index_map)


def combine_kernel(plan, flags_ref, *refs):
    count = sum(terms for parts in plan for _, _, terms in parts)
    ins, outs = list(refs[:count]), refs[count:]
    for parts, out_ref in zip(plan, outs):
        for lead, row, terms in parts:
            value = None
            for ref in ins[:terms]:
                part = ref[...] if terms == 1 else ref[...].astype(F32)
                value = part if value is None else value + part
            ins = ins[terms:]
            value = value.astype(BF16)
            if lead is not None:
                out_ref[lead] = value
            elif row is not None:
                size = value.shape[-2]
                start = row if isinstance(row, int) else pl.multiple_of(row(flags_ref) * size, size)
                where = (slice(None),) * (value.ndim - 2) + (pl.ds(start, size), slice(None))
                out_ref[where] = value
            else:
                out_ref[...] = value


def combine(flags, *outs):
    ins = [t for _, parts in outs for _, _, terms in parts for t in terms]
    plan = [[(lead, row, len(terms)) for lead, row, terms in parts] for _, parts in outs]

    def full(shape):
        return pl.BlockSpec(shape, lambda *_: (0,) * len(shape))

    return kernel_call(
        functools.partial(combine_kernel, plan),
        "combine",
        (1,),
        [flags],
        ins,
        [(struct(shape), full(shape)) for shape, _ in outs],
        vmem=32,
        time=3,
    )


def summed(shape, *terms):
    return shape, [(None, None, terms)]


def pre_grad_store(grad, slope_ref, pre_ref, sum_ref):
    pre = (grad * slope_ref[...].astype(F32)).astype(BF16)
    pre_ref[...] = pre
    sum_ref[...] = column_sum(pre.astype(F32))


def pre_grad_own_kernel(low_ref, weight_ref, slope_ref, pre_ref, sum_ref):
    pre_grad_store(dot(low_ref[...], weight_ref[...], NT), slope_ref, pre_ref, sum_ref)


def pre_grad_own(low, weight, slope):
    rows, width = low.shape
    units = weight.shape[0]
    tile = min(512, units)
    column = lambda j: (0, j)
    return kernel_call(
        pre_grad_own_kernel,
        "pre_grad_own",
        (units // tile,),
        [],
        [
            (low, whole(low)),
            (weight, pl.BlockSpec((tile, width), lambda j: (j, 0))),
            (slope, pl.BlockSpec((rows, tile), column)),
        ],
        [
            (struct((rows, units)), pl.BlockSpec((rows, tile), column)),
            (struct((1, units), F32), pl.BlockSpec((1, tile), column)),
        ],
        vmem=24,
        pinned=[1],
    )


def pre_grad_far_kernel(per, nat_ref, low_ref, slope_ref, *refs):
    *pieces, pre_ref, sum_ref = refs
    for k, piece in enumerate(pieces):

        @pl.when(pl.program_id(0) // per == k)
        def _(piece=piece):
            pre_grad_store(dot(low_ref[...], piece[...], NT), slope_ref, pre_ref, sum_ref)


def pre_grad_far(nat, low, pieces, slope):
    rows, width = low.shape
    size = pieces[0].shape[0]
    tile = min(512, size)
    per = size // tile
    units = size * len(pieces)
    column = lambda j, nat: (0, nat[j // per] * per + j % per)

    def piece_spec(k):
        return pl.BlockSpec((tile, width), lambda j, nat: (jnp.clip(j - k * per, 0, per - 1), 0))

    return kernel_call(
        functools.partial(pre_grad_far_kernel, per),
        "pre_grad_far",
        (len(pieces) * per,),
        [nat],
        [(low, whole(low)), (slope, pl.BlockSpec((rows, tile), column))]
        + [(p, piece_spec(k)) for k, p in enumerate(pieces)],
        [
            (struct((rows, units)), pl.BlockSpec((rows, tile), column)),
            (struct((1, units), F32), pl.BlockSpec((1, tile), column)),
        ],
        vmem=24,
        time=8,
        pinned=range(2, 2 + len(pieces)),
    )


def add_sums(sums_ref, rows):
    @pl.when(pl.program_id(0) == 0)
    def _():
        sums_ref[...] = jnp.zeros_like(sums_ref)

    for k, row in enumerate(rows):
        sums_ref[k : k + 1, :] += row


def middle_grad_kernel(
    nat_ref, at_ref, own_ref, far_ref, weight_ref, middle_ref, cot_ref, recv_ref, loss_ref, gain_ref, *refs
):
    *pieces, grad_ref, low_ref, sums_ref, total_ref = refs
    total_ref[...] = dot(own_ref[...], weight_ref[...], NT)
    for k, piece in enumerate(pieces):
        total_ref[:, chunk_of(nat_ref, k, piece.shape[0])] += dot(far_ref[...], piece[...], NT)
    grad = total_ref[...]
    scaled, inverse = centred(middle_ref[...])
    mine = pl.program_id(0) < pl.num_programs(0) // 2
    top = jnp.where(mine, cot_ref[0].astype(F32), recv_ref[...].astype(F32)) * loss_ref[...]
    grad_middle = top + norm_input_grad(grad, scaled, inverse, gain_ref[...])
    grad_ref[...] = grad_middle
    low_ref[...] = grad_middle.astype(BF16)
    add_sums(
        sums_ref,
        [column_sum(grad * scaled), column_sum(grad), column_sum(grad_middle), column_sum(top)],
    )


def middle_grad(nat, at, own, far, weight, pieces, middle, cot, recv, loss, gain, chunk):
    count, width = middle.shape
    row = pl.BlockSpec((chunk, width), lambda j, *_: (j, 0))
    units = pl.BlockSpec((chunk, own.shape[1]), lambda j, *_: (j, 0))
    steps = count // chunk // 2
    return kernel_call(
        middle_grad_kernel,
        "middle_grad",
        (count // chunk,),
        [nat, at],
        [
            (own, units),
            (far, units),
            (weight, whole(weight)),
            (middle, row),
            (cot, pl.BlockSpec((1, chunk, width), lambda j, nat, at: (at[0], jnp.minimum(j, steps - 1), 0))),
            (recv, pl.BlockSpec((chunk, width), lambda j, *_: (jnp.maximum(j - steps, 0), 0))),
        ]
        + [(v, whole(v)) for v in (loss, gain, *pieces)],
        [
            (struct((count, width), F32), row),
            (struct((count, width)), row),
            (struct((8, width), F32), pl.BlockSpec((8, width), lambda j, *_: (0, 0))),
        ],
        [pltpu.VMEM((chunk, width), F32)],
        time=14,
        pinned=[2, 3, 4, 5, *range(8, 8 + len(pieces))],
    )


def attended_grad_kernel(nat_ref, low_ref, weight_ref, *refs):
    *pieces, own_ref, far_ref = refs
    own_ref[...] = dot(low_ref[...], weight_ref[...], NT).astype(BF16)
    for k, piece in enumerate(pieces):
        far_ref[:, chunk_of(nat_ref, k, piece.shape[0])] = dot(low_ref[...], piece[...], NT).astype(BF16)


def attended_grad(nat, low, weight, pieces, chunk):
    count, width = low.shape
    heads = weight.shape[0]
    out = (struct((count, heads)), pl.BlockSpec((chunk, heads), lambda j, nat: (j, 0)))
    return kernel_call(
        attended_grad_kernel,
        "attended_grad",
        (count // chunk,),
        [nat],
        [(low, pl.BlockSpec((chunk, width), lambda j, nat: (j, 0)))] + [(v, whole(v)) for v in (weight, *pieces)],
        [out, out],
        pinned=range(1, 2 + len(pieces)),
    )


def output_own_kernel(own_ref, weight_ref, out_ref):
    out_ref[...] = dot(own_ref[...], weight_ref[...], NN)


def output_own(first, count, own, weight, chunk):
    units = own.shape[1]
    width = weight.shape[1]
    return kernel_call(
        output_own_kernel,
        "output_own",
        (count,),
        [],
        [(own, pl.BlockSpec((chunk, units), lambda j: (j + first, 0))), (weight, whole(weight))],
        [(struct((count * chunk, width), F32), pl.BlockSpec((chunk, width), lambda j: (j, 0)))],
        vmem=20,
        time=4,
        pinned=range(2),
    )[0]


def output_kernel(nat_ref, far_ref, own_ref, middle_ref, bias_ref, *refs):
    *pieces, out_ref = refs
    total = own_ref[...]
    for k, piece in enumerate(pieces):
        total = total + dot(far_ref[:, chunk_of(nat_ref, k, piece.shape[0])], piece[...], NN)
    out_ref[...] = (middle_ref[...] + total + bias_ref[...]).astype(BF16)


def output_layer(nat, first, count, far, own, pieces, middle, bias, chunk):
    width = middle.shape[1]
    row = pl.BlockSpec((chunk, width), lambda j, nat: (j + first, 0))
    here = pl.BlockSpec((chunk, width), lambda j, nat: (j, 0))
    return kernel_call(
        output_kernel,
        "output_layer",
        (count,),
        [nat],
        [(far, pl.BlockSpec((chunk, far.shape[1]), lambda j, nat: (j + first, 0))), (own, here), (middle, row)]
        + [(v, whole(v)) for v in (bias, *pieces)],
        [(struct((count * chunk, width)), pl.BlockSpec((chunk, width), lambda j, nat: (j, 0)))],
        vmem=24,
        time=6,
        pinned=range(4 + len(pieces)),
    )[0]


def input_grad_kernel(own_count, nat_ref, far_ref, weight_ref, rows_ref, lead_ref, grad_ref, gain_ref, *refs):
    owns, refs = refs[:own_count], refs[own_count:]
    *pieces, out_ref, low_ref, sums_ref, total_ref = refs
    total = None
    at = 0
    for own in owns:
        size = own.shape[2]
        for c in range(3):
            part = dot(own[c], weight_ref[c, :, at : at + size], NT)
            total = part if total is None else total + part
        at += size
    total_ref[...] = total
    for k, piece in enumerate(pieces):
        part = dot(far_ref[0], piece[0], NT) + dot(far_ref[1], piece[1], NT) + dot(far_ref[2], piece[2], NT)
        total_ref[:, chunk_of(nat_ref, k, piece.shape[1])] += part
    grad = total_ref[...]
    scaled, inverse = centred(rows_ref[...].astype(F32) + lead_ref[...])
    grad_shifted = grad_ref[...] + norm_input_grad(grad, scaled, inverse, gain_ref[...])
    out_ref[...] = grad_shifted
    low_ref[...] = grad_shifted.astype(BF16)
    bias_rows = [
        jnp.concatenate([column_sum(d[c].astype(F32)) for d in (*owns, far_ref)], axis=1) for c in (0, 2)
    ]
    add_sums(
        sums_ref, [column_sum(grad * scaled), column_sum(grad), column_sum(grad_shifted), *bias_rows]
    )


def input_grads(nat, owns, far, weight, pieces, rows, lead, grad_middle, gain, chunk):
    count, width = rows.shape
    row = pl.BlockSpec((chunk, width), lambda j, nat: (j, 0))
    heads = lambda d: pl.BlockSpec((3, chunk, d.shape[2]), lambda j, nat: (0, j, 0))
    steps = count // chunk
    half = pl.BlockSpec((chunk, width), lambda j, nat: (jnp.maximum(j - steps // 2, 0), 0))
    return kernel_call(
        functools.partial(input_grad_kernel, len(owns)),
        "input_grads",
        (steps,),
        [nat],
        [
            (far, heads(far)),
            (weight, whole(weight)),
            (rows, row),
            (lead, whole(lead)),
            (grad_middle, row),
            (gain, whole(gain)),
        ]
        + [(d, heads(d)) for d in owns]
        + [(p, whole(p)) for p in pieces],
        [
            (struct((count, width), F32), row),
            (struct((count // 2, width)), half),
            (struct((8, width), F32), pl.BlockSpec((8, width), lambda j, nat: (0, 0))),
        ],
        [pltpu.VMEM((chunk, width), F32)],
        time=14,
        pinned=[0, 1, 2, 4, *range(6, 6 + len(owns) + len(pieces))],
    )


def pack_kernel(buckets, flags_ref, one_ref, two_ref, own_ref, far_ref, out_ref):
    width = one_ref.shape[1]
    half = width // 2
    first = flags_ref[0] == 0
    rows = lax.broadcasted_iota(jnp.int32, (buckets, width), 0)
    out_ref[:buckets] = jnp.where(rows == flags_ref[7], one_ref[2:3], 0.0)
    out_ref[buckets : buckets + 2] = one_ref[:2]
    out_ref[buckets + 2 : buckets + 6] = two_ref[:4]
    bias = one_ref[3:5]
    swapped = jnp.concatenate([bias[:, half:], bias[:, :half]], axis=1)
    out_ref[buckets + 6 : buckets + 8] = jnp.where(first, bias, swapped)
    own, far = own_ref[...], far_ref[...]
    count = own.shape[1] // width
    for k in range(count):
        columns = slice(k * width, (k + 1) * width)
        low, high = own[:, columns], far[:, columns]
        out_ref[buckets + 8 + k : buckets + 9 + k] = jnp.where(first, low, high)
        out_ref[buckets + 8 + count + k : buckets + 9 + count + k] = jnp.where(first, high, low)


def pack_vectors(flags, buckets, one, two, own, far):
    width = one.shape[1]
    rows = buckets + 8 + 2 * own.shape[1] // width
    return kernel_call(
        functools.partial(pack_kernel, buckets),
        "pack_vectors",
        (1,),
        [flags],
        [(v, whole(v)) for v in (one, two, own, far)],
        [(struct((rows, width), F32), pl.BlockSpec((rows, width), lambda *_: (0, 0)))],
        vmem=8,
        time=1,
    )[0]


def finish_turned_kernel(_, *refs):
    *pieces, out_ref = refs
    for k, piece in enumerate(pieces):

        @pl.when(pl.program_id(0) == k)
        def _(piece=piece):
            out_ref[...] = piece[...].astype(F32).T


def finish_turned(nat, pieces):
    rows, columns = pieces[0].shape
    return kernel_call(
        finish_turned_kernel,
        "finish",
        (4,),
        [nat],
        [(p, whole(p)) for p in pieces],
        [(struct((columns, 4 * rows), F32), pl.BlockSpec((columns, rows), lambda s, nat: (0, nat[s])))],
        vmem=16,
        time=2,
    )[0]


def source_spec(block, which, steps, place):
    def index(s, j, *_):
        return place(jnp.where(s == which, j, jnp.where(s < which, 0, steps - 1)))

    return pl.BlockSpec(block, index)


def finish_rows_kernel(_, *refs):
    *pieces, out_ref = refs
    for k, piece in enumerate(pieces):

        @pl.when(pl.program_id(0) == k)
        def _(piece=piece):
            out_ref[...] = piece[0].astype(F32)


def finish_rows(at, pieces):
    halves, rows, columns = pieces[0].shape
    block = (1, rows, columns)
    return kernel_call(
        finish_rows_kernel,
        "finish",
        (2, halves),
        [at],
        [(p, source_spec(block, k, halves, lambda j: (j, 0, 0))) for k, p in enumerate(pieces)],
        [
            (
                struct((2 * halves * rows, columns), F32),
                pl.BlockSpec((rows, columns), lambda s, j, at: (at[s] * halves + j, 0)),
            )
        ],
        vmem=20,
        time=5,
    )[0]


def finish_columns_kernel(at_ref, mine_ref, theirs_ref, out_ref):
    first = at_ref[0] == 0
    one, two = mine_ref[0].astype(F32), theirs_ref[0].astype(F32)
    columns = one.shape[1]
    out_ref[:, :columns] = jnp.where(first, one, two)
    out_ref[:, columns:] = jnp.where(first, two, one)


def finish_columns(at, pieces):
    halves, rows, columns = pieces[0].shape
    tile = min(512, rows)
    per = rows // tile
    spec = pl.BlockSpec((1, tile, columns), lambda j, at: (j // per, j % per, 0))
    return kernel_call(
        finish_columns_kernel,
        "finish",
        (halves * per,),
        [at],
        [(p, spec) for p in pieces],
        [(struct((halves * rows, 2 * columns), F32), pl.BlockSpec((tile, 2 * columns), lambda j, at: (j, 0)))],
        vmem=20,
        time=5,
    )[0]


def finish_stack_kernel(count, at_ref, *refs):
    pieces, out_ref = refs[:count], refs[-1]
    for k, piece in enumerate(pieces):

        @pl.when(pl.program_id(0) == k)
        def _(piece=piece):
            out_ref[0] = jnp.concatenate([piece[0, 0].astype(F32), piece[1, 0].astype(F32)], axis=1)


def finish_stack(nat, first, pieces, *so_far):
    _, stack, rows, columns = pieces[0].shape
    block = (2, 1, rows, columns)
    count = len(pieces)
    return kernel_call(
        functools.partial(finish_stack_kernel, count),
        "finish",
        (count, stack),
        [nat],
        [(p, source_spec(block, k, stack, lambda j: (0, j, 0, 0))) for k, p in enumerate(pieces)]
        + [(v, pl.BlockSpec(memory_space=pl.ANY)) for v in so_far],
        [
            (
                struct((stack, 4 * rows, 2 * columns), F32),
                pl.BlockSpec((1, rows, 2 * columns), lambda s, j, nat: (j, nat[first + s], 0)),
            )
        ],
        vmem=16,
        time=3,
        alias=count if so_far else None,
    )[0]


def hold(*values):
    return lax.optimization_barrier(values)


def fast_body(
    tokens,
    cotangent,
    buckets,
    counts,
    lead_table,
    norm1_gain,
    norm1_shift,
    w_qkv,
    qv_bias,
    w_out,
    out_bias,
    norm2_gain,
    norm2_shift,
    w_fc1,
    fc1_bias,
    w_fc2,
    fc2_bias,
):
    replicas = lax.axis_size("dp")
    levels = replicas.bit_length() - 1
    dp_at, mp_at = lax.axis_index("dp"), lax.axis_index("mp")
    bits = [(dp_at >> level) & 1 for level in range(levels)]

    def over_x(value):
        return lax.ppermute(value, "mp", [(0, 1), (1, 0)])

    def over(level, value):
        return over_mask(1 << level, value)

    def over_mask(mask, value):
        return lax.ppermute(value, "dp", [(i, i ^ mask) for i in range(replicas)])

    def joined(bit, mine, theirs, axis=0):
        return jnp.where(
            bit == 0,
            jnp.concatenate([mine, theirs], axis),
            jnp.concatenate([theirs, mine], axis),
        )

    def part(value, index, count, axis=0):
        size = value.shape[axis] // count
        return lax.dynamic_slice_in_dim(value, index * size, size, axis)

    half_rows, width = tokens.shape[1:]
    heads_width = w_qkv.shape[2]
    units = w_fc1.shape[1]
    chunk = 256
    core, side = bits[0], bits[1]
    bucket = lax.dynamic_index_in_dim(buckets, mp_at, 0, keepdims=False)
    at = jnp.stack([mp_at, core, 1 - core, side, 1 - side, bits[2], bits[3], bucket]).astype(jnp.int32)
    mine = core * 2 + side
    shared_nat = jnp.stack([mine, mine ^ 1, mine ^ 2, mine ^ 3]).astype(jnp.int32)
    core_first_nat = jnp.stack([mine, mine ^ 2, mine ^ 1, mine ^ 3]).astype(jnp.int32)

    def row_of(vector):
        return vector.astype(F32)[None]

    small = jnp.concatenate([qv_bias.reshape(-1), fc1_bias])
    small_rows = -(-small.shape[0] // width)
    small_rows_padded = -(-small_rows // 16) * 16
    small = jnp.pad(small, (0, small_rows_padded * width - small.shape[0])).reshape(-1, width)
    token_recv = over_x(jnp.concatenate([part(tokens, 1 - mp_at, 2)[0], small]))

    count_f = counts.astype(F32)
    loss_weight = jnp.mean(count_f) / lax.dynamic_index_in_dim(count_f, bucket, 0, keepdims=False)
    loss_row = jnp.broadcast_to(loss_weight, (1, width))
    lead = lax.dynamic_index_in_dim(lead_table, bucket, 0).astype(F32)
    own_qkv = jnp.transpose(w_qkv, (1, 0, 2))

    def bias_three(bias):
        bias_f = bias.astype(F32)
        return jnp.stack([bias_f[0], jnp.zeros_like(bias_f[0]), bias_f[1]])

    (
        token_recv, qkv_send, out_send, fc1_send, cot_send, fc2_send, at, shared_nat, core_first_nat, loss_row, loss_weight, lead,
        gain_one, gain_two, shift_one, shift_two, out_row, fc1_row, fc2_row, own_bias,
    ) = hold(
        token_recv,
        part(own_qkv, mine, 4, 1),
        part(w_out, core, 2),
        part(w_fc1, mine, 4),
        part(cotangent, 1 - mp_at, 2)[0],
        part(w_fc2, core, 2),
        at,
        shared_nat,
        core_first_nat,
        loss_row,
        loss_weight,
        lead,
        row_of(norm1_gain),
        row_of(norm2_gain),
        row_of(norm1_shift),
        row_of(norm2_shift),
        row_of(out_bias),
        row_of(fc1_bias),
        row_of(fc2_bias),
        bias_three(qv_bias),
    )
    keep_half, send_half, pair_nat = at[1:2], at[2:3], at[1:3]
    far_small = token_recv[half_rows:].reshape(-1)
    far_bias = bias_three(far_small[: 2 * heads_width].reshape(2, heads_width))
    far_fc1_bias = row_of(far_small[2 * heads_width : 2 * heads_width + units])

    qkv_x = over_x(qkv_send)
    rows, normed_one, own_heads = project_own(
        at[:1], tokens, token_recv, lead, gain_one, shift_one, own_qkv, own_bias, chunk
    )
    own_heads, qkv_x, out_send, fc1_send, far_bias, far_fc1_bias = hold(
        own_heads, qkv_x, out_send, fc1_send, far_bias, far_fc1_bias
    )

    qkv_y = over(1, qkv_x)
    out_x = over_x(out_send)
    fc1_x = over_x(fc1_send)
    own_attended, own_powers, own_inverse = attend(own_heads)
    own_attended, qkv_x, qkv_y, out_x = hold(own_attended, qkv_x, qkv_y, out_x)

    far_qkv = [qkv_x, qkv_y, over(0, qkv_x), over(0, qkv_y)]
    far_out = [out_x, over(0, out_x)]
    far_heads = project_far(shared_nat, normed_one, far_bias, far_qkv)
    far_heads, fc1_x, cot_send = hold(far_heads, fc1_x, cot_send)

    fc1_y = over(1, fc1_x)
    cot_recv = over_x(cot_send)
    far_attended, far_powers, far_inverse = attend(far_heads)
    middle, normed_two = middle_layer(
        pair_nat, own_attended, far_attended, w_out, far_out, rows, lead,
        out_row, gain_two, shift_two, chunk,
    )
    normed_two, fc1_x, fc1_y, cot_recv, fc2_send = hold(
        normed_two, fc1_x, fc1_y, cot_recv, fc2_send
    )

    def mine_y(flags):
        return flags[3]

    def theirs_y(flags):
        return flags[4]

    def mine_z(flags):
        return flags[5]

    def theirs_z(flags):
        return 1 - flags[5]

    def mine_z2(flags):
        return flags[6]

    def theirs_z2(flags):
        return 1 - flags[6]

    def zero(_):
        return 0

    def one(_):
        return 1

    def first_y(own_down, far_down):
        size = own_down.shape[0] // 2
        return (2 * size, own_down.shape[1]), [
            (None, 0, [term(own_down, theirs_y, size)]),
            (None, size, [term(far_down, theirs_y, size)]),
        ]

    def second_y(own_up, recv_x):
        size = own_up.shape[0] // 2
        return summed((size, own_up.shape[1]), term(own_up, theirs_y, size), term(recv_x, theirs_y, size))

    def second_x(far_down, recv_y):
        size = far_down.shape[0] // 2
        return summed((size, far_down.shape[1]), term(far_down, mine_y, size), term(recv_y, one, size))

    def z_half(which, own_up, recv_x, recv_up, own_down, recv_y, recv_down):
        size = own_up.shape[0] // 4

        def within(side_of, start=0):
            return lambda flags: (start + side_of(flags)) * 2 + which(flags)

        upper = [term(own_up, within(mine_y), size), term(recv_x, within(mine_y), size), term(recv_up, which, size)]
        lower = [term(own_down, within(mine_y), size), term(recv_y, within(zero), size), term(recv_down, which, size)]
        return (2, size, own_up.shape[1]), [(0, None, upper), (1, None, lower)]

    def z_sides(mine, recv):
        shape = list(mine.shape)
        shape[-2] *= 2
        return tuple(shape), [(None, mine_z, [term(mine)]), (None, theirs_z, [term(recv)])]

    def y_sides(mine, recv):
        shape = list(mine.shape)
        shape[-2] *= 2
        return tuple(shape), [(None, mine_y, [term(mine)]), (None, theirs_y, [term(recv)])]

    masks = {1: 8, 2: 4, 3: 12}

    def quarter_z(k):
        def index(flags):
            first = 1 - flags[5] if k & 2 else flags[5]
            second = 1 - flags[6] if k & 1 else flags[6]
            return first * 2 + second

        return index

    fc2_x = over_x(fc2_send)
    far_fc1 = [fc1_x, fc1_y, over(0, fc1_x), over(0, fc1_y)]
    cot_rows = jnp.concatenate([part(cotangent, mp_at, 2)[0], cot_recv])
    grad_low = (cot_rows.astype(F32) * loss_weight).astype(BF16)
    own_hidden, own_slope = hidden_layer(shared_nat, normed_two, fc1_row, [w_fc1], chunk)
    far_hidden, far_slope = hidden_layer(shared_nat, normed_two, far_fc1_bias, far_fc1, chunk)
    far_send = grad_right_half(send_half, far_hidden, grad_low)
    own_send = grad_right_half(send_half, own_hidden, grad_low)
    own_pre, own_fc1_bias = pre_grad_own(grad_low, w_fc2, own_slope)
    fc1_own_send = grad_left_half(send_half, normed_two, own_pre)
    far_send, own_send, fc2_x, grad_low, far_hidden, own_pre, fc1_own_send = hold(
        far_send, own_send, fc2_x, grad_low, far_hidden, own_pre, fc1_own_send
    )

    far_recv, own_recv, fc2_core, fc1_own_recv = over(0, far_send), over(0, own_send), over(0, fc2_x), over(0, fc1_own_send)
    far_up, far_down = grad_right_half(keep_half, far_hidden, grad_low, far_recv)
    own_up, own_down = grad_right_half(keep_half, own_hidden, grad_low, own_recv)
    far_up, far_down, own_up, own_down, fc2_core, fc1_own_recv = hold(
        far_up, far_down, own_up, own_down, fc2_core, fc1_own_recv
    )

    half_width = width // 2
    fc2_x1 = over_x(far_up)
    fc2_y1 = over(1, combine(at, first_y(own_down, far_down))[0])
    far_fc2 = [fc2_x, fc2_core]
    far_pre, far_fc1_bias_sum = pre_grad_far(pair_nat, grad_low, far_fc2, far_slope)
    fc1_far_send = grad_left_half(send_half, normed_two, far_pre)
    fc1_own_up, fc1_own_down = grad_left_half(keep_half, normed_two, own_pre, fc1_own_recv, split=True)
    chunks = half_rows // chunk
    mlp_low = output_own(chunks, chunks, own_hidden, w_fc2, chunk)
    fc1_far_send, fc1_own_up, fc1_own_down, fc2_x1, fc2_y1, far_pre, mlp_low = hold(
        fc1_far_send, fc1_own_up, fc1_own_down, fc2_x1, fc2_y1, far_pre, mlp_low
    )

    send_y, send_x = combine(at, second_y(own_up, fc2_x1), second_x(far_down, fc2_y1))
    fc2_y2, fc2_x2 = over(1, send_y), over_x(send_x)
    fc1_far_recv = over(0, fc1_far_send)
    grad_middle, grad_branch, sums_two = middle_grad(
        shared_nat, at[:1], own_pre, far_pre, w_fc1, far_fc1, middle, cotangent, cot_recv, loss_row, gain_two, chunk
    )
    own_grad_att, far_grad_att = attended_grad(pair_nat, grad_branch, w_out, far_out, chunk)
    out_far_send = grad_left_half(send_half, grad_branch, far_attended)
    out_own_send = grad_left_half(send_half, grad_branch, own_attended)
    fc1_far_up, fc1_far_down = grad_left_half(keep_half, normed_two, far_pre, fc1_far_recv, split=True)
    out_far_recv, out_own_recv = over(0, out_far_send), over(0, out_own_send)
    out_far_sum = grad_left_half(keep_half, grad_branch, far_attended, out_far_recv)
    out_own_sum = grad_left_half(keep_half, grad_branch, own_attended, out_own_recv)
    far_grad_att, own_grad_att, fc2_y2, fc2_x2, fc1_far_up, fc1_far_down, out_far_sum, out_own_sum = hold(
        far_grad_att, own_grad_att, fc2_y2, fc2_x2, fc1_far_up, fc1_far_down, out_far_sum, out_own_sum
    )

    fc2_terms = (own_up, fc2_x1, fc2_y2, own_down, fc2_y1, fc2_x2)
    fc2_send, fc2_mine, send_y = combine(
        at, z_half(theirs_z, *fc2_terms), z_half(mine_z, *fc2_terms), first_y(fc1_own_down, fc1_far_down)
    )
    fc1_x1, fc1_y1, fc2_recv = over_x(fc1_far_up), over(1, send_y), over(2, fc2_send)
    pairs = heads_width // (2 * HD)
    far_dqkv = attend_back(0, pairs, far_heads, far_powers, far_inverse, far_attended, far_grad_att)
    far_dqkv, own_grad_att, fc1_x1, fc1_y1, out_far_sum, fc2_recv = hold(
        far_dqkv, own_grad_att, fc1_x1, fc1_y1, out_far_sum, fc2_recv
    )

    half_rows_out = half_width // 2
    out_shape = (half_rows_out, heads_width)
    z_shape = (2, fc2_mine.shape[1] // 2, fc2_mine.shape[2])
    send_y, send_x, fc2_send, fc2_mine = combine(
        at,
        second_y(fc1_own_up, fc1_x1),
        second_x(fc1_far_down, fc1_y1),
        summed(z_shape, term(fc2_mine, theirs_z2, z_shape[1]), term(fc2_recv, theirs_z2, z_shape[1])),
        summed(z_shape, term(fc2_mine, mine_z2, z_shape[1]), term(fc2_recv, mine_z2, z_shape[1])),
    )
    fc1_y2, fc1_x2, fc2_recv, out_recv = over(1, send_y), over_x(send_x), over(3, fc2_send), over_x(out_far_sum)
    qkv_far_recv = over(0, grad_left_half(send_half, normed_one, far_dqkv))
    qkv_far_keep = grad_left_half(keep_half, normed_one, far_dqkv)
    own_a = attend_back(0, pairs // 2, own_heads, own_powers, own_inverse, own_attended, own_grad_att)
    own_a_send = grad_left_half(send_half, normed_one, own_a)
    own_a_send, own_grad_att, fc1_y2, fc1_x2, out_recv, qkv_far_recv, qkv_far_keep, fc2_recv = hold(
        own_a_send, own_grad_att, fc1_y2, fc1_x2, out_recv, qkv_far_recv, qkv_far_keep, fc2_recv
    )

    side_a = heads_width // 2
    own_a_recv = over(0, own_a_send)
    fc1_terms = (fc1_own_up, fc1_x1, fc1_y2, fc1_own_down, fc1_y1, fc1_x2)
    qkv_send, fc1_send, fc1_mine, fc2_mine, out_send = combine(
        at,
        summed((3, half_width, side_a), term(qkv_far_keep, column=0), term(qkv_far_recv, column=0)),
        z_half(theirs_z, *fc1_terms),
        z_half(mine_z, *fc1_terms),
        summed(fc2_mine.shape, term(fc2_mine), term(fc2_recv)),
        summed(out_shape, term(out_own_sum, theirs_y, half_rows_out), term(out_recv, theirs_y, half_rows_out)),
    )
    qkv_first, fc1_recv, fc2_recv, out_y = over_x(qkv_send), over(2, fc1_send), over(3, fc2_mine), over(1, out_send)
    own_b = attend_back(pairs // 2, pairs - pairs // 2, own_heads, own_powers, own_inverse, own_attended, own_grad_att)
    own_a_sum = grad_left_half(keep_half, normed_one, own_a, own_a_recv)
    own_b_send = grad_left_half(send_half, normed_one, own_b)
    own_b, own_b_send, own_a_sum, fc2_recv, out_y, qkv_first, qkv_far_keep, qkv_far_recv, fc1_recv = hold(
        own_b, own_b_send, own_a_sum, fc2_recv, out_y, qkv_first, qkv_far_keep, qkv_far_recv, fc1_recv
    )

    own_b_recv = over(0, own_b_send)
    a_shape = (3, half_rows_out, side_a)
    qkv_send, fc1_mine, a_send, out_mine, fc2_mine = combine(
        at,
        summed((3, half_width, side_a), term(qkv_far_keep, column=1), term(qkv_far_recv, column=1)),
        summed(fc1_mine.shape, term(fc1_mine), term(fc1_recv)),
        summed(a_shape, term(own_a_sum, theirs_y, half_rows_out), term(qkv_first, theirs_y, half_rows_out)),
        summed(
            out_shape,
            term(out_own_sum, mine_y, half_rows_out),
            term(out_recv, mine_y, half_rows_out),
            term(out_y),
        ),
        ((2, 2 * z_shape[1], z_shape[2]), [(None, mine_z2, [term(fc2_mine)]), (None, theirs_z2, [term(fc2_recv)])]),
    )
    qkv_second, fc1_recv, a_y = over_x(qkv_send), over(3, fc1_mine), over(1, a_send)
    fc2_recv = over(2, fc2_mine)
    grad_shifted, grad_send, sums_one = input_grads(
        shared_nat, [own_a, own_b], far_dqkv, own_qkv, far_qkv, rows, lead, grad_middle, gain_one, chunk
    )
    own_b_sum = grad_left_half(keep_half, normed_one, own_b, own_b_recv)
    grad_shifted, grad_send, sums_one, a_y, qkv_second, own_b_sum, out_mine, fc2_mine, fc2_recv, fc1_recv, own_hidden, far_hidden = hold(
        grad_shifted, grad_send, sums_one, a_y, qkv_second, own_b_sum, out_mine, fc2_mine, fc2_recv, fc1_recv, own_hidden, far_hidden
    )

    b_send, fc2_mine, fc1_mine = combine(
        at,
        summed(a_shape, term(own_b_sum, theirs_y, half_rows_out), term(qkv_second, theirs_y, half_rows_out)),
        z_sides(fc2_mine, fc2_recv),
        summed(fc1_mine.shape, term(fc1_mine), term(fc1_recv)),
    )
    b_y, fc1_recv = over(1, b_send), over(2, fc1_mine)
    grad_recv = over_x(grad_send)
    vectors = pack_vectors(at, counts.shape[0], sums_one, sums_two, own_fc1_bias, far_fc1_bias_sum)
    vectors_recv = over(1, vectors)
    b_y, vectors_recv, fc1_mine, fc1_recv, own_hidden, fc2_mine = hold(
        b_y, vectors_recv, fc1_mine, fc1_recv, own_hidden, fc2_mine
    )

    z_rows = half_rows_out // 4

    def qkv_quarter(k):
        def within(flags):
            return mine_y(flags) * 4 + quarter_z(k)(flags)

        parts = [
            (side_k, None, [term(total, within, z_rows), term(recv, within, z_rows), term(recv_y, quarter_z(k), z_rows)])
            for side_k, (total, recv, recv_y) in enumerate(((own_a_sum, qkv_first, a_y), (own_b_sum, qkv_second, b_y)))
        ]
        return (2, 3, z_rows, side_a), parts

    *qkv_sends, qkv_mine, fc1_mine = combine(
        at,
        *[qkv_quarter(k) for k in masks],
        qkv_quarter(0),
        z_sides(fc1_mine, fc1_recv),
    )
    qkv_recv = [over_mask(mask, sent) for mask, sent in zip(masks.values(), qkv_sends)]
    fc2_y = over(1, fc2_mine)
    vectors = vectors + vectors_recv
    output_low = output_layer(pair_nat, chunks, chunks, far_hidden, mlp_low, far_fc2, middle, fc2_row, chunk)
    mlp_high = output_own(0, chunks, own_hidden, w_fc2, chunk)
    mlp_high, output_low, grad_recv, vectors, fc1_mine, fc2_mine, fc2_y, *qkv_recv = hold(
        mlp_high, output_low, grad_recv, vectors, fc1_mine, fc2_mine, fc2_y, *qkv_recv
    )

    qkv_mine, fc2_half = combine(
        at,
        summed(qkv_mine.shape, *[term(v) for v in (qkv_mine, *qkv_recv)]),
        y_sides(fc2_mine, fc2_y),
    )
    qkv_parts = [qkv_mine] + [over_mask(mask, qkv_mine) for mask in masks.values()]
    fc1_y = over(1, fc1_mine)
    output_recv = over_x(output_low)
    output_high = output_layer(pair_nat, 0, chunks, far_hidden, mlp_high, far_fc2, middle, fc2_row, chunk)
    out_z = over(2, out_mine)
    fc2_grad = finish_columns(pair_nat, [fc2_half, over(0, fc2_half)])
    vectors, fc1_y, fc2_grad, out_mine, out_z, grad_recv, output_recv, output_high, *qkv_parts = hold(
        vectors, fc1_y, fc2_grad, out_mine, out_z, grad_recv, output_recv, output_high, *qkv_parts
    )

    qkv_mine, fc1_half, out_mine = combine(
        at,
        (
            (2, 3, half_rows_out, side_a),
            [(None, quarter_z(k), [term(v)]) for k, v in zip((0, *masks), qkv_parts)],
        ),
        y_sides(fc1_mine, fc1_y),
        summed(out_shape, term(out_mine), term(out_z)),
    )
    qkv_y, qkv_core = over(1, qkv_mine), over(0, qkv_mine)
    fc1_core = over(0, fc1_half)
    out_z = over(3, out_mine)
    vectors = vectors + over_x(vectors)
    vectors_recv = over(2, vectors)
    input_grad = joined(mp_at, grad_shifted[None, :half_rows], grad_recv[None].astype(F32))
    fc1_grad = finish_rows(pair_nat, [fc1_half, fc1_core])
    qkv_mine, qkv_y, qkv_core, vectors_recv, fc1_grad, out_mine, out_z, input_grad = hold(
        qkv_mine, qkv_y, qkv_core, vectors_recv, fc1_grad, out_mine, out_z, input_grad
    )

    qkv_last = over(0, qkv_y)
    out_mine = combine(at, summed(out_shape, term(out_mine), term(out_z)))[0]
    out_y, out_core = over(1, out_mine), over(0, out_mine)
    qkv_grad = finish_stack(core_first_nat, 0, [qkv_mine, qkv_core])
    block_output = joined(mp_at, output_high[None], output_recv[None])
    vectors = vectors + vectors_recv
    vectors_recv = over(3, vectors)
    qkv_last, qkv_grad, vectors_recv, out_y, out_core, block_output = hold(
        qkv_last, qkv_grad, vectors_recv, out_y, out_core, block_output
    )

    vectors = vectors + vectors_recv
    vectors = vectors + over(0, vectors)
    out_grad = finish_turned(core_first_nat, [out_mine, out_core, out_y, over(0, out_y)])
    qkv_grad = finish_stack(core_first_nat, 2, [qkv_y, qkv_last], qkv_grad)
    qkv_grad = jnp.transpose(qkv_grad, (1, 0, 2))

    table = counts.shape[0]
    lead_grad, singles, rest = vectors[:table], vectors[table : table + 6], vectors[table + 6 :]
    qv_bias_grad = part(rest[:2], mp_at, 2, 1)
    fc1_bias_grad = part(rest[2:].reshape(-1), mp_at, 2)
    return (
        block_output,
        input_grad,
        lead_grad,
        singles[0],
        singles[1],
        qkv_grad,
        qv_bias_grad,
        out_grad,
        singles[4],
        singles[2],
        singles[3],
        fc1_grad,
        fc1_bias_grad,
        fc2_grad,
        singles[5],
    )


def solution(mesh):
    in_specs = (
        P("dp", "mp", None),
        P("dp", "mp", None),
        P("dp"),
        P(),
        P(),
        P(),
        P(),
        P(None, None, "mp"),
        P(None, "mp"),
        P("mp", None),
        P(),
        P(),
        P(),
        P(None, "mp"),
        P("mp"),
        P("mp", None),
        P(),
    )
    out_specs = (
        P("dp", "mp", None),
        P("dp", "mp", None),
        P(),
        P(),
        P(),
        P(None, None, "mp"),
        P(None, "mp"),
        P("mp", None),
        P(),
        P(),
        P(),
        P(None, "mp"),
        P("mp"),
        P("mp", None),
        P(),
    )
    def local(*args):
        replicas = lax.axis_size("dp")
        samples, half_rows, width = args[0].shape
        heads_width, units = args[7].shape[2], args[13].shape[1]
        fits = samples == 2 and lax.axis_size("mp") == 2 and replicas == 16
        even = half_rows % 256 == 0 and width == 2 * heads_width == 1024 and units == 2 * width
        return (fast_body if fits and even else body)(*args)

    return jax.shard_map(local, mesh=mesh, in_specs=in_specs, out_specs=out_specs, check_vma=False)
```

```python
import functools
import math

import jax
import jax.numpy as jnp
from jax import lax
from jax.experimental import pallas as pl
from jax.experimental.pallas import tpu as pltpu
from jax.sharding import PartitionSpec as P

HD = 64


EPS = 1e-05


def norm_forward(values, norm_gain, norm_shift):
    center = values - jnp.mean(values, axis=-1, keepdims=True)
    inverse = lax.rsqrt(jnp.mean(center * center, axis=-1, keepdims=True) + EPS)
    scaled = center * inverse
    return (scaled * norm_gain + norm_shift, scaled, inverse)


def norm_backward(grad_out, scaled, inverse, norm_gain):
    grad_scaled = grad_out * norm_gain
    grad_mean = jnp.mean(grad_scaled, axis=-1, keepdims=True)
    cross_mean = jnp.mean(grad_scaled * scaled, axis=-1, keepdims=True)
    grad_in = inverse * (grad_scaled - grad_mean - scaled * cross_mean)
    gain_grad = jnp.sum(grad_out * scaled, axis=(0, 1))
    shift_grad = jnp.sum(grad_out, axis=(0, 1))
    return (grad_in, gain_grad, shift_grad)


def gelu_slope(pre_act):
    normal_cdf = 0.5 * (1.0 + lax.erf(pre_act * 0.7071067811865476))
    return normal_cdf + pre_act * jnp.exp(-0.5 * pre_act * pre_act) * 0.3989422804014327


def attention_forward(query_all, key_all, value_all, block_rows):
    block_count = query_all.shape[0] // block_rows
    query_blocks = query_all.reshape((block_count, block_rows) + query_all.shape[1:])

    def one_block(query_block):
        scores = (
            jnp.einsum("qshd,kshd->shqk", query_block, key_all, preferred_element_type=jnp.float32)
            * 0.125
        )
        row_max = jnp.max(scores, axis=-1, keepdims=True)
        powers = jnp.exp(scores - row_max)
        exp_total = jnp.sum(powers, axis=-1, keepdims=True)
        attn_weights = (powers / exp_total).astype(jnp.bfloat16)
        attended = jnp.einsum(
            "shqk,kshd->qshd", attn_weights, value_all, preferred_element_type=jnp.float32
        )
        return (attended.astype(jnp.bfloat16), (row_max + jnp.log(exp_total))[..., 0])

    attended, log_total = lax.map(one_block, query_blocks)
    return (attended.reshape(query_all.shape), log_total)


def attention_backward(query_all, key_all, value_all, grad_attended, log_total, block_rows):
    block_count = query_all.shape[0] // block_rows
    query_blocks = query_all.reshape((block_count, block_rows) + query_all.shape[1:])
    grad_blocks = grad_attended.reshape((block_count, block_rows) + query_all.shape[1:])

    def one_block(running, sliced):
        key_grad, value_grad = running
        query_block, grad_block, log_block = sliced
        scores = (
            jnp.einsum("qshd,kshd->shqk", query_block, key_all, preferred_element_type=jnp.float32)
            * 0.125
        )
        attn_weights = jnp.exp(scores - log_block[..., None])
        weight_low = attn_weights.astype(jnp.bfloat16)
        grad_weights = jnp.einsum(
            "qshd,kshd->shqk", grad_block, value_all, preferred_element_type=jnp.float32
        )
        inner = jnp.sum(attn_weights * grad_weights, axis=-1, keepdims=True)
        grad_scores = (attn_weights * (grad_weights - inner)).astype(jnp.bfloat16)
        query_grad = (
            jnp.einsum("shqk,kshd->qshd", grad_scores, key_all, preferred_element_type=jnp.float32)
            * 0.125
        )
        key_grad = (
            key_grad
            + jnp.einsum(
                "shqk,qshd->kshd", grad_scores, query_block, preferred_element_type=jnp.float32
            )
            * 0.125
        )
        value_grad = value_grad + jnp.einsum(
            "shqk,qshd->kshd", weight_low, grad_block, preferred_element_type=jnp.float32
        )
        return ((key_grad, value_grad), query_grad.astype(jnp.bfloat16))

    zero_grad = jnp.zeros(key_all.shape, jnp.float32)
    (key_grad, value_grad), query_grad = lax.scan(
        one_block, (zero_grad, zero_grad), (query_blocks, grad_blocks, log_total)
    )
    return (
        query_grad.reshape(query_all.shape),
        key_grad.astype(jnp.bfloat16),
        value_grad.astype(jnp.bfloat16),
    )


def body(
    tokens,
    cotangent,
    buckets,
    counts,
    lead_table,
    norm1_gain,
    norm1_shift,
    w_qkv,
    qv_bias,
    w_out,
    out_bias,
    norm2_gain,
    norm2_shift,
    w_fc1,
    fc1_bias,
    w_fc2,
    fc2_bias,
):
    samples_here = tokens.shape[0]
    local_rows = tokens.shape[1]
    local_width = w_qkv.shape[2]
    local_heads = local_width // HD
    seq_len = local_rows * lax.axis_size("mp")
    block_rows = min(512, seq_len)
    head_shape = (seq_len, samples_here, local_heads, HD)
    count_f = counts.astype(jnp.float32)
    onehot = (buckets[:, None] == jnp.arange(counts.shape[0], dtype=jnp.int32)[None, :]).astype(
        jnp.float32
    )
    loss_weight = jnp.mean(count_f) / jnp.sum(onehot * count_f[None, :], axis=1)
    lead_rows = jnp.dot(
        onehot,
        lead_table.astype(jnp.float32),
        precision=lax.Precision.HIGHEST,
        preferred_element_type=jnp.float32,
    )
    shifted = jnp.swapaxes(tokens, 0, 1).astype(jnp.float32) + lead_rows[None]
    normed_one, scaled_one, inverse_one = norm_forward(
        shifted, norm1_gain.astype(jnp.float32), norm1_shift.astype(jnp.float32)
    )
    normed_one = normed_one.astype(jnp.bfloat16)
    normed_full = lax.all_gather(normed_one, "mp", axis=0, tiled=True)
    project = jnp.einsum("tsd,dcf->tscf", normed_full, w_qkv, preferred_element_type=jnp.float32)
    bias_f = qv_bias.astype(jnp.float32)
    query_all = (project[:, :, 0] + bias_f[0]).astype(jnp.bfloat16).reshape(head_shape)
    key_all = project[:, :, 1].astype(jnp.bfloat16).reshape(head_shape)
    value_all = (project[:, :, 2] + bias_f[1]).astype(jnp.bfloat16).reshape(head_shape)
    attended, log_total = attention_forward(query_all, key_all, value_all, block_rows)
    attended_flat = attended.reshape(seq_len, samples_here, local_width)
    picked = attended_flat
    branch = lax.psum_scatter(
        jnp.einsum("tsf,fd->tsd", picked, w_out, preferred_element_type=jnp.float32),
        "mp",
        scatter_dimension=0,
        tiled=True,
    )
    middle = shifted + branch + out_bias.astype(jnp.float32)
    gain_two = norm2_gain.astype(jnp.float32)
    normed_two, scaled_two, inverse_two = norm_forward(
        middle, gain_two, norm2_shift.astype(jnp.float32)
    )
    normed_two = normed_two.astype(jnp.bfloat16)
    grad_top = jnp.swapaxes(cotangent, 0, 1).astype(jnp.float32) * loss_weight[None, :, None]
    grad_low = grad_top.astype(jnp.bfloat16)
    fc1_full, fc1_bias_full, fc2_full = (
        lax.all_gather(w_fc1, "mp", axis=1, tiled=True),
        lax.all_gather(fc1_bias, "mp", axis=0, tiled=True),
        lax.all_gather(w_fc2, "mp", axis=0, tiled=True),
    )
    pre_act = jnp.einsum(
        "tsd,df->tsf", normed_two, fc1_full, preferred_element_type=jnp.float32
    ) + fc1_bias_full.astype(jnp.float32)
    hidden = jax.nn.gelu(pre_act, approximate=False).astype(jnp.bfloat16)
    mlp_branch = jnp.einsum("tsf,fd->tsd", hidden, fc2_full, preferred_element_type=jnp.float32)
    output = middle + mlp_branch + fc2_bias.astype(jnp.float32)
    grad_hidden = jnp.einsum("tsd,fd->tsf", grad_low, fc2_full, preferred_element_type=jnp.float32)
    grad_pre = (grad_hidden * gelu_slope(pre_act)).astype(jnp.bfloat16)
    grad_normed_two = jnp.einsum(
        "tsf,df->tsd", grad_pre, fc1_full, preferred_element_type=jnp.float32
    )
    fc1_part = jnp.einsum("tsd,tsf->df", normed_two, grad_pre, preferred_element_type=jnp.float32)
    fc1_bias_part = jnp.sum(grad_pre.astype(jnp.float32), axis=(0, 1))
    fc2_part = jnp.einsum("tsf,tsd->fd", hidden, grad_low, preferred_element_type=jnp.float32)
    fc1_grad, fc1_bias_grad, fc2_grad = (
        lax.psum_scatter(
            fc1_part.astype(jnp.bfloat16), "mp", scatter_dimension=1, tiled=True
        ).astype(jnp.float32),
        lax.psum_scatter(
            fc1_bias_part.astype(jnp.bfloat16), "mp", scatter_dimension=0, tiled=True
        ).astype(jnp.float32),
        lax.psum_scatter(
            fc2_part.astype(jnp.bfloat16), "mp", scatter_dimension=0, tiled=True
        ).astype(jnp.float32),
    )
    fc2_bias_grad = jnp.sum(grad_top, axis=(0, 1))
    grad_from_norm, gain_two_grad, shift_two_grad = norm_backward(
        grad_normed_two, scaled_two, inverse_two, gain_two
    )
    grad_middle = grad_top + grad_from_norm
    out_bias_grad = jnp.sum(grad_middle, axis=(0, 1))
    grad_branch = grad_middle.astype(jnp.bfloat16)
    grad_branch_full = lax.all_gather(grad_branch, "mp", axis=0, tiled=True)
    out_grad = jnp.einsum(
        "tsf,tsd->fd", attended_flat, grad_branch_full, preferred_element_type=jnp.float32
    )
    grad_attended = jnp.einsum(
        "tsd,fd->tsf", grad_branch_full, w_out, preferred_element_type=jnp.float32
    ).astype(jnp.bfloat16)
    query_grad, key_grad, value_grad = attention_backward(
        query_all, key_all, value_all, grad_attended.reshape(head_shape), log_total, block_rows
    )
    grad_project = jnp.stack([query_grad, key_grad, value_grad], axis=2).reshape(
        seq_len, samples_here, 3, local_width
    )
    qkv_grad = jnp.einsum(
        "tsd,tscf->dcf", normed_full, grad_project, preferred_element_type=jnp.float32
    )
    query_bias_grad = jnp.sum(query_grad.astype(jnp.float32), axis=(0, 1)).reshape(local_width)
    value_bias_grad = jnp.sum(value_grad.astype(jnp.float32), axis=(0, 1)).reshape(local_width)
    qv_bias_grad = jnp.stack([query_bias_grad, value_bias_grad])
    picked = grad_project
    grad_normed_one = lax.psum_scatter(
        jnp.einsum("tscf,dcf->tsd", picked, w_qkv, preferred_element_type=jnp.float32).astype(
            jnp.bfloat16
        ),
        "mp",
        scatter_dimension=0,
        tiled=True,
    ).astype(jnp.float32)
    grad_in_one, gain_one_grad, shift_one_grad = norm_backward(
        grad_normed_one, scaled_one, inverse_one, norm1_gain.astype(jnp.float32)
    )
    grad_shifted = grad_middle + grad_in_one
    lead_grad = jnp.dot(
        onehot.T,
        jnp.sum(grad_shifted, axis=0),
        precision=lax.Precision.HIGHEST,
        preferred_element_type=jnp.float32,
    )
    small_grads = jnp.stack(
        [gain_one_grad, shift_one_grad, out_bias_grad, gain_two_grad, shift_two_grad, fc2_bias_grad]
    )
    lead_grad, small_grads = lax.psum((lead_grad, small_grads), ("dp", "mp"))
    qkv_grad, qv_bias_grad, out_grad, fc1_grad, fc1_bias_grad, fc2_grad = (
        lax.psum(qkv_grad.astype(jnp.bfloat16), "dp").astype(jnp.float32),
        lax.psum(qv_bias_grad.astype(jnp.bfloat16), "dp").astype(jnp.float32),
        lax.psum(out_grad.astype(jnp.bfloat16), "dp").astype(jnp.float32),
        lax.psum(fc1_grad.astype(jnp.bfloat16), "dp").astype(jnp.float32),
        lax.psum(fc1_bias_grad.astype(jnp.bfloat16), "dp").astype(jnp.float32),
        lax.psum(fc2_grad.astype(jnp.bfloat16), "dp").astype(jnp.float32),
    )
    block_output = jnp.swapaxes(output, 0, 1).astype(jnp.bfloat16)
    input_grad = jnp.swapaxes(grad_shifted, 0, 1)
    return (
        block_output,
        input_grad,
        lead_grad,
        small_grads[0],
        small_grads[1],
        qkv_grad,
        qv_bias_grad,
        out_grad,
        small_grads[2],
        small_grads[3],
        small_grads[4],
        fc1_grad,
        fc1_bias_grad,
        fc2_grad,
        small_grads[5],
    )


F32 = jnp.float32
BF16 = jnp.bfloat16
NN = (((1,), (0,)), ((), ()))
NT = (((1,), (1,)), ((), ()))
TN = (((0,), (0,)), ((), ()))
MIB = 1 << 20


def dot(left, right, dims):
    return lax.dot_general(left, right, dims, preferred_element_type=F32)


def whole(array):
    return pl.BlockSpec(array.shape, lambda *_: (0,) * array.ndim, pipeline_mode=pl.Buffered(1))


def kernel_call(body, name, grid, scalars, ins, outs, scratch=(), vmem=26, time=6, pinned=(), alias=None):
    spec = pltpu.PrefetchScalarGridSpec(
        num_scalar_prefetch=len(scalars),
        grid=grid,
        in_specs=[spec for _, spec in ins],
        out_specs=[spec for _, spec in outs],
        scratch_shapes=list(scratch),
    )
    return pl.pallas_call(
        body,
        out_shape=[shape for shape, _ in outs],
        grid_spec=spec,
        compiler_params=pltpu.CompilerParams(vmem_limit_bytes=vmem * MIB),
        input_output_aliases={} if alias is None else {len(scalars) + alias: 0},
        cost_estimate=pl.CostEstimate(flops=MIB, transcendentals=0, bytes_accessed=int(time * 2 * MIB)),
        name=name,
    )(
        *scalars,
        *[
            pltpu.with_memory_space_constraint(array, pltpu.HBM) if k in pinned else array
            for k, (array, _) in enumerate(ins)
        ],
    )


def struct(shape, dtype=BF16):
    return jax.ShapeDtypeStruct(shape, dtype)


def centred(values):
    center = values - jnp.mean(values, axis=-1, keepdims=True)
    inverse = lax.rsqrt(jnp.mean(center * center, axis=-1, keepdims=True) + EPS)
    return center * inverse, inverse


def norm_input_grad(grad_out, scaled, inverse, gain):
    grad_scaled = grad_out * gain
    grad_mean = jnp.mean(grad_scaled, axis=-1, keepdims=True)
    cross_mean = jnp.mean(grad_scaled * scaled, axis=-1, keepdims=True)
    return inverse * (grad_scaled - grad_mean - scaled * cross_mean)


def column_sum(values):
    return jnp.sum(values, axis=0, keepdims=True)


def chunk_of(nat_ref, index, size):
    return pl.ds(pl.multiple_of(nat_ref[index] * size, size), size)


def attention_forward_kernel(block, qkv_ref, out_ref, power_ref, inverse_ref):
    rows_all = qkv_ref.shape[1]
    steps = [(head, start) for head in range(2) for start in range(0, rows_all, block)]

    def scores_of(head, start):
        lanes = slice(HD * head, HD * head + HD)
        query = qkv_ref[0, start : start + block, lanes] * BF16(0.125)
        return dot(qkv_ref[1, :, lanes], query, NT)

    outs = [[], []]
    ahead = scores_of(*steps[0])
    for k, (head, start) in enumerate(steps):
        scores = ahead
        if k + 1 < len(steps):
            ahead = scores_of(*steps[k + 1])
        lanes = slice(HD * head, HD * head + HD)
        rows = slice(start, start + block)
        powers = jnp.exp2((scores - jnp.max(scores, axis=0, keepdims=True)) * 1.4426950408889634)
        inverse = 1.0 / jnp.sum(powers, axis=0, keepdims=True)
        power_low = powers.astype(BF16)
        power_ref[head, :, rows] = power_low
        inverse_ref[0, head : head + 1, rows] = inverse
        outs[head].append(dot(qkv_ref[2, :, lanes], power_low, TN) * inverse)
    heads = [jnp.concatenate(parts, axis=1) for parts in outs]
    out_ref[...] = jnp.concatenate(heads, axis=0).T.astype(BF16)


def attend(qkv):
    _, rows, width = qkv.shape
    pairs = width // (2 * HD)
    return kernel_call(
        functools.partial(attention_forward_kernel, min(512, rows)),
        "attention_forward",
        (pairs,),
        [],
        [(qkv, pl.BlockSpec((3, rows, 2 * HD), lambda j: (0, 0, j)))],
        [
            (struct((rows, width)), pl.BlockSpec((rows, 2 * HD), lambda j: (0, j))),
            (pltpu.HBM((2 * pairs, rows, rows), BF16), pl.BlockSpec((2, rows, rows), lambda j: (j, 0, 0))),
            (struct((pairs, 2, rows), F32), pl.BlockSpec((1, 2, rows), lambda j: (j, 0, 0))),
        ],
        vmem=28,
        time=4 * pairs,
        pinned=[0],
    )


def attention_backward_kernel(block, qkv_ref, power_ref, inverse_ref, out_ref, grad_ref, dqkv_ref, sums_ref):
    rows_all = qkv_ref.shape[1]
    out_t = out_ref[...].astype(F32).T
    grad_t = grad_ref[...].astype(F32).T
    heads = []
    for head in range(2):
        lanes = slice(HD * head, HD * head + HD)
        inverse = inverse_ref[0, head : head + 1, :]
        grad_head = grad_t[lanes]
        inner = jnp.sum(grad_head * out_t[lanes], axis=0, keepdims=True) * inverse
        grad_scaled = grad_head * inverse
        heads.append((inner, grad_scaled.astype(BF16), grad_scaled.T.astype(BF16), lanes))
    steps = [(head, start) for head in range(2) for start in range(0, rows_all, block)]

    def grad_power_of(head, start):
        _, grad_low_t, _, lanes = heads[head]
        return dot(qkv_ref[2, :, lanes], grad_low_t[:, start : start + block], NN)

    ahead = grad_power_of(*steps[0])
    sums = [[None, None, []], [None, None, []]]
    for k, (head, start) in enumerate(steps):
        grad_power = ahead
        if k + 1 < len(steps):
            ahead = grad_power_of(*steps[k + 1])
        inner, _, grad_low, lanes = heads[head]
        rows = slice(start, start + block)
        power = power_ref[head, :, rows]
        grad_scores = (power.astype(F32) * (grad_power - inner[:, rows])).astype(BF16)
        key_part = dot(grad_scores, qkv_ref[0, rows, lanes] * BF16(0.125), NN)
        value_part = dot(power, grad_low[rows], NN)
        own = sums[head]
        own[0] = key_part if own[0] is None else own[0] + key_part
        own[1] = value_part if own[1] is None else own[1] + value_part
        own[2].append(dot(qkv_ref[1, :, lanes].T, grad_scores, NN))
    for (_, _, _, lanes), (key_grad, value_grad, query_grads) in zip(heads, sums):
        sums_ref[0, :, lanes] = jnp.concatenate(query_grads, axis=1).T * 0.125
        sums_ref[1, :, lanes] = key_grad
        sums_ref[2, :, lanes] = value_grad
    dqkv_ref[...] = sums_ref[...].astype(BF16)


def attend_back(first, count, qkv, powers, inverse, attended, grad_attended):
    _, rows, width = qkv.shape
    block = (3, rows, 2 * HD)
    flat = pl.BlockSpec((rows, 2 * HD), lambda j: (0, j + first))
    return kernel_call(
        functools.partial(attention_backward_kernel, min(256, rows)),
        "attention_backward",
        (count,),
        [],
        [
            (qkv, pl.BlockSpec(block, lambda j: (0, 0, j + first))),
            (powers, pl.BlockSpec((2, rows, rows), lambda j: (j + first, 0, 0))),
            (inverse, pl.BlockSpec((1, 2, rows), lambda j: (j + first, 0, 0))),
            (attended, flat),
            (grad_attended, flat),
        ],
        [(struct((3, rows, 2 * HD * count)), pl.BlockSpec(block, lambda j: (0, 0, j)))],
        [pltpu.VMEM(block, F32)],
        vmem=28,
        time=5.5 * count,
        pinned=range(5),
    )[0]


def project_own_kernel(at_ref, tokens_ref, recv_ref, lead_ref, gain_ref, shift_ref, weight_ref, bias_ref, rows_ref, normed_ref, heads_ref):
    own = pl.program_id(0) < pl.num_programs(0) // 2
    tokens = jnp.where(own, tokens_ref[0].astype(F32), recv_ref[...].astype(F32))
    rows_ref[...] = tokens.astype(BF16)
    scaled, _ = centred(tokens + lead_ref[...])
    normed = (scaled * gain_ref[...] + shift_ref[...]).astype(BF16)
    normed_ref[...] = normed
    for c in range(3):
        heads_ref[c] = (dot(normed, weight_ref[c], NN) + bias_ref[c : c + 1]).astype(BF16)


def project_own(at, tokens, recv, lead, gain, shift, weight, bias, chunk):
    half, width = tokens.shape[1:]
    heads = weight.shape[2]
    steps = half // chunk
    row = pl.BlockSpec((chunk, width), lambda j, at: (j, 0))
    return kernel_call(
        project_own_kernel,
        "project_own",
        (2 * steps,),
        [at],
        [
            (tokens, pl.BlockSpec((1, chunk, width), lambda j, at: (at[0], jnp.minimum(j, steps - 1), 0))),
            (recv, pl.BlockSpec((chunk, width), lambda j, at: (jnp.maximum(j - steps, 0), 0))),
            *[(v, whole(v)) for v in (lead, gain, shift, weight, bias)],
        ],
        [
            (struct((2 * half, width)), row),
            (struct((2 * half, width)), row),
            (pltpu.HBM((3, 2 * half, heads), BF16), pl.BlockSpec((3, chunk, heads), lambda j, at: (0, j, 0))),
        ],
        pinned=[0, 1, 5],
    )


def project_far_kernel(nat_ref, normed_ref, bias_ref, *refs):
    *pieces, heads_ref = refs
    size = pieces[0].shape[1]
    total = bias_ref[0]
    for k, piece in enumerate(pieces):
        total = total + dot(normed_ref[:, chunk_of(nat_ref, k, size)], piece[0], NN)
    heads_ref[0] = total.astype(BF16)


def project_far(nat, normed, bias, pieces):
    rows = normed.shape[0]
    heads = pieces[0].shape[2]
    first = lambda j, nat: (j, 0, 0)
    return kernel_call(
        project_far_kernel,
        "project_far",
        (3,),
        [nat],
        [
            (normed, whole(normed)),
            (bias[:, None], pl.BlockSpec((1, 1, heads), first)),
            *[(p, pl.BlockSpec((1, *p.shape[1:]), first)) for p in pieces],
        ],
        [(pltpu.HBM((3, rows, heads), BF16), pl.BlockSpec((1, rows, heads), first))],
    )[0]


def middle_kernel(nat_ref, own_ref, far_ref, weight_ref, rows_ref, lead_ref, bias_ref, gain_ref, shift_ref, *refs):
    *pieces, middle_ref, normed_ref = refs
    total = dot(own_ref[...], weight_ref[...], NN)
    for k, piece in enumerate(pieces):
        total = total + dot(far_ref[:, chunk_of(nat_ref, k, piece.shape[0])], piece[...], NN)
    middle = rows_ref[...].astype(F32) + lead_ref[...] + total + bias_ref[...]
    middle_ref[...] = middle
    scaled, _ = centred(middle)
    normed_ref[...] = (scaled * gain_ref[...] + shift_ref[...]).astype(BF16)


def middle_layer(nat, own, far, weight, pieces, rows, lead, bias, gain, shift, chunk):
    count, width = rows.shape
    row = pl.BlockSpec((chunk, width), lambda j, nat: (j, 0))
    heads = pl.BlockSpec((chunk, own.shape[1]), lambda j, nat: (j, 0))
    return kernel_call(
        middle_kernel,
        "middle_layer",
        (count // chunk,),
        [nat],
        [(own, heads), (far, heads), (weight, whole(weight)), (rows, row)]
        + [(v, whole(v)) for v in (lead, bias, gain, shift, *pieces)],
        [(pltpu.HBM((count, width), F32), row), (struct((count, width)), row)],
        pinned=[2, 3],
    )


def gelu_store(pre_act, rows, hidden_ref, slope_ref):
    cdf = 0.5 * (1.0 + lax.erf(pre_act * 0.7071067811865476))
    hidden_ref[rows] = (pre_act * cdf).astype(BF16)
    density = jnp.exp(-0.5 * pre_act * pre_act) * 0.3989422804014327
    slope_ref[rows] = (cdf + pre_act * density).astype(BF16)


def hidden_kernel(block, nat_ref, normed_ref, bias_ref, *refs):
    *pieces, hidden_ref, slope_ref = refs
    size = pieces[0].shape[0]
    for start in range(0, normed_ref.shape[0], block):
        rows = slice(start, start + block)
        pre_act = bias_ref[...]
        for k, piece in enumerate(pieces):
            lanes = slice(None) if len(pieces) == 1 else chunk_of(nat_ref, k, size)
            pre_act = pre_act + dot(normed_ref[rows, lanes], piece[...], NN)
        gelu_store(pre_act, rows, hidden_ref, slope_ref)


def hidden_layer(nat, normed, bias, pieces, chunk):
    rows = normed.shape[0]
    units = pieces[0].shape[1]
    tile = min(512, units)
    column = lambda j, nat: (0, j)
    return kernel_call(
        functools.partial(hidden_kernel, chunk),
        "hidden_layer",
        (units // tile,),
        [nat],
        [(normed, whole(normed)), (bias, pl.BlockSpec((1, tile), column))]
        + [(p, pl.BlockSpec((p.shape[0], tile), column)) for p in pieces],
        [(struct((rows, units)), pl.BlockSpec((rows, tile), column))] * 2,
        vmem=20,
        time=10,
        pinned=range(2, 2 + len(pieces)),
    )


def product_kernel(outs, add_count, by_step, _, left_ref, right_ref, *refs):
    adds, out_refs = refs[:add_count], refs[add_count:]
    stacked = len(right_ref.shape) == 3
    value = dot(left_ref[...], right_ref[0] if stacked else right_ref[...], TN)
    for add in adds:
        value = value + (add[0] if stacked else add[...]).astype(F32)
    value = value.astype(BF16)
    if stacked:
        out_refs[0][0] = value
    elif outs == 1:
        out_refs[0][...] = value
    elif by_step:
        for k, out_ref in enumerate(out_refs):

            @pl.when(pl.program_id(0) == k)
            def _(out_ref=out_ref):
                out_ref[...] = value
    else:
        size = value.shape[0] // outs
        for k, out_ref in enumerate(out_refs):
            out_ref[...] = value[k * size : (k + 1) * size]


def grad_right_half(half, left, right, *add):
    rows, columns = left.shape
    kept = right.shape[1] // 2
    tile = columns // 2
    out_spec = pl.BlockSpec((tile, kept), lambda j, half: (j, 0))
    outs = 2 if add else 1
    split = [(struct((tile, kept)), pl.BlockSpec((tile, kept), lambda j, half: (0, 0)))] * 2
    result = kernel_call(
        functools.partial(product_kernel, outs, len(add), True),
        "grad_right_half",
        (2,),
        [half],
        [
            (left, pl.BlockSpec((rows, tile), lambda j, half: (0, j))),
            (right, pl.BlockSpec((rows, kept), lambda j, half: (0, half[0]))),
        ]
        + [(a, out_spec) for a in add],
        split if add else [(struct((columns, kept)), out_spec)],
        vmem=20,
        time=3,
    )
    return result if add else result[0]


def grad_left_half(half, left, right, *add, split=False):
    rows = left.shape[0]
    kept = left.shape[1] // 2
    columns = right.shape[-1]
    tile = min(1024, columns)
    outs = 2 if split else 1
    left_spec = pl.BlockSpec((rows, kept), lambda j, half: (0, half[0]))
    if right.ndim == 3:
        grid, out_shape = (right.shape[0],), (right.shape[0], kept, columns)
        right_spec = pl.BlockSpec((1, rows, columns), lambda j, half: (j, 0, 0))
        add_spec = out_spec = pl.BlockSpec((1, kept, columns), lambda j, half: (j, 0, 0))
    else:
        grid, out_shape = (columns // tile,), (kept // outs, columns)
        right_spec = pl.BlockSpec((rows, tile), lambda j, half: (0, j))
        add_spec = pl.BlockSpec((kept, tile), lambda j, half: (0, j))
        out_spec = pl.BlockSpec((kept // outs, tile), lambda j, half: (0, j))
    result = kernel_call(
        functools.partial(product_kernel, outs, len(add), False),
        "grad_left_half",
        grid,
        [half],
        [(left, left_spec), (right, right_spec)] + [(a, add_spec) for a in add],
        [(struct(out_shape), out_spec)] * outs,
        vmem=20,
        time=3,
    )
    return result if split else result[0]


def term(array, at=None, size=None, column=None):
    block, index = list(array.shape), [None] * array.ndim
    if size is not None:
        block[-2], index[-2] = size, at
    if column is not None:
        block[-1], index[-1] = array.shape[-1] // 2, lambda _: column

    def index_map(_, flags):
        return tuple(0 if f is None else f(flags) for f in index)

    return array, pl.BlockSpec(tuple(block), index_map)


def combine_kernel(plan, flags_ref, *refs):
    count = sum(terms for parts in plan for _, _, terms in parts)
    ins, outs = list(refs[:count]), refs[count:]
    for parts, out_ref in zip(plan, outs):
        for lead, row, terms in parts:
            value = None
            for ref in ins[:terms]:
                part = ref[...] if terms == 1 else ref[...].astype(F32)
                value = part if value is None else value + part
            ins = ins[terms:]
            value = value.astype(BF16)
            if lead is not None:
                out_ref[lead] = value
            elif row is not None:
                size = value.shape[-2]
                start = row if isinstance(row, int) else pl.multiple_of(row(flags_ref) * size, size)
                where = (slice(None),) * (value.ndim - 2) + (pl.ds(start, size), slice(None))
                out_ref[where] = value
            else:
                out_ref[...] = value


def combine(flags, *outs):
    ins = [t for _, parts in outs for _, _, terms in parts for t in terms]
    plan = [[(lead, row, len(terms)) for lead, row, terms in parts] for _, parts in outs]

    def full(shape):
        return pl.BlockSpec(shape, lambda *_: (0,) * len(shape))

    return kernel_call(
        functools.partial(combine_kernel, plan),
        "combine",
        (1,),
        [flags],
        ins,
        [(struct(shape), full(shape)) for shape, _ in outs],
        vmem=32,
        time=3,
    )


def summed(shape, *terms):
    return shape, [(None, None, terms)]


def pre_grad_store(grad, slope_ref, pre_ref, sum_ref):
    pre = (grad * slope_ref[...].astype(F32)).astype(BF16)
    pre_ref[...] = pre
    sum_ref[...] = column_sum(pre.astype(F32))


def pre_grad_own_kernel(low_ref, weight_ref, slope_ref, pre_ref, sum_ref):
    pre_grad_store(dot(low_ref[...], weight_ref[...], NT), slope_ref, pre_ref, sum_ref)


def pre_grad_own(low, weight, slope):
    rows, width = low.shape
    units = weight.shape[0]
    tile = min(512, units)
    column = lambda j: (0, j)
    return kernel_call(
        pre_grad_own_kernel,
        "pre_grad_own",
        (units // tile,),
        [],
        [
            (low, whole(low)),
            (weight, pl.BlockSpec((tile, width), lambda j: (j, 0))),
            (slope, pl.BlockSpec((rows, tile), column)),
        ],
        [
            (struct((rows, units)), pl.BlockSpec((rows, tile), column)),
            (struct((1, units), F32), pl.BlockSpec((1, tile), column)),
        ],
        vmem=20,
        pinned=[1],
    )


def pre_grad_far_kernel(per, nat_ref, low_ref, slope_ref, *refs):
    *pieces, pre_ref, sum_ref = refs
    for k, piece in enumerate(pieces):

        @pl.when(pl.program_id(0) // per == k)
        def _(piece=piece):
            pre_grad_store(dot(low_ref[...], piece[...], NT), slope_ref, pre_ref, sum_ref)


def pre_grad_far(nat, low, pieces, slope):
    rows, width = low.shape
    size = pieces[0].shape[0]
    tile = min(512, size)
    per = size // tile
    units = size * len(pieces)
    column = lambda j, nat: (0, nat[j // per] * per + j % per)

    def piece_spec(k):
        return pl.BlockSpec((tile, width), lambda j, nat: (jnp.clip(j - k * per, 0, per - 1), 0))

    return kernel_call(
        functools.partial(pre_grad_far_kernel, per),
        "pre_grad_far",
        (len(pieces) * per,),
        [nat],
        [(low, whole(low)), (slope, pl.BlockSpec((rows, tile), column))]
        + [(p, piece_spec(k)) for k, p in enumerate(pieces)],
        [
            (struct((rows, units)), pl.BlockSpec((rows, tile), column)),
            (struct((1, units), F32), pl.BlockSpec((1, tile), column)),
        ],
        vmem=20,
        time=8,
        pinned=range(2, 2 + len(pieces)),
    )


def add_sums(sums_ref, rows):
    @pl.when(pl.program_id(0) == 0)
    def _():
        sums_ref[...] = jnp.zeros_like(sums_ref)

    for k, row in enumerate(rows):
        sums_ref[k : k + 1, :] += row


def middle_grad_kernel(
    nat_ref, at_ref, own_ref, far_ref, weight_ref, middle_ref, cot_ref, recv_ref, loss_ref, gain_ref, *refs
):
    *pieces, grad_ref, low_ref, sums_ref, total_ref = refs
    total_ref[...] = dot(own_ref[...], weight_ref[...], NT)
    for k, piece in enumerate(pieces):
        total_ref[:, chunk_of(nat_ref, k, piece.shape[0])] += dot(far_ref[...], piece[...], NT)
    grad = total_ref[...]
    scaled, inverse = centred(middle_ref[...])
    mine = pl.program_id(0) < pl.num_programs(0) // 2
    top = jnp.where(mine, cot_ref[0].astype(F32), recv_ref[...].astype(F32)) * loss_ref[...]
    grad_middle = top + norm_input_grad(grad, scaled, inverse, gain_ref[...])
    grad_ref[...] = grad_middle
    low_ref[...] = grad_middle.astype(BF16)
    add_sums(
        sums_ref,
        [column_sum(grad * scaled), column_sum(grad), column_sum(grad_middle), column_sum(top)],
    )


def middle_grad(nat, at, own, far, weight, pieces, middle, cot, recv, loss, gain, chunk):
    count, width = middle.shape
    row = pl.BlockSpec((chunk, width), lambda j, *_: (j, 0))
    units = pl.BlockSpec((chunk, own.shape[1]), lambda j, *_: (j, 0))
    steps = count // chunk // 2
    return kernel_call(
        middle_grad_kernel,
        "middle_grad",
        (count // chunk,),
        [nat, at],
        [
            (own, units),
            (far, units),
            (weight, whole(weight)),
            (middle, row),
            (cot, pl.BlockSpec((1, chunk, width), lambda j, nat, at: (at[0], jnp.minimum(j, steps - 1), 0))),
            (recv, pl.BlockSpec((chunk, width), lambda j, *_: (jnp.maximum(j - steps, 0), 0))),
        ]
        + [(v, whole(v)) for v in (loss, gain, *pieces)],
        [
            (struct((count, width), F32), row),
            (struct((count, width)), row),
            (struct((8, width), F32), pl.BlockSpec((8, width), lambda j, *_: (0, 0))),
        ],
        [pltpu.VMEM((chunk, width), F32)],
        time=14,
        pinned=[2, 3, 4, 5, *range(8, 8 + len(pieces))],
    )


def attended_grad_kernel(nat_ref, low_ref, weight_ref, *refs):
    *pieces, own_ref, far_ref = refs
    own_ref[...] = dot(low_ref[...], weight_ref[...], NT).astype(BF16)
    for k, piece in enumerate(pieces):
        far_ref[:, chunk_of(nat_ref, k, piece.shape[0])] = dot(low_ref[...], piece[...], NT).astype(BF16)


def attended_grad(nat, low, weight, pieces, chunk):
    count, width = low.shape
    heads = weight.shape[0]
    out = (struct((count, heads)), pl.BlockSpec((chunk, heads), lambda j, nat: (j, 0)))
    return kernel_call(
        attended_grad_kernel,
        "attended_grad",
        (count // chunk,),
        [nat],
        [(low, pl.BlockSpec((chunk, width), lambda j, nat: (j, 0)))] + [(v, whole(v)) for v in (weight, *pieces)],
        [out, out],
        pinned=range(1, 2 + len(pieces)),
    )


def output_own_kernel(own_ref, weight_ref, out_ref):
    out_ref[...] = dot(own_ref[...], weight_ref[...], NN)


def output_own(first, count, own, weight, chunk):
    units = own.shape[1]
    width = weight.shape[1]
    return kernel_call(
        output_own_kernel,
        "output_own",
        (count,),
        [],
        [(own, pl.BlockSpec((chunk, units), lambda j: (j + first, 0))), (weight, whole(weight))],
        [(struct((count * chunk, width), F32), pl.BlockSpec((chunk, width), lambda j: (j, 0)))],
        vmem=20,
        time=4,
        pinned=range(2),
    )[0]


def output_kernel(nat_ref, far_ref, own_ref, middle_ref, bias_ref, *refs):
    *pieces, out_ref = refs
    total = own_ref[...]
    for k, piece in enumerate(pieces):
        total = total + dot(far_ref[:, chunk_of(nat_ref, k, piece.shape[0])], piece[...], NN)
    out_ref[...] = (middle_ref[...] + total + bias_ref[...]).astype(BF16)


def output_layer(nat, first, count, far, own, pieces, middle, bias, chunk):
    width = middle.shape[1]
    row = pl.BlockSpec((chunk, width), lambda j, nat: (j + first, 0))
    here = pl.BlockSpec((chunk, width), lambda j, nat: (j, 0))
    return kernel_call(
        output_kernel,
        "output_layer",
        (count,),
        [nat],
        [(far, pl.BlockSpec((chunk, far.shape[1]), lambda j, nat: (j + first, 0))), (own, here), (middle, row)]
        + [(v, whole(v)) for v in (bias, *pieces)],
        [(struct((count * chunk, width)), pl.BlockSpec((chunk, width), lambda j, nat: (j, 0)))],
        vmem=20,
        time=6,
        pinned=range(4 + len(pieces)),
    )[0]


def input_grad_kernel(own_count, nat_ref, far_ref, weight_ref, rows_ref, lead_ref, grad_ref, gain_ref, *refs):
    owns, refs = refs[:own_count], refs[own_count:]
    *pieces, out_ref, low_ref, sums_ref, total_ref = refs
    total = None
    at = 0
    for own in owns:
        size = own.shape[2]
        for c in range(3):
            part = dot(own[c], weight_ref[c, :, at : at + size], NT)
            total = part if total is None else total + part
        at += size
    total_ref[...] = total
    for k, piece in enumerate(pieces):
        part = dot(far_ref[0], piece[0], NT) + dot(far_ref[1], piece[1], NT) + dot(far_ref[2], piece[2], NT)
        total_ref[:, chunk_of(nat_ref, k, piece.shape[1])] += part
    grad = total_ref[...]
    scaled, inverse = centred(rows_ref[...].astype(F32) + lead_ref[...])
    grad_shifted = grad_ref[...] + norm_input_grad(grad, scaled, inverse, gain_ref[...])
    out_ref[...] = grad_shifted
    low_ref[...] = grad_shifted.astype(BF16)
    bias_rows = [
        jnp.concatenate([column_sum(d[c].astype(F32)) for d in (*owns, far_ref)], axis=1) for c in (0, 2)
    ]
    add_sums(
        sums_ref, [column_sum(grad * scaled), column_sum(grad), column_sum(grad_shifted), *bias_rows]
    )


def input_grads(nat, owns, far, weight, pieces, rows, lead, grad_middle, gain, chunk):
    count, width = rows.shape
    row = pl.BlockSpec((chunk, width), lambda j, nat: (j, 0))
    heads = lambda d: pl.BlockSpec((3, chunk, d.shape[2]), lambda j, nat: (0, j, 0))
    steps = count // chunk
    half = pl.BlockSpec((chunk, width), lambda j, nat: (jnp.maximum(j - steps // 2, 0), 0))
    return kernel_call(
        functools.partial(input_grad_kernel, len(owns)),
        "input_grads",
        (steps,),
        [nat],
        [
            (far, heads(far)),
            (weight, whole(weight)),
            (rows, row),
            (lead, whole(lead)),
            (grad_middle, row),
            (gain, whole(gain)),
        ]
        + [(d, heads(d)) for d in owns]
        + [(p, whole(p)) for p in pieces],
        [
            (struct((count, width), F32), row),
            (struct((count // 2, width)), half),
            (struct((8, width), F32), pl.BlockSpec((8, width), lambda j, nat: (0, 0))),
        ],
        [pltpu.VMEM((chunk, width), F32)],
        time=14,
        pinned=[0, 1, 2, 4, *range(6, 6 + len(owns) + len(pieces))],
    )


def pack_kernel(buckets, flags_ref, one_ref, two_ref, own_ref, far_ref, out_ref):
    width = one_ref.shape[1]
    half = width // 2
    first = flags_ref[0] == 0
    rows = lax.broadcasted_iota(jnp.int32, (buckets, width), 0)
    out_ref[:buckets] = jnp.where(rows == flags_ref[7], one_ref[2:3], 0.0)
    out_ref[buckets : buckets + 2] = one_ref[:2]
    out_ref[buckets + 2 : buckets + 6] = two_ref[:4]
    bias = one_ref[3:5]
    swapped = jnp.concatenate([bias[:, half:], bias[:, :half]], axis=1)
    out_ref[buckets + 6 : buckets + 8] = jnp.where(first, bias, swapped)
    own, far = own_ref[...], far_ref[...]
    count = own.shape[1] // width
    for k in range(count):
        columns = slice(k * width, (k + 1) * width)
        low, high = own[:, columns], far[:, columns]
        out_ref[buckets + 8 + k : buckets + 9 + k] = jnp.where(first, low, high)
        out_ref[buckets + 8 + count + k : buckets + 9 + count + k] = jnp.where(first, high, low)


def pack_vectors(flags, buckets, one, two, own, far):
    width = one.shape[1]
    rows = buckets + 8 + 2 * own.shape[1] // width
    return kernel_call(
        functools.partial(pack_kernel, buckets),
        "pack_vectors",
        (1,),
        [flags],
        [(v, whole(v)) for v in (one, two, own, far)],
        [(struct((rows, width), F32), pl.BlockSpec((rows, width), lambda *_: (0, 0)))],
        vmem=8,
        time=1,
    )[0]


def finish_turned_kernel(_, *refs):
    *pieces, out_ref = refs
    for k, piece in enumerate(pieces):

        @pl.when(pl.program_id(0) == k)
        def _(piece=piece):
            out_ref[...] = piece[...].astype(F32).T


def finish_turned(nat, pieces):
    rows, columns = pieces[0].shape
    return kernel_call(
        finish_turned_kernel,
        "finish",
        (4,),
        [nat],
        [(p, whole(p)) for p in pieces],
        [(struct((columns, 4 * rows), F32), pl.BlockSpec((columns, rows), lambda s, nat: (0, nat[s])))],
        vmem=16,
        time=2,
    )[0]


def source_spec(block, which, steps, place):
    def index(s, j, *_):
        return place(jnp.where(s == which, j, jnp.where(s < which, 0, steps - 1)))

    return pl.BlockSpec(block, index)


def finish_rows_kernel(_, *refs):
    *pieces, out_ref = refs
    for k, piece in enumerate(pieces):

        @pl.when(pl.program_id(0) == k)
        def _(piece=piece):
            out_ref[...] = piece[0].astype(F32)


def finish_rows(at, pieces):
    halves, rows, columns = pieces[0].shape
    block = (1, rows, columns)
    return kernel_call(
        finish_rows_kernel,
        "finish",
        (2, halves),
        [at],
        [(p, source_spec(block, k, halves, lambda j: (j, 0, 0))) for k, p in enumerate(pieces)],
        [
            (
                struct((2 * halves * rows, columns), F32),
                pl.BlockSpec((rows, columns), lambda s, j, at: (at[s] * halves + j, 0)),
            )
        ],
        vmem=20,
        time=5,
    )[0]


def finish_columns_kernel(at_ref, mine_ref, theirs_ref, out_ref):
    first = at_ref[0] == 0
    one, two = mine_ref[0].astype(F32), theirs_ref[0].astype(F32)
    columns = one.shape[1]
    out_ref[:, :columns] = jnp.where(first, one, two)
    out_ref[:, columns:] = jnp.where(first, two, one)


def finish_columns(at, pieces):
    halves, rows, columns = pieces[0].shape
    tile = min(512, rows)
    per = rows // tile
    spec = pl.BlockSpec((1, tile, columns), lambda j, at: (j // per, j % per, 0))
    return kernel_call(
        finish_columns_kernel,
        "finish",
        (halves * per,),
        [at],
        [(p, spec) for p in pieces],
        [(struct((halves * rows, 2 * columns), F32), pl.BlockSpec((tile, 2 * columns), lambda j, at: (j, 0)))],
        vmem=20,
        time=5,
    )[0]


def finish_stack_kernel(count, at_ref, *refs):
    pieces, out_ref = refs[:count], refs[-1]
    for k, piece in enumerate(pieces):

        @pl.when(pl.program_id(0) == k)
        def _(piece=piece):
            out_ref[0] = jnp.concatenate([piece[0, 0].astype(F32), piece[1, 0].astype(F32)], axis=1)


def finish_stack(nat, first, pieces, *so_far):
    _, stack, rows, columns = pieces[0].shape
    block = (2, 1, rows, columns)
    count = len(pieces)
    return kernel_call(
        functools.partial(finish_stack_kernel, count),
        "finish",
        (count, stack),
        [nat],
        [(p, source_spec(block, k, stack, lambda j: (0, j, 0, 0))) for k, p in enumerate(pieces)]
        + [(v, pl.BlockSpec(memory_space=pl.ANY)) for v in so_far],
        [
            (
                struct((stack, 4 * rows, 2 * columns), F32),
                pl.BlockSpec((1, rows, 2 * columns), lambda s, j, nat: (j, nat[first + s], 0)),
            )
        ],
        vmem=16,
        time=3,
        alias=count if so_far else None,
    )[0]


def hold(*values):
    return lax.optimization_barrier(values)


def fast_body(
    tokens,
    cotangent,
    buckets,
    counts,
    lead_table,
    norm1_gain,
    norm1_shift,
    w_qkv,
    qv_bias,
    w_out,
    out_bias,
    norm2_gain,
    norm2_shift,
    w_fc1,
    fc1_bias,
    w_fc2,
    fc2_bias,
):
    replicas = lax.axis_size("dp")
    levels = replicas.bit_length() - 1
    dp_at, mp_at = lax.axis_index("dp"), lax.axis_index("mp")
    bits = [(dp_at >> level) & 1 for level in range(levels)]

    def over_x(value):
        return lax.ppermute(value, "mp", [(0, 1), (1, 0)])

    def over(level, value):
        return over_mask(1 << level, value)

    def over_mask(mask, value):
        return lax.ppermute(value, "dp", [(i, i ^ mask) for i in range(replicas)])

    def joined(bit, mine, theirs, axis=0):
        return jnp.where(
            bit == 0,
            jnp.concatenate([mine, theirs], axis),
            jnp.concatenate([theirs, mine], axis),
        )

    def part(value, index, count, axis=0):
        size = value.shape[axis] // count
        return lax.dynamic_slice_in_dim(value, index * size, size, axis)

    half_rows, width = tokens.shape[1:]
    heads_width = w_qkv.shape[2]
    units = w_fc1.shape[1]
    chunk = 256
    core, side = bits[0], bits[1]
    bucket = lax.dynamic_index_in_dim(buckets, mp_at, 0, keepdims=False)
    at = jnp.stack([mp_at, core, 1 - core, side, 1 - side, bits[2], bits[3], bucket]).astype(jnp.int32)
    mine = core * 2 + side
    shared_nat = jnp.stack([mine, mine ^ 1, mine ^ 2, mine ^ 3]).astype(jnp.int32)
    core_first_nat = jnp.stack([mine, mine ^ 2, mine ^ 1, mine ^ 3]).astype(jnp.int32)

    def row_of(vector):
        return vector.astype(F32)[None]

    small = jnp.concatenate([qv_bias.reshape(-1), fc1_bias])
    small_rows = -(-small.shape[0] // width)
    small_rows_padded = -(-small_rows // 16) * 16
    small = jnp.pad(small, (0, small_rows_padded * width - small.shape[0])).reshape(-1, width)
    token_recv = over_x(jnp.concatenate([part(tokens, 1 - mp_at, 2)[0], small]))

    count_f = counts.astype(F32)
    loss_weight = jnp.mean(count_f) / lax.dynamic_index_in_dim(count_f, bucket, 0, keepdims=False)
    loss_row = jnp.broadcast_to(loss_weight, (1, width))
    lead = lax.dynamic_index_in_dim(lead_table, bucket, 0).astype(F32)
    own_qkv = jnp.transpose(w_qkv, (1, 0, 2))

    def bias_three(bias):
        bias_f = bias.astype(F32)
        return jnp.stack([bias_f[0], jnp.zeros_like(bias_f[0]), bias_f[1]])

    (
        token_recv, qkv_send, out_send, fc1_send, cot_send, fc2_send, at, shared_nat, core_first_nat, loss_row, loss_weight, lead,
        gain_one, gain_two, shift_one, shift_two, out_row, fc1_row, fc2_row, own_bias,
    ) = hold(
        token_recv,
        part(own_qkv, mine, 4, 1),
        part(w_out, core, 2),
        part(w_fc1, mine, 4),
        part(cotangent, 1 - mp_at, 2)[0],
        part(w_fc2, core, 2),
        at,
        shared_nat,
        core_first_nat,
        loss_row,
        loss_weight,
        lead,
        row_of(norm1_gain),
        row_of(norm2_gain),
        row_of(norm1_shift),
        row_of(norm2_shift),
        row_of(out_bias),
        row_of(fc1_bias),
        row_of(fc2_bias),
        bias_three(qv_bias),
    )
    keep_half, send_half, pair_nat = at[1:2], at[2:3], at[1:3]
    far_small = token_recv[half_rows:].reshape(-1)
    far_bias = bias_three(far_small[: 2 * heads_width].reshape(2, heads_width))
    far_fc1_bias = row_of(far_small[2 * heads_width : 2 * heads_width + units])

    qkv_x = over_x(qkv_send)
    rows, normed_one, own_heads = project_own(
        at[:1], tokens, token_recv, lead, gain_one, shift_one, own_qkv, own_bias, chunk
    )
    own_heads, qkv_x, out_send, fc1_send, far_bias, far_fc1_bias = hold(
        own_heads, qkv_x, out_send, fc1_send, far_bias, far_fc1_bias
    )

    qkv_y = over(1, qkv_x)
    out_x = over_x(out_send)
    fc1_x = over_x(fc1_send)
    own_attended, own_powers, own_inverse = attend(own_heads)
    own_attended, qkv_x, qkv_y, out_x = hold(own_attended, qkv_x, qkv_y, out_x)

    far_qkv = [qkv_x, qkv_y, over(0, qkv_x), over(0, qkv_y)]
    far_out = [out_x, over(0, out_x)]
    far_heads = project_far(shared_nat, normed_one, far_bias, far_qkv)
    far_heads, fc1_x, cot_send = hold(far_heads, fc1_x, cot_send)

    fc1_y = over(1, fc1_x)
    cot_recv = over_x(cot_send)
    far_attended, far_powers, far_inverse = attend(far_heads)
    middle, normed_two = middle_layer(
        pair_nat, own_attended, far_attended, w_out, far_out, rows, lead,
        out_row, gain_two, shift_two, chunk,
    )
    normed_two, fc1_x, fc1_y, cot_recv, fc2_send = hold(
        normed_two, fc1_x, fc1_y, cot_recv, fc2_send
    )

    def mine_y(flags):
        return flags[3]

    def theirs_y(flags):
        return flags[4]

    def mine_z(flags):
        return flags[5]

    def theirs_z(flags):
        return 1 - flags[5]

    def mine_z2(flags):
        return flags[6]

    def theirs_z2(flags):
        return 1 - flags[6]

    def zero(_):
        return 0

    def one(_):
        return 1

    def first_y(own_down, far_down):
        size = own_down.shape[0] // 2
        return (2 * size, own_down.shape[1]), [
            (None, 0, [term(own_down, theirs_y, size)]),
            (None, size, [term(far_down, theirs_y, size)]),
        ]

    def second_y(own_up, recv_x):
        size = own_up.shape[0] // 2
        return summed((size, own_up.shape[1]), term(own_up, theirs_y, size), term(recv_x, theirs_y, size))

    def second_x(far_down, recv_y):
        size = far_down.shape[0] // 2
        return summed((size, far_down.shape[1]), term(far_down, mine_y, size), term(recv_y, one, size))

    def z_half(which, own_up, recv_x, recv_up, own_down, recv_y, recv_down):
        size = own_up.shape[0] // 4

        def within(side_of, start=0):
            return lambda flags: (start + side_of(flags)) * 2 + which(flags)

        upper = [term(own_up, within(mine_y), size), term(recv_x, within(mine_y), size), term(recv_up, which, size)]
        lower = [term(own_down, within(mine_y), size), term(recv_y, within(zero), size), term(recv_down, which, size)]
        return (2, size, own_up.shape[1]), [(0, None, upper), (1, None, lower)]

    def z_sides(mine, recv):
        shape = list(mine.shape)
        shape[-2] *= 2
        return tuple(shape), [(None, mine_z, [term(mine)]), (None, theirs_z, [term(recv)])]

    def y_sides(mine, recv):
        shape = list(mine.shape)
        shape[-2] *= 2
        return tuple(shape), [(None, mine_y, [term(mine)]), (None, theirs_y, [term(recv)])]

    masks = {1: 8, 2: 4, 3: 12}

    def quarter_z(k):
        def index(flags):
            first = 1 - flags[5] if k & 2 else flags[5]
            second = 1 - flags[6] if k & 1 else flags[6]
            return first * 2 + second

        return index

    fc2_x = over_x(fc2_send)
    far_fc1 = [fc1_x, fc1_y, over(0, fc1_x), over(0, fc1_y)]
    cot_rows = jnp.concatenate([part(cotangent, mp_at, 2)[0], cot_recv])
    grad_low = (cot_rows.astype(F32) * loss_weight).astype(BF16)
    own_hidden, own_slope = hidden_layer(shared_nat, normed_two, fc1_row, [w_fc1], chunk)
    far_hidden, far_slope = hidden_layer(shared_nat, normed_two, far_fc1_bias, far_fc1, chunk)
    far_send = grad_right_half(send_half, far_hidden, grad_low)
    own_send = grad_right_half(send_half, own_hidden, grad_low)
    own_pre, own_fc1_bias = pre_grad_own(grad_low, w_fc2, own_slope)
    fc1_own_send = grad_left_half(send_half, normed_two, own_pre)
    far_send, own_send, fc2_x, grad_low, far_hidden, own_pre, fc1_own_send = hold(
        far_send, own_send, fc2_x, grad_low, far_hidden, own_pre, fc1_own_send
    )

    far_recv, own_recv, fc2_core, fc1_own_recv = over(0, far_send), over(0, own_send), over(0, fc2_x), over(0, fc1_own_send)
    far_up, far_down = grad_right_half(keep_half, far_hidden, grad_low, far_recv)
    own_up, own_down = grad_right_half(keep_half, own_hidden, grad_low, own_recv)
    far_up, far_down, own_up, own_down, fc2_core, fc1_own_recv = hold(
        far_up, far_down, own_up, own_down, fc2_core, fc1_own_recv
    )

    half_width = width // 2
    fc2_x1 = over_x(far_up)
    fc2_y1 = over(1, combine(at, first_y(own_down, far_down))[0])
    far_fc2 = [fc2_x, fc2_core]
    far_pre, far_fc1_bias_sum = pre_grad_far(pair_nat, grad_low, far_fc2, far_slope)
    fc1_far_send = grad_left_half(send_half, normed_two, far_pre)
    fc1_own_up, fc1_own_down = grad_left_half(keep_half, normed_two, own_pre, fc1_own_recv, split=True)
    chunks = half_rows // chunk
    mlp_low = output_own(chunks, chunks, own_hidden, w_fc2, chunk)
    fc1_far_send, fc1_own_up, fc1_own_down, fc2_x1, fc2_y1, far_pre, mlp_low = hold(
        fc1_far_send, fc1_own_up, fc1_own_down, fc2_x1, fc2_y1, far_pre, mlp_low
    )

    send_y, send_x = combine(at, second_y(own_up, fc2_x1), second_x(far_down, fc2_y1))
    fc2_y2, fc2_x2 = over(1, send_y), over_x(send_x)
    fc1_far_recv = over(0, fc1_far_send)
    grad_middle, grad_branch, sums_two = middle_grad(
        shared_nat, at[:1], own_pre, far_pre, w_fc1, far_fc1, middle, cotangent, cot_recv, loss_row, gain_two, chunk
    )
    own_grad_att, far_grad_att = attended_grad(pair_nat, grad_branch, w_out, far_out, chunk)
    out_far_send = grad_left_half(send_half, grad_branch, far_attended)
    out_own_send = grad_left_half(send_half, grad_branch, own_attended)
    fc1_far_up, fc1_far_down = grad_left_half(keep_half, normed_two, far_pre, fc1_far_recv, split=True)
    out_far_recv, out_own_recv = over(0, out_far_send), over(0, out_own_send)
    out_far_sum = grad_left_half(keep_half, grad_branch, far_attended, out_far_recv)
    out_own_sum = grad_left_half(keep_half, grad_branch, own_attended, out_own_recv)
    far_grad_att, own_grad_att, fc2_y2, fc2_x2, fc1_far_up, fc1_far_down, out_far_sum, out_own_sum = hold(
        far_grad_att, own_grad_att, fc2_y2, fc2_x2, fc1_far_up, fc1_far_down, out_far_sum, out_own_sum
    )

    fc2_terms = (own_up, fc2_x1, fc2_y2, own_down, fc2_y1, fc2_x2)
    fc2_send, fc2_mine, send_y = combine(
        at, z_half(theirs_z, *fc2_terms), z_half(mine_z, *fc2_terms), first_y(fc1_own_down, fc1_far_down)
    )
    fc1_x1, fc1_y1, fc2_recv = over_x(fc1_far_up), over(1, send_y), over(2, fc2_send)
    pairs = heads_width // (2 * HD)
    far_dqkv = attend_back(0, pairs, far_heads, far_powers, far_inverse, far_attended, far_grad_att)
    far_dqkv, own_grad_att, fc1_x1, fc1_y1, out_far_sum, fc2_recv = hold(
        far_dqkv, own_grad_att, fc1_x1, fc1_y1, out_far_sum, fc2_recv
    )

    half_rows_out = half_width // 2
    out_shape = (half_rows_out, heads_width)
    z_shape = (2, fc2_mine.shape[1] // 2, fc2_mine.shape[2])
    send_y, send_x, fc2_send, fc2_mine = combine(
        at,
        second_y(fc1_own_up, fc1_x1),
        second_x(fc1_far_down, fc1_y1),
        summed(z_shape, term(fc2_mine, theirs_z2, z_shape[1]), term(fc2_recv, theirs_z2, z_shape[1])),
        summed(z_shape, term(fc2_mine, mine_z2, z_shape[1]), term(fc2_recv, mine_z2, z_shape[1])),
    )
    fc1_y2, fc1_x2, fc2_recv, out_recv = over(1, send_y), over_x(send_x), over(3, fc2_send), over_x(out_far_sum)
    qkv_far_recv = over(0, grad_left_half(send_half, normed_one, far_dqkv))
    qkv_far_keep = grad_left_half(keep_half, normed_one, far_dqkv)
    own_a = attend_back(0, pairs // 2, own_heads, own_powers, own_inverse, own_attended, own_grad_att)
    own_a_send = grad_left_half(send_half, normed_one, own_a)
    own_a_send, own_grad_att, fc1_y2, fc1_x2, out_recv, qkv_far_recv, qkv_far_keep, fc2_recv = hold(
        own_a_send, own_grad_att, fc1_y2, fc1_x2, out_recv, qkv_far_recv, qkv_far_keep, fc2_recv
    )

    side_a = heads_width // 2
    own_a_recv = over(0, own_a_send)
    fc1_terms = (fc1_own_up, fc1_x1, fc1_y2, fc1_own_down, fc1_y1, fc1_x2)
    qkv_send, fc1_send, fc1_mine, fc2_mine, out_send = combine(
        at,
        summed((3, half_width, side_a), term(qkv_far_keep, column=0), term(qkv_far_recv, column=0)),
        z_half(theirs_z, *fc1_terms),
        z_half(mine_z, *fc1_terms),
        summed(fc2_mine.shape, term(fc2_mine), term(fc2_recv)),
        summed(out_shape, term(out_own_sum, theirs_y, half_rows_out), term(out_recv, theirs_y, half_rows_out)),
    )
    qkv_first, fc1_recv, fc2_recv, out_y = over_x(qkv_send), over(2, fc1_send), over(3, fc2_mine), over(1, out_send)
    own_b = attend_back(pairs // 2, pairs - pairs // 2, own_heads, own_powers, own_inverse, own_attended, own_grad_att)
    own_a_sum = grad_left_half(keep_half, normed_one, own_a, own_a_recv)
    own_b_send = grad_left_half(send_half, normed_one, own_b)
    own_b, own_b_send, own_a_sum, fc2_recv, out_y, qkv_first, qkv_far_keep, qkv_far_recv, fc1_recv = hold(
        own_b, own_b_send, own_a_sum, fc2_recv, out_y, qkv_first, qkv_far_keep, qkv_far_recv, fc1_recv
    )

    own_b_recv = over(0, own_b_send)
    a_shape = (3, half_rows_out, side_a)
    qkv_send, fc1_mine, a_send, out_mine, fc2_mine = combine(
        at,
        summed((3, half_width, side_a), term(qkv_far_keep, column=1), term(qkv_far_recv, column=1)),
        summed(fc1_mine.shape, term(fc1_mine), term(fc1_recv)),
        summed(a_shape, term(own_a_sum, theirs_y, half_rows_out), term(qkv_first, theirs_y, half_rows_out)),
        summed(
            out_shape,
            term(out_own_sum, mine_y, half_rows_out),
            term(out_recv, mine_y, half_rows_out),
            term(out_y),
        ),
        ((2, 2 * z_shape[1], z_shape[2]), [(None, mine_z2, [term(fc2_mine)]), (None, theirs_z2, [term(fc2_recv)])]),
    )
    qkv_second, fc1_recv, a_y = over_x(qkv_send), over(3, fc1_mine), over(1, a_send)
    fc2_recv = over(2, fc2_mine)
    grad_shifted, grad_send, sums_one = input_grads(
        shared_nat, [own_a, own_b], far_dqkv, own_qkv, far_qkv, rows, lead, grad_middle, gain_one, chunk
    )
    own_b_sum = grad_left_half(keep_half, normed_one, own_b, own_b_recv)
    grad_shifted, grad_send, sums_one, a_y, qkv_second, own_b_sum, out_mine, fc2_mine, fc2_recv, fc1_recv, own_hidden, far_hidden = hold(
        grad_shifted, grad_send, sums_one, a_y, qkv_second, own_b_sum, out_mine, fc2_mine, fc2_recv, fc1_recv, own_hidden, far_hidden
    )

    b_send, fc2_mine, fc1_mine = combine(
        at,
        summed(a_shape, term(own_b_sum, theirs_y, half_rows_out), term(qkv_second, theirs_y, half_rows_out)),
        z_sides(fc2_mine, fc2_recv),
        summed(fc1_mine.shape, term(fc1_mine), term(fc1_recv)),
    )
    b_y, fc1_recv = over(1, b_send), over(2, fc1_mine)
    grad_recv = over_x(grad_send)
    vectors = pack_vectors(at, counts.shape[0], sums_one, sums_two, own_fc1_bias, far_fc1_bias_sum)
    vectors_recv = over(1, vectors)
    b_y, vectors_recv, fc1_mine, fc1_recv, own_hidden, fc2_mine = hold(
        b_y, vectors_recv, fc1_mine, fc1_recv, own_hidden, fc2_mine
    )

    z_rows = half_rows_out // 4

    def qkv_quarter(k):
        def within(flags):
            return mine_y(flags) * 4 + quarter_z(k)(flags)

        parts = [
            (side_k, None, [term(total, within, z_rows), term(recv, within, z_rows), term(recv_y, quarter_z(k), z_rows)])
            for side_k, (total, recv, recv_y) in enumerate(((own_a_sum, qkv_first, a_y), (own_b_sum, qkv_second, b_y)))
        ]
        return (2, 3, z_rows, side_a), parts

    *qkv_sends, qkv_mine, fc1_mine = combine(
        at,
        *[qkv_quarter(k) for k in masks],
        qkv_quarter(0),
        z_sides(fc1_mine, fc1_recv),
    )
    qkv_recv = [over_mask(mask, sent) for mask, sent in zip(masks.values(), qkv_sends)]
    fc2_y = over(1, fc2_mine)
    vectors = vectors + vectors_recv
    output_low = output_layer(pair_nat, chunks, chunks, far_hidden, mlp_low, far_fc2, middle, fc2_row, chunk)
    mlp_high = output_own(0, chunks, own_hidden, w_fc2, chunk)
    mlp_high, output_low, grad_recv, vectors, fc1_mine, fc2_mine, fc2_y, *qkv_recv = hold(
        mlp_high, output_low, grad_recv, vectors, fc1_mine, fc2_mine, fc2_y, *qkv_recv
    )

    qkv_mine, fc2_half = combine(
        at,
        summed(qkv_mine.shape, *[term(v) for v in (qkv_mine, *qkv_recv)]),
        y_sides(fc2_mine, fc2_y),
    )
    qkv_parts = [qkv_mine] + [over_mask(mask, qkv_mine) for mask in masks.values()]
    fc1_y = over(1, fc1_mine)
    output_recv = over_x(output_low)
    output_high = output_layer(pair_nat, 0, chunks, far_hidden, mlp_high, far_fc2, middle, fc2_row, chunk)
    out_z = over(2, out_mine)
    fc2_grad = finish_columns(pair_nat, [fc2_half, over(0, fc2_half)])
    vectors, fc1_y, fc2_grad, out_mine, out_z, grad_recv, output_recv, output_high, *qkv_parts = hold(
        vectors, fc1_y, fc2_grad, out_mine, out_z, grad_recv, output_recv, output_high, *qkv_parts
    )

    qkv_mine, fc1_half, out_mine = combine(
        at,
        (
            (2, 3, half_rows_out, side_a),
            [(None, quarter_z(k), [term(v)]) for k, v in zip((0, *masks), qkv_parts)],
        ),
        y_sides(fc1_mine, fc1_y),
        summed(out_shape, term(out_mine), term(out_z)),
    )
    qkv_y, qkv_core = over(1, qkv_mine), over(0, qkv_mine)
    fc1_core = over(0, fc1_half)
    out_z = over(3, out_mine)
    vectors = vectors + over_x(vectors)
    vectors_recv = over(2, vectors)
    input_grad = joined(mp_at, grad_shifted[None, :half_rows], grad_recv[None].astype(F32))
    fc1_grad = finish_rows(pair_nat, [fc1_half, fc1_core])
    qkv_mine, qkv_y, qkv_core, vectors_recv, fc1_grad, out_mine, out_z, input_grad = hold(
        qkv_mine, qkv_y, qkv_core, vectors_recv, fc1_grad, out_mine, out_z, input_grad
    )

    qkv_last = over(0, qkv_y)
    out_mine = combine(at, summed(out_shape, term(out_mine), term(out_z)))[0]
    out_y, out_core = over(1, out_mine), over(0, out_mine)
    qkv_grad = finish_stack(core_first_nat, 0, [qkv_mine, qkv_core])
    block_output = joined(mp_at, output_high[None], output_recv[None])
    vectors = vectors + vectors_recv
    vectors_recv = over(3, vectors)
    qkv_last, qkv_grad, vectors_recv, out_y, out_core, block_output = hold(
        qkv_last, qkv_grad, vectors_recv, out_y, out_core, block_output
    )

    vectors = vectors + vectors_recv
    vectors = vectors + over(0, vectors)
    out_grad = finish_turned(core_first_nat, [out_mine, out_core, out_y, over(0, out_y)])
    qkv_grad = finish_stack(core_first_nat, 2, [qkv_y, qkv_last], qkv_grad)
    qkv_grad = jnp.transpose(qkv_grad, (1, 0, 2))

    table = counts.shape[0]
    lead_grad, singles, rest = vectors[:table], vectors[table : table + 6], vectors[table + 6 :]
    qv_bias_grad = part(rest[:2], mp_at, 2, 1)
    fc1_bias_grad = part(rest[2:].reshape(-1), mp_at, 2)
    return (
        block_output,
        input_grad,
        lead_grad,
        singles[0],
        singles[1],
        qkv_grad,
        qv_bias_grad,
        out_grad,
        singles[4],
        singles[2],
        singles[3],
        fc1_grad,
        fc1_bias_grad,
        fc2_grad,
        singles[5],
    )


def solution(mesh):
    in_specs = (
        P("dp", "mp", None),
        P("dp", "mp", None),
        P("dp"),
        P(),
        P(),
        P(),
        P(),
        P(None, None, "mp"),
        P(None, "mp"),
        P("mp", None),
        P(),
        P(),
        P(),
        P(None, "mp"),
        P("mp"),
        P("mp", None),
        P(),
    )
    out_specs = (
        P("dp", "mp", None),
        P("dp", "mp", None),
        P(),
        P(),
        P(),
        P(None, None, "mp"),
        P(None, "mp"),
        P("mp", None),
        P(),
        P(),
        P(),
        P(None, "mp"),
        P("mp"),
        P("mp", None),
        P(),
    )
    def local(*args):
        replicas = lax.axis_size("dp")
        samples, half_rows, width = args[0].shape
        heads_width, units = args[7].shape[2], args[13].shape[1]
        fits = samples == 2 and lax.axis_size("mp") == 2 and replicas == 16
        even = half_rows % 256 == 0 and width == 2 * heads_width == 1024 and units == 2 * width
        return (fast_body if fits and even else body)(*args)

    return jax.shard_map(local, mesh=mesh, in_specs=in_specs, out_specs=out_specs, check_vma=False)
```
